32 devices in a mesh: rep: 8 (over z, y), shard: 4 (over x, core).
Axes of the slice: x: 2, y: 2, z: 4, core: 2. Of those that a mesh axis runs over, the one named last changes fastest.
Arguments:
- hidden_in: bfloat16 [32768, 768], P(('rep', 'shard')), may hold values from -6 to 6
- mask_ids: int32 [32768], P(('rep', 'shard')), may hold values 0 or 1
- time_ids: int32 [16, 9], replicated, may hold values from 0 to 999
- time_table: float32 [1000, 128], replicated, may hold values from -6 to 6
- w_qkv: bfloat16 [768, 2304], P('shard'), may hold values from -0.21875 to 0.21875
- w_proj: bfloat16 [768, 768], P('shard'), may hold values from -6 to 6
- w_up: bfloat16 [768, 3072], P('shard'), may hold values from -0.21875 to 0.21875
- w_down: bfloat16 [3072, 768], P('shard'), may hold values from -0.109375 to 0.109375
- w_ada: bfloat16 [128, 4608], P('shard'), may hold values from -0.5 to 0.5
- gain_attn: bfloat16 [768], P('shard'), may hold values from 0.25 to 1.75
- gain_mlp: bfloat16 [768], P('shard'), may hold values from 0.25 to 1.75
- bias_up: bfloat16 [3072], P('shard'), may hold values from -3 to 3
- bias_down: bfloat16 [768], P('shard'), may hold values from -3 to 3
- bias_ada: bfloat16 [4608], P('shard'), may hold values from -3 to 3
- mask_embed: bfloat16 [768], P('shard'), may hold values from -6 to 6
- cotangent: bfloat16 [32768, 768], P(('rep', 'shard')), may hold values from -6 to 6
Outputs:
- block_out: bfloat16 [32768, 768], P(('rep', 'shard'))
- grad_hidden: float32 [32768, 768], P(('rep', 'shard'))
- grad_time: float32 [1000, 128], replicated
- grad_qkv: float32 [768, 2304], P('shard')
- grad_proj: float32 [768, 768], P('shard')
- grad_up: float32 [768, 3072], P('shard')
- grad_down: float32 [3072, 768], P('shard')
- grad_ada: float32 [128, 4608], P('shard')
- grad_gain_attn: float32 [768], P('shard')
- grad_gain_mlp: float32 [768], P('shard')
- grad_bias_up: float32 [3072], P('shard')
- grad_bias_down: float32 [768], P('shard')
- grad_bias_ada: float32 [4608], P('shard')
- grad_mask_embed: float32 [768], P('shard')
The draws below stay inside these ranges and needn't reach their ends.
All inputs are finite; a program needn't handle non-finite values. No bound on the sum of `mask_ids` on one device may be relied on, other than what follows from the above.
Results may differ from the reference program's by a relative error of at most 0.0085.
The reference program's roundings to bfloat16 on the way count: a program that leaves them out, or rounds other values in their place, can miss the bound.
Values may be sent and summed in bfloat16 or wider, within the bound.
No kernel may reach another device: no remote copies, remote signals or barrier semaphores. Data moves between devices by JAX's collectives and lax.ppermute only.
A program may use at most 192 MiB of HBM per device.

```python
import jax
import jax.numpy as jnp
from jax import lax

D = 768
HEADS = 12
HDIM = 64
FF = 3072
CDIM = 128
STEPS = 1000
CLEN = 128
CONTS = 8
PROMPT = 1024
PAIR_GROUPS = 1
GROUPS = 16
TOKENS = 32768
N_REP = 8
N_SHARD = 4


def touch_ends(values, own_key, smallest, top_value):
    longest = values.shape.index(max(values.shape))
    spots = []
    for shift in (0, 1):
        where = [jax.random.randint(jax.random.fold_in(own_key, axis), (), 0, length) for axis, length in enumerate(values.shape)]
        where[longest] = (where[longest] + shift) % values.shape[longest]
        spots.append(tuple(where))
    return values.at[spots[0]].set(smallest).at[spots[1]].set(top_value)


def raised(result, rng, source, target, blocks, factor):
    owner, partner = [(jnp.arange(result.shape[dim]) // (result.shape[dim] // blocks)).reshape([-1 if axis == dim else 1 for axis in range(result.ndim)]) for dim in (source, target)]
    chosen = jax.random.permutation(rng, blocks)[partner]
    strong = (owner == chosen) | (owner == (partner + blocks // 2) % blocks)
    return jnp.where(strong, factor * result, result)


def level_of(key, dims, cuts, low, top_value):
    def one(dim, shards_of):
        draws = jax.random.uniform(jax.random.fold_in(jax.random.fold_in(key, 6), dim), (shards_of,), jnp.float32, low / len(cuts), top_value / len(cuts))
        return jnp.repeat(jnp.exp(draws), dims[dim] // shards_of).reshape((-1,) + (1,) * (len(dims) - dim - 1))

    level = one(*cuts[0])
    for cut in cuts[1:]:
        level = level * one(*cut)
    return level


def normal_values(key, dims, width, bound, shards=(), kind=jnp.bfloat16):
    factor_of = level_of(key, dims, shards, -0.22, 0.18) if shards else 1.0
    entries = jax.random.normal(key, dims, jnp.float32) * width * factor_of
    return jnp.minimum(jnp.maximum(entries, -bound), bound).astype(kind)


def heavy_noise(stream_key, shape, deviation, limit, pieces, heavy, kind=jnp.bfloat16):
    drawn = deviation * jax.random.normal(stream_key, shape, jnp.float32)
    if pieces:
        drawn = drawn * level_of(stream_key, shape, pieces, -0.22, 0.18)
    return jnp.clip(raised(drawn, jax.random.fold_in(stream_key, 3), *heavy), -limit, limit).astype(kind)


def setup_inputs(seed: int = 0) -> dict:
    arg_keys = jax.random.split(jax.random.key(seed), 17)
    return {
        "hidden_in": heavy_noise(arg_keys[0], (TOKENS, D), 1.0, 6.0, ((0, 32),), (0, 1, 32, 2.75)),
        "mask_ids": touch_ends((jax.random.randint(arg_keys[1], (TOKENS,), 0, 4) < 1).astype(jnp.int32), jax.random.fold_in(arg_keys[1], 1), 0, 1),
        "time_ids": touch_ends(jax.random.randint(arg_keys[2], (GROUPS, CONTS + 1), 0, STEPS), jax.random.fold_in(arg_keys[2], 1), 0, STEPS - 1).astype(jnp.int32),
        "time_table": normal_values(arg_keys[3], (STEPS, CDIM), 1.0, 6.0, (), jnp.float32),
        "w_qkv": normal_values(arg_keys[4], (D, 3 * D), D ** -0.5, 0.21875, ((0, 4),)),
        "w_proj": normal_values(arg_keys[5], (D, D), (max(1, D // PROMPT)) ** -0.5, 6.0, ((0, 4),)),
        "w_up": normal_values(arg_keys[6], (D, FF), D ** -0.5, 0.21875, ((0, 4),)),
        "w_down": normal_values(arg_keys[7], (FF, D), FF ** -0.5, 0.109375, ((0, 4),)),
        "w_ada": normal_values(arg_keys[8], (CDIM, 6 * D), CDIM ** -0.5, 0.5, ((0, 4),)),
        "gain_attn": jnp.clip(1.0 + 0.15 * jax.random.normal(arg_keys[9], (D,), jnp.float32), 0.25, 1.75).astype(jnp.bfloat16),
        "gain_mlp": jnp.clip(1.0 + 0.15 * jax.random.normal(arg_keys[10], (D,), jnp.float32), 0.25, 1.75).astype(jnp.bfloat16),
        "bias_up": normal_values(arg_keys[11], (FF,), 0.5, 3.0, ((0, 4),)),
        "bias_down": normal_values(arg_keys[12], (D,), 0.5, 3.0, ((0, 4),)),
        "bias_ada": normal_values(arg_keys[13], (6 * D,), 0.5, 3.0, ((0, 4),)),
        "mask_embed": normal_values(arg_keys[14], (D,), 1.0, 6.0, ((0, 4),)),
        "cotangent": normal_values(arg_keys[15], (TOKENS, D), 1.0, 6.0, ((0, 32),)),
    }


@jax.custom_vjp
def low(v):
    return lax.optimization_barrier(v.astype(jnp.bfloat16)).astype(jnp.float32)

@jax.custom_vjp
def low_back(v):
    return v

def low_keep(v):
    return (low(v), None)

def low_pass(kept, grad):
    return (grad,)

def back_keep(v):
    return (v, None)

def back_low(kept, grad):
    return (low(grad),)
low.defvjp(low_keep, low_pass)
low_back.defvjp(back_keep, back_low)
eps_norm = 1e-06

def matmul(left_mat, right_mat):
    return jnp.dot(left_mat, right_mat, preferred_element_type=jnp.float32, precision=lax.Precision.HIGHEST)

def einsum_exact(form, left_mat, right_mat):
    return jnp.einsum(form, left_mat, right_mat, precision=lax.Precision.HIGHEST)

def layer_norm(values):
    mean_value = lax.optimization_barrier(jnp.mean(values, -1, keepdims=True))
    centered = values - mean_value
    return centered * lax.rsqrt(lax.optimization_barrier(jnp.mean(centered * centered, -1, keepdims=True)) + eps_norm)

def rotary(values, angles):
    half_dim = HDIM // 2
    cosine = jnp.cos(angles)[:, None, :]
    sine_val = jnp.sin(angles)[:, None, :]
    first_half = values[..., :half_dim]
    second = values[..., half_dim:]
    return jnp.concatenate([first_half * cosine - second * sine_val, first_half * sine_val + second * cosine], -1)

def softmax_rows(scores):
    shifted = jnp.exp(scores - lax.optimization_barrier(jnp.max(scores, -1, keepdims=True)))
    return shifted / lax.optimization_barrier(jnp.sum(shifted, -1, keepdims=True))

def group_forward(params, tokens_grp, mask_grp, times_grp):
    w_qkv, w_proj, w_up, w_down, w_ada, gain_attn, gain_mlp, bias_up, bias_down, bias_ada, mask_embed, time_table = params
    row_count = 2 * PROMPT
    cond = time_table[times_grp]
    silu_c = low(jax.nn.silu(cond))
    modul = matmul(silu_c, w_ada) + bias_ada
    tok_mod = jnp.concatenate([jnp.broadcast_to(modul[:1], (PROMPT, 6 * D)), jnp.repeat(modul[1:], CLEN, axis=0)], 0)
    shift_attn, scale_attn, gate_attn, shift_mlp, scale_mlp, gate_mlp = jnp.split(tok_mod, 6, axis=1)
    start = jnp.where(mask_grp[:, None] == 1, mask_embed[None, :], tokens_grp)
    attn_input = low(layer_norm(start) * gain_attn * (1.0 + scale_attn) + shift_attn)
    qkv = low_back(matmul(attn_input, w_qkv))
    places = jnp.arange(PROMPT, dtype=jnp.int32)
    positions = jnp.concatenate([places, PROMPT + places % CLEN], 0).astype(jnp.float32)
    freqs = 10000.0 ** (-(2.0 * jnp.arange(HDIM // 2, dtype=jnp.float32)) / HDIM)
    angles = positions[:, None] * freqs[None, :]
    queries = low(rotary(qkv[:, :D].reshape(row_count, HEADS, HDIM), angles))
    keys_all = low(rotary(qkv[:, D:2 * D].reshape(row_count, HEADS, HDIM), angles))
    values_all = low(qkv[:, 2 * D:].reshape(row_count, HEADS, HDIM))
    scaling = HDIM ** (-0.5)
    query_pr, key_pr, value_pr = (queries[:PROMPT], keys_all[:PROMPT], values_all[:PROMPT])
    query_co = queries[PROMPT:].reshape(CONTS, CLEN, HEADS, HDIM)
    key_co = keys_all[PROMPT:].reshape(CONTS, CLEN, HEADS, HDIM)
    value_co = values_all[PROMPT:].reshape(CONTS, CLEN, HEADS, HDIM)
    score_pp = low_back(scaling * einsum_exact('qhd,khd->hqk', query_pr, key_pr))
    prob_pp = low(softmax_rows(score_pp))
    out_pr = einsum_exact('hqk,khd->qhd', prob_pp, value_pr)
    score_cp = einsum_exact('cqhd,khd->hcqk', query_co, key_pr)
    score_cc = einsum_exact('cqhd,ckhd->hcqk', query_co, key_co)
    score_co = low_back(scaling * jnp.concatenate([score_cp, score_cc], -1))
    prob_co = low(softmax_rows(score_co))
    out_co = einsum_exact('hcqk,khd->cqhd', prob_co[..., :PROMPT], value_pr) + einsum_exact('hcqk,ckhd->cqhd', prob_co[..., PROMPT:], value_co)
    attn_o = low(low_back(jnp.concatenate([out_pr.reshape(PROMPT, D), out_co.reshape(PROMPT, D)], 0)))
    attn_proj = low_back(matmul(attn_o, w_proj))
    middle = start + gate_attn * attn_proj
    mlp_input = low(layer_norm(middle) * gain_mlp * (1.0 + scale_mlp) + shift_mlp)
    pre_act = low_back(matmul(mlp_input, w_up) + bias_up)
    act_low = low(jax.nn.gelu(pre_act, approximate=True))
    mlp_out = low_back(matmul(act_low, w_down) + bias_down)
    return middle + gate_mlp * mlp_out

def reference(hidden_in, mask_ids, time_ids, time_table, w_qkv, w_proj, w_up, w_down, w_ada, gain_attn, gain_mlp, bias_up, bias_down, bias_ada, mask_embed, cotangent):
    weights = (w_qkv, w_proj, w_up, w_down, w_ada, gain_attn, gain_mlp, bias_up, bias_down, bias_ada, mask_embed)
    params = tuple((array_in.astype(jnp.float32) for array_in in weights)) + (time_table.astype(jnp.float32),)
    pair_count = N_REP * N_SHARD // 2
    half_len = PROMPT // 2

    def to_groups(array_in):
        tail_shape = array_in.shape[1:]
        shaped = array_in.reshape((pair_count, 2, PAIR_GROUPS, 2, half_len) + tail_shape)
        shaped = jnp.transpose(shaped, (0, 2, 3, 1, 4) + tuple(range(5, 5 + len(tail_shape))))
        return shaped.reshape((GROUPS, 2 * PROMPT) + tail_shape)

    def from_groups(array_in):
        tail_shape = array_in.shape[2:]
        shaped = array_in.reshape((pair_count, PAIR_GROUPS, 2, 2, half_len) + tail_shape)
        shaped = jnp.transpose(shaped, (0, 3, 1, 2, 4) + tuple(range(5, 5 + len(tail_shape))))
        return shaped.reshape((TOKENS,) + tail_shape)
    mask_grp = to_groups(mask_ids)

    def forward(param_set, tokens):

        def step(carry_val, scan_item):
            return (carry_val, jax.checkpoint(group_forward)(param_set, scan_item[0], scan_item[1], scan_item[2]))
        carry_val, group_outs = lax.scan(step, jnp.zeros((), jnp.float32), (to_groups(tokens), mask_grp, time_ids))
        return from_groups(group_outs)
    primal, pullback = jax.vjp(forward, params, hidden_in.astype(jnp.float32))
    grad_params, grad_hidden = pullback(cotangent.astype(jnp.float32))
    return (primal.astype(jnp.bfloat16), grad_hidden, grad_params[11], grad_params[0], grad_params[1], grad_params[2], grad_params[3], grad_params[4], grad_params[5], grad_params[6], grad_params[7], grad_params[8], grad_params[9], grad_params[10])
```

```python
from functools import partial

import jax
import jax.numpy as jnp
from jax import lax
from jax.sharding import PartitionSpec as P

D = 768
HEADS = 12
HDIM = 64
STEPS = 1000
CLEN = 128
CONTS = 8
PROMPT = 1024


eps_norm = 1e-06
neg_large = -1e30


def partner(value, axis, apart):
    mask = 2**apart
    pairs = [(source, source ^ mask) for source in range(lax.axis_size(axis))]
    return lax.ppermute(value, axis, pairs)


def bit_masks(size):
    count = size.bit_length() - 1
    return [1 << k if k < 2 else 3 << (k - 1) for k in range(count)]


def swap(value, axis, mask):
    pairs = [(source, source ^ mask) for source in range(lax.axis_size(axis))]
    return lax.ppermute(value, axis, pairs)


def gather_rows(piece):
    size = lax.axis_size("shard")
    mine = lax.axis_index("shard")
    pieces = {0: piece}
    mask = size // 2
    while mask:
        for offset in list(pieces):
            pieces[offset | mask] = swap(pieces[offset], "shard", mask)
        mask //= 2
    rows = piece.shape[0]
    whole = jnp.zeros((rows * size,) + piece.shape[1:], piece.dtype)
    for offset, part in pieces.items():
        whole = lax.dynamic_update_slice_in_dim(whole, part, (mine ^ offset) * rows, 0)
    return whole


def reduce_weight(grad):
    size = lax.axis_size("shard")
    mine = lax.axis_index("shard")
    rows, width = grad.shape[0] // size, grad.shape[1]
    value = grad.astype(jnp.bfloat16)
    mask = 1
    while mask < size:
        bit = (mine // mask) % 2
        halves = value.reshape(-1, 2, rows, width)
        keep = lax.dynamic_index_in_dim(halves, bit, 1, False)
        send = lax.dynamic_index_in_dim(halves, 1 - bit, 1, False)
        got = swap(send, "shard", mask)
        value = (keep.astype(jnp.float32) + got.astype(jnp.float32)).astype(jnp.bfloat16)
        mask *= 2
    value = value.reshape(rows, width)
    for step in bit_masks(lax.axis_size("rep")):
        got = swap(value, "rep", step)
        total = value.astype(jnp.float32) + got.astype(jnp.float32)
        value = total.astype(jnp.bfloat16)
    return total


def reduce_small(values):
    for mask in bit_masks(lax.axis_size("shard")):
        values = values + swap(values, "shard", mask)
    for mask in bit_masks(lax.axis_size("rep")):
        values = values + swap(values, "rep", mask)
    return values


def layer_norm(values):
    mean_value = jnp.mean(values, -1, keepdims=True)
    centered = values - mean_value
    inv_std = lax.rsqrt(jnp.mean(centered * centered, -1, keepdims=True) + eps_norm)
    return (centered * inv_std, inv_std)


def norm_back(gradient, normed, inv_std):
    return inv_std * (
        gradient
        - jnp.mean(gradient, -1, keepdims=True)
        - normed * jnp.mean(gradient * normed, -1, keepdims=True)
    )


def rotary(values, cosine, sine_val):
    half_dim = values.shape[-1] // 2
    first_half = values[..., :half_dim]
    second = values[..., half_dim:]
    return jnp.concatenate(
        [first_half * cosine - second * sine_val, first_half * sine_val + second * cosine], -1
    )


def product(left_mat, right_mat):
    return jnp.dot(left_mat, right_mat, preferred_element_type=jnp.float32)


def times_trans(left_mat, right_mat):
    return lax.dot_general(
        left_mat, right_mat, (((1,), (1,)), ((), ())), preferred_element_type=jnp.float32
    )


def contract(left_mat, right_mat):
    return lax.dot_general(
        left_mat, right_mat, (((0,), (0,)), ((), ())), preferred_element_type=jnp.float32
    )


def split_heads(values):
    groups = values.shape[0] // PROMPT
    return values.reshape(groups, PROMPT, HEADS, HDIM).transpose(2, 0, 1, 3)


def merge_heads(values):
    groups = values.shape[1]
    return values.transpose(1, 2, 0, 3).reshape(groups * PROMPT, HEADS * HDIM)


def blocks(values):
    return values.reshape(values.shape[0], CONTS, CLEN, HDIM)


def own_allowed():
    return (jnp.arange(CONTS, dtype=jnp.int32) >= CONTS // 2)[None, :, None, None]


def head_forward(operands):
    queries, key_main, value_main, key_own, value_own = operands
    scaling = HDIM ** (-0.5)
    query_blk = blocks(queries)
    score_main = (
        jnp.einsum("gcqd,gkd->gcqk", query_blk, key_main, preferred_element_type=jnp.float32)
        * scaling
    )
    score_own = (
        jnp.einsum(
            "gcqd,gckd->gcqk", query_blk, blocks(key_own), preferred_element_type=jnp.float32
        )
        * scaling
    )
    score_own = jnp.where(own_allowed(), score_own, neg_large)
    row_max = jnp.maximum(jnp.max(score_main, -1), jnp.max(score_own, -1))
    denom_sum = jnp.sum(jnp.exp(score_main - row_max[..., None]), -1) + jnp.sum(
        jnp.exp(score_own - row_max[..., None]), -1
    )
    log_sum = row_max + jnp.log(denom_sum)
    prob_main = jnp.exp(score_main - log_sum[..., None]).astype(jnp.bfloat16)
    prob_own = jnp.exp(score_own - log_sum[..., None]).astype(jnp.bfloat16)
    output = jnp.einsum("gcqk,gkd->gcqd", prob_main, value_main, preferred_element_type=jnp.float32)
    output = output + jnp.einsum(
        "gcqk,gckd->gcqd", prob_own, blocks(value_own), preferred_element_type=jnp.float32
    )
    return (output.reshape(queries.shape[0], PROMPT, HDIM), log_sum)


def head_backward(operands):
    queries, key_main, value_main, key_own, value_own, log_sum, grad_out = operands
    scaling = HDIM ** (-0.5)
    groups = queries.shape[0]
    query_blk = blocks(queries)
    grad_blk = blocks(grad_out)
    key_blk = blocks(key_own)
    score_main = (
        jnp.einsum("gcqd,gkd->gcqk", query_blk, key_main, preferred_element_type=jnp.float32)
        * scaling
    )
    prob_main = jnp.exp(score_main - log_sum[..., None])
    score_own = (
        jnp.einsum("gcqd,gckd->gcqk", query_blk, key_blk, preferred_element_type=jnp.float32)
        * scaling
    )
    score_own = jnp.where(own_allowed(), score_own, neg_large)
    prob_own = jnp.exp(score_own - log_sum[..., None])
    grad_prob_main = jnp.einsum(
        "gcqd,gkd->gcqk", grad_blk, value_main, preferred_element_type=jnp.float32
    )
    grad_prob_own = jnp.einsum(
        "gcqd,gckd->gcqk", grad_blk, blocks(value_own), preferred_element_type=jnp.float32
    )
    row_dot = jnp.sum(grad_prob_main * prob_main, -1) + jnp.sum(grad_prob_own * prob_own, -1)
    grad_value_main = jnp.einsum(
        "gcqk,gcqd->gkd",
        prob_main.astype(jnp.bfloat16),
        grad_blk,
        preferred_element_type=jnp.float32,
    )
    grad_value_own = jnp.einsum(
        "gcqk,gcqd->gckd",
        prob_own.astype(jnp.bfloat16),
        grad_blk,
        preferred_element_type=jnp.float32,
    ).reshape(groups, PROMPT, HDIM)
    grad_score_main = (prob_main * (grad_prob_main - row_dot[..., None])).astype(jnp.bfloat16)
    grad_score_own = (prob_own * (grad_prob_own - row_dot[..., None])).astype(jnp.bfloat16)
    grad_query = jnp.einsum(
        "gcqk,gkd->gcqd", grad_score_main, key_main, preferred_element_type=jnp.float32
    )
    grad_query = grad_query + jnp.einsum(
        "gcqk,gckd->gcqd", grad_score_own, key_blk, preferred_element_type=jnp.float32
    )
    grad_key_main = (
        jnp.einsum("gcqk,gcqd->gkd", grad_score_main, query_blk, preferred_element_type=jnp.float32)
        * scaling
    )
    grad_key_own = (
        jnp.einsum(
            "gcqk,gcqd->gckd", grad_score_own, query_blk, preferred_element_type=jnp.float32
        ).reshape(groups, PROMPT, HDIM)
        * scaling
    )
    return (
        (grad_query * scaling).reshape(groups, PROMPT, HDIM),
        grad_key_main,
        grad_value_main,
        grad_key_own,
        grad_value_own,
    )


def on_device(
    hidden_in,
    mask_ids,
    time_ids,
    time_table,
    w_qkv,
    w_proj,
    w_up,
    w_down,
    w_ada,
    gain_attn,
    gain_mlp,
    bias_up,
    bias_down,
    bias_ada,
    mask_embed,
    cotangent,
):
    vectors = (gain_attn, gain_mlp, bias_up, bias_down, bias_ada, mask_embed)
    lengths = [v.shape[0] for v in vectors]
    row = jnp.pad(jnp.concatenate(vectors), (0, w_ada.shape[1] - sum(lengths)))
    n_shard = lax.axis_size("shard")
    packed = gather_rows(jnp.concatenate([w_ada, row[None]], 0)[None])
    ada_mat = packed[:, :-1].reshape(-1, w_ada.shape[1])
    full_vectors = []
    start_at = 0
    for length in lengths:
        full_vectors.append(packed[:, -1, start_at : start_at + length].reshape(-1))
        start_at += length
    attn_gain, mlp_gain, up_bias, down_bias, ada_bias, embed_vec = full_vectors
    qkv_mat = gather_rows(w_qkv)
    proj_mat = gather_rows(w_proj)
    up_mat = gather_rows(w_up)
    down_mat = gather_rows(w_down)
    shard_index = lax.axis_index("shard")
    rep_index = lax.axis_index("rep")
    half_index = shard_index % 2
    is_first = half_index == 0
    pair_index = (rep_index * lax.axis_size("shard") + shard_index) // 2
    tok_count = hidden_in.shape[0]
    groups = tok_count // PROMPT
    half_len = PROMPT // 2
    shape_four = (groups, CONTS, CLEN, D)
    my_times = lax.dynamic_slice_in_dim(time_ids, pair_index * groups, groups, 0).reshape(-1)
    one_hot = (my_times[:, None] == jnp.arange(STEPS, dtype=jnp.int32)[None, :]).astype(jnp.float32)
    cond = jnp.dot(one_hot, time_table, precision=lax.Precision.HIGHEST)
    silu_value, silu_back = jax.vjp(jax.nn.silu, cond)
    silu_low = silu_value.astype(jnp.bfloat16)
    modul = (product(silu_low, ada_mat) + ada_bias.astype(jnp.float32)).reshape(
        groups, CONTS + 1, 6 * D
    )
    block_ids = jnp.arange(CONTS, dtype=jnp.int32)
    seg_index = jnp.where(
        block_ids < CONTS // 2, 0, 1 + half_index * (CONTS // 2) + block_ids - CONTS // 2
    )
    select = (seg_index[:, None] == jnp.arange(CONTS + 1, dtype=jnp.int32)[None, :]).astype(
        jnp.float32
    )
    tok_mod = jnp.einsum("bs,gsf->gbf", select, modul, precision=lax.Precision.HIGHEST)
    shift_attn, scale_attn, gate_attn, shift_mlp, scale_mlp, gate_mlp = jnp.split(
        tok_mod[:, :, None, :], 6, axis=3
    )
    masked = (mask_ids == 1).reshape(groups, CONTS, CLEN, 1)
    start = jnp.where(
        masked, embed_vec.astype(jnp.float32), hidden_in.astype(jnp.float32).reshape(shape_four)
    )
    normed_attn, inv_attn = layer_norm(start)
    attn_gain_f = attn_gain.astype(jnp.float32)
    attn_input = (
        (normed_attn * attn_gain_f * (1.0 + scale_attn) + shift_attn)
        .astype(jnp.bfloat16)
        .reshape(tok_count, D)
    )
    qkv = product(attn_input, qkv_mat)
    local_ids = jnp.arange(tok_count, dtype=jnp.int32) % PROMPT
    positions = jnp.where(
        local_ids // CLEN < CONTS // 2, half_index * half_len + local_ids, PROMPT + local_ids % CLEN
    ).astype(jnp.float32)
    freqs = 10000.0 ** (-(2.0 * jnp.arange(HDIM // 2, dtype=jnp.float32)) / HDIM)
    angles = positions[:, None] * freqs[None, :]
    cosine = jnp.cos(angles)[:, None, :]
    sine_val = jnp.sin(angles)[:, None, :]
    queries = (
        rotary(qkv[:, :D].reshape(tok_count, HEADS, HDIM), cosine, sine_val)
        .astype(jnp.bfloat16)
        .reshape(tok_count, D)
    )
    keys_low = (
        rotary(qkv[:, D : 2 * D].reshape(tok_count, HEADS, HDIM), cosine, sine_val)
        .astype(jnp.bfloat16)
        .reshape(tok_count, D)
    )
    values_low = qkv[:, 2 * D :].astype(jnp.bfloat16)
    own_keys = keys_low.reshape(groups, PROMPT, D)[:, :half_len]
    own_values = values_low.reshape(groups, PROMPT, D)[:, :half_len]
    received = partner((own_keys, own_values), "shard", 0)
    key_main = jnp.where(
        is_first,
        jnp.concatenate([own_keys, received[0]], 1),
        jnp.concatenate([received[0], own_keys], 1),
    ).reshape(tok_count, D)
    value_main = jnp.where(
        is_first,
        jnp.concatenate([own_values, received[1]], 1),
        jnp.concatenate([received[1], own_values], 1),
    ).reshape(tok_count, D)
    operands = (
        split_heads(queries),
        split_heads(key_main),
        split_heads(value_main),
        split_heads(keys_low),
        split_heads(values_low),
    )
    attn_out, log_sum = lax.map(head_forward, operands)
    attn_low = merge_heads(attn_out).astype(jnp.bfloat16)
    attn_proj = product(attn_low, proj_mat).reshape(shape_four)
    middle = start + gate_attn * attn_proj
    normed_mlp, inv_mlp = layer_norm(middle)
    mlp_gain_f = mlp_gain.astype(jnp.float32)
    mlp_input = (
        (normed_mlp * mlp_gain_f * (1.0 + scale_mlp) + shift_mlp)
        .astype(jnp.bfloat16)
        .reshape(tok_count, D)
    )
    pre_act = product(mlp_input, up_mat) + up_bias.astype(jnp.float32)
    act_value, gelu_back = jax.vjp(partial(jax.nn.gelu, approximate=True), pre_act)
    act_low = act_value.astype(jnp.bfloat16)
    mlp_out = (product(act_low, down_mat) + down_bias.astype(jnp.float32)).reshape(shape_four)
    block_out = (middle + gate_mlp * mlp_out).astype(jnp.bfloat16).reshape(tok_count, D)
    qkv_back, proj_back, up_back, down_back, ada_back = qkv_mat, proj_mat, up_mat, down_mat, ada_mat
    grad_top = cotangent.astype(jnp.float32).reshape(shape_four)
    grad_gate_mlp = jnp.sum(grad_top * mlp_out, 2)
    grad_branch = (gate_mlp * grad_top).astype(jnp.bfloat16).reshape(tok_count, D)
    grad_down = contract(act_low, grad_branch)
    grad_bias_down = jnp.sum(grad_branch.astype(jnp.float32), 0)
    grad_act = times_trans(grad_branch, down_back)
    grad_pre = gelu_back(grad_act)[0].astype(jnp.bfloat16)
    grad_up = contract(mlp_input, grad_pre)
    grad_bias_up = jnp.sum(grad_pre.astype(jnp.float32), 0)
    grad_n_two = times_trans(grad_pre, up_back).reshape(shape_four)
    grad_shift_mlp = jnp.sum(grad_n_two, 2)
    grad_scale_mlp = jnp.sum(grad_n_two * normed_mlp * mlp_gain_f, 2)
    grad_affine_mlp = grad_n_two * (1.0 + scale_mlp)
    grad_gain_mlp = jnp.sum(grad_affine_mlp * normed_mlp, (0, 1, 2))
    grad_middle = grad_top + norm_back(grad_affine_mlp * mlp_gain_f, normed_mlp, inv_mlp)
    grad_gate_attn = jnp.sum(grad_middle * attn_proj, 2)
    grad_att = (gate_attn * grad_middle).astype(jnp.bfloat16).reshape(tok_count, D)
    grad_proj = contract(attn_low, grad_att)
    grad_attn_o = times_trans(grad_att, proj_back).astype(jnp.bfloat16)
    back_ops = operands + (log_sum, split_heads(grad_attn_o))
    grad_queries, grad_key_main, grad_value_main, grad_key_own, grad_value_own = lax.map(
        head_backward, back_ops
    )
    key_main_grp = merge_heads(grad_key_main).reshape(groups, PROMPT, D)
    value_main_grp = merge_heads(grad_value_main).reshape(groups, PROMPT, D)
    mine_keys = jnp.where(is_first, key_main_grp[:, :half_len], key_main_grp[:, half_len:])
    other_keys = jnp.where(is_first, key_main_grp[:, half_len:], key_main_grp[:, :half_len])
    mine_values = jnp.where(is_first, value_main_grp[:, :half_len], value_main_grp[:, half_len:])
    other_values = jnp.where(is_first, value_main_grp[:, half_len:], value_main_grp[:, :half_len])
    returned = partner((other_keys, other_values), "shard", 0)
    zero_half = jnp.zeros((groups, half_len, D), jnp.float32)
    grad_keys = jnp.concatenate([mine_keys + returned[0], zero_half], 1).reshape(
        tok_count, D
    ) + merge_heads(grad_key_own)
    grad_values = jnp.concatenate([mine_values + returned[1], zero_half], 1).reshape(
        tok_count, D
    ) + merge_heads(grad_value_own)
    query_raw = rotary(
        merge_heads(grad_queries).reshape(tok_count, HEADS, HDIM), cosine, -sine_val
    ).reshape(tok_count, D)
    key_raw = rotary(grad_keys.reshape(tok_count, HEADS, HDIM), cosine, -sine_val).reshape(
        tok_count, D
    )
    grad_qkv_low = jnp.concatenate([query_raw, key_raw, grad_values], 1).astype(jnp.bfloat16)
    grad_qkv = contract(attn_input, grad_qkv_low)
    grad_n_one = times_trans(grad_qkv_low, qkv_back).reshape(shape_four)
    grad_shift_attn = jnp.sum(grad_n_one, 2)
    grad_scale_attn = jnp.sum(grad_n_one * normed_attn * attn_gain_f, 2)
    grad_affine_attn = grad_n_one * (1.0 + scale_attn)
    grad_gain_attn = jnp.sum(grad_affine_attn * normed_attn, (0, 1, 2))
    grad_start = grad_middle + norm_back(grad_affine_attn * attn_gain_f, normed_attn, inv_attn)
    grad_hidden = jnp.where(masked, 0.0, grad_start).reshape(tok_count, D)
    grad_mask_embed = jnp.sum(jnp.where(masked, grad_start, 0.0), (0, 1, 2))
    grad_mod = jnp.concatenate(
        [
            grad_shift_attn,
            grad_scale_attn,
            grad_gate_attn,
            grad_shift_mlp,
            grad_scale_mlp,
            grad_gate_mlp,
        ],
        -1,
    )
    grad_seg = jnp.einsum("bs,gbf->gsf", select, grad_mod, precision=lax.Precision.HIGHEST).reshape(
        groups * (CONTS + 1), 6 * D
    )
    grad_ada = lax.dot_general(
        silu_low.astype(jnp.float32),
        grad_seg,
        (((0,), (0,)), ((), ())),
        precision=lax.Precision.HIGHEST,
    )
    grad_bias_ada = jnp.sum(grad_seg, 0)
    grad_silu = lax.dot_general(
        grad_seg,
        ada_back.astype(jnp.float32),
        (((1,), (1,)), ((), ())),
        precision=lax.Precision.HIGHEST,
    )
    grad_cond = silu_back(grad_silu)[0]
    small = (
        grad_gain_attn,
        grad_gain_mlp,
        grad_bias_up,
        grad_bias_down,
        grad_bias_ada,
        grad_mask_embed,
    )
    small_rows = jnp.concatenate(small).reshape(-1, 128)
    n_rows = small_rows.shape[0]
    all_rows = jnp.zeros((n_rows + time_ids.size, 128), jnp.float32)
    all_rows = lax.dynamic_update_slice_in_dim(all_rows, small_rows, 0, 0)
    all_rows = lax.dynamic_update_slice_in_dim(
        all_rows, grad_cond, n_rows + pair_index * grad_cond.shape[0], 0
    )
    all_rows = reduce_small(all_rows)
    hot_all = (time_ids.reshape(-1)[:, None] == jnp.arange(STEPS, dtype=jnp.int32)[None, :]).astype(
        jnp.float32
    )
    grad_time = lax.dot_general(
        hot_all, all_rows[n_rows:], (((0,), (0,)), ((), ())), precision=lax.Precision.HIGHEST
    )
    flat = all_rows[:n_rows].reshape(-1)
    small_out = []
    start_at = 0
    for value in small:
        length = value.shape[0]
        part = flat[start_at : start_at + length].reshape(n_shard, -1)
        small_out.append(lax.dynamic_index_in_dim(part, shard_index, 0, False))
        start_at += length
    return (
        block_out,
        grad_hidden,
        grad_time,
        reduce_weight(grad_qkv),
        reduce_weight(grad_proj),
        reduce_weight(grad_up),
        reduce_weight(grad_down),
        reduce_weight(grad_ada),
    ) + tuple(small_out)


def solution(mesh):
    in_specs = (
        P(("rep", "shard"), None),
        P(("rep", "shard")),
        P(),
        P(),
        P("shard", None),
        P("shard", None),
        P("shard", None),
        P("shard", None),
        P("shard", None),
        P("shard"),
        P("shard"),
        P("shard"),
        P("shard"),
        P("shard"),
        P("shard"),
        P(("rep", "shard"), None),
    )
    out_specs = (
        P(("rep", "shard"), None),
        P(("rep", "shard"), None),
        P(),
        P("shard", None),
        P("shard", None),
        P("shard", None),
        P("shard", None),
        P("shard", None),
        P("shard"),
        P("shard"),
        P("shard"),
        P("shard"),
        P("shard"),
        P("shard"),
    )
    return jax.shard_map(
        on_device, mesh=mesh, in_specs=in_specs, out_specs=out_specs, check_vma=False
    )
```

```python
from functools import partial

import jax
import jax.numpy as jnp
from jax import lax
from jax.experimental import pallas as pl
from jax.experimental.pallas import tpu as pltpu
from jax.sharding import PartitionSpec as P

D = 768
HEADS = 12
HDIM = 64
STEPS = 1000
CLEN = 128
CONTS = 8
PROMPT = 1024


eps_norm = 1e-06


def partner(value, axis, apart):
    mask = 2**apart
    pairs = [(source, source ^ mask) for source in range(lax.axis_size(axis))]
    return lax.ppermute(value, axis, pairs)


def bit_masks(size):
    count = size.bit_length() - 1
    return [1 << k if k < 2 else 3 << (k - 1) for k in range(count)]


def swap(value, axis, mask):
    pairs = [(source, source ^ mask) for source in range(lax.axis_size(axis))]
    return lax.ppermute(value, axis, pairs)


def gather_rows(piece):
    size = lax.axis_size("shard")
    mine = lax.axis_index("shard")
    pieces = {0: piece}
    mask = size // 2
    while mask:
        for offset in list(pieces):
            pieces[offset | mask] = swap(pieces[offset], "shard", mask)
        mask //= 2
    rows = piece.shape[0]
    whole = jnp.zeros((rows * size,) + piece.shape[1:], piece.dtype)
    for offset, part in pieces.items():
        whole = lax.dynamic_update_slice_in_dim(whole, part, (mine ^ offset) * rows, 0)
    return whole


def reduce_weight(grad):
    size = lax.axis_size("shard")
    mine = lax.axis_index("shard")
    rows, width = grad.shape[0] // size, grad.shape[1]
    value = grad.astype(jnp.bfloat16)
    mask = 1
    while mask < size:
        bit = (mine // mask) % 2
        halves = value.reshape(-1, 2, rows, width)
        keep = lax.dynamic_index_in_dim(halves, bit, 1, False)
        send = lax.dynamic_index_in_dim(halves, 1 - bit, 1, False)
        got = swap(send, "shard", mask)
        value = (keep.astype(jnp.float32) + got.astype(jnp.float32)).astype(jnp.bfloat16)
        mask *= 2
    value = value.reshape(rows, width)
    for step in bit_masks(lax.axis_size("rep")):
        got = swap(value, "rep", step)
        total = value.astype(jnp.float32) + got.astype(jnp.float32)
        value = total.astype(jnp.bfloat16)
    return total


def reduce_small(values):
    for mask in bit_masks(lax.axis_size("shard")):
        values = values + swap(values, "shard", mask)
    for mask in bit_masks(lax.axis_size("rep")):
        values = values + swap(values, "rep", mask)
    return values


def layer_norm(values):
    mean_value = jnp.mean(values, -1, keepdims=True)
    centered = values - mean_value
    inv_std = lax.rsqrt(jnp.mean(centered * centered, -1, keepdims=True) + eps_norm)
    return (centered * inv_std, inv_std)


def norm_back(gradient, normed, inv_std):
    return inv_std * (
        gradient
        - jnp.mean(gradient, -1, keepdims=True)
        - normed * jnp.mean(gradient * normed, -1, keepdims=True)
    )


def rotary(values, cosine, sine_val):
    half_dim = values.shape[-1] // 2
    first_half = values[..., :half_dim]
    second = values[..., half_dim:]
    return jnp.concatenate(
        [first_half * cosine - second * sine_val, first_half * sine_val + second * cosine], -1
    )


def product(left_mat, right_mat):
    return jnp.dot(left_mat, right_mat, preferred_element_type=jnp.float32)


def times_trans(left_mat, right_mat):
    return lax.dot_general(
        left_mat, right_mat, (((1,), (1,)), ((), ())), preferred_element_type=jnp.float32
    )


def contract(left_mat, right_mat):
    return lax.dot_general(
        left_mat, right_mat, (((0,), (0,)), ((), ())), preferred_element_type=jnp.float32
    )


def nt(left, right):
    return lax.dot_general(left, right, (((1,), (1,)), ((), ())), preferred_element_type=jnp.float32)


def nn(left, right):
    return lax.dot_general(left, right, (((1,), (0,)), ((), ())), preferred_element_type=jnp.float32)


def head_only(values, head):
    lane = lax.broadcasted_iota(jnp.int32, values.shape, 1)
    return jnp.where((lane < HDIM) if head == 0 else (lane >= HDIM), values, jnp.zeros_like(values))


HALF = PROMPT // 2
TILE = HALF
PAIRS = HEADS // 2


def attn_fwd_kernel(q_ref, k_ref, v_ref, kr_ref, vr_ref, o_ref, lse_ref):
    k_own, kr = k_ref[...], kr_ref[...]
    v_own_t, vr_t = v_ref[...].T, vr_ref[...].T
    for start in range(0, PROMPT, TILE):
        outs = []
        q_tile = q_ref[pl.ds(start, TILE), :]
        cols = [slice(c, c + CLEN) for c in range(0, TILE, CLEN)]
        rows = [slice(start + c, start + c + CLEN) for c in range(0, TILE, CLEN)]
        for head in range(2):
            q_head = head_only(q_tile, head)
            lanes = slice(HDIM * head, HDIM * (head + 1))
            keys = [(nt(k_own[:HALF], q_head)), nt(kr, q_head)]
            if start >= HALF:
                keys.append(jnp.concatenate([nt(k_own[r], q_head[c]) for r, c in zip(rows, cols)], 1))
            top = jnp.max(keys[0], 0, keepdims=True)
            for part in keys[1:]:
                top = jnp.maximum(top, jnp.max(part, 0, keepdims=True))
            powers = [jnp.exp(part - top) for part in keys]
            total = jnp.sum(powers[0], 0, keepdims=True)
            for part in powers[1:]:
                total = total + jnp.sum(part, 0, keepdims=True)
            lse_ref[0, pl.ds(head, 1), pl.ds(start, TILE)] = top + jnp.log(total)
            scale = 1.0 / total
            probs = [(part * scale).astype(jnp.bfloat16) for part in powers]
            out = nn(v_own_t[lanes, :HALF], probs[0]) + nn(vr_t[lanes], probs[1])
            if start >= HALF:
                out = out + jnp.concatenate(
                    [nn(v_own_t[lanes, r], probs[2][:, c]) for r, c in zip(rows, cols)], 1
                )
            outs.append(out)
        o_ref[pl.ds(start, TILE), :] = jnp.concatenate(outs, 0).T.astype(jnp.bfloat16)


def attn_bwd_kernel(
    q_ref, k_ref, v_ref, kr_ref, vr_ref, g_ref, lse_ref, dq_ref, dk_ref, dv_ref, dkr_ref, dvr_ref
):
    k_own, v_own, kr, vr = k_ref[...], v_ref[...], kr_ref[...], vr_ref[...]
    k_own_t, kr_t = k_own.T, kr.T
    first = lax.broadcasted_iota(jnp.int32, (HALF, 2 * HDIM), 1) < HDIM
    for start in range(0, PROMPT, TILE):
        tile = pl.ds(start, TILE)
        q_tile, g_tile = q_ref[tile, :], g_ref[tile, :]
        cols = [slice(c, c + CLEN) for c in range(0, TILE, CLEN)]
        rows = [slice(start + c, start + c + CLEN) for c in range(0, TILE, CLEN)]
        dqs, dks, dvs = [], [], []
        for head in range(2):
            q_head, g_head = head_only(q_tile, head), head_only(g_tile, head)
            lanes = slice(HDIM * head, HDIM * (head + 1))
            scores = [nt(k_own[:HALF], q_head), nt(kr, q_head)]
            dps = [nt(v_own[:HALF], g_head), nt(vr, g_head)]
            if start >= HALF:
                scores.append(jnp.concatenate([nt(k_own[r], q_head[c]) for r, c in zip(rows, cols)], 1))
                dps.append(jnp.concatenate([nt(v_own[r], g_head[c]) for r, c in zip(rows, cols)], 1))
            lse = lse_ref[0, pl.ds(head, 1), tile]
            probs = [jnp.exp(part - lse) for part in scores]
            row_dot = jnp.sum(probs[0] * dps[0], 0, keepdims=True)
            for p_part, d_part in zip(probs[1:], dps[1:]):
                row_dot = row_dot + jnp.sum(p_part * d_part, 0, keepdims=True)
            ds = [(p * (d - row_dot)).astype(jnp.bfloat16) for p, d in zip(probs, dps)]
            probs = [p.astype(jnp.bfloat16) for p in probs]
            dq = nn(k_own_t[lanes, :HALF], ds[0]) + nn(kr_t[lanes], ds[1])
            dk = [nn(ds[0], q_tile), nn(ds[1], q_tile)]
            dv = [nn(probs[0], g_tile), nn(probs[1], g_tile)]
            if start >= HALF:
                dq = dq + jnp.concatenate(
                    [nn(k_own_t[lanes, r], ds[2][:, c]) for r, c in zip(rows, cols)], 1
                )
                dk.append(jnp.concatenate([nn(ds[2][:, c], q_tile[c]) for c in cols], 0))
                dv.append(jnp.concatenate([nn(probs[2][:, c], g_tile[c]) for c in cols], 0))
            dqs.append(dq)
            dks.append(dk)
            dvs.append(dv)
        dq_ref[tile, :] = jnp.concatenate(dqs, 0).T * HDIM**-0.5
        for own_ref, other_ref, parts in ((dk_ref, dkr_ref, dks), (dv_ref, dvr_ref, dvs)):
            merged = [jnp.where(first, a, b) for a, b in zip(*parts)]
            if start == 0:
                own_ref[pl.ds(0, HALF), :] = merged[0]
                other_ref[...] = merged[1]
            else:
                own_ref[pl.ds(0, HALF), :] += merged[0]
                other_ref[...] += merged[1]
                own_ref[tile, :] = merged[2]


VMEM_LIMIT = 60 * 2**20


def lane_block(rows):
    return pl.BlockSpec((rows, 2 * HDIM), lambda pair: (0, pair))


def attn_fwd(q, k, v, kr, vr):
    return pl.pallas_call(
        attn_fwd_kernel,
        grid=(PAIRS,),
        in_specs=[lane_block(PROMPT)] * 3 + [lane_block(HALF)] * 2,
        out_specs=[lane_block(PROMPT), pl.BlockSpec((1, 2, PROMPT), lambda pair: (pair, 0, 0))],
        out_shape=[
            jax.ShapeDtypeStruct((PROMPT, D), jnp.bfloat16),
            jax.ShapeDtypeStruct((PAIRS, 2, PROMPT), jnp.float32),
        ],
        compiler_params=pltpu.CompilerParams(vmem_limit_bytes=VMEM_LIMIT),
        cost_estimate=pl.CostEstimate(flops=12 * 10**9, bytes_accessed=10 * 2**20, transcendentals=14 * 10**6),
    )(q, k, v, kr, vr)


def attn_bwd(q, k, v, kr, vr, g, lse):
    return pl.pallas_call(
        attn_bwd_kernel,
        grid=(PAIRS,),
        in_specs=[lane_block(PROMPT)] * 3
        + [lane_block(HALF)] * 2
        + [lane_block(PROMPT), pl.BlockSpec((1, 2, PROMPT), lambda pair: (pair, 0, 0))],
        out_specs=[lane_block(PROMPT)] * 3 + [lane_block(HALF)] * 2,
        out_shape=[jax.ShapeDtypeStruct((n, D), jnp.float32) for n in (PROMPT, PROMPT, PROMPT, HALF, HALF)],
        compiler_params=pltpu.CompilerParams(vmem_limit_bytes=VMEM_LIMIT),
        cost_estimate=pl.CostEstimate(flops=30 * 10**9, bytes_accessed=24 * 2**20, transcendentals=14 * 10**6),
    )(q, k, v, kr, vr, g, lse)


def on_device(
    hidden_in,
    mask_ids,
    time_ids,
    time_table,
    w_qkv,
    w_proj,
    w_up,
    w_down,
    w_ada,
    gain_attn,
    gain_mlp,
    bias_up,
    bias_down,
    bias_ada,
    mask_embed,
    cotangent,
):
    vectors = (gain_attn, gain_mlp, bias_up, bias_down, bias_ada, mask_embed)
    lengths = [v.shape[0] for v in vectors]
    row = jnp.pad(jnp.concatenate(vectors), (0, w_ada.shape[1] - sum(lengths)))
    n_shard = lax.axis_size("shard")
    packed = gather_rows(jnp.concatenate([w_ada, row[None]], 0)[None])
    ada_mat = packed[:, :-1].reshape(-1, w_ada.shape[1])
    full_vectors = []
    start_at = 0
    for length in lengths:
        full_vectors.append(packed[:, -1, start_at : start_at + length].reshape(-1))
        start_at += length
    attn_gain, mlp_gain, up_bias, down_bias, ada_bias, embed_vec = full_vectors
    qkv_mat = gather_rows(w_qkv)
    proj_mat = gather_rows(w_proj)
    up_mat = gather_rows(w_up)
    down_mat = gather_rows(w_down)
    shard_index = lax.axis_index("shard")
    rep_index = lax.axis_index("rep")
    half_index = shard_index % 2
    pair_index = (rep_index * lax.axis_size("shard") + shard_index) // 2
    tok_count = hidden_in.shape[0]
    groups = tok_count // PROMPT
    half_len = PROMPT // 2
    shape_four = (groups, CONTS, CLEN, D)
    my_times = lax.dynamic_slice_in_dim(time_ids, pair_index * groups, groups, 0).reshape(-1)
    one_hot = (my_times[:, None] == jnp.arange(STEPS, dtype=jnp.int32)[None, :]).astype(jnp.float32)
    cond = jnp.dot(one_hot, time_table, precision=lax.Precision.HIGHEST)
    silu_value, silu_back = jax.vjp(jax.nn.silu, cond)
    silu_low = silu_value.astype(jnp.bfloat16)
    modul = (product(silu_low, ada_mat) + ada_bias.astype(jnp.float32)).reshape(
        groups, CONTS + 1, 6 * D
    )
    block_ids = jnp.arange(CONTS, dtype=jnp.int32)
    seg_index = jnp.where(
        block_ids < CONTS // 2, 0, 1 + half_index * (CONTS // 2) + block_ids - CONTS // 2
    )
    select = (seg_index[:, None] == jnp.arange(CONTS + 1, dtype=jnp.int32)[None, :]).astype(
        jnp.float32
    )
    tok_mod = jnp.einsum("bs,gsf->gbf", select, modul, precision=lax.Precision.HIGHEST)
    shift_attn, scale_attn, gate_attn, shift_mlp, scale_mlp, gate_mlp = jnp.split(
        tok_mod[:, :, None, :], 6, axis=3
    )
    masked = (mask_ids == 1).reshape(groups, CONTS, CLEN, 1)
    start = jnp.where(
        masked, embed_vec.astype(jnp.float32), hidden_in.astype(jnp.float32).reshape(shape_four)
    )
    normed_attn, inv_attn = layer_norm(start)
    attn_gain_f = attn_gain.astype(jnp.float32)
    attn_input = (
        (normed_attn * attn_gain_f * (1.0 + scale_attn) + shift_attn)
        .astype(jnp.bfloat16)
        .reshape(tok_count, D)
    )
    qkv = product(attn_input, qkv_mat)
    local_ids = jnp.arange(tok_count, dtype=jnp.int32) % PROMPT
    positions = jnp.where(
        local_ids // CLEN < CONTS // 2, half_index * half_len + local_ids, PROMPT + local_ids % CLEN
    ).astype(jnp.float32)
    freqs = 10000.0 ** (-(2.0 * jnp.arange(HDIM // 2, dtype=jnp.float32)) / HDIM)
    angles = positions[:, None] * freqs[None, :]
    cosine = jnp.cos(angles)[:, None, :]
    sine_val = jnp.sin(angles)[:, None, :]
    queries = (
        rotary(qkv[:, :D].reshape(tok_count, HEADS, HDIM), cosine, sine_val)
        .reshape(tok_count, D)
    )
    queries = (queries * HDIM**-0.5).astype(jnp.bfloat16)
    keys_low = (
        rotary(qkv[:, D : 2 * D].reshape(tok_count, HEADS, HDIM), cosine, sine_val)
        .astype(jnp.bfloat16)
        .reshape(tok_count, D)
    )
    values_low = qkv[:, 2 * D :].astype(jnp.bfloat16)
    received = partner((keys_low[:half_len], values_low[:half_len]), "shard", 0)
    attn_low, log_sum = attn_fwd(queries, keys_low, values_low, received[0], received[1])
    attn_proj = product(attn_low, proj_mat).reshape(shape_four)
    middle = start + gate_attn * attn_proj
    normed_mlp, inv_mlp = layer_norm(middle)
    mlp_gain_f = mlp_gain.astype(jnp.float32)
    mlp_input = (
        (normed_mlp * mlp_gain_f * (1.0 + scale_mlp) + shift_mlp)
        .astype(jnp.bfloat16)
        .reshape(tok_count, D)
    )
    pre_act = product(mlp_input, up_mat) + up_bias.astype(jnp.float32)
    act_value, gelu_back = jax.vjp(partial(jax.nn.gelu, approximate=True), pre_act)
    act_low = act_value.astype(jnp.bfloat16)
    mlp_out = (product(act_low, down_mat) + down_bias.astype(jnp.float32)).reshape(shape_four)
    block_out = (middle + gate_mlp * mlp_out).astype(jnp.bfloat16).reshape(tok_count, D)
    qkv_back, proj_back, up_back, down_back, ada_back = qkv_mat, proj_mat, up_mat, down_mat, ada_mat
    grad_top = cotangent.astype(jnp.float32).reshape(shape_four)
    grad_gate_mlp = jnp.sum(grad_top * mlp_out, 2)
    grad_branch = (gate_mlp * grad_top).astype(jnp.bfloat16).reshape(tok_count, D)
    grad_down = contract(act_low, grad_branch)
    grad_bias_down = jnp.sum(grad_branch.astype(jnp.float32), 0)
    grad_act = times_trans(grad_branch, down_back)
    grad_pre = gelu_back(grad_act)[0].astype(jnp.bfloat16)
    grad_up = contract(mlp_input, grad_pre)
    grad_bias_up = jnp.sum(grad_pre.astype(jnp.float32), 0)
    grad_n_two = times_trans(grad_pre, up_back).reshape(shape_four)
    grad_shift_mlp = jnp.sum(grad_n_two, 2)
    grad_scale_mlp = jnp.sum(grad_n_two * normed_mlp * mlp_gain_f, 2)
    grad_affine_mlp = grad_n_two * (1.0 + scale_mlp)
    grad_gain_mlp = jnp.sum(grad_affine_mlp * normed_mlp, (0, 1, 2))
    grad_middle = grad_top + norm_back(grad_affine_mlp * mlp_gain_f, normed_mlp, inv_mlp)
    grad_gate_attn = jnp.sum(grad_middle * attn_proj, 2)
    grad_att = (gate_attn * grad_middle).astype(jnp.bfloat16).reshape(tok_count, D)
    grad_proj = contract(attn_low, grad_att)
    grad_attn_o = times_trans(grad_att, proj_back).astype(jnp.bfloat16)
    grad_queries, grad_keys, grad_values, other_keys, other_values = attn_bwd(
        queries, keys_low, values_low, received[0], received[1], grad_attn_o, log_sum
    )
    returned = partner((other_keys, other_values), "shard", 0)
    grad_keys = jnp.concatenate([grad_keys[:half_len] + returned[0], grad_keys[half_len:]], 0)
    grad_values = jnp.concatenate([grad_values[:half_len] + returned[1], grad_values[half_len:]], 0)
    query_raw = rotary(
        grad_queries.reshape(tok_count, HEADS, HDIM), cosine, -sine_val
    ).reshape(tok_count, D)
    key_raw = rotary(grad_keys.reshape(tok_count, HEADS, HDIM), cosine, -sine_val).reshape(
        tok_count, D
    )
    grad_qkv_low = jnp.concatenate([query_raw, key_raw, grad_values], 1).astype(jnp.bfloat16)
    grad_qkv = contract(attn_input, grad_qkv_low)
    grad_n_one = times_trans(grad_qkv_low, qkv_back).reshape(shape_four)
    grad_shift_attn = jnp.sum(grad_n_one, 2)
    grad_scale_attn = jnp.sum(grad_n_one * normed_attn * attn_gain_f, 2)
    grad_affine_attn = grad_n_one * (1.0 + scale_attn)
    grad_gain_attn = jnp.sum(grad_affine_attn * normed_attn, (0, 1, 2))
    grad_start = grad_middle + norm_back(grad_affine_attn * attn_gain_f, normed_attn, inv_attn)
    grad_hidden = jnp.where(masked, 0.0, grad_start).reshape(tok_count, D)
    grad_mask_embed = jnp.sum(jnp.where(masked, grad_start, 0.0), (0, 1, 2))
    grad_mod = jnp.concatenate(
        [
            grad_shift_attn,
            grad_scale_attn,
            grad_gate_attn,
            grad_shift_mlp,
            grad_scale_mlp,
            grad_gate_mlp,
        ],
        -1,
    )
    grad_seg = jnp.einsum("bs,gbf->gsf", select, grad_mod, precision=lax.Precision.HIGHEST).reshape(
        groups * (CONTS + 1), 6 * D
    )
    grad_ada = lax.dot_general(
        silu_low.astype(jnp.float32),
        grad_seg,
        (((0,), (0,)), ((), ())),
        precision=lax.Precision.HIGHEST,
    )
    grad_bias_ada = jnp.sum(grad_seg, 0)
    grad_silu = lax.dot_general(
        grad_seg,
        ada_back.astype(jnp.float32),
        (((1,), (1,)), ((), ())),
        precision=lax.Precision.HIGHEST,
    )
    grad_cond = silu_back(grad_silu)[0]
    small = (
        grad_gain_attn,
        grad_gain_mlp,
        grad_bias_up,
        grad_bias_down,
        grad_bias_ada,
        grad_mask_embed,
    )
    small_rows = jnp.concatenate(small).reshape(-1, 128)
    n_rows = small_rows.shape[0]
    all_rows = jnp.zeros((n_rows + time_ids.size, 128), jnp.float32)
    all_rows = lax.dynamic_update_slice_in_dim(all_rows, small_rows, 0, 0)
    all_rows = lax.dynamic_update_slice_in_dim(
        all_rows, grad_cond, n_rows + pair_index * grad_cond.shape[0], 0
    )
    all_rows = reduce_small(all_rows)
    hot_all = (time_ids.reshape(-1)[:, None] == jnp.arange(STEPS, dtype=jnp.int32)[None, :]).astype(
        jnp.float32
    )
    grad_time = lax.dot_general(
        hot_all, all_rows[n_rows:], (((0,), (0,)), ((), ())), precision=lax.Precision.HIGHEST
    )
    flat = all_rows[:n_rows].reshape(-1)
    small_out = []
    start_at = 0
    for value in small:
        length = value.shape[0]
        part = flat[start_at : start_at + length].reshape(n_shard, -1)
        small_out.append(lax.dynamic_index_in_dim(part, shard_index, 0, False))
        start_at += length
    return (
        block_out,
        grad_hidden,
        grad_time,
        reduce_weight(grad_qkv),
        reduce_weight(grad_proj),
        reduce_weight(grad_up),
        reduce_weight(grad_down),
        reduce_weight(grad_ada),
    ) + tuple(small_out)


def solution(mesh):
    in_specs = (
        P(("rep", "shard"), None),
        P(("rep", "shard")),
        P(),
        P(),
        P("shard", None),
        P("shard", None),
        P("shard", None),
        P("shard", None),
        P("shard", None),
        P("shard"),
        P("shard"),
        P("shard"),
        P("shard"),
        P("shard"),
        P("shard"),
        P(("rep", "shard"), None),
    )
    out_specs = (
        P(("rep", "shard"), None),
        P(("rep", "shard"), None),
        P(),
        P("shard", None),
        P("shard", None),
        P("shard", None),
        P("shard", None),
        P("shard", None),
        P("shard"),
        P("shard"),
        P("shard"),
        P("shard"),
        P("shard"),
        P("shard"),
    )
    return jax.shard_map(
        on_device, mesh=mesh, in_specs=in_specs, out_specs=out_specs, check_vma=False
    )
```

```python
from functools import partial

import jax
import jax.numpy as jnp
from jax import lax
from jax.experimental import pallas as pl
from jax.experimental.pallas import tpu as pltpu
from jax.sharding import PartitionSpec as P

D = 768
HEADS = 12
HDIM = 64
FF = 3072
STEPS = 1000
CLEN = 128
CONTS = 8
PROMPT = 1024
HALF = PROMPT // 2
PAIRS = HEADS // 2
GROUP = 256
N_GROUP = D // GROUP
TILE = 256
SUB = TILE // CLEN
CHUNK = 512
eps_norm = 1e-06
bf16 = jnp.bfloat16
f32 = jnp.float32
VMEM_LIMIT = 62 * 2**20


def nt(left, right):
    return lax.dot_general(left, right, (((1,), (1,)), ((), ())), preferred_element_type=f32)


def nn(left, right):
    return lax.dot_general(left, right, (((1,), (0,)), ((), ())), preferred_element_type=f32)


def tn(left, right):
    return lax.dot_general(left, right, (((0,), (0,)), ((), ())), preferred_element_type=f32)


def exact(left, right, contract):
    return lax.dot_general(
        left, right, (contract, ((), ())), preferred_element_type=f32, precision=lax.Precision.HIGHEST
    )


def layer_norm(values):
    mean_value = jnp.mean(values, -1, keepdims=True)
    centered = values - mean_value
    inv_std = lax.rsqrt(jnp.mean(centered * centered, -1, keepdims=True) + eps_norm)
    return (centered * inv_std, inv_std)


def norm_back(gradient, normed, inv_std):
    return inv_std * (
        gradient
        - jnp.mean(gradient, -1, keepdims=True)
        - normed * jnp.mean(gradient * normed, -1, keepdims=True)
    )


def rotate(values, cosine, sine):
    lane = lax.broadcasted_iota(jnp.int32, cosine.shape, 1) % HDIM
    out = []
    for col in range(0, values.shape[1], 128):
        part = values[:, col : col + 128]
        other = jnp.where(lane < HDIM // 2, pltpu.roll(part, 96, 1), pltpu.roll(part, 32, 1))
        out.append(part * cosine + other * sine)
    return out[0] if len(out) == 1 else jnp.concatenate(out, 1)


def whole(shape):
    return pl.BlockSpec(shape, lambda *_: (0,) * len(shape))


ANY = pl.BlockSpec(memory_space=pl.ANY)
SCALAR = pl.BlockSpec(memory_space=pltpu.SMEM)


def place(pieces, spec, place_ref, target, sem):
    mine = place_ref[0]
    copies = []
    for (offset, split, part), piece in zip(spec, pieces):
        rows = piece.shape[0]
        if offset is None:
            where = target
        else:
            start = (mine ^ offset) * (split * rows)
            if split > 1:
                start = start + (place_ref[3 if split == 2 else 4] ^ part) * rows
            where = target.at[pl.ds(pl.multiple_of(start, 16), rows)]
        copies.append(pltpu.make_async_copy(piece, where, sem))
    return copies


class Weight:
    def __init__(self, spec, arrays):
        self.spec = tuple(spec)
        self.arrays = list(arrays)
        self.count = len(self.arrays)

    def tied(self, *values):
        arrays, _ = lax.optimization_barrier((self.arrays, values))
        return Weight(self.spec, arrays)


def qkv_kernel(
    spec, place_ref, hid_ref, mask_ref, embed_ref, mods_ref, gain_ref, cos_ref, sin_ref, *rest
):
    n = len(spec)
    pieces = rest[:n]
    x_ref, q_ref, kvp_ref, kvc_ref, w_ref, sem = rest[n:]
    step = pl.program_id(0)

    @pl.when(step == 0)
    def _():
        copies = place(pieces, spec, place_ref, w_ref, sem)
        for copy in copies:
            copy.start()

        @pl.loop(0, CONTS)
        def _(block):
            rows = pl.ds(pl.multiple_of(block * CLEN, CLEN), CLEN)
            start = jnp.where(mask_ref[rows, :] > 0.5, embed_ref[...], hid_ref[rows, :].astype(f32))
            normed, _inv = layer_norm(start)
            row = pl.ds(block, 1)
            shift, scale = mods_ref[row, 0:D], mods_ref[row, D : 2 * D]
            x_ref[rows, :] = (normed * gain_ref[...] * (1.0 + scale) + shift).astype(bf16)

        for copy in copies:
            copy.wait()

    x = x_ref[...]
    cosine, sine = cos_ref[...], sin_ref[...]

    def part(third):
        return nn(x, w_ref[:, pl.ds(pl.multiple_of(third * D + step * GROUP, 128), GROUP)])

    q_ref[...] = (rotate(part(0), cosine, sine) * HDIM**-0.5).astype(bf16)
    k = rotate(part(1), cosine, sine).astype(bf16)
    kvp_ref[0], kvc_ref[0] = k[:HALF], k[HALF:]
    v = part(2).astype(bf16)
    kvp_ref[1], kvc_ref[1] = v[:HALF], v[HALF:]


def qkv_call(place_ids, hidden, mask, embed, mods, gain, cosine, sine, weight):
    n = weight.count
    width = weight.arrays[0].shape[1]
    half = pl.BlockSpec((2, HALF, GROUP), lambda g: (0, 0, g))
    return pl.pallas_call(
        partial(qkv_kernel, weight.spec),
        grid=(N_GROUP,),
        in_specs=[
            SCALAR,
            whole((PROMPT, D)),
            whole((PROMPT, 1)),
            whole((1, D)),
            whole(mods.shape),
            whole((1, D)),
            whole((PROMPT, 128)),
            whole((PROMPT, 128)),
        ]
        + [ANY] * n,
        out_specs=[whole((PROMPT, D)), pl.BlockSpec((PROMPT, GROUP), lambda g: (0, g)), half, half],
        out_shape=[
            jax.ShapeDtypeStruct((PROMPT, D), bf16),
            jax.ShapeDtypeStruct((PROMPT, D), bf16),
            jax.ShapeDtypeStruct((2, HALF, D), bf16),
            jax.ShapeDtypeStruct((2, HALF, D), bf16),
        ],
        scratch_shapes=[pltpu.VMEM((D, width), bf16), pltpu.SemaphoreType.DMA],
        compiler_params=pltpu.CompilerParams(vmem_limit_bytes=VMEM_LIMIT),
        cost_estimate=pl.CostEstimate(flops=4 * 10**9, bytes_accessed=12 * 2**20, transcendentals=0),
        name="qkv",
    )(place_ids, hidden, mask, embed, mods, gain, cosine, sine, *weight.arrays)


def head_only(values, head):
    lane = lax.broadcasted_iota(jnp.int32, values.shape, 1)
    return jnp.where((lane < HDIM) if head == 0 else (lane >= HDIM), values, jnp.zeros_like(values))


def key_parts(prompt, other, own, rows, first):
    parts = [nt(prompt, rows), nt(other, rows)]
    if not first:
        cols = range(0, HALF, CLEN)
        parts.append(
            jnp.concatenate([nt(own[c : c + CLEN], rows[c : c + CLEN]) for c in cols], 1)
        )
    return parts


def attn_fwd_kernel(q_ref, kvp_ref, kvc_ref, kvr_ref, o_ref, lse_ref):
    kp, kc, kr = kvp_ref[0], kvc_ref[0], kvr_ref[0]
    vp_t, vc_t, vr_t = kvp_ref[1].T, kvc_ref[1].T, kvr_ref[1].T
    for start in (0, HALF):
        outs = []
        q_tile = q_ref[pl.ds(start, HALF), :]
        for head in range(2):
            lanes = slice(HDIM * head, HDIM * (head + 1))
            scores = key_parts(kp, kr, kc, head_only(q_tile, head), start == 0)
            top = jnp.max(scores[0], 0, keepdims=True)
            for part in scores[1:]:
                top = jnp.maximum(top, jnp.max(part, 0, keepdims=True))
            powers = [jnp.exp(part - top) for part in scores]
            total = jnp.sum(powers[0], 0, keepdims=True)
            for part in powers[1:]:
                total = total + jnp.sum(part, 0, keepdims=True)
            lse_ref[0, pl.ds(head, 1), pl.ds(start, HALF)] = top + jnp.log(total)
            scale = 1.0 / total
            probs = [(part * scale).astype(bf16) for part in powers]
            out = nn(vp_t[lanes], probs[0]) + nn(vr_t[lanes], probs[1])
            if start:
                cols = [slice(c, c + CLEN) for c in range(0, HALF, CLEN)]
                out = out + jnp.concatenate([nn(vc_t[lanes, c], probs[2][:, c]) for c in cols], 1)
            outs.append(out)
        o_ref[pl.ds(start, HALF), :] = jnp.concatenate(outs, 0).T.astype(bf16)


def pair_block(rows, first=0):
    return pl.BlockSpec((rows, 2 * HDIM), lambda pair: (0, first + pair))


def pair_half(first=0):
    return pl.BlockSpec((2, HALF, 2 * HDIM), lambda pair: (0, 0, first + pair))


def lse_block(first=0):
    return pl.BlockSpec((1, 2, PROMPT), lambda pair: (first + pair, 0, 0))


def attn_fwd(first, pairs, q, kvp, kvc, kvr, before=None):
    inputs = (q, kvp, kvc, kvr)
    in_specs = [pair_block(PROMPT, first)] + [pair_half(first)] * 3
    body = attn_fwd_kernel
    aliases = {}
    if before is not None:
        inputs += tuple(before)
        in_specs += [ANY, ANY]
        aliases = {4: 0, 5: 1}

        def body(q_ref, kvp_ref, kvc_ref, kvr_ref, _o, _lse, o_ref, lse_ref):
            attn_fwd_kernel(q_ref, kvp_ref, kvc_ref, kvr_ref, o_ref, lse_ref)

    return pl.pallas_call(
        body,
        grid=(pairs,),
        in_specs=in_specs,
        out_specs=[pair_block(PROMPT, first), lse_block(first)],
        out_shape=[
            jax.ShapeDtypeStruct((PROMPT, D), bf16),
            jax.ShapeDtypeStruct((PAIRS, 2, PROMPT), f32),
        ],
        input_output_aliases=aliases,
        compiler_params=pltpu.CompilerParams(vmem_limit_bytes=VMEM_LIMIT),
        cost_estimate=pl.CostEstimate(
            flops=3 * 10**9 * pairs, bytes_accessed=10 * 2**20, transcendentals=0
        ),
        name=f"attn_fwd{first}",
    )(*inputs)


def attn_bwd_kernel(
    _ids, q_ref, kvp_ref, kvc_ref, kvr_ref, g_ref, lse_ref, cos_ref, sin_ref, gq_ref, gc_ref, dp_ref, dr_ref
):
    kp, kc, kr = kvp_ref[0], kvc_ref[0], kvr_ref[0]
    vp, vc, vr = kvp_ref[1], kvc_ref[1], kvr_ref[1]
    kp_t, kc_t, kr_t = kp.T, kc.T, kr.T
    first = lax.broadcasted_iota(jnp.int32, (HALF, 2 * HDIM), 1) < HDIM
    for start in (0, HALF):
        tile = pl.ds(start, HALF)
        q_tile, g_tile = q_ref[tile, :], g_ref[tile, :]
        cols = [slice(c, c + CLEN) for c in range(0, HALF, CLEN)]
        dqs, dks, dvs = [], [], []
        for head in range(2):
            lanes = slice(HDIM * head, HDIM * (head + 1))
            scores = key_parts(kp, kr, kc, head_only(q_tile, head), start == 0)
            dps = key_parts(vp, vr, vc, head_only(g_tile, head), start == 0)
            lse = lse_ref[0, pl.ds(head, 1), tile]
            probs = [jnp.exp(part - lse) for part in scores]
            row_dot = jnp.sum(probs[0] * dps[0], 0, keepdims=True)
            for p_part, d_part in zip(probs[1:], dps[1:]):
                row_dot = row_dot + jnp.sum(p_part * d_part, 0, keepdims=True)
            ds = [(p * (d - row_dot)).astype(bf16) for p, d in zip(probs, dps)]
            probs = [p.astype(bf16) for p in probs]
            dq = nn(kp_t[lanes], ds[0]) + nn(kr_t[lanes], ds[1])
            dk = [nn(ds[0], q_tile), nn(ds[1], q_tile)]
            dv = [nn(probs[0], g_tile), nn(probs[1], g_tile)]
            if start:
                dq = dq + jnp.concatenate([nn(kc_t[lanes, c], ds[2][:, c]) for c in cols], 1)
                dk.append(jnp.concatenate([nn(ds[2][:, c], q_tile[c]) for c in cols], 0))
                dv.append(jnp.concatenate([nn(probs[2][:, c], g_tile[c]) for c in cols], 0))
            dqs.append(dq)
            dks.append(dk)
            dvs.append(dv)
        cosine, sine = cos_ref[tile, :], sin_ref[tile, :]
        dq = jnp.concatenate(dqs, 0).T * HDIM**-0.5
        gq_ref[tile, :] = rotate(dq, cosine, -sine).astype(bf16)
        for which, parts in enumerate((dks, dvs)):
            merged = [jnp.where(first, a, b) for a, b in zip(*parts)]
            if start:
                dp_ref[which] += merged[0]
                dr_ref[which] += merged[1]
                last = merged[2] if which else rotate(merged[2], cosine, -sine)
                gc_ref[which] = last.astype(bf16)
            else:
                dp_ref[which] = merged[0]
                dr_ref[which] = merged[1]


def attn_bwd(ids, group, q, kvp, kvc, kvr, g, lse, cosine, sine):
    pairs = GROUP // (2 * HDIM)
    first = group * pairs
    return pl.pallas_call(
        attn_bwd_kernel,
        grid=(pairs,),
        in_specs=[SCALAR, pair_block(PROMPT, first)]
        + [pair_half(first)] * 3
        + [pair_block(PROMPT, first), lse_block(first), whole((PROMPT, 128)), whole((PROMPT, 128))],
        out_specs=[pair_block(PROMPT), pair_half(), pair_half(), pair_half()],
        out_shape=[
            jax.ShapeDtypeStruct((PROMPT, GROUP), bf16),
            jax.ShapeDtypeStruct((2, HALF, GROUP), bf16),
            jax.ShapeDtypeStruct((2, HALF, GROUP), f32),
            jax.ShapeDtypeStruct((2, HALF, GROUP), f32),
        ],
        compiler_params=pltpu.CompilerParams(vmem_limit_bytes=VMEM_LIMIT),
        cost_estimate=pl.CostEstimate(flops=11 * 10**9, bytes_accessed=8 * 2**20, transcendentals=0),
        name=f"attn_bwd{group}",
    )(ids, q, kvp, kvc, kvr, g, lse, cosine, sine)


def up_kernel(
    specs,
    place_ref,
    o_ref,
    hid_ref,
    mask_ref,
    embed_ref,
    mods_ref,
    gain_ref,
    bias_ref,
    cot_ref,
    *rest,
):
    pieces, rest = take(specs, rest)
    ap_ref, mid_ref, x_ref, act_ref, gpre_ref, gmlp_ref, gbu_ref, gbd_ref = rest[:8]
    proj_ref, up_ref, down_ref, sems = rest[8:]
    step = pl.program_id(0)
    targets = (proj_ref, up_ref, down_ref)
    copies = [
        place(part, spec, place_ref, target, sems.at[i])
        for i, (part, spec, target) in enumerate(zip(pieces, specs, targets))
    ]

    @pl.when(step == 0)
    def _():
        for group in copies:
            for copy in group:
                copy.start()
        gbu_ref[...] = jnp.zeros_like(gbu_ref)
        gbd_ref[...] = jnp.zeros_like(gbd_ref)
        for copy in copies[0]:
            copy.wait()

    attn_proj = nn(o_ref[...], proj_ref[...])
    ap_ref[...] = attn_proj
    for sub in range(SUB):
        rows = slice(sub * CLEN, (sub + 1) * CLEN)
        row = pl.ds(step * SUB + sub, 1)
        start = jnp.where(mask_ref[rows, :] > 0.5, embed_ref[...], hid_ref[rows, :].astype(f32))
        middle = start + mods_ref[row, 2 * D : 3 * D] * attn_proj[rows]
        mid_ref[rows, :] = middle
        normed, _inv = layer_norm(middle)
        shift, scale = mods_ref[row, 3 * D : 4 * D], mods_ref[row, 4 * D : 5 * D]
        x_ref[rows, :] = (normed * gain_ref[...] * (1.0 + scale) + shift).astype(bf16)
        g_mlp = (mods_ref[row, 5 * D : 6 * D] * cot_ref[rows, :].astype(f32)).astype(bf16)
        gmlp_ref[rows, :] = g_mlp
        gbd_ref[...] += jnp.sum(g_mlp.astype(f32), 0, keepdims=True)

    @pl.when(step == 0)
    def _():
        for group in copies[1:]:
            for copy in group:
                copy.wait()

    x, g_mlp = x_ref[...], gmlp_ref[...]
    root = (2.0 / jnp.pi) ** 0.5
    for col in range(0, FF, CHUNK):
        cols = slice(col, col + CHUNK)
        pre = nn(x, up_ref[:, cols]) + bias_ref[:, cols]
        square = pre * pre
        curve = jnp.tanh(root * pre * (1.0 + 0.044715 * square))
        half_up = 0.5 * (1.0 + curve)
        act_ref[:, cols] = (pre * half_up).astype(bf16)
        slope = half_up + (0.5 * root) * pre * (1.0 - curve * curve) * (1.0 + 0.134145 * square)
        g_pre = (nt(g_mlp, down_ref[cols, :]) * slope).astype(bf16)
        gpre_ref[:, cols] = g_pre
        gbu_ref[:, cols] += jnp.sum(g_pre.astype(f32), 0, keepdims=True)


def take(specs, refs):
    pieces = []
    for spec in specs:
        pieces.append(refs[: len(spec)])
        refs = refs[len(spec) :]
    return pieces, refs


def tile_block(width):
    return pl.BlockSpec((TILE, width), lambda step: (step, 0))


def weight_scratch():
    return [
        pltpu.VMEM((D, D), bf16),
        pltpu.VMEM((D, FF), bf16),
        pltpu.VMEM((FF, D), bf16),
        pltpu.SemaphoreType.DMA((3,)),
    ]


def up_call(place_ids, attn_o, hidden, mask, embed, mods, gain, bias, cot, proj, up, down):
    weights = (proj, up, down)
    n = sum(w.count for w in weights)
    specs = tuple(w.spec for w in weights)
    arrays = [a for w in weights for a in w.arrays]
    rows = PROMPT
    return pl.pallas_call(
        partial(up_kernel, specs),
        grid=(rows // TILE,),
        in_specs=[
            SCALAR,
            tile_block(D),
            tile_block(D),
            tile_block(1),
            whole((1, D)),
            whole(mods.shape),
            whole((1, D)),
            whole((1, FF)),
            tile_block(D),
        ]
        + [ANY] * n,
        out_specs=[tile_block(D)] * 3
        + [tile_block(FF)] * 2
        + [tile_block(D), whole((1, FF)), whole((1, D))],
        out_shape=[
            jax.ShapeDtypeStruct((rows, D), f32),
            jax.ShapeDtypeStruct((rows, D), f32),
            jax.ShapeDtypeStruct((rows, D), bf16),
            jax.ShapeDtypeStruct((rows, FF), bf16),
            jax.ShapeDtypeStruct((rows, FF), bf16),
            jax.ShapeDtypeStruct((rows, D), bf16),
            jax.ShapeDtypeStruct((1, FF), f32),
            jax.ShapeDtypeStruct((1, D), f32),
        ],
        scratch_shapes=weight_scratch(),
        compiler_params=pltpu.CompilerParams(vmem_limit_bytes=VMEM_LIMIT),
        cost_estimate=pl.CostEstimate(flops=12 * 10**9, bytes_accessed=40 * 2**20, transcendentals=0),
        name="mlp_up",
    )(place_ids, attn_o, hidden, mask, embed, mods, gain, bias, cot, *arrays)


def down_kernel(specs, place_ref, act_ref, gpre_ref, mid_ref, ap_ref, cot_ref, mods_ref, gain_ref, bias_ref, *rest):
    pieces, rest = take(specs, rest)
    out_ref, dmid_ref, gatt_ref, go_ref, stat_ref, ggain_ref = rest[:6]
    proj_ref, up_ref, down_ref, sems = rest[6:]
    step = pl.program_id(0)
    targets = (proj_ref, up_ref, down_ref)
    copies = [
        place(part, spec, place_ref, target, sems.at[i])
        for i, (part, spec, target) in enumerate(zip(pieces, specs, targets))
    ]

    @pl.when(step == 0)
    def _():
        for i in (2, 1, 0):
            for copy in copies[i]:
                copy.start()
        ggain_ref[...] = jnp.zeros_like(ggain_ref)
        for copy in copies[2]:
            copy.wait()

    mlp_out = nn(act_ref[...], down_ref[...]) + bias_ref[...]

    @pl.when(step == 0)
    def _():
        for i in (1, 0):
            for copy in copies[i]:
                copy.wait()

    g_n = nt(gpre_ref[...], up_ref[...])
    for sub in range(SUB):
        rows = slice(sub * CLEN, (sub + 1) * CLEN)
        row = pl.ds(step * SUB + sub, 1)
        middle, cot, grad = mid_ref[rows, :], cot_ref[rows, :].astype(f32), g_n[rows]
        gate_attn, gate_mlp = mods_ref[row, 2 * D : 3 * D], mods_ref[row, 5 * D : 6 * D]
        scale = 1.0 + mods_ref[row, 4 * D : 5 * D]
        out_ref[rows, :] = (middle + gate_mlp * mlp_out[rows]).astype(bf16)
        normed, inv_std = layer_norm(middle)
        along = jnp.sum(grad * normed, 0, keepdims=True)
        ggain_ref[...] += along * scale
        d_middle = cot + norm_back(grad * (scale * gain_ref[...]), normed, inv_std)
        dmid_ref[rows, :] = d_middle
        gatt_ref[rows, :] = (gate_attn * d_middle).astype(bf16)
        stat_ref[row, 0:D] = jnp.sum(d_middle * ap_ref[rows, :], 0, keepdims=True)
        stat_ref[row, D : 2 * D] = jnp.sum(grad, 0, keepdims=True)
        stat_ref[row, 2 * D : 3 * D] = along * gain_ref[...]
        stat_ref[row, 3 * D : 4 * D] = jnp.sum(cot * mlp_out[rows], 0, keepdims=True)
    go_ref[...] = nt(gatt_ref[...], proj_ref[...]).astype(bf16)


def down_call(place_ids, act, gpre, middle, attn_proj, cot, mods, gain, bias, proj, up, down):
    weights = (proj, up, down)
    n = sum(w.count for w in weights)
    specs = tuple(w.spec for w in weights)
    arrays = [a for w in weights for a in w.arrays]
    rows = PROMPT
    return pl.pallas_call(
        partial(down_kernel, specs),
        grid=(rows // TILE,),
        in_specs=[
            SCALAR,
            tile_block(FF),
            tile_block(FF),
            tile_block(D),
            tile_block(D),
            tile_block(D),
            whole(mods.shape),
            whole((1, D)),
            whole((1, D)),
        ]
        + [ANY] * n,
        out_specs=[tile_block(D)] * 4 + [whole((CONTS, 4 * D)), whole((1, D))],
        out_shape=[
            jax.ShapeDtypeStruct((rows, D), bf16),
            jax.ShapeDtypeStruct((rows, D), f32),
            jax.ShapeDtypeStruct((rows, D), bf16),
            jax.ShapeDtypeStruct((rows, D), bf16),
            jax.ShapeDtypeStruct((CONTS, 4 * D), f32),
            jax.ShapeDtypeStruct((1, D), f32),
        ],
        scratch_shapes=weight_scratch(),
        compiler_params=pltpu.CompilerParams(vmem_limit_bytes=VMEM_LIMIT),
        cost_estimate=pl.CostEstimate(flops=12 * 10**9, bytes_accessed=40 * 2**20, transcendentals=0),
        name="mlp_down",
    )(place_ids, act, gpre, middle, attn_proj, cot, mods, gain, bias, *arrays)


def split_store(total, keep_ref, send_ref, core, lead, at):
    for pair in range(total.shape[0] // lead // 2):
        even = total[2 * pair * lead : (2 * pair + 1) * lead].astype(bf16)
        odd = total[(2 * pair + 1) * lead : (2 * pair + 2) * lead].astype(bf16)
        keep_ref[pair, at : at + lead, :] = jnp.where(core == 0, even, odd)
        send_ref[pair, at : at + lead, :] = jnp.where(core == 0, odd, even)


def wgrad_kernel(lead, place_ref, left_ref, right_ref, keep_ref, send_ref):
    split_store(tn(left_ref[...], right_ref[...]), keep_ref, send_ref, place_ref[1], lead, 0)


def wgrad_call(place_ids, left, right, n, name):
    lead = D // n
    blocks = right.shape[1] // D
    out = pl.BlockSpec((n // 2, lead, D), lambda j: (0, j, 0))
    shape = jax.ShapeDtypeStruct((n // 2, blocks * lead, D), bf16)
    return pl.pallas_call(
        partial(wgrad_kernel, lead),
        grid=(blocks,),
        in_specs=[SCALAR, whole((PROMPT, D)), pl.BlockSpec((PROMPT, D), lambda j: (0, j))],
        out_specs=[out, out],
        out_shape=[shape, shape],
        compiler_params=pltpu.CompilerParams(vmem_limit_bytes=VMEM_LIMIT),
        cost_estimate=pl.CostEstimate(
            flops=2 * 10**9 * blocks, bytes_accessed=4 * 2**20 * blocks, transcendentals=0
        ),
        name=name,
    )(place_ids, left, right)


def down_grad_kernel(_ids, left_ref, right_ref, keep_ref, send_ref):
    half = pl.num_programs(0) // 2
    total = tn(left_ref[...], right_ref[...]).astype(bf16)

    @pl.when(pl.program_id(0) < half)
    def _():
        send_ref[0] = total

    @pl.when(pl.program_id(0) >= half)
    def _():
        keep_ref[0] = total


def down_grad_call(place_ids, act, g_mlp, n):
    rows = FF // n
    half = n // 2

    def shard(j, ids):
        core = ids[1]
        return 0, jnp.where(j < half, 2 * j + 1 - core, 2 * (j - half) + core)

    shape = jax.ShapeDtypeStruct((half, rows, D), bf16)
    return pl.pallas_call(
        down_grad_kernel,
        grid_spec=pltpu.PrefetchScalarGridSpec(
            num_scalar_prefetch=1,
            grid=(n,),
            in_specs=[pl.BlockSpec((PROMPT, rows), shard), pl.BlockSpec((PROMPT, D), lambda j, ids: (0, 0))],
            out_specs=[
                pl.BlockSpec((1, rows, D), lambda j, ids: (jnp.maximum(j - half, 0), 0, 0)),
                pl.BlockSpec((1, rows, D), lambda j, ids: (jnp.minimum(j, half - 1), 0, 0)),
            ],
        ),
        out_shape=[shape, shape],
        compiler_params=pltpu.CompilerParams(vmem_limit_bytes=VMEM_LIMIT),
        cost_estimate=pl.CostEstimate(flops=8 * 10**9, bytes_accessed=16 * 2**20, transcendentals=0),
        name="down_grad",
    )(place_ids, act, g_mlp)


def down_grad_any(place_ids, act, g_mlp, n):
    if (FF // n) % 128 == 0 and n == 4:
        return down_grad_call(place_ids, act, g_mlp, n)
    full = wide_grad_call(act, g_mlp)
    core = lax.axis_index("shard") % 2
    parts = full.reshape(n // 2, 2, -1, D)
    keep = lax.dynamic_index_in_dim(parts, core, 1, False)
    return keep, lax.dynamic_index_in_dim(parts, 1 - core, 1, False)


def wide_grad_kernel(left_ref, right_ref, out_ref):
    out_ref[...] = tn(left_ref[...], right_ref[...]).astype(bf16)


def wide_grad_call(act, g_mlp):
    return pl.pallas_call(
        wide_grad_kernel,
        grid=(FF // D,),
        in_specs=[pl.BlockSpec((PROMPT, D), lambda j: (0, j)), whole((PROMPT, D))],
        out_specs=pl.BlockSpec((D, D), lambda j: (j, 0)),
        out_shape=jax.ShapeDtypeStruct((FF, D), bf16),
        compiler_params=pltpu.CompilerParams(vmem_limit_bytes=VMEM_LIMIT),
        name="wide_grad",
    )(act, g_mlp)


def qkv_grad_kernel(lead, with_proj, with_ada, place_ref, x_ref, gq_ref, gc_ref, dp_ref, got_ref, cos_ref, sin_ref, *rest):
    keep_ref, send_ref, g_ref = rest[-3:]
    core = place_ref[1]
    g_ref[:, 0:GROUP] = gq_ref[...]
    total_k = dp_ref[0] + got_ref[0].astype(f32)
    total_v = dp_ref[1] + got_ref[1].astype(f32)
    g_ref[0:HALF, GROUP : 2 * GROUP] = rotate(total_k, cos_ref[...], -sin_ref[...]).astype(bf16)
    g_ref[0:HALF, 2 * GROUP : 3 * GROUP] = total_v.astype(bf16)
    g_ref[HALF:PROMPT, GROUP : 2 * GROUP] = gc_ref[0]
    g_ref[HALF:PROMPT, 2 * GROUP : 3 * GROUP] = gc_ref[1]
    split_store(tn(x_ref[...], g_ref[...]), keep_ref, send_ref, core, lead, 0)
    at = lead
    if with_proj:
        split_store(tn(rest[0][...], rest[1][...]), keep_ref, send_ref, core, lead, at)
        at += lead
        rest = rest[2:]
    if with_ada:
        cond = rest[0][...]
        silu = (cond / (1.0 + jnp.exp(-cond))).astype(bf16).astype(f32)
        few = cond.shape[1] * lead // D
        for col in range(4):
            total = exact(silu, rest[1][:, col * D : (col + 1) * D], ((0,), (0,)))
            split_store(total, keep_ref, send_ref, core, few, at)
            at += few


def qkv_grad_call(place_ids, x, gq, gc, dp, got, cosine, sine, n, name, proj, ada):
    lead = D // n
    rows = lead
    extra = []
    if proj is not None:
        extra += list(proj)
        rows += lead
    if ada is not None:
        extra += list(ada)
        rows += 4 * (ada[0].shape[1] // n)
    out = whole((n // 2, rows, D))
    shape = jax.ShapeDtypeStruct((n // 2, rows, D), bf16)
    return pl.pallas_call(
        partial(qkv_grad_kernel, lead, proj is not None, ada is not None),
        grid=(1,),
        in_specs=[
            SCALAR,
            whole((PROMPT, D)),
            whole((PROMPT, GROUP)),
            whole((2, HALF, GROUP)),
            whole((2, HALF, GROUP)),
            whole((2, HALF, GROUP)),
            whole((HALF, 128)),
            whole((HALF, 128)),
        ]
        + [whole(e.shape) for e in extra],
        out_specs=[out, out, whole((PROMPT, D))],
        out_shape=[shape, shape, jax.ShapeDtypeStruct((PROMPT, D), bf16)],
        compiler_params=pltpu.CompilerParams(vmem_limit_bytes=VMEM_LIMIT),
        cost_estimate=pl.CostEstimate(flops=3 * 10**9, bytes_accessed=8 * 2**20, transcendentals=0),
        name=name,
    )(place_ids, x, gq, gc, dp, got, cosine, sine, *extra)


def start_kernel(spec, place_ref, hid_ref, mask_ref, embed_ref, mods_ref, gain_ref, dmid_ref, *rest):
    n = len(spec)
    grads, pieces = rest[:N_GROUP], rest[N_GROUP : N_GROUP + n]
    gh_ref, stat_ref, ggain_ref, gmask_ref, w_ref, sem = rest[N_GROUP + n :]
    step = pl.program_id(0)

    @pl.when(step == 0)
    def _():
        copies = place(pieces, spec, place_ref, w_ref, sem)
        for copy in copies:
            copy.start()
        ggain_ref[...] = jnp.zeros_like(ggain_ref)
        gmask_ref[...] = jnp.zeros_like(gmask_ref)
        for copy in copies:
            copy.wait()

    g_n = None
    for group in range(N_GROUP):
        for third in range(3):
            at = third * D + group * GROUP
            term = nt(grads[group][:, third * GROUP : (third + 1) * GROUP], w_ref[:, at : at + GROUP])
            g_n = term if g_n is None else g_n + term
    for sub in range(SUB):
        rows = slice(sub * CLEN, (sub + 1) * CLEN)
        row = pl.ds(step * SUB + sub, 1)
        masked = mask_ref[rows, :] > 0.5
        start = jnp.where(masked, embed_ref[...], hid_ref[rows, :].astype(f32))
        normed, inv_std = layer_norm(start)
        scale = 1.0 + mods_ref[row, D : 2 * D]
        grad = g_n[rows]
        along = jnp.sum(grad * normed, 0, keepdims=True)
        ggain_ref[...] += along * scale
        stat_ref[row, 0:D] = jnp.sum(grad, 0, keepdims=True)
        stat_ref[row, D : 2 * D] = along * gain_ref[...]
        d_start = dmid_ref[rows, :] + norm_back(grad * (scale * gain_ref[...]), normed, inv_std)
        gh_ref[rows, :] = jnp.where(masked, 0.0, d_start)
        gmask_ref[...] += jnp.sum(jnp.where(masked, d_start, 0.0), 0, keepdims=True)


def start_call(place_ids, hidden, mask, embed, mods, gain, d_middle, grads, weight):
    n = weight.count
    rows = PROMPT
    return pl.pallas_call(
        partial(start_kernel, weight.spec),
        grid=(rows // TILE,),
        in_specs=[
            SCALAR,
            tile_block(D),
            tile_block(1),
            whole((1, D)),
            whole(mods.shape),
            whole((1, D)),
            tile_block(D),
        ]
        + [tile_block(D)] * N_GROUP
        + [ANY] * n,
        out_specs=[tile_block(D), whole((CONTS, 2 * D)), whole((1, D)), whole((1, D))],
        out_shape=[
            jax.ShapeDtypeStruct((rows, D), f32),
            jax.ShapeDtypeStruct((CONTS, 2 * D), f32),
            jax.ShapeDtypeStruct((1, D), f32),
            jax.ShapeDtypeStruct((1, D), f32),
        ],
        scratch_shapes=[pltpu.VMEM((D, 3 * D), bf16), pltpu.SemaphoreType.DMA],
        compiler_params=pltpu.CompilerParams(vmem_limit_bytes=VMEM_LIMIT),
        cost_estimate=pl.CostEstimate(flops=4 * 10**9, bytes_accessed=16 * 2**20, transcendentals=0),
        name="start_grad",
    )(place_ids, hidden, mask, embed, mods, gain, d_middle, *grads, *weight.arrays)


def pack_kernel(*refs):
    out_ref = refs[-1]
    out_ref[...] = jnp.zeros_like(out_ref)
    for i, ref in enumerate(refs[:-1]):
        out_ref[i : i + 1, 0 : ref.shape[0]] = ref[...].astype(f32).reshape(1, -1)


def pack_call(vectors):
    shape = (8, max(v.shape[0] for v in vectors))
    return pl.pallas_call(
        pack_kernel,
        grid=(1,),
        in_specs=[whole(v.shape) for v in vectors],
        out_specs=whole(shape),
        out_shape=jax.ShapeDtypeStruct(shape, f32),
        name="pack",
    )(*vectors)


def mods_kernel(spec, lengths, times_ref, place_ref, table_ref, *rest):
    n = len(spec)
    pieces, rest = rest[:n], rest[n:]
    count = len(lengths)
    n_row = len(rest) - count - 6
    rows, rest = rest[:n_row], rest[n_row:]
    mods_ref, cond_ref, ada_ref = rest[:3]
    out_refs = rest[3 : 3 + count - 1]
    bias_ref, row_ref, sem, row_sem = rest[3 + count - 1 :]
    copies = place(pieces, spec, place_ref, ada_ref, sem)
    row_copies = [
        pltpu.make_async_copy(row, row_ref.at[place_ref[0] ^ offset], row_sem) for offset, row in enumerate(rows)
    ]
    for copy in row_copies + copies:
        copy.start()
    for block in range(CONTS):
        cond_ref[pl.ds(block, 1), :] = table_ref[pl.ds(times_ref[block], 1), :]
    cond = cond_ref[...]
    silu = (cond / (1.0 + jnp.exp(-cond))).astype(bf16)
    for copy in row_copies:
        copy.wait()
    for shard in range(n_row):
        for i, (length, ref) in enumerate(zip(lengths, (*out_refs, bias_ref))):
            ref[0:1, shard * length : (shard + 1) * length] = row_ref[shard, i : i + 1, 0:length]
    for copy in copies:
        copy.wait()
    mods_ref[...] = nn(silu, ada_ref[...]) + bias_ref[...]


def mods_call(times, place_ids, table, weight, rows, lengths):
    width = weight.arrays[0].shape[1]
    n = len(rows)
    vectors = [(1, n * length) for length in lengths]
    shapes = [(CONTS, width), (CONTS, table.shape[1])]
    return pl.pallas_call(
        partial(mods_kernel, weight.spec, tuple(lengths)),
        in_specs=[SCALAR, SCALAR, whole(table.shape)] + [ANY] * (weight.count + n),
        out_specs=[whole(s) for s in shapes] + [whole((table.shape[1], width))] + [whole(v) for v in vectors[:-1]],
        out_shape=[jax.ShapeDtypeStruct(s, f32) for s in shapes]
        + [jax.ShapeDtypeStruct((table.shape[1], width), bf16)]
        + [jax.ShapeDtypeStruct(v, f32) for v in vectors[:-1]],
        grid=(1,),
        scratch_shapes=[
            pltpu.VMEM(vectors[-1], f32),
            pltpu.VMEM((n,) + rows[0].shape, f32),
            pltpu.SemaphoreType.DMA,
            pltpu.SemaphoreType.DMA,
        ],
        compiler_params=pltpu.CompilerParams(vmem_limit_bytes=VMEM_LIMIT),
        cost_estimate=pl.CostEstimate(flops=10**9, bytes_accessed=4 * 2**20, transcendentals=0),
        name="mods",
    )(times, place_ids, table, *weight.arrays, *rows)


def last_kernel(
    lead, time_rows, place_ref, cond_ref, ada_ref, stat1_ref, stat2_ref, ga_ref, gm_ref, bu_ref, bd_ref, me_ref,
    keep_ref, send_ref, small_ref,
):
    core, pair = place_ref[1], place_ref[2]
    cond = cond_ref[...]
    gate = 1.0 / (1.0 + jnp.exp(-cond))
    silu = (cond * gate).astype(bf16).astype(f32)
    stat1, stat2 = stat1_ref[...], stat2_ref[...]
    ada_late = exact(silu, stat1, ((0,), (0,)))
    ada = ada_ref[...].astype(f32)
    g_silu = exact(stat1, ada[:, : 2 * D], ((1,), (1,))) + exact(stat2, ada[:, 2 * D :], ((1,), (1,)))
    g_cond = g_silu * (gate * (1.0 + cond * (1.0 - gate)))
    small_ref[...] = jnp.zeros_like(small_ref)
    at = time_rows
    small_ref[at : at + 1, :] = ga_ref[...]
    small_ref[at + 1 : at + 2, :] = gm_ref[...]
    for i in range(FF // D):
        small_ref[at + 2 + i : at + 3 + i, :] = bu_ref[:, i * D : (i + 1) * D]
    small_ref[at + 6 : at + 7, :] = bd_ref[...]
    for i in range(2):
        small_ref[at + 7 + i : at + 8 + i, :] = jnp.sum(stat1[:, i * D : (i + 1) * D], 0, keepdims=True)
    for i in range(4):
        small_ref[at + 9 + i : at + 10 + i, :] = jnp.sum(stat2[:, i * D : (i + 1) * D], 0, keepdims=True)
    small_ref[at + 13 : at + 14, :] = me_ref[...]
    half = CONTS // 2
    prompt = jnp.sum(g_cond[:half], 0, keepdims=True)
    values = [prompt] + [g_cond[half + i : half + i + 1] for i in range(half)]
    base = pair * (CONTS + 1)
    where_to = [base] + [base + 1 + core * half + i for i in range(half)]
    for lane in range(D // 128):
        row = lax.broadcasted_iota(jnp.int32, (time_rows, 128), 0) + lane * time_rows
        placed = jnp.zeros((time_rows, 128), f32)
        for index, value in zip(where_to, values):
            placed = placed + jnp.where(row == index, value, 0.0)
        small_ref[0:time_rows, lane * 128 : (lane + 1) * 128] = placed
    small = small_ref[...]
    high = small.astype(bf16)
    rows = small.shape[0]
    low = (small[time_rows:] - high[time_rows:].astype(f32)).astype(bf16)
    for j in range(keep_ref.shape[0]):
        for col in range(2):
            split_store(ada_late[:, col * D : (col + 1) * D], keep_ref, send_ref, core, lead, col * lead)
        row = 2 * lead
        for ref in (keep_ref, send_ref):
            ref[j, row : row + rows, :] = high
            ref[j, row + rows : row + rows + 16, :] = low


def last_call(place_ids, cond, ada, stat1, stat2, vectors, n, time_rows):
    lead = ada.shape[0] // n
    rows = 16 + time_rows
    args = (cond, ada, stat1, stat2) + tuple(vectors)
    out = whole((n // 2, 2 * lead + rows + 16, D))
    shape = jax.ShapeDtypeStruct((n // 2, 2 * lead + rows + 16, D), bf16)
    return pl.pallas_call(
        partial(last_kernel, lead, time_rows),
        grid=(1,),
        in_specs=[SCALAR] + [whole(a.shape) for a in args],
        out_specs=[out, out],
        out_shape=[shape, shape],
        scratch_shapes=[pltpu.VMEM((rows, D), f32)],
        compiler_params=pltpu.CompilerParams(vmem_limit_bytes=VMEM_LIMIT),
        cost_estimate=pl.CostEstimate(flops=10**8, bytes_accessed=2 * 2**20, transcendentals=0),
        name="last",
    )(place_ids, *args)


def swap(value, axis, mask):
    pairs = [(source, source ^ mask) for source in range(lax.axis_size(axis))]
    return lax.ppermute(value, axis, pairs)


def gather_far(piece):
    pieces = {0: piece}
    mask = lax.axis_size("shard") // 2
    while mask > 1:
        for offset in list(pieces):
            pieces[offset | mask] = swap(pieces[offset], "shard", mask)
        mask //= 2
    return pieces


def gather_near(pieces):
    pieces = dict(pieces)
    for offset in list(pieces):
        pieces[offset | 1] = swap(pieces[offset], "shard", 1)
    return [pieces[offset] for offset in range(len(pieces))]


def sides():
    rep = lax.axis_index("rep")
    return rep % 2, rep % 4


def far_parts(piece, split=1):
    rows = piece.shape[0] // split
    if split == 1 or rows % 16:
        return 1, gather_far(piece)
    side = sides()[0 if split == 2 else 1]
    found = gather_far(lax.dynamic_slice_in_dim(piece, side * rows, rows, 0))
    found[0] = piece
    return split, found


def far_weight(split, found, tie=None):
    if tie is not None:
        found, _ = lax.optimization_barrier((found, tie))
    spec, arrays = [], []
    for offset, part in found.items():
        if split == 1 or not offset:
            spec.append((offset, 1, 0))
            arrays.append(part)
            continue
        spec += [(offset, split, code) for code in range(split)]
        arrays += [part] + [swap(part, "rep", code) for code in range(1, split)]
    return Weight(spec, arrays)


def near_weight(far):
    spec, arrays = list(far.spec), list(far.arrays)
    for (offset, split, code), part in zip(far.spec, far.arrays):
        spec.append((offset | 1, split, code))
        arrays.append(swap(part, "shard", 1))
    if all(part.shape[0] % 16 == 0 for part in arrays):
        return Weight(spec, arrays)
    mine = lax.axis_index("shard")
    rows = arrays[0].shape[0]
    out = jnp.zeros((rows * len(arrays),) + arrays[0].shape[1:], arrays[0].dtype)
    for (offset, _split, _code), part in zip(spec, arrays):
        out = lax.dynamic_update_slice_in_dim(out, part, (mine ^ offset) * rows, 0)
    return Weight([(None, 1, 0)], [out])


def add_plain(left, right):
    return left.astype(f32) + right.astype(f32)


def add_packed(left, right):
    rows = left.shape[-2] - 16
    total = add_plain(left[..., :rows, :], right[..., :rows, :])
    rest = add_plain(left[..., rows:, :], right[..., rows:, :])
    return jnp.concatenate([total[..., : rows - 16, :], total[..., rows - 16 :, :] + rest], -2)


def pack_plain(value):
    return value.astype(bf16)


def pack_packed(value):
    high = value.astype(bf16)
    low = value[..., -16:, :] - high[..., -16:, :].astype(f32)
    return jnp.concatenate([high, low.astype(bf16)], -2)


def reduce_chain(keep, send, steps, add=add_plain, pack=pack_plain):
    mine, rep = lax.axis_index("shard"), lax.axis_index("rep")
    got = yield swap(send, "shard", 1)
    value = pack(add(keep, got))
    mask = 2
    while mask < lax.axis_size("shard"):
        bit = (mine // mask) % 2
        halves = value.reshape((-1, 2) + value.shape[1:])
        keep = lax.dynamic_index_in_dim(halves, bit, 1, False)
        got = yield swap(lax.dynamic_index_in_dim(halves, 1 - bit, 1, False), "shard", mask)
        value = pack(add(keep, got))
        mask *= 2
    value = value[0]
    more = range(3, lax.axis_size("rep").bit_length() - 1)
    steps = [(bit, "all") for bit in more] + list(steps)
    for at, kind in steps:
        bit = (rep >> at) % 2
        if kind == "split":
            halves = value.reshape(2, -1, value.shape[-1])
            keep = lax.dynamic_index_in_dim(halves, bit, 0, False)
            got = yield swap(lax.dynamic_index_in_dim(halves, 1 - bit, 0, False), "rep", 1 << at)
            value = pack(add(keep, got))
        elif kind == "join":
            got = yield swap(value, "rep", 1 << at)
            first, second = jnp.where(bit == 0, value, got), jnp.where(bit == 0, got, value)
            value = jnp.concatenate([first, second], 0)
        else:
            got = yield swap(value, "rep", 1 << at)
            last, value = (value, got), pack(add(value, got))
    return last


class Schedule:
    def __init__(self, ids, rows):
        self.ids = ids
        self.chains = {}
        self.sent = {}
        self.done = {}
        self.final = {}
        self.rows = rows

    def begin(self, name, keep, send, *how):
        chain = reduce_chain(keep, send, *how)
        self.chains[name] = chain
        self.sent[name] = next(chain)

    def sync(self, *names, after=()):
        for name in names or (None,):
            if name is not None and name not in self.sent:
                continue
            got = self.sent.pop(name, None)
            self.ids, got, after = lax.optimization_barrier((self.ids, got, tuple(after)))
            if got is None:
                continue
            try:
                self.sent[name] = self.chains[name].send(got)
            except StopIteration as stop:
                self.done[name] = stop.value
                if name in self.rows:
                    self.final[name] = finish_blocks(stop.value, self.rows[name], f"finish_{name}")

    def finish(self, *names):
        for name in names:
            self.sync(name)
        while self.sent:
            self.sync(next(iter(self.sent)))


def add_two(a_ref, b_ref):
    return a_ref[...].astype(f32) + b_ref[...].astype(f32)


def finish_kernel(a_ref, b_ref, out_ref):
    out_ref[...] = add_two(a_ref, b_ref)


def finish_blocks(pair, rows, name):
    count = pair[0].shape[0] // rows
    return pl.pallas_call(
        finish_kernel,
        grid=(count,),
        in_specs=[pl.BlockSpec((rows, D), lambda j: (j, 0))] * 2,
        out_specs=pl.BlockSpec((rows, D), lambda j: (0, j)),
        out_shape=jax.ShapeDtypeStruct((rows, count * D), f32),
        cost_estimate=pl.CostEstimate(flops=10**7, bytes_accessed=4 * 2**20, transcendentals=0),
        name=name,
    )(*pair)


def finish_qkv_kernel(lead, *refs):
    qkv_ref, proj_ref = refs[2 * N_GROUP :]
    for group in range(N_GROUP):
        total = add_two(refs[2 * group].at[0:lead], refs[2 * group + 1].at[0:lead])
        for third in range(3):
            at = third * D + group * GROUP
            qkv_ref[:, at : at + GROUP] = total[:, third * GROUP : (third + 1) * GROUP]
    proj_ref[...] = add_two(refs[0].at[lead : 2 * lead], refs[1].at[lead : 2 * lead])


def finish_qkv(pairs, lead):
    arrays = [a for pair in pairs for a in pair]
    shapes = [(lead, 3 * D), (lead, D)]
    return pl.pallas_call(
        partial(finish_qkv_kernel, lead),
        grid=(1,),
        in_specs=[whole(a.shape) for a in arrays],
        out_specs=[whole(s) for s in shapes],
        out_shape=[jax.ShapeDtypeStruct(s, f32) for s in shapes],
        cost_estimate=pl.CostEstimate(flops=10**7, bytes_accessed=4 * 2**20, transcendentals=0),
        name="finish_qkv",
    )(*arrays)


def finish_last_kernel(
    n, lead, time_rows, few, place_ref, ids_ref, a_ref, b_ref, ea_ref, eb_ref, ada_ref, time_ref, *out_refs
):
    mine = place_ref[0]
    for i in range(2):
        rows = slice(i * few, (i + 1) * few)
        ada_ref[:, i * D : (i + 1) * D] = add_two(a_ref.at[rows], b_ref.at[rows])
    for i in range(4):
        rows = slice(lead + i * few, lead + (i + 1) * few)
        ada_ref[:, (2 + i) * D : (3 + i) * D] = add_two(ea_ref.at[rows], eb_ref.at[rows])
    at = 2 * few
    times = add_two(a_ref.at[at : at + time_rows], b_ref.at[at : at + time_rows])
    times = jnp.concatenate([times[:, i * 128 : (i + 1) * 128] for i in range(D // 128)], 0)
    steps = lax.broadcasted_iota(jnp.int32, (STEPS, times.shape[0]), 0)
    hot = jnp.where(steps == ids_ref[...], 1.0, 0.0).astype(f32)
    time_ref[...] = exact(hot, times, ((1,), (0,)))
    at += time_rows
    high = add_two(a_ref.at[at : at + 16], b_ref.at[at : at + 16])
    small = high + add_two(a_ref.at[at + 16 : at + 32], b_ref.at[at + 16 : at + 32])
    first = 0
    for ref, count in zip(out_refs, (1, 1, 4, 1, 6, 1)):
        flat = jnp.concatenate([small[first + i : first + i + 1] for i in range(count)], 1)
        size = count * D // n
        share = flat[:, 0:size]
        for shard in range(1, n):
            share = jnp.where(mine == shard, flat[:, shard * size : (shard + 1) * size], share)
        ref[...] = share.reshape(size)
        first += count


def finish_last(place_ids, ids, pair, early, n, time_rows, few):
    lead = D // n
    sizes = [(count * D // n,) for count in (1, 1, 4, 1, 6, 1)]
    shapes = [(few, 6 * D), (STEPS, 128)] + sizes
    arrays = [ids, *pair, *early]
    return pl.pallas_call(
        partial(finish_last_kernel, n, lead, time_rows, few),
        grid=(1,),
        in_specs=[SCALAR] + [whole(a.shape) for a in arrays],
        out_specs=[whole(s) for s in shapes],
        out_shape=[jax.ShapeDtypeStruct(s, f32) for s in shapes],
        cost_estimate=pl.CostEstimate(flops=10**7, bytes_accessed=4 * 2**20, transcendentals=0),
        compiler_params=pltpu.CompilerParams(vmem_limit_bytes=VMEM_LIMIT),
        name="finish_last",
    )(place_ids, *arrays)


ROUTES = {'down': ((1, 'all'), (0, 'all'), (2, 'all')),
 'last': ((1, 'all'), (0, 'all'), (2, 'all')),
 'qkv0': ((1, 'split'), (2, 'all'), (1, 'join'), (0, 'all')),
 'qkv1': ((1, 'split'), (2, 'all'), (1, 'join'), (0, 'all')),
 'qkv2': ((1, 'split'), (2, 'all'), (1, 'join'), (0, 'all')),
 'up': ((1, 'split'), (2, 'all'), (1, 'join'), (0, 'all'))}
SYNCS = (('down',),
 ('up',),
 ('down', 'up'),
 (),
 ('qkv0', 'down', 'up'),
 ('qkv0', 'qkv1'),
 (),
 ('qkv2', 'qkv1', 'up'),
 ('qkv0',
  'qkv2',
  'last',
  'qkv1',
  'down',
  'up',
  'last',
  'qkv2',
  'qkv0',
  'last',
  'qkv1',
  'last',
  'qkv0',
  'qkv2',
  'qkv1',
  'qkv0',
  'last',
  'qkv2',
  'qkv1',
  'qkv2'),
 ('down', 'up'))


def on_device(
    hidden_in,
    mask_ids,
    time_ids,
    time_table,
    w_qkv,
    w_proj,
    w_up,
    w_down,
    w_ada,
    gain_attn,
    gain_mlp,
    bias_up,
    bias_down,
    bias_ada,
    mask_embed,
    cotangent,
):
    n = lax.axis_size("shard")
    mine = lax.axis_index("shard")
    core = mine % 2
    pair = (lax.axis_index("rep") * n + mine) // 2
    ids = jnp.stack([mine, core, pair, *sides()]).astype(jnp.int32)
    barrier = lax.optimization_barrier

    vectors = (gain_attn, gain_mlp, bias_up, bias_down, mask_embed, bias_ada)
    lengths = [v.shape[0] for v in vectors]
    row_far = gather_far(pack_call(vectors))
    ada_far = far_weight(*far_parts(w_ada))
    qkv_far = far_weight(*far_parts(w_qkv, 4))
    ada_weight = near_weight(ada_far)
    rows = gather_near(row_far)
    (proj_own, up_own, down_own), _ = barrier(((w_proj, w_up, w_down), ada_far.arrays))
    proj_far = far_weight(*far_parts(proj_own))
    up_parts = far_parts(up_own, 2)
    down_parts = far_parts(down_own, 2)

    block = jnp.arange(CONTS, dtype=jnp.int32)
    seg = jnp.where(block < CONTS // 2, 0, 1 + core * (CONTS // 2) + block - CONTS // 2)
    my_times = lax.dynamic_slice_in_dim(time_ids, pair, 1, 0)
    times = jnp.sum(jnp.where(seg[:, None] == jnp.arange(CONTS + 1, dtype=jnp.int32)[None], my_times, 0), 1)
    mods, cond, ada_mat, attn_gain, mlp_gain, up_bias, down_bias, embed = mods_call(
        times, ids, time_table, ada_weight, rows, lengths
    )

    local = jnp.arange(PROMPT, dtype=jnp.int32)
    positions = jnp.where(local < HALF, core * HALF + local, PROMPT + local % CLEN).astype(f32)
    freqs = 10000.0 ** (-(2.0 * jnp.arange(HDIM // 2, dtype=f32)) / HDIM)
    lanes = jnp.tile(freqs, 4)
    angles = positions[:, None] * lanes[None, :]
    sign = jnp.where(jnp.arange(128) % HDIM < HDIM // 2, -1.0, 1.0).astype(f32)
    cosine, sine = jnp.cos(angles), jnp.sin(angles) * sign[None, :]
    mask = (mask_ids == 1).astype(f32)[:, None]

    qkv_weight = near_weight(qkv_far.tied(mods))
    x, q, kvp, kvc = qkv_call(ids, hidden_in, mask, embed, mods, attn_gain, cosine, sine, qkv_weight)
    kvr = swap(kvp, "shard", 1)
    up_far = far_weight(*up_parts, kvp)
    down_far = far_weight(*down_parts, kvp)
    early = attn_fwd(0, 4, q, kvp, kvc, kvr)
    proj_weight = near_weight(proj_far.tied(early))
    up_weight = near_weight(up_far.tied(early))
    down_weight = near_weight(down_far.tied(early))
    early, _ = barrier((early, (proj_weight.arrays, up_far.arrays, down_far.arrays)))
    attn_o, lse = attn_fwd(4, 2, q, kvp, kvc, kvr, early)
    attn_proj, middle, x_mlp, act, g_pre, g_mlp, g_bias_up, g_bias_down = up_call(
        ids, attn_o, hidden_in, mask, embed, mods, mlp_gain, up_bias, cotangent, proj_weight, up_weight, down_weight
    )
    plan = Schedule(ids, {"down": FF // n, "up": D // n})
    down_keep, down_send = down_grad_any(plan.ids, act, g_mlp, n)
    plan.begin("down", down_keep, down_send, ROUTES["down"])
    plan.sync(after=(down_keep,))
    up_keep, up_send = wgrad_call(plan.ids, x_mlp, g_pre, n, "up_grad")
    plan.begin("up", up_keep, up_send, ROUTES["up"])
    plan.sync(*SYNCS[9], after=(up_keep,))
    block_out, d_middle, g_att, g_o, stat2, g_gain_mlp = down_call(
        plan.ids, act, g_pre, middle, attn_proj, cotangent, mods, mlp_gain, down_bias, proj_weight, up_weight, down_weight
    )
    plan.sync(*SYNCS[0], after=(g_o,))
    parts, others = [], []

    def backward(group):
        gq, gc, dp, dr = attn_bwd(plan.ids, group, q, kvp, kvc, kvr, g_o, lse, cosine, sine)
        parts.append((gq, gc, dp))
        others.append(swap(dr, "shard", 1))
        return gq

    grads = []

    def weight(group, proj, ada):
        keep, send, total = qkv_grad_call(
            plan.ids, x, *parts[group], others[group], cosine, sine, n, f"qkv_grad{group}", proj, ada
        )
        grads.append(total)
        plan.begin(f"qkv{group}", keep, send, ROUTES[f"qkv{group}"])
        return total

    last = backward(0)
    plan.sync(*SYNCS[1], after=(last,))
    last = backward(1)
    plan.sync(*SYNCS[2], after=(last,))
    last = weight(0, (attn_o, g_att), None)
    plan.sync(*SYNCS[3], after=(last,))
    last = backward(2)
    plan.sync(*SYNCS[4], after=(last,))
    last = weight(1, None, (cond, stat2))
    plan.sync(*SYNCS[5], after=(last,))
    last = weight(2, None, None)
    plan.sync(*SYNCS[6], after=(last,))
    grad_hidden, stat1, g_gain_attn, g_mask = start_call(
        plan.ids, hidden_in, mask, embed, mods, attn_gain, d_middle, grads, qkv_weight
    )
    plan.sync(*SYNCS[7], after=(stat1,))
    time_rows = -(-time_ids.size // 6 // 8) * 8
    vector_grads = (g_gain_attn, g_gain_mlp, g_bias_up, g_bias_down, g_mask)
    keep, send = last_call(plan.ids, cond, ada_mat, stat1, stat2, vector_grads, n, time_rows)
    plan.begin("last", keep, send, ROUTES["last"], add_packed, pack_packed)
    plan.finish(*SYNCS[8])

    done = plan.done
    few = w_ada.shape[0]
    flat_ids = time_ids.reshape(1, -1)
    flat_ids = jnp.pad(flat_ids, ((0, 0), (0, 6 * time_rows - flat_ids.shape[1])), constant_values=-1)
    grad_qkv, grad_proj = finish_qkv([done[f"qkv{g}"] for g in range(N_GROUP)], D // n)
    grad_ada, grad_time, *shares = finish_last(plan.ids, flat_ids, done["last"], done["qkv1"], n, time_rows, few)
    return (block_out, grad_hidden, grad_time, grad_qkv, grad_proj, plan.final["up"], plan.final["down"], grad_ada, *shares)


def solution(mesh):
    in_specs = (
        P(("rep", "shard"), None),
        P(("rep", "shard")),
        P(),
        P(),
        P("shard", None),
        P("shard", None),
        P("shard", None),
        P("shard", None),
        P("shard", None),
        P("shard"),
        P("shard"),
        P("shard"),
        P("shard"),
        P("shard"),
        P("shard"),
        P(("rep", "shard"), None),
    )
    out_specs = (
        P(("rep", "shard"), None),
        P(("rep", "shard"), None),
        P(),
        P("shard", None),
        P("shard", None),
        P("shard", None),
        P("shard", None),
        P("shard", None),
        P("shard"),
        P("shard"),
        P("shard"),
        P("shard"),
        P("shard"),
        P("shard"),
    )
    return jax.shard_map(
        on_device, mesh=mesh, in_specs=in_specs, out_specs=out_specs, check_vma=False
    )
```

```python
from functools import partial

import jax
import jax.numpy as jnp
from jax import lax
from jax.experimental import pallas as pl
from jax.experimental.pallas import tpu as pltpu
from jax.sharding import PartitionSpec as P

D = 768
HEADS = 12
HDIM = 64
FF = 3072
STEPS = 1000
CLEN = 128
CONTS = 8
PROMPT = 1024
HALF = PROMPT // 2
PAIRS = HEADS // 2
GROUP = 256
N_GROUP = D // GROUP
TILE = 256
SUB = TILE // CLEN
CHUNK = 512
eps_norm = 1e-06
bf16 = jnp.bfloat16
f32 = jnp.float32
VMEM_LIMIT = 62 * 2**20
COSTS = {'attn_bwd0': 52.5,
 'attn_bwd1': 52.8,
 'attn_bwd2': 53.4,
 'attn_fwd0': 55.5,
 'attn_fwd1': 55.5,
 'attn_fwd4': 30.9,
 'down_grad': 31.5,
 'finish_down': 8.4,
 'finish_last': 9.6,
 'finish_qkv': 9.0,
 'finish_up': 11.7,
 'last': 14.7,
 'mlp_down': 75.6,
 'mlp_up': 74.4,
 'mods': 10.5,
 'pack': 4.2,
 'qkv': 33.6,
 'qkv_grad0': 25.5,
 'qkv_grad1': 21.9,
 'qkv_grad2': 16.8,
 'start_grad': 35.1,
 'up_grad': 27.6,
 'wide_grad': 27}


def cost(name):
    return pl.CostEstimate(flops=int(COSTS.get(name, 1.0) * 1e9), bytes_accessed=0, transcendentals=0)


def nt(left, right):
    return lax.dot_general(left, right, (((1,), (1,)), ((), ())), preferred_element_type=f32)


def nn(left, right):
    return lax.dot_general(left, right, (((1,), (0,)), ((), ())), preferred_element_type=f32)


def tn(left, right):
    return lax.dot_general(left, right, (((0,), (0,)), ((), ())), preferred_element_type=f32)


def exact(left, right, contract):
    return lax.dot_general(
        left, right, (contract, ((), ())), preferred_element_type=f32, precision=lax.Precision.HIGHEST
    )


def layer_norm(values):
    mean_value = jnp.mean(values, -1, keepdims=True)
    centered = values - mean_value
    inv_std = lax.rsqrt(jnp.mean(centered * centered, -1, keepdims=True) + eps_norm)
    return (centered * inv_std, inv_std)


def norm_back(gradient, normed, inv_std):
    return inv_std * (
        gradient
        - jnp.mean(gradient, -1, keepdims=True)
        - normed * jnp.mean(gradient * normed, -1, keepdims=True)
    )


def rotate(values, cosine, sine):
    lane = lax.broadcasted_iota(jnp.int32, cosine.shape, 1) % HDIM
    out = []
    for col in range(0, values.shape[1], 128):
        part = values[:, col : col + 128]
        other = jnp.where(lane < HDIM // 2, pltpu.roll(part, 96, 1), pltpu.roll(part, 32, 1))
        out.append(part * cosine + other * sine)
    return out[0] if len(out) == 1 else jnp.concatenate(out, 1)


def whole(shape):
    return pl.BlockSpec(shape, lambda *_: (0,) * len(shape))


ANY = pl.BlockSpec(memory_space=pl.ANY)
SCALAR = pl.BlockSpec(memory_space=pltpu.SMEM)


def place(pieces, spec, place_ref, target, sem):
    mine = place_ref[0]
    copies = []
    for (offset, split, part), piece in zip(spec, pieces):
        rows = piece.shape[0]
        if offset is None:
            where = target
        else:
            start = (mine ^ offset) * (split * rows)
            if split > 1:
                start = start + (place_ref[3 if split == 2 else 4] ^ part) * rows
            where = target.at[pl.ds(pl.multiple_of(start, 16), rows)]
        copies.append(pltpu.make_async_copy(piece, where, sem))
    return copies


class Weight:
    def __init__(self, spec, arrays):
        self.spec = tuple(spec)
        self.arrays = list(arrays)
        self.count = len(self.arrays)

    def tied(self, *values):
        arrays, _ = lax.optimization_barrier((self.arrays, values))
        return Weight(self.spec, arrays)


def qkv_kernel(
    spec, place_ref, hid_ref, mask_ref, embed_ref, mods_ref, gain_ref, cos_ref, sin_ref, *rest
):
    n = len(spec)
    pieces = rest[:n]
    x_ref, q_ref, kvp_ref, kvc_ref, w_ref, sem = rest[n:]
    step = pl.program_id(0)

    @pl.when(step == 0)
    def _():
        copies = place(pieces, spec, place_ref, w_ref, sem)
        for copy in copies:
            copy.start()

        @pl.loop(0, CONTS)
        def _(block):
            rows = pl.ds(pl.multiple_of(block * CLEN, CLEN), CLEN)
            start = jnp.where(mask_ref[rows, :] > 0.5, embed_ref[...], hid_ref[rows, :].astype(f32))
            normed, _inv = layer_norm(start)
            row = pl.ds(block, 1)
            shift, scale = mods_ref[row, 0:D], mods_ref[row, D : 2 * D]
            x_ref[rows, :] = (normed * gain_ref[...] * (1.0 + scale) + shift).astype(bf16)

        for copy in copies:
            copy.wait()

    x = x_ref[...]
    cosine, sine = cos_ref[...], sin_ref[...]

    def part(third):
        return nn(x, w_ref[:, pl.ds(pl.multiple_of(third * D + step * GROUP, 128), GROUP)])

    q_ref[...] = (rotate(part(0), cosine, sine) * HDIM**-0.5).astype(bf16)
    k = rotate(part(1), cosine, sine).astype(bf16)
    kvp_ref[0], kvc_ref[0] = k[:HALF], k[HALF:]
    v = part(2).astype(bf16)
    kvp_ref[1], kvc_ref[1] = v[:HALF], v[HALF:]


def qkv_call(place_ids, hidden, mask, embed, mods, gain, cosine, sine, weight):
    n = weight.count
    width = weight.arrays[0].shape[1]
    half = pl.BlockSpec((2, HALF, GROUP), lambda g: (0, 0, g))
    return pl.pallas_call(
        partial(qkv_kernel, weight.spec),
        grid=(N_GROUP,),
        in_specs=[
            SCALAR,
            whole((PROMPT, D)),
            whole((PROMPT, 1)),
            whole((1, D)),
            whole(mods.shape),
            whole((1, D)),
            whole((PROMPT, 128)),
            whole((PROMPT, 128)),
        ]
        + [ANY] * n,
        out_specs=[whole((PROMPT, D)), pl.BlockSpec((PROMPT, GROUP), lambda g: (0, g)), half, half],
        out_shape=[
            jax.ShapeDtypeStruct((PROMPT, D), bf16),
            jax.ShapeDtypeStruct((PROMPT, D), bf16),
            jax.ShapeDtypeStruct((2, HALF, D), bf16),
            jax.ShapeDtypeStruct((2, HALF, D), bf16),
        ],
        scratch_shapes=[pltpu.VMEM((D, width), bf16), pltpu.SemaphoreType.DMA],
        compiler_params=pltpu.CompilerParams(vmem_limit_bytes=VMEM_LIMIT),
        cost_estimate=cost("qkv"),
        name="qkv",
    )(place_ids, hidden, mask, embed, mods, gain, cosine, sine, *weight.arrays)


def head_only(values, head):
    lane = lax.broadcasted_iota(jnp.int32, values.shape, 1)
    return jnp.where((lane < HDIM) if head == 0 else (lane >= HDIM), values, jnp.zeros_like(values))


def key_parts(prompt, other, own, rows, first):
    parts = [nt(prompt, rows), nt(other, rows)]
    if not first:
        cols = range(0, HALF, CLEN)
        parts.append(
            jnp.concatenate([nt(own[c : c + CLEN], rows[c : c + CLEN]) for c in cols], 1)
        )
    return parts


def attn_fwd_kernel(q_ref, kvp_ref, kvc_ref, kvr_ref, o_ref, lse_ref):
    kp, kc, kr = kvp_ref[0], kvc_ref[0], kvr_ref[0]
    vp_t, vc_t, vr_t = kvp_ref[1].T, kvc_ref[1].T, kvr_ref[1].T
    for start in (0, HALF):
        outs = []
        q_tile = q_ref[pl.ds(start, HALF), :]
        for head in range(2):
            lanes = slice(HDIM * head, HDIM * (head + 1))
            scores = key_parts(kp, kr, kc, head_only(q_tile, head), start == 0)
            top = jnp.max(scores[0], 0, keepdims=True)
            for part in scores[1:]:
                top = jnp.maximum(top, jnp.max(part, 0, keepdims=True))
            powers = [jnp.exp(part - top) for part in scores]
            total = jnp.sum(powers[0], 0, keepdims=True)
            for part in powers[1:]:
                total = total + jnp.sum(part, 0, keepdims=True)
            lse_ref[0, pl.ds(head, 1), pl.ds(start, HALF)] = top + jnp.log(total)
            scale = 1.0 / total
            probs = [(part * scale).astype(bf16) for part in powers]
            out = nn(vp_t[lanes], probs[0]) + nn(vr_t[lanes], probs[1])
            if start:
                cols = [slice(c, c + CLEN) for c in range(0, HALF, CLEN)]
                out = out + jnp.concatenate([nn(vc_t[lanes, c], probs[2][:, c]) for c in cols], 1)
            outs.append(out)
        o_ref[pl.ds(start, HALF), :] = jnp.concatenate(outs, 0).T.astype(bf16)


def pair_block(rows, first=0):
    return pl.BlockSpec((rows, 2 * HDIM), lambda pair: (0, first + pair))


def pair_half(first=0):
    return pl.BlockSpec((2, HALF, 2 * HDIM), lambda pair: (0, 0, first + pair))


def lse_block(first=0):
    return pl.BlockSpec((1, 2, PROMPT), lambda pair: (first + pair, 0, 0))


def attn_fwd(first, pairs, q, kvp, kvc, kvr, before=None):
    inputs = (q, kvp, kvc, kvr)
    in_specs = [pair_block(PROMPT, first)] + [pair_half(first)] * 3
    body = attn_fwd_kernel
    aliases = {}
    if before is not None:
        inputs += tuple(before)
        in_specs += [ANY, ANY]
        aliases = {4: 0, 5: 1}

        def body(q_ref, kvp_ref, kvc_ref, kvr_ref, _o, _lse, o_ref, lse_ref):
            attn_fwd_kernel(q_ref, kvp_ref, kvc_ref, kvr_ref, o_ref, lse_ref)

    return pl.pallas_call(
        body,
        grid=(pairs,),
        in_specs=in_specs,
        out_specs=[pair_block(PROMPT, first), lse_block(first)],
        out_shape=[
            jax.ShapeDtypeStruct((PROMPT, D), bf16),
            jax.ShapeDtypeStruct((PAIRS, 2, PROMPT), f32),
        ],
        input_output_aliases=aliases,
        compiler_params=pltpu.CompilerParams(vmem_limit_bytes=VMEM_LIMIT),
        cost_estimate=cost(f"attn_fwd{first}"),
        name=f"attn_fwd{first}",
    )(*inputs)


def attn_bwd_kernel(
    _ids, q_ref, kvp_ref, kvc_ref, kvr_ref, g_ref, lse_ref, cos_ref, sin_ref, gq_ref, gc_ref, dp_ref, dr_ref
):
    kp, kc, kr = kvp_ref[0], kvc_ref[0], kvr_ref[0]
    vp, vc, vr = kvp_ref[1], kvc_ref[1], kvr_ref[1]
    kp_t, kc_t, kr_t = kp.T, kc.T, kr.T
    first = lax.broadcasted_iota(jnp.int32, (HALF, 2 * HDIM), 1) < HDIM
    for start in (0, HALF):
        tile = pl.ds(start, HALF)
        q_tile, g_tile = q_ref[tile, :], g_ref[tile, :]
        cols = [slice(c, c + CLEN) for c in range(0, HALF, CLEN)]
        dqs, dks, dvs = [], [], []
        for head in range(2):
            lanes = slice(HDIM * head, HDIM * (head + 1))
            scores = key_parts(kp, kr, kc, head_only(q_tile, head), start == 0)
            dps = key_parts(vp, vr, vc, head_only(g_tile, head), start == 0)
            lse = lse_ref[0, pl.ds(head, 1), tile]
            probs = [jnp.exp(part - lse) for part in scores]
            row_dot = jnp.sum(probs[0] * dps[0], 0, keepdims=True)
            for p_part, d_part in zip(probs[1:], dps[1:]):
                row_dot = row_dot + jnp.sum(p_part * d_part, 0, keepdims=True)
            ds = [(p * (d - row_dot)).astype(bf16) for p, d in zip(probs, dps)]
            probs = [p.astype(bf16) for p in probs]
            dq = nn(kp_t[lanes], ds[0]) + nn(kr_t[lanes], ds[1])
            dk = [nn(ds[0], q_tile), nn(ds[1], q_tile)]
            dv = [nn(probs[0], g_tile), nn(probs[1], g_tile)]
            if start:
                dq = dq + jnp.concatenate([nn(kc_t[lanes, c], ds[2][:, c]) for c in cols], 1)
                dk.append(jnp.concatenate([nn(ds[2][:, c], q_tile[c]) for c in cols], 0))
                dv.append(jnp.concatenate([nn(probs[2][:, c], g_tile[c]) for c in cols], 0))
            dqs.append(dq)
            dks.append(dk)
            dvs.append(dv)
        cosine, sine = cos_ref[tile, :], sin_ref[tile, :]
        dq = jnp.concatenate(dqs, 0).T * HDIM**-0.5
        gq_ref[tile, :] = rotate(dq, cosine, -sine).astype(bf16)
        for which, parts in enumerate((dks, dvs)):
            merged = [jnp.where(first, a, b) for a, b in zip(*parts)]
            if start:
                dp_ref[which] += merged[0]
                dr_ref[which] += merged[1]
                last = merged[2] if which else rotate(merged[2], cosine, -sine)
                gc_ref[which] = last.astype(bf16)
            else:
                dp_ref[which] = merged[0]
                dr_ref[which] = merged[1]


def attn_bwd(ids, group, q, kvp, kvc, kvr, g, lse, cosine, sine):
    pairs = GROUP // (2 * HDIM)
    first = group * pairs
    return pl.pallas_call(
        attn_bwd_kernel,
        grid=(pairs,),
        in_specs=[SCALAR, pair_block(PROMPT, first)]
        + [pair_half(first)] * 3
        + [pair_block(PROMPT, first), lse_block(first), whole((PROMPT, 128)), whole((PROMPT, 128))],
        out_specs=[pair_block(PROMPT), pair_half(), pair_half(), pair_half()],
        out_shape=[
            jax.ShapeDtypeStruct((PROMPT, GROUP), bf16),
            jax.ShapeDtypeStruct((2, HALF, GROUP), bf16),
            jax.ShapeDtypeStruct((2, HALF, GROUP), f32),
            jax.ShapeDtypeStruct((2, HALF, GROUP), f32),
        ],
        compiler_params=pltpu.CompilerParams(vmem_limit_bytes=VMEM_LIMIT),
        cost_estimate=cost(f"attn_bwd{group}"),
        name=f"attn_bwd{group}",
    )(ids, q, kvp, kvc, kvr, g, lse, cosine, sine)


def up_kernel(
    specs,
    place_ref,
    o_ref,
    hid_ref,
    mask_ref,
    embed_ref,
    mods_ref,
    gain_ref,
    bias_ref,
    cot_ref,
    *rest,
):
    pieces, rest = take(specs, rest)
    ap_ref, mid_ref, x_ref, act_ref, gpre_ref, gmlp_ref, gbu_ref, gbd_ref = rest[:8]
    proj_ref, up_ref, down_ref, sems = rest[8:]
    step = pl.program_id(0)
    targets = (proj_ref, up_ref, down_ref)
    copies = [
        place(part, spec, place_ref, target, sems.at[i])
        for i, (part, spec, target) in enumerate(zip(pieces, specs, targets))
    ]

    @pl.when(step == 0)
    def _():
        for group in copies:
            for copy in group:
                copy.start()
        gbu_ref[...] = jnp.zeros_like(gbu_ref)
        gbd_ref[...] = jnp.zeros_like(gbd_ref)
        for copy in copies[0]:
            copy.wait()

    attn_proj = nn(o_ref[...], proj_ref[...])
    ap_ref[...] = attn_proj
    for sub in range(SUB):
        rows = slice(sub * CLEN, (sub + 1) * CLEN)
        row = pl.ds(step * SUB + sub, 1)
        start = jnp.where(mask_ref[rows, :] > 0.5, embed_ref[...], hid_ref[rows, :].astype(f32))
        middle = start + mods_ref[row, 2 * D : 3 * D] * attn_proj[rows]
        mid_ref[rows, :] = middle
        normed, _inv = layer_norm(middle)
        shift, scale = mods_ref[row, 3 * D : 4 * D], mods_ref[row, 4 * D : 5 * D]
        x_ref[rows, :] = (normed * gain_ref[...] * (1.0 + scale) + shift).astype(bf16)
        g_mlp = (mods_ref[row, 5 * D : 6 * D] * cot_ref[rows, :].astype(f32)).astype(bf16)
        gmlp_ref[rows, :] = g_mlp
        gbd_ref[...] += jnp.sum(g_mlp.astype(f32), 0, keepdims=True)

    @pl.when(step == 0)
    def _():
        for group in copies[1:]:
            for copy in group:
                copy.wait()

    x, g_mlp = x_ref[...], gmlp_ref[...]
    root = (2.0 / jnp.pi) ** 0.5
    for col in range(0, FF, CHUNK):
        cols = slice(col, col + CHUNK)
        pre = nn(x, up_ref[:, cols]) + bias_ref[:, cols]
        square = pre * pre
        curve = jnp.tanh(root * pre * (1.0 + 0.044715 * square))
        half_up = 0.5 * (1.0 + curve)
        act_ref[:, cols] = (pre * half_up).astype(bf16)
        slope = half_up + (0.5 * root) * pre * (1.0 - curve * curve) * (1.0 + 0.134145 * square)
        g_pre = (nt(g_mlp, down_ref[cols, :]) * slope).astype(bf16)
        gpre_ref[:, cols] = g_pre
        gbu_ref[:, cols] += jnp.sum(g_pre.astype(f32), 0, keepdims=True)


def take(specs, refs):
    pieces = []
    for spec in specs:
        pieces.append(refs[: len(spec)])
        refs = refs[len(spec) :]
    return pieces, refs


def tile_block(width):
    return pl.BlockSpec((TILE, width), lambda step: (step, 0))


def weight_scratch():
    return [
        pltpu.VMEM((D, D), bf16),
        pltpu.VMEM((D, FF), bf16),
        pltpu.VMEM((FF, D), bf16),
        pltpu.SemaphoreType.DMA((3,)),
    ]


def up_call(place_ids, attn_o, hidden, mask, embed, mods, gain, bias, cot, proj, up, down):
    weights = (proj, up, down)
    n = sum(w.count for w in weights)
    specs = tuple(w.spec for w in weights)
    arrays = [a for w in weights for a in w.arrays]
    rows = PROMPT
    return pl.pallas_call(
        partial(up_kernel, specs),
        grid=(rows // TILE,),
        in_specs=[
            SCALAR,
            tile_block(D),
            tile_block(D),
            tile_block(1),
            whole((1, D)),
            whole(mods.shape),
            whole((1, D)),
            whole((1, FF)),
            tile_block(D),
        ]
        + [ANY] * n,
        out_specs=[tile_block(D)] * 3
        + [tile_block(FF)] * 2
        + [tile_block(D), whole((1, FF)), whole((1, D))],
        out_shape=[
            jax.ShapeDtypeStruct((rows, D), f32),
            jax.ShapeDtypeStruct((rows, D), f32),
            jax.ShapeDtypeStruct((rows, D), bf16),
            jax.ShapeDtypeStruct((rows, FF), bf16),
            jax.ShapeDtypeStruct((rows, FF), bf16),
            jax.ShapeDtypeStruct((rows, D), bf16),
            jax.ShapeDtypeStruct((1, FF), f32),
            jax.ShapeDtypeStruct((1, D), f32),
        ],
        scratch_shapes=weight_scratch(),
        compiler_params=pltpu.CompilerParams(vmem_limit_bytes=VMEM_LIMIT),
        cost_estimate=cost("mlp_up"),
        name="mlp_up",
    )(place_ids, attn_o, hidden, mask, embed, mods, gain, bias, cot, *arrays)


def down_kernel(specs, place_ref, act_ref, gpre_ref, mid_ref, ap_ref, cot_ref, mods_ref, gain_ref, bias_ref, *rest):
    pieces, rest = take(specs, rest)
    out_ref, dmid_ref, gatt_ref, go_ref, stat_ref, ggain_ref = rest[:6]
    proj_ref, up_ref, down_ref, sems = rest[6:]
    step = pl.program_id(0)
    targets = (proj_ref, up_ref, down_ref)
    copies = [
        place(part, spec, place_ref, target, sems.at[i])
        for i, (part, spec, target) in enumerate(zip(pieces, specs, targets))
    ]

    @pl.when(step == 0)
    def _():
        for i in (2, 1, 0):
            for copy in copies[i]:
                copy.start()
        ggain_ref[...] = jnp.zeros_like(ggain_ref)
        for copy in copies[2]:
            copy.wait()

    mlp_out = nn(act_ref[...], down_ref[...]) + bias_ref[...]

    @pl.when(step == 0)
    def _():
        for i in (1, 0):
            for copy in copies[i]:
                copy.wait()

    g_n = nt(gpre_ref[...], up_ref[...])
    for sub in range(SUB):
        rows = slice(sub * CLEN, (sub + 1) * CLEN)
        row = pl.ds(step * SUB + sub, 1)
        middle, cot, grad = mid_ref[rows, :], cot_ref[rows, :].astype(f32), g_n[rows]
        gate_attn, gate_mlp = mods_ref[row, 2 * D : 3 * D], mods_ref[row, 5 * D : 6 * D]
        scale = 1.0 + mods_ref[row, 4 * D : 5 * D]
        out_ref[rows, :] = (middle + gate_mlp * mlp_out[rows]).astype(bf16)
        normed, inv_std = layer_norm(middle)
        along = jnp.sum(grad * normed, 0, keepdims=True)
        ggain_ref[...] += along * scale
        d_middle = cot + norm_back(grad * (scale * gain_ref[...]), normed, inv_std)
        dmid_ref[rows, :] = d_middle
        gatt_ref[rows, :] = (gate_attn * d_middle).astype(bf16)
        stat_ref[row, 0:D] = jnp.sum(d_middle * ap_ref[rows, :], 0, keepdims=True)
        stat_ref[row, D : 2 * D] = jnp.sum(grad, 0, keepdims=True)
        stat_ref[row, 2 * D : 3 * D] = along * gain_ref[...]
        stat_ref[row, 3 * D : 4 * D] = jnp.sum(cot * mlp_out[rows], 0, keepdims=True)
    go_ref[...] = nt(gatt_ref[...], proj_ref[...]).astype(bf16)


def down_call(place_ids, act, gpre, middle, attn_proj, cot, mods, gain, bias, proj, up, down):
    weights = (proj, up, down)
    n = sum(w.count for w in weights)
    specs = tuple(w.spec for w in weights)
    arrays = [a for w in weights for a in w.arrays]
    rows = PROMPT
    return pl.pallas_call(
        partial(down_kernel, specs),
        grid=(rows // TILE,),
        in_specs=[
            SCALAR,
            tile_block(FF),
            tile_block(FF),
            tile_block(D),
            tile_block(D),
            tile_block(D),
            whole(mods.shape),
            whole((1, D)),
            whole((1, D)),
        ]
        + [ANY] * n,
        out_specs=[tile_block(D)] * 4 + [whole((CONTS, 4 * D)), whole((1, D))],
        out_shape=[
            jax.ShapeDtypeStruct((rows, D), bf16),
            jax.ShapeDtypeStruct((rows, D), f32),
            jax.ShapeDtypeStruct((rows, D), bf16),
            jax.ShapeDtypeStruct((rows, D), bf16),
            jax.ShapeDtypeStruct((CONTS, 4 * D), f32),
            jax.ShapeDtypeStruct((1, D), f32),
        ],
        scratch_shapes=weight_scratch(),
        compiler_params=pltpu.CompilerParams(vmem_limit_bytes=VMEM_LIMIT),
        cost_estimate=cost("mlp_down"),
        name="mlp_down",
    )(place_ids, act, gpre, middle, attn_proj, cot, mods, gain, bias, *arrays)


def split_store(total, keep_ref, send_ref, core, lead, at):
    for pair in range(total.shape[0] // lead // 2):
        even = total[2 * pair * lead : (2 * pair + 1) * lead].astype(bf16)
        odd = total[(2 * pair + 1) * lead : (2 * pair + 2) * lead].astype(bf16)
        keep_ref[pair, at : at + lead, :] = jnp.where(core == 0, even, odd)
        send_ref[pair, at : at + lead, :] = jnp.where(core == 0, odd, even)


def wgrad_kernel(lead, place_ref, left_ref, right_ref, keep_ref, send_ref):
    split_store(tn(left_ref[...], right_ref[...]), keep_ref, send_ref, place_ref[1], lead, 0)


def wgrad_call(place_ids, left, right, n, name):
    lead = D // n
    blocks = right.shape[1] // D
    out = pl.BlockSpec((n // 2, lead, D), lambda j: (0, j, 0))
    shape = jax.ShapeDtypeStruct((n // 2, blocks * lead, D), bf16)
    return pl.pallas_call(
        partial(wgrad_kernel, lead),
        grid=(blocks,),
        in_specs=[SCALAR, whole((PROMPT, D)), pl.BlockSpec((PROMPT, D), lambda j: (0, j))],
        out_specs=[out, out],
        out_shape=[shape, shape],
        compiler_params=pltpu.CompilerParams(vmem_limit_bytes=VMEM_LIMIT),
        cost_estimate=cost(name),
        name=name,
    )(place_ids, left, right)


def down_grad_kernel(_ids, left_ref, right_ref, keep_ref, send_ref):
    half = pl.num_programs(0) // 2
    total = tn(left_ref[...], right_ref[...]).astype(bf16)

    @pl.when(pl.program_id(0) < half)
    def _():
        send_ref[0] = total

    @pl.when(pl.program_id(0) >= half)
    def _():
        keep_ref[0] = total


def down_grad_call(place_ids, act, g_mlp, n):
    rows = FF // n
    half = n // 2

    def shard(j, ids):
        core = ids[1]
        return 0, jnp.where(j < half, 2 * j + 1 - core, 2 * (j - half) + core)

    shape = jax.ShapeDtypeStruct((half, rows, D), bf16)
    return pl.pallas_call(
        down_grad_kernel,
        grid_spec=pltpu.PrefetchScalarGridSpec(
            num_scalar_prefetch=1,
            grid=(n,),
            in_specs=[pl.BlockSpec((PROMPT, rows), shard), pl.BlockSpec((PROMPT, D), lambda j, ids: (0, 0))],
            out_specs=[
                pl.BlockSpec((1, rows, D), lambda j, ids: (jnp.maximum(j - half, 0), 0, 0)),
                pl.BlockSpec((1, rows, D), lambda j, ids: (jnp.minimum(j, half - 1), 0, 0)),
            ],
        ),
        out_shape=[shape, shape],
        compiler_params=pltpu.CompilerParams(vmem_limit_bytes=VMEM_LIMIT),
        cost_estimate=cost("down_grad"),
        name="down_grad",
    )(place_ids, act, g_mlp)


def down_grad_any(place_ids, act, g_mlp, n):
    if (FF // n) % 128 == 0 and n == 4:
        return down_grad_call(place_ids, act, g_mlp, n)
    full = wide_grad_call(act, g_mlp)
    core = lax.axis_index("shard") % 2
    parts = full.reshape(n // 2, 2, -1, D)
    keep = lax.dynamic_index_in_dim(parts, core, 1, False)
    return keep, lax.dynamic_index_in_dim(parts, 1 - core, 1, False)


def wide_grad_kernel(left_ref, right_ref, out_ref):
    out_ref[...] = tn(left_ref[...], right_ref[...]).astype(bf16)


def wide_grad_call(act, g_mlp):
    return pl.pallas_call(
        wide_grad_kernel,
        grid=(FF // D,),
        in_specs=[pl.BlockSpec((PROMPT, D), lambda j: (0, j)), whole((PROMPT, D))],
        out_specs=pl.BlockSpec((D, D), lambda j: (j, 0)),
        out_shape=jax.ShapeDtypeStruct((FF, D), bf16),
        compiler_params=pltpu.CompilerParams(vmem_limit_bytes=VMEM_LIMIT),
        name="wide_grad",
    )(act, g_mlp)


def qkv_grad_kernel(lead, with_proj, with_ada, place_ref, x_ref, gq_ref, gc_ref, dp_ref, got_ref, cos_ref, sin_ref, *rest):
    keep_ref, send_ref, g_ref = rest[-3:]
    core = place_ref[1]
    g_ref[:, 0:GROUP] = gq_ref[...]
    total_k = dp_ref[0] + got_ref[0].astype(f32)
    total_v = dp_ref[1] + got_ref[1].astype(f32)
    g_ref[0:HALF, GROUP : 2 * GROUP] = rotate(total_k, cos_ref[...], -sin_ref[...]).astype(bf16)
    g_ref[0:HALF, 2 * GROUP : 3 * GROUP] = total_v.astype(bf16)
    g_ref[HALF:PROMPT, GROUP : 2 * GROUP] = gc_ref[0]
    g_ref[HALF:PROMPT, 2 * GROUP : 3 * GROUP] = gc_ref[1]
    split_store(tn(x_ref[...], g_ref[...]), keep_ref, send_ref, core, lead, 0)
    at = lead
    if with_proj:
        split_store(tn(rest[0][...], rest[1][...]), keep_ref, send_ref, core, lead, at)
        at += lead
        rest = rest[2:]
    if with_ada:
        cond = rest[0][...]
        silu = (cond / (1.0 + jnp.exp(-cond))).astype(bf16).astype(f32)
        few = cond.shape[1] * lead // D
        for col in range(4):
            total = exact(silu, rest[1][:, col * D : (col + 1) * D], ((0,), (0,)))
            split_store(total, keep_ref, send_ref, core, few, at)
            at += few


def qkv_grad_call(place_ids, x, gq, gc, dp, got, cosine, sine, n, name, proj, ada):
    lead = D // n
    rows = lead
    extra = []
    if proj is not None:
        extra += list(proj)
        rows += lead
    if ada is not None:
        extra += list(ada)
        rows += 4 * (ada[0].shape[1] // n)
    out = whole((n // 2, rows, D))
    shape = jax.ShapeDtypeStruct((n // 2, rows, D), bf16)
    return pl.pallas_call(
        partial(qkv_grad_kernel, lead, proj is not None, ada is not None),
        grid=(1,),
        in_specs=[
            SCALAR,
            whole((PROMPT, D)),
            whole((PROMPT, GROUP)),
            whole((2, HALF, GROUP)),
            whole((2, HALF, GROUP)),
            whole((2, HALF, GROUP)),
            whole((HALF, 128)),
            whole((HALF, 128)),
        ]
        + [whole(e.shape) for e in extra],
        out_specs=[out, out, whole((PROMPT, D))],
        out_shape=[shape, shape, jax.ShapeDtypeStruct((PROMPT, D), bf16)],
        compiler_params=pltpu.CompilerParams(vmem_limit_bytes=VMEM_LIMIT),
        cost_estimate=cost(name),
        name=name,
    )(place_ids, x, gq, gc, dp, got, cosine, sine, *extra)


def start_kernel(spec, place_ref, hid_ref, mask_ref, embed_ref, mods_ref, gain_ref, dmid_ref, *rest):
    n = len(spec)
    grads, pieces = rest[:N_GROUP], rest[N_GROUP : N_GROUP + n]
    gh_ref, stat_ref, ggain_ref, gmask_ref, w_ref, sem = rest[N_GROUP + n :]
    step = pl.program_id(0)

    @pl.when(step == 0)
    def _():
        copies = place(pieces, spec, place_ref, w_ref, sem)
        for copy in copies:
            copy.start()
        ggain_ref[...] = jnp.zeros_like(ggain_ref)
        gmask_ref[...] = jnp.zeros_like(gmask_ref)
        for copy in copies:
            copy.wait()

    g_n = None
    for group in range(N_GROUP):
        for third in range(3):
            at = third * D + group * GROUP
            term = nt(grads[group][:, third * GROUP : (third + 1) * GROUP], w_ref[:, at : at + GROUP])
            g_n = term if g_n is None else g_n + term
    for sub in range(SUB):
        rows = slice(sub * CLEN, (sub + 1) * CLEN)
        row = pl.ds(step * SUB + sub, 1)
        masked = mask_ref[rows, :] > 0.5
        start = jnp.where(masked, embed_ref[...], hid_ref[rows, :].astype(f32))
        normed, inv_std = layer_norm(start)
        scale = 1.0 + mods_ref[row, D : 2 * D]
        grad = g_n[rows]
        along = jnp.sum(grad * normed, 0, keepdims=True)
        ggain_ref[...] += along * scale
        stat_ref[row, 0:D] = jnp.sum(grad, 0, keepdims=True)
        stat_ref[row, D : 2 * D] = along * gain_ref[...]
        d_start = dmid_ref[rows, :] + norm_back(grad * (scale * gain_ref[...]), normed, inv_std)
        gh_ref[rows, :] = jnp.where(masked, 0.0, d_start)
        gmask_ref[...] += jnp.sum(jnp.where(masked, d_start, 0.0), 0, keepdims=True)


def start_call(place_ids, hidden, mask, embed, mods, gain, d_middle, grads, weight):
    n = weight.count
    rows = PROMPT
    return pl.pallas_call(
        partial(start_kernel, weight.spec),
        grid=(rows // TILE,),
        in_specs=[
            SCALAR,
            tile_block(D),
            tile_block(1),
            whole((1, D)),
            whole(mods.shape),
            whole((1, D)),
            tile_block(D),
        ]
        + [tile_block(D)] * N_GROUP
        + [ANY] * n,
        out_specs=[tile_block(D), whole((CONTS, 2 * D)), whole((1, D)), whole((1, D))],
        out_shape=[
            jax.ShapeDtypeStruct((rows, D), f32),
            jax.ShapeDtypeStruct((CONTS, 2 * D), f32),
            jax.ShapeDtypeStruct((1, D), f32),
            jax.ShapeDtypeStruct((1, D), f32),
        ],
        scratch_shapes=[pltpu.VMEM((D, 3 * D), bf16), pltpu.SemaphoreType.DMA],
        compiler_params=pltpu.CompilerParams(vmem_limit_bytes=VMEM_LIMIT),
        cost_estimate=cost("start_grad"),
        name="start_grad",
    )(place_ids, hidden, mask, embed, mods, gain, d_middle, *grads, *weight.arrays)


def pack_kernel(*refs):
    out_ref = refs[-1]
    out_ref[...] = jnp.zeros_like(out_ref)
    for i, ref in enumerate(refs[:-1]):
        out_ref[i : i + 1, 0 : ref.shape[0]] = ref[...].astype(f32).reshape(1, -1)


def pack_call(vectors):
    shape = (8, max(v.shape[0] for v in vectors))
    return pl.pallas_call(
        pack_kernel,
        grid=(1,),
        in_specs=[whole(v.shape) for v in vectors],
        out_specs=whole(shape),
        out_shape=jax.ShapeDtypeStruct(shape, f32),
        name="pack",
    )(*vectors)


def mods_kernel(spec, lengths, times_ref, place_ref, table_ref, *rest):
    n = len(spec)
    pieces, rest = rest[:n], rest[n:]
    count = len(lengths)
    n_row = len(rest) - count - 6
    rows, rest = rest[:n_row], rest[n_row:]
    mods_ref, cond_ref, ada_ref = rest[:3]
    out_refs = rest[3 : 3 + count - 1]
    bias_ref, row_ref, sem, row_sem = rest[3 + count - 1 :]
    copies = place(pieces, spec, place_ref, ada_ref, sem)
    row_copies = [
        pltpu.make_async_copy(row, row_ref.at[place_ref[0] ^ offset], row_sem) for offset, row in enumerate(rows)
    ]
    for copy in row_copies + copies:
        copy.start()
    for block in range(CONTS):
        cond_ref[pl.ds(block, 1), :] = table_ref[pl.ds(times_ref[block], 1), :]
    cond = cond_ref[...]
    silu = (cond / (1.0 + jnp.exp(-cond))).astype(bf16)
    for copy in row_copies:
        copy.wait()
    for shard in range(n_row):
        for i, (length, ref) in enumerate(zip(lengths, (*out_refs, bias_ref))):
            ref[0:1, shard * length : (shard + 1) * length] = row_ref[shard, i : i + 1, 0:length]
    for copy in copies:
        copy.wait()
    mods_ref[...] = nn(silu, ada_ref[...]) + bias_ref[...]


def mods_call(times, place_ids, table, weight, rows, lengths):
    width = weight.arrays[0].shape[1]
    n = len(rows)
    vectors = [(1, n * length) for length in lengths]
    shapes = [(CONTS, width), (CONTS, table.shape[1])]
    return pl.pallas_call(
        partial(mods_kernel, weight.spec, tuple(lengths)),
        in_specs=[SCALAR, SCALAR, whole(table.shape)] + [ANY] * (weight.count + n),
        out_specs=[whole(s) for s in shapes] + [whole((table.shape[1], width))] + [whole(v) for v in vectors[:-1]],
        out_shape=[jax.ShapeDtypeStruct(s, f32) for s in shapes]
        + [jax.ShapeDtypeStruct((table.shape[1], width), bf16)]
        + [jax.ShapeDtypeStruct(v, f32) for v in vectors[:-1]],
        grid=(1,),
        scratch_shapes=[
            pltpu.VMEM(vectors[-1], f32),
            pltpu.VMEM((n,) + rows[0].shape, f32),
            pltpu.SemaphoreType.DMA,
            pltpu.SemaphoreType.DMA,
        ],
        compiler_params=pltpu.CompilerParams(vmem_limit_bytes=VMEM_LIMIT),
        cost_estimate=cost("mods"),
        name="mods",
    )(times, place_ids, table, *weight.arrays, *rows)


def last_kernel(
    lead, time_rows, place_ref, cond_ref, ada_ref, stat1_ref, stat2_ref, ga_ref, gm_ref, bu_ref, bd_ref, me_ref,
    keep_ref, send_ref, small_ref,
):
    core, pair = place_ref[1], place_ref[2]
    cond = cond_ref[...]
    gate = 1.0 / (1.0 + jnp.exp(-cond))
    silu = (cond * gate).astype(bf16).astype(f32)
    stat1, stat2 = stat1_ref[...], stat2_ref[...]
    ada_late = exact(silu, stat1, ((0,), (0,)))
    ada = ada_ref[...].astype(f32)
    g_silu = exact(stat1, ada[:, : 2 * D], ((1,), (1,))) + exact(stat2, ada[:, 2 * D :], ((1,), (1,)))
    g_cond = g_silu * (gate * (1.0 + cond * (1.0 - gate)))
    small_ref[...] = jnp.zeros_like(small_ref)
    at = time_rows
    small_ref[at : at + 1, :] = ga_ref[...]
    small_ref[at + 1 : at + 2, :] = gm_ref[...]
    for i in range(FF // D):
        small_ref[at + 2 + i : at + 3 + i, :] = bu_ref[:, i * D : (i + 1) * D]
    small_ref[at + 6 : at + 7, :] = bd_ref[...]
    for i in range(2):
        small_ref[at + 7 + i : at + 8 + i, :] = jnp.sum(stat1[:, i * D : (i + 1) * D], 0, keepdims=True)
    for i in range(4):
        small_ref[at + 9 + i : at + 10 + i, :] = jnp.sum(stat2[:, i * D : (i + 1) * D], 0, keepdims=True)
    small_ref[at + 13 : at + 14, :] = me_ref[...]
    half = CONTS // 2
    prompt = jnp.sum(g_cond[:half], 0, keepdims=True)
    values = [prompt] + [g_cond[half + i : half + i + 1] for i in range(half)]
    base = pair * (CONTS + 1)
    where_to = [base] + [base + 1 + core * half + i for i in range(half)]
    for lane in range(D // 128):
        row = lax.broadcasted_iota(jnp.int32, (time_rows, 128), 0) + lane * time_rows
        placed = jnp.zeros((time_rows, 128), f32)
        for index, value in zip(where_to, values):
            placed = placed + jnp.where(row == index, value, 0.0)
        small_ref[0:time_rows, lane * 128 : (lane + 1) * 128] = placed
    small = small_ref[...]
    high = small.astype(bf16)
    rows = small.shape[0]
    low = (small[time_rows:] - high[time_rows:].astype(f32)).astype(bf16)
    for j in range(keep_ref.shape[0]):
        for col in range(2):
            split_store(ada_late[:, col * D : (col + 1) * D], keep_ref, send_ref, core, lead, col * lead)
        row = 2 * lead
        for ref in (keep_ref, send_ref):
            ref[j, row : row + rows, :] = high
            ref[j, row + rows : row + rows + 16, :] = low


def last_call(place_ids, cond, ada, stat1, stat2, vectors, n, time_rows):
    lead = ada.shape[0] // n
    rows = 16 + time_rows
    args = (cond, ada, stat1, stat2) + tuple(vectors)
    out = whole((n // 2, 2 * lead + rows + 16, D))
    shape = jax.ShapeDtypeStruct((n // 2, 2 * lead + rows + 16, D), bf16)
    return pl.pallas_call(
        partial(last_kernel, lead, time_rows),
        grid=(1,),
        in_specs=[SCALAR] + [whole(a.shape) for a in args],
        out_specs=[out, out],
        out_shape=[shape, shape],
        scratch_shapes=[pltpu.VMEM((rows, D), f32)],
        compiler_params=pltpu.CompilerParams(vmem_limit_bytes=VMEM_LIMIT),
        cost_estimate=cost("last"),
        name="last",
    )(place_ids, *args)


def swap(value, axis, mask):
    pairs = [(source, source ^ mask) for source in range(lax.axis_size(axis))]
    return lax.ppermute(value, axis, pairs)


def gather_far(piece):
    pieces = {0: piece}
    mask = lax.axis_size("shard") // 2
    while mask > 1:
        for offset in list(pieces):
            pieces[offset | mask] = swap(pieces[offset], "shard", mask)
        mask //= 2
    return pieces


def gather_near(pieces):
    pieces = dict(pieces)
    for offset in list(pieces):
        pieces[offset | 1] = swap(pieces[offset], "shard", 1)
    return [pieces[offset] for offset in range(len(pieces))]


def sides():
    rep = lax.axis_index("rep")
    return rep % 2, rep % 4


def far_parts(piece, split=1):
    rows = piece.shape[0] // split
    if split == 1 or rows % 16:
        return 1, gather_far(piece)
    side = sides()[0 if split == 2 else 1]
    found = gather_far(lax.dynamic_slice_in_dim(piece, side * rows, rows, 0))
    found[0] = piece
    return split, found


def far_weight(split, found, tie=None):
    if tie is not None:
        found, _ = lax.optimization_barrier((found, tie))
    spec, arrays = [], []
    for offset, part in found.items():
        if split == 1 or not offset:
            spec.append((offset, 1, 0))
            arrays.append(part)
            continue
        spec += [(offset, split, code) for code in range(split)]
        arrays += [part] + [swap(part, "rep", code) for code in range(1, split)]
    return Weight(spec, arrays)


def near_weight(far):
    spec, arrays = list(far.spec), list(far.arrays)
    for (offset, split, code), part in zip(far.spec, far.arrays):
        spec.append((offset | 1, split, code))
        arrays.append(swap(part, "shard", 1))
    if all(part.shape[0] % 16 == 0 for part in arrays):
        return Weight(spec, arrays)
    mine = lax.axis_index("shard")
    rows = arrays[0].shape[0]
    out = jnp.zeros((rows * len(arrays),) + arrays[0].shape[1:], arrays[0].dtype)
    for (offset, _split, _code), part in zip(spec, arrays):
        out = lax.dynamic_update_slice_in_dim(out, part, (mine ^ offset) * rows, 0)
    return Weight([(None, 1, 0)], [out])


def add_plain(left, right):
    return left.astype(f32) + right.astype(f32)


def add_packed(left, right):
    rows = left.shape[-2] - 16
    total = add_plain(left[..., :rows, :], right[..., :rows, :])
    rest = add_plain(left[..., rows:, :], right[..., rows:, :])
    return jnp.concatenate([total[..., : rows - 16, :], total[..., rows - 16 :, :] + rest], -2)


def pack_plain(value):
    return value.astype(bf16)


def pack_packed(value):
    high = value.astype(bf16)
    low = value[..., -16:, :] - high[..., -16:, :].astype(f32)
    return jnp.concatenate([high, low.astype(bf16)], -2)


def reduce_chain(keep, send, steps, add=add_plain, pack=pack_plain):
    mine, rep = lax.axis_index("shard"), lax.axis_index("rep")
    got = yield send, swap(send, "shard", 1)
    value = pack(add(keep, got))
    mask = 2
    while mask < lax.axis_size("shard"):
        bit = (mine // mask) % 2
        halves = value.reshape((-1, 2) + value.shape[1:])
        keep = lax.dynamic_index_in_dim(halves, bit, 1, False)
        send = lax.dynamic_index_in_dim(halves, 1 - bit, 1, False)
        got = yield send, swap(send, "shard", mask)
        value = pack(add(keep, got))
        mask *= 2
    value = value[0]
    more = range(3, lax.axis_size("rep").bit_length() - 1)
    steps = [(bit, "all") for bit in more] + list(steps)
    for at, kind in steps:
        bit = (rep >> at) % 2
        if kind == "split":
            halves = value.reshape(2, -1, value.shape[-1])
            keep = lax.dynamic_index_in_dim(halves, bit, 0, False)
            send = lax.dynamic_index_in_dim(halves, 1 - bit, 0, False)
            got = yield send, swap(send, "rep", 1 << at)
            value = pack(add(keep, got))
        elif kind == "join":
            got = yield value, swap(value, "rep", 1 << at)
            last = (value, got, at)
            first, second = jnp.where(bit == 0, value, got), jnp.where(bit == 0, got, value)
            value = jnp.concatenate([first, second], 0)
        else:
            got = yield value, swap(value, "rep", 1 << at)
            last, value = (value, got, None), pack(add(value, got))
    return last


class Schedule:
    def __init__(self, ids, rows):
        self.ids = ids
        self.chains = {}
        self.sent = {}
        self.done = {}
        self.final = {}
        self.rows = rows

    def begin(self, name, keep, send, *how):
        chain = reduce_chain(keep, send, *how)
        self.chains[name] = chain
        _sent, self.sent[name] = next(chain)

    def start(self, name, keep, send, names):
        (send,) = self.sync(*(other for other in names if other != name), after=(send,))
        self.begin(name, keep, send, ROUTES[name])
        self.sync(*(other for other in names if other == name), after=(send,))

    def sync(self, *names, after=()):
        for name in names or (None,):
            if name is not None and name not in self.sent:
                continue
            got = self.sent.pop(name, None)
            self.ids, got, after = lax.optimization_barrier((self.ids, got, tuple(after)))
            if got is None:
                continue
            try:
                sent, self.sent[name] = self.chains[name].send(got)
                self.ids, _ = lax.optimization_barrier((self.ids, sent))
            except StopIteration as stop:
                self.done[name] = stop.value
                if name in self.rows:
                    self.final[name] = finish_blocks(self.ids, stop.value, *self.rows[name], f"finish_{name}")
        return after

    def finish(self, *names):
        for name in names:
            self.sync(name)
        while self.sent:
            self.sync(next(iter(self.sent)))


def add_two(a_ref, b_ref):
    return a_ref[...].astype(f32) + b_ref[...].astype(f32)


def bit_of(place_ref, at):
    return place_ref[4] // (1 << at) % 2


def whole_sum(place_ref, a_ref, b_ref, at):
    if at is None:
        return add_two(a_ref, b_ref)
    first, second = a_ref[...].astype(f32), b_ref[...].astype(f32)
    swapped = bit_of(place_ref, at) == 1
    return jnp.concatenate([jnp.where(swapped, second, first), jnp.where(swapped, first, second)], 0)


def finish_kernel(at, place_ref, a_ref, b_ref, out_ref):
    if at is None:
        out_ref[...] = add_two(a_ref, b_ref)
    else:
        late = 2 * pl.program_id(0) // pl.num_programs(0)
        out_ref[...] = jnp.where(late == bit_of(place_ref, at), a_ref[...], b_ref[...]).astype(f32)


def finish_blocks(place_ids, result, rows, wide, name):
    a, b, at = result
    count = (a.shape[0] if at is None else 2 * a.shape[0]) // rows
    had = a.shape[0] // rows
    block = pl.BlockSpec((rows, D), lambda j: (j % had, 0))
    return pl.pallas_call(
        partial(finish_kernel, at),
        grid=(count,),
        in_specs=[SCALAR, block, block],
        out_specs=pl.BlockSpec((rows, D), lambda j: (0, j) if wide else (j, 0)),
        out_shape=jax.ShapeDtypeStruct((rows, count * D) if wide else (count * rows, D), f32),
        cost_estimate=cost(name),
        name=name,
    )(place_ids, a, b)


def finish_qkv_kernel(lead, ats, place_ref, *refs):
    qkv_ref, proj_ref = refs[2 * N_GROUP :]
    for group, at in enumerate(ats):
        total = whole_sum(place_ref, refs[2 * group], refs[2 * group + 1], at)
        for third in range(3):
            col = third * D + group * GROUP
            qkv_ref[:, col : col + GROUP] = total[:lead, third * GROUP : (third + 1) * GROUP]
        if group == 0:
            proj_ref[...] = total[lead : 2 * lead]


def finish_qkv(place_ids, results, lead):
    arrays = [a for result in results for a in result[:2]]
    shapes = [(lead, 3 * D), (lead, D)]
    return pl.pallas_call(
        partial(finish_qkv_kernel, lead, tuple(result[2] for result in results)),
        grid=(1,),
        in_specs=[SCALAR] + [whole(a.shape) for a in arrays],
        out_specs=[whole(s) for s in shapes],
        out_shape=[jax.ShapeDtypeStruct(s, f32) for s in shapes],
        cost_estimate=cost("finish_qkv"),
        compiler_params=pltpu.CompilerParams(vmem_limit_bytes=VMEM_LIMIT),
        name="finish_qkv",
    )(place_ids, *arrays)


def finish_last_kernel(
    n, lead, time_rows, few, early_at, place_ref, ids_ref, a_ref, b_ref, ea_ref, eb_ref, ada_ref, time_ref, *out_refs
):
    mine = place_ref[0]
    for i in range(2):
        rows = slice(i * few, (i + 1) * few)
        ada_ref[:, i * D : (i + 1) * D] = add_two(a_ref.at[rows], b_ref.at[rows])
    early = whole_sum(place_ref, ea_ref, eb_ref, early_at)
    for i in range(4):
        ada_ref[:, (2 + i) * D : (3 + i) * D] = early[lead + i * few : lead + (i + 1) * few]
    at = 2 * few
    times = add_two(a_ref.at[at : at + time_rows], b_ref.at[at : at + time_rows])
    times = jnp.concatenate([times[:, i * 128 : (i + 1) * 128] for i in range(D // 128)], 0)
    steps = lax.broadcasted_iota(jnp.int32, (STEPS, times.shape[0]), 0)
    hot = jnp.where(steps == ids_ref[...], 1.0, 0.0).astype(f32)
    time_ref[...] = exact(hot, times, ((1,), (0,)))
    at += time_rows
    high = add_two(a_ref.at[at : at + 16], b_ref.at[at : at + 16])
    small = high + add_two(a_ref.at[at + 16 : at + 32], b_ref.at[at + 16 : at + 32])
    first = 0
    for ref, count in zip(out_refs, (1, 1, 4, 1, 6, 1)):
        flat = jnp.concatenate([small[first + i : first + i + 1] for i in range(count)], 1)
        size = count * D // n
        share = flat[:, 0:size]
        for shard in range(1, n):
            share = jnp.where(mine == shard, flat[:, shard * size : (shard + 1) * size], share)
        ref[...] = share.reshape(size)
        first += count


def finish_last(place_ids, ids, pair, early, n, time_rows, few):
    lead = D // n
    sizes = [(count * D // n,) for count in (1, 1, 4, 1, 6, 1)]
    shapes = [(few, 6 * D), (STEPS, 128)] + sizes
    arrays = [ids, *pair[:2], *early[:2]]
    return pl.pallas_call(
        partial(finish_last_kernel, n, lead, time_rows, few, early[2]),
        grid=(1,),
        in_specs=[SCALAR] + [whole(a.shape) for a in arrays],
        out_specs=[whole(s) for s in shapes],
        out_shape=[jax.ShapeDtypeStruct(s, f32) for s in shapes],
        cost_estimate=cost("finish_last"),
        compiler_params=pltpu.CompilerParams(vmem_limit_bytes=VMEM_LIMIT),
        name="finish_last",
    )(place_ids, *arrays)


ROUTES = {'down': ((1, 'all'), (2, 'all'), (0, 'all')),
 'last': ((0, 'all'), (1, 'all'), (2, 'all')),
 'qkv0': ((1, 'all'), (2, 'all'), (0, 'all')),
 'qkv1': ((0, 'split'), (1, 'split'), (2, 'all'), (1, 'join'), (0, 'join')),
 'qkv2': ((0, 'split'), (1, 'split'), (2, 'all'), (1, 'join'), (0, 'join')),
 'up': ((0, 'split'), (1, 'split'), (2, 'all'), (1, 'join'), (0, 'join'))}
SYNCS = (('up', 'down'),
 (),
 ('up', 'down'),
 (),
 ('up', 'qkv0'),
 ('up',),
 ('qkv1', 'qkv0', 'qkv2', 'down'),
 ('qkv1', 'up', 'qkv0', 'qkv2'),
 ('up',
  'down',
  'last',
  'qkv1',
  'qkv2',
  'last',
  'up',
  'qkv1',
  'qkv2',
  'qkv0',
  'last',
  'qkv1',
  'qkv2',
  'last',
  'qkv1',
  'qkv2',
  'qkv0',
  'qkv1',
  'qkv2',
  'last'),
 ('down',))


def on_device(
    hidden_in,
    mask_ids,
    time_ids,
    time_table,
    w_qkv,
    w_proj,
    w_up,
    w_down,
    w_ada,
    gain_attn,
    gain_mlp,
    bias_up,
    bias_down,
    bias_ada,
    mask_embed,
    cotangent,
):
    n = lax.axis_size("shard")
    mine = lax.axis_index("shard")
    core = mine % 2
    pair = (lax.axis_index("rep") * n + mine) // 2
    ids = jnp.stack([mine, core, pair, *sides()]).astype(jnp.int32)
    barrier = lax.optimization_barrier

    vectors = (gain_attn, gain_mlp, bias_up, bias_down, mask_embed, bias_ada)
    lengths = [v.shape[0] for v in vectors]
    row_far = gather_far(pack_call(vectors))
    local = jnp.arange(PROMPT, dtype=jnp.int32)
    positions = jnp.where(local < HALF, core * HALF + local, PROMPT + local % CLEN).astype(f32)
    freqs = 10000.0 ** (-(2.0 * jnp.arange(HDIM // 2, dtype=f32)) / HDIM)
    lanes = jnp.tile(freqs, 4)
    angles = positions[:, None] * lanes[None, :]
    sign = jnp.where(jnp.arange(128) % HDIM < HDIM // 2, -1.0, 1.0).astype(f32)
    cosine, sine = jnp.cos(angles), jnp.sin(angles) * sign[None, :]
    mask = (mask_ids == 1).astype(f32)[:, None]
    ada_far = far_weight(*far_parts(w_ada), (cosine, sine, mask))
    qkv_far = far_weight(*far_parts(w_qkv, 4))
    ada_weight = near_weight(ada_far)
    rows = gather_near(row_far)
    (proj_own, up_own, down_own), _ = barrier(((w_proj, w_up, w_down), ada_far.arrays))
    up_split, up_found = far_parts(up_own, 4)
    proj_far = far_weight(*far_parts(proj_own))
    down_split, down_found = far_parts(down_own, 2)

    block = jnp.arange(CONTS, dtype=jnp.int32)
    seg = jnp.where(block < CONTS // 2, 0, 1 + core * (CONTS // 2) + block - CONTS // 2)
    my_times = lax.dynamic_slice_in_dim(time_ids, pair, 1, 0)
    times = jnp.sum(jnp.where(seg[:, None] == jnp.arange(CONTS + 1, dtype=jnp.int32)[None], my_times, 0), 1)
    mods, cond, ada_mat, attn_gain, mlp_gain, up_bias, down_bias, embed = mods_call(
        times, ids, time_table, ada_weight, rows, lengths
    )

    qkv_weight = near_weight(qkv_far.tied(mods))
    x, q, kvp, kvc = qkv_call(ids, hidden_in, mask, embed, mods, attn_gain, cosine, sine, qkv_weight)
    kvp, (proj_far.arrays, up_found) = barrier((kvp, (proj_far.arrays, up_found)))
    kvr = swap(kvp, "shard", 1)
    up_far = far_weight(up_split, up_found)
    early = attn_fwd(0, 4, q, kvp, kvc, kvr)
    early, up_far.arrays, down_found = barrier((early, up_far.arrays, down_found))
    proj_weight = near_weight(proj_far.tied(early))
    up_weight = near_weight(up_far.tied(early))
    early, _ = barrier((early, proj_weight.arrays))
    down_far = far_weight(down_split, down_found)
    attn_o, lse = attn_fwd(4, 2, q, kvp, kvc, kvr, early)
    attn_o, down_far.arrays = barrier((attn_o, down_far.arrays))
    down_weight = near_weight(down_far.tied(attn_o))
    attn_proj, middle, x_mlp, act, g_pre, g_mlp, g_bias_up, g_bias_down = up_call(
        ids, attn_o, hidden_in, mask, embed, mods, mlp_gain, up_bias, cotangent, proj_weight, up_weight, down_weight
    )
    plan = Schedule(ids, {"down": (FF // n // 2, False), "up": (D // n, True)})
    down_keep, down_send = down_grad_any(plan.ids, act, g_mlp, n)
    plan.begin("down", down_keep, down_send, ROUTES["down"])
    plan.sync(after=(down_keep,))
    up_keep, up_send = wgrad_call(plan.ids, x_mlp, g_pre, n, "up_grad")
    plan.start("up", up_keep, up_send, SYNCS[9])
    block_out, d_middle, g_att, g_o, stat2, g_gain_mlp = down_call(
        plan.ids, act, g_pre, middle, attn_proj, cotangent, mods, mlp_gain, down_bias, proj_weight, up_weight, down_weight
    )
    plan.sync(*SYNCS[0], after=(g_o,))
    parts, others = [], []

    def backward(group, names):
        gq, gc, dp, dr = attn_bwd(plan.ids, group, q, kvp, kvc, kvr, g_o, lse, cosine, sine)
        parts.append((gq, gc, dp))
        (dr,) = plan.sync(*names, after=(dr,))
        others.append(swap(dr, "shard", 1))

    grads = []

    def weight(group, proj, ada, names):
        keep, send, total = qkv_grad_call(
            plan.ids, x, *parts[group], others[group], cosine, sine, n, f"qkv_grad{group}", proj, ada
        )
        grads.append(total)
        plan.start(f"qkv{group}", keep, send, names)

    backward(0, SYNCS[1])
    backward(1, SYNCS[2])
    weight(0, (attn_o, g_att), None, SYNCS[3])
    backward(2, SYNCS[4])
    weight(1, None, (cond, stat2), SYNCS[5])
    weight(2, None, None, SYNCS[6])
    grad_hidden, stat1, g_gain_attn, g_mask = start_call(
        plan.ids, hidden_in, mask, embed, mods, attn_gain, d_middle, grads, qkv_weight
    )
    plan.sync(*SYNCS[7], after=(stat1,))
    time_rows = -(-time_ids.size // 6 // 8) * 8
    vector_grads = (g_gain_attn, g_gain_mlp, g_bias_up, g_bias_down, g_mask)
    keep, send = last_call(plan.ids, cond, ada_mat, stat1, stat2, vector_grads, n, time_rows)
    plan.begin("last", keep, send, ROUTES["last"], add_packed, pack_packed)
    plan.finish(*SYNCS[8])

    done = plan.done
    few = w_ada.shape[0]
    flat_ids = time_ids.reshape(1, -1)
    flat_ids = jnp.pad(flat_ids, ((0, 0), (0, 6 * time_rows - flat_ids.shape[1])), constant_values=-1)
    grad_qkv, grad_proj = finish_qkv(plan.ids, [done[f"qkv{g}"] for g in range(N_GROUP)], D // n)
    grad_ada, grad_time, *shares = finish_last(plan.ids, flat_ids, done["last"], done["qkv1"], n, time_rows, few)
    return (block_out, grad_hidden, grad_time, grad_qkv, grad_proj, plan.final["up"], plan.final["down"], grad_ada, *shares)


def solution(mesh):
    in_specs = (
        P(("rep", "shard"), None),
        P(("rep", "shard")),
        P(),
        P(),
        P("shard", None),
        P("shard", None),
        P("shard", None),
        P("shard", None),
        P("shard", None),
        P("shard"),
        P("shard"),
        P("shard"),
        P("shard"),
        P("shard"),
        P("shard"),
        P(("rep", "shard"), None),
    )
    out_specs = (
        P(("rep", "shard"), None),
        P(("rep", "shard"), None),
        P(),
        P("shard", None),
        P("shard", None),
        P("shard", None),
        P("shard", None),
        P("shard", None),
        P("shard"),
        P("shard"),
        P("shard"),
        P("shard"),
        P("shard"),
        P("shard"),
    )
    return jax.shard_map(
        on_device, mesh=mesh, in_specs=in_specs, out_specs=out_specs, check_vma=False
    )
```

```python
from functools import partial

import jax
import jax.numpy as jnp
from jax import lax
from jax.experimental import pallas as pl
from jax.experimental.pallas import tpu as pltpu
from jax.sharding import PartitionSpec as P

D = 768
HEADS = 12
HDIM = 64
FF = 3072
STEPS = 1000
CLEN = 128
CONTS = 8
PROMPT = 1024
HALF = PROMPT // 2
PAIRS = HEADS // 2
GROUP = 256
N_GROUP = D // GROUP
TILE = 256
SUB = TILE // CLEN
CHUNK = 512
eps_norm = 1e-06
bf16 = jnp.bfloat16
f32 = jnp.float32
VMEM_LIMIT = 62 * 2**20
COSTS = {'attn_bwd0': 52.5,
 'attn_bwd1': 52.8,
 'attn_bwd2': 53.4,
 'attn_fwd0': 55.5,
 'attn_fwd1': 55.5,
 'attn_fwd4': 30.9,
 'down_grad': 31.5,
 'finish_down': 8.4,
 'finish_last': 9.6,
 'finish_qkv': 9.0,
 'finish_up': 11.7,
 'last': 14.7,
 'mlp_down': 75.6,
 'mlp_up': 74.4,
 'mods': 19.5,
 'pack': 4.2,
 'qkv': 25.5,
 'qkv_grad0': 25.5,
 'qkv_grad1': 21.9,
 'qkv_grad2': 16.8,
 'start_grad': 35.1,
 'up_grad': 27.6,
 'wide_grad': 27}


def cost(name):
    return pl.CostEstimate(flops=int(COSTS.get(name, 1.0) * 1e9), bytes_accessed=0, transcendentals=0)


def nt(left, right):
    return lax.dot_general(left, right, (((1,), (1,)), ((), ())), preferred_element_type=f32)


def nn(left, right):
    return lax.dot_general(left, right, (((1,), (0,)), ((), ())), preferred_element_type=f32)


def tn(left, right):
    return lax.dot_general(left, right, (((0,), (0,)), ((), ())), preferred_element_type=f32)


def exact(left, right, contract):
    return lax.dot_general(
        left, right, (contract, ((), ())), preferred_element_type=f32, precision=lax.Precision.HIGHEST
    )


def layer_norm(values):
    mean_value = jnp.mean(values, -1, keepdims=True)
    centered = values - mean_value
    inv_std = lax.rsqrt(jnp.mean(centered * centered, -1, keepdims=True) + eps_norm)
    return (centered * inv_std, inv_std)


def norm_back(gradient, normed, inv_std):
    return inv_std * (
        gradient
        - jnp.mean(gradient, -1, keepdims=True)
        - normed * jnp.mean(gradient * normed, -1, keepdims=True)
    )


def rotate(values, cosine, sine):
    lane = lax.broadcasted_iota(jnp.int32, cosine.shape, 1) % HDIM
    out = []
    for col in range(0, values.shape[1], 128):
        part = values[:, col : col + 128]
        other = jnp.where(lane < HDIM // 2, pltpu.roll(part, 96, 1), pltpu.roll(part, 32, 1))
        out.append(part * cosine + other * sine)
    return out[0] if len(out) == 1 else jnp.concatenate(out, 1)


def whole(shape):
    return pl.BlockSpec(shape, lambda *_: (0,) * len(shape))


ANY = pl.BlockSpec(memory_space=pl.ANY)
SCALAR = pl.BlockSpec(memory_space=pltpu.SMEM)


def place(pieces, spec, place_ref, target, sem):
    mine = place_ref[0]
    copies = []
    for (offset, split, part), piece in zip(spec, pieces):
        rows = piece.shape[0]
        if offset is None:
            where = target
        else:
            start = (mine ^ offset) * (split * rows)
            if split > 1:
                start = start + (place_ref[3 if split == 2 else 4] ^ part) * rows
            where = target.at[pl.ds(pl.multiple_of(start, 16), rows)]
        copies.append(pltpu.make_async_copy(piece, where, sem))
    return copies


class Weight:
    def __init__(self, spec, arrays):
        self.spec = tuple(spec)
        self.arrays = list(arrays)
        self.count = len(self.arrays)

    def tied(self, *values):
        arrays, _ = lax.optimization_barrier((self.arrays, values))
        return Weight(self.spec, arrays)


def qkv_kernel(
    spec, place_ref, x_ref, cos_ref, sin_ref, *rest
):
    n = len(spec)
    pieces = rest[:n]
    q_ref, kvp_ref, kvc_ref, w_ref, sem = rest[n:]
    step = pl.program_id(0)

    @pl.when(step == 0)
    def _():
        copies = place(pieces, spec, place_ref, w_ref, sem)
        for copy in copies:
            copy.start()
        for copy in copies:
            copy.wait()

    x = x_ref[...]
    cosine, sine = cos_ref[...], sin_ref[...]

    def part(third):
        return nn(x, w_ref[:, pl.ds(pl.multiple_of(third * D + step * GROUP, 128), GROUP)])

    q_ref[...] = (rotate(part(0), cosine, sine) * HDIM**-0.5).astype(bf16)
    k = rotate(part(1), cosine, sine).astype(bf16)
    kvp_ref[0], kvc_ref[0] = k[:HALF], k[HALF:]
    v = part(2).astype(bf16)
    kvp_ref[1], kvc_ref[1] = v[:HALF], v[HALF:]


def qkv_call(place_ids, x, cosine, sine, weight):
    n = weight.count
    width = weight.arrays[0].shape[1]
    half = pl.BlockSpec((2, HALF, GROUP), lambda g: (0, 0, g))
    return pl.pallas_call(
        partial(qkv_kernel, weight.spec),
        grid=(N_GROUP,),
        in_specs=[
            SCALAR,
            whole((PROMPT, D)),
            whole((PROMPT, 128)),
            whole((PROMPT, 128)),
        ]
        + [ANY] * n,
        out_specs=[pl.BlockSpec((PROMPT, GROUP), lambda g: (0, g)), half, half],
        out_shape=[
            jax.ShapeDtypeStruct((PROMPT, D), bf16),
            jax.ShapeDtypeStruct((2, HALF, D), bf16),
            jax.ShapeDtypeStruct((2, HALF, D), bf16),
        ],
        scratch_shapes=[pltpu.VMEM((D, width), bf16), pltpu.SemaphoreType.DMA],
        compiler_params=pltpu.CompilerParams(vmem_limit_bytes=VMEM_LIMIT),
        cost_estimate=cost("qkv"),
        name="qkv",
    )(place_ids, x, cosine, sine, *weight.arrays)


def head_only(values, head):
    lane = lax.broadcasted_iota(jnp.int32, values.shape, 1)
    return jnp.where((lane < HDIM) if head == 0 else (lane >= HDIM), values, jnp.zeros_like(values))


def key_parts(prompt, other, own, rows, first):
    parts = [nt(prompt, rows), nt(other, rows)]
    if not first:
        cols = range(0, HALF, CLEN)
        parts.append(
            jnp.concatenate([nt(own[c : c + CLEN], rows[c : c + CLEN]) for c in cols], 1)
        )
    return parts


def attn_fwd_kernel(q_ref, kvp_ref, kvc_ref, kvr_ref, o_ref, lse_ref):
    kp, kc, kr = kvp_ref[0], kvc_ref[0], kvr_ref[0]
    vp_t, vc_t, vr_t = kvp_ref[1].T, kvc_ref[1].T, kvr_ref[1].T
    for start in (0, HALF):
        outs = []
        q_tile = q_ref[pl.ds(start, HALF), :]
        for head in range(2):
            lanes = slice(HDIM * head, HDIM * (head + 1))
            scores = key_parts(kp, kr, kc, head_only(q_tile, head), start == 0)
            top = jnp.max(scores[0], 0, keepdims=True)
            for part in scores[1:]:
                top = jnp.maximum(top, jnp.max(part, 0, keepdims=True))
            powers = [jnp.exp(part - top) for part in scores]
            total = jnp.sum(powers[0], 0, keepdims=True)
            for part in powers[1:]:
                total = total + jnp.sum(part, 0, keepdims=True)
            lse_ref[0, pl.ds(head, 1), pl.ds(start, HALF)] = top + jnp.log(total)
            scale = 1.0 / total
            probs = [(part * scale).astype(bf16) for part in powers]
            out = nn(vp_t[lanes], probs[0]) + nn(vr_t[lanes], probs[1])
            if start:
                cols = [slice(c, c + CLEN) for c in range(0, HALF, CLEN)]
                out = out + jnp.concatenate([nn(vc_t[lanes, c], probs[2][:, c]) for c in cols], 1)
            outs.append(out)
        o_ref[pl.ds(start, HALF), :] = jnp.concatenate(outs, 0).T.astype(bf16)


def pair_block(rows, first=0):
    return pl.BlockSpec((rows, 2 * HDIM), lambda pair: (0, first + pair))


def pair_half(first=0):
    return pl.BlockSpec((2, HALF, 2 * HDIM), lambda pair: (0, 0, first + pair))


def lse_block(first=0):
    return pl.BlockSpec((1, 2, PROMPT), lambda pair: (first + pair, 0, 0))


def attn_fwd(first, pairs, q, kvp, kvc, kvr, before=None):
    inputs = (q, kvp, kvc, kvr)
    in_specs = [pair_block(PROMPT, first)] + [pair_half(first)] * 3
    body = attn_fwd_kernel
    aliases = {}
    if before is not None:
        inputs += tuple(before)
        in_specs += [ANY, ANY]
        aliases = {4: 0, 5: 1}

        def body(q_ref, kvp_ref, kvc_ref, kvr_ref, _o, _lse, o_ref, lse_ref):
            attn_fwd_kernel(q_ref, kvp_ref, kvc_ref, kvr_ref, o_ref, lse_ref)

    return pl.pallas_call(
        body,
        grid=(pairs,),
        in_specs=in_specs,
        out_specs=[pair_block(PROMPT, first), lse_block(first)],
        out_shape=[
            jax.ShapeDtypeStruct((PROMPT, D), bf16),
            jax.ShapeDtypeStruct((PAIRS, 2, PROMPT), f32),
        ],
        input_output_aliases=aliases,
        compiler_params=pltpu.CompilerParams(vmem_limit_bytes=VMEM_LIMIT),
        cost_estimate=cost(f"attn_fwd{first}"),
        name=f"attn_fwd{first}",
    )(*inputs)


def attn_bwd_kernel(
    _ids, q_ref, kvp_ref, kvc_ref, kvr_ref, g_ref, lse_ref, cos_ref, sin_ref, gq_ref, gc_ref, dp_ref, dr_ref
):
    kp, kc, kr = kvp_ref[0], kvc_ref[0], kvr_ref[0]
    vp, vc, vr = kvp_ref[1], kvc_ref[1], kvr_ref[1]
    kp_t, kc_t, kr_t = kp.T, kc.T, kr.T
    first = lax.broadcasted_iota(jnp.int32, (HALF, 2 * HDIM), 1) < HDIM
    for start in (0, HALF):
        tile = pl.ds(start, HALF)
        q_tile, g_tile = q_ref[tile, :], g_ref[tile, :]
        cols = [slice(c, c + CLEN) for c in range(0, HALF, CLEN)]
        dqs, dks, dvs = [], [], []
        for head in range(2):
            lanes = slice(HDIM * head, HDIM * (head + 1))
            scores = key_parts(kp, kr, kc, head_only(q_tile, head), start == 0)
            dps = key_parts(vp, vr, vc, head_only(g_tile, head), start == 0)
            lse = lse_ref[0, pl.ds(head, 1), tile]
            probs = [jnp.exp(part - lse) for part in scores]
            row_dot = jnp.sum(probs[0] * dps[0], 0, keepdims=True)
            for p_part, d_part in zip(probs[1:], dps[1:]):
                row_dot = row_dot + jnp.sum(p_part * d_part, 0, keepdims=True)
            ds = [(p * (d - row_dot)).astype(bf16) for p, d in zip(probs, dps)]
            probs = [p.astype(bf16) for p in probs]
            dq = nn(kp_t[lanes], ds[0]) + nn(kr_t[lanes], ds[1])
            dk = [nn(ds[0], q_tile), nn(ds[1], q_tile)]
            dv = [nn(probs[0], g_tile), nn(probs[1], g_tile)]
            if start:
                dq = dq + jnp.concatenate([nn(kc_t[lanes, c], ds[2][:, c]) for c in cols], 1)
                dk.append(jnp.concatenate([nn(ds[2][:, c], q_tile[c]) for c in cols], 0))
                dv.append(jnp.concatenate([nn(probs[2][:, c], g_tile[c]) for c in cols], 0))
            dqs.append(dq)
            dks.append(dk)
            dvs.append(dv)
        cosine, sine = cos_ref[tile, :], sin_ref[tile, :]
        dq = jnp.concatenate(dqs, 0).T * HDIM**-0.5
        gq_ref[tile, :] = rotate(dq, cosine, -sine).astype(bf16)
        for which, parts in enumerate((dks, dvs)):
            merged = [jnp.where(first, a, b) for a, b in zip(*parts)]
            if start:
                dp_ref[which] += merged[0]
                dr_ref[which] += merged[1]
                last = merged[2] if which else rotate(merged[2], cosine, -sine)
                gc_ref[which] = last.astype(bf16)
            else:
                dp_ref[which] = merged[0]
                dr_ref[which] = merged[1]


def attn_bwd(ids, group, q, kvp, kvc, kvr, g, lse, cosine, sine):
    pairs = GROUP // (2 * HDIM)
    first = group * pairs
    return pl.pallas_call(
        attn_bwd_kernel,
        grid=(pairs,),
        in_specs=[SCALAR, pair_block(PROMPT, first)]
        + [pair_half(first)] * 3
        + [pair_block(PROMPT, first), lse_block(first), whole((PROMPT, 128)), whole((PROMPT, 128))],
        out_specs=[pair_block(PROMPT), pair_half(), pair_half(), pair_half()],
        out_shape=[
            jax.ShapeDtypeStruct((PROMPT, GROUP), bf16),
            jax.ShapeDtypeStruct((2, HALF, GROUP), bf16),
            jax.ShapeDtypeStruct((2, HALF, GROUP), f32),
            jax.ShapeDtypeStruct((2, HALF, GROUP), f32),
        ],
        compiler_params=pltpu.CompilerParams(vmem_limit_bytes=VMEM_LIMIT),
        cost_estimate=cost(f"attn_bwd{group}"),
        name=f"attn_bwd{group}",
    )(ids, q, kvp, kvc, kvr, g, lse, cosine, sine)


def up_kernel(
    specs,
    place_ref,
    o_ref,
    hid_ref,
    mask_ref,
    embed_ref,
    mods_ref,
    gain_ref,
    bias_ref,
    cot_ref,
    *rest,
):
    pieces, rest = take(specs, rest)
    ap_ref, mid_ref, x_ref, act_ref, gpre_ref, gmlp_ref, gbu_ref, gbd_ref = rest[:8]
    proj_ref, up_ref, down_ref, sems = rest[8:]
    step = pl.program_id(0)
    targets = (proj_ref, up_ref, down_ref)
    copies = [
        place(part, spec, place_ref, target, sems.at[i])
        for i, (part, spec, target) in enumerate(zip(pieces, specs, targets))
    ]

    @pl.when(step == 0)
    def _():
        for group in copies:
            for copy in group:
                copy.start()
        gbu_ref[...] = jnp.zeros_like(gbu_ref)
        gbd_ref[...] = jnp.zeros_like(gbd_ref)
        for copy in copies[0]:
            copy.wait()

    attn_proj = nn(o_ref[...], proj_ref[...])
    ap_ref[...] = attn_proj
    for sub in range(SUB):
        rows = slice(sub * CLEN, (sub + 1) * CLEN)
        row = pl.ds(step * SUB + sub, 1)
        start = jnp.where(mask_ref[rows, :] > 0.5, embed_ref[...], hid_ref[rows, :].astype(f32))
        middle = start + mods_ref[row, 2 * D : 3 * D] * attn_proj[rows]
        mid_ref[rows, :] = middle
        normed, _inv = layer_norm(middle)
        shift, scale = mods_ref[row, 3 * D : 4 * D], mods_ref[row, 4 * D : 5 * D]
        x_ref[rows, :] = (normed * gain_ref[...] * (1.0 + scale) + shift).astype(bf16)
        g_mlp = (mods_ref[row, 5 * D : 6 * D] * cot_ref[rows, :].astype(f32)).astype(bf16)
        gmlp_ref[rows, :] = g_mlp
        gbd_ref[...] += jnp.sum(g_mlp.astype(f32), 0, keepdims=True)

    @pl.when(step == 0)
    def _():
        for group in copies[1:]:
            for copy in group:
                copy.wait()

    x, g_mlp = x_ref[...], gmlp_ref[...]
    root = (2.0 / jnp.pi) ** 0.5
    for col in range(0, FF, CHUNK):
        cols = slice(col, col + CHUNK)
        pre = nn(x, up_ref[:, cols]) + bias_ref[:, cols]
        square = pre * pre
        curve = jnp.tanh(root * pre * (1.0 + 0.044715 * square))
        half_up = 0.5 * (1.0 + curve)
        act_ref[:, cols] = (pre * half_up).astype(bf16)
        slope = half_up + (0.5 * root) * pre * (1.0 - curve * curve) * (1.0 + 0.134145 * square)
        g_pre = (nt(g_mlp, down_ref[cols, :]) * slope).astype(bf16)
        gpre_ref[:, cols] = g_pre
        gbu_ref[:, cols] += jnp.sum(g_pre.astype(f32), 0, keepdims=True)


def take(specs, refs):
    pieces = []
    for spec in specs:
        pieces.append(refs[: len(spec)])
        refs = refs[len(spec) :]
    return pieces, refs


def tile_block(width):
    return pl.BlockSpec((TILE, width), lambda step: (step, 0))


def weight_scratch():
    return [
        pltpu.VMEM((D, D), bf16),
        pltpu.VMEM((D, FF), bf16),
        pltpu.VMEM((FF, D), bf16),
        pltpu.SemaphoreType.DMA((3,)),
    ]


def up_call(place_ids, attn_o, hidden, mask, embed, mods, gain, bias, cot, proj, up, down):
    weights = (proj, up, down)
    n = sum(w.count for w in weights)
    specs = tuple(w.spec for w in weights)
    arrays = [a for w in weights for a in w.arrays]
    rows = PROMPT
    return pl.pallas_call(
        partial(up_kernel, specs),
        grid=(rows // TILE,),
        in_specs=[
            SCALAR,
            tile_block(D),
            tile_block(D),
            tile_block(1),
            whole((1, D)),
            whole(mods.shape),
            whole((1, D)),
            whole((1, FF)),
            tile_block(D),
        ]
        + [ANY] * n,
        out_specs=[tile_block(D)] * 3
        + [tile_block(FF)] * 2
        + [tile_block(D), whole((1, FF)), whole((1, D))],
        out_shape=[
            jax.ShapeDtypeStruct((rows, D), f32),
            jax.ShapeDtypeStruct((rows, D), f32),
            jax.ShapeDtypeStruct((rows, D), bf16),
            jax.ShapeDtypeStruct((rows, FF), bf16),
            jax.ShapeDtypeStruct((rows, FF), bf16),
            jax.ShapeDtypeStruct((rows, D), bf16),
            jax.ShapeDtypeStruct((1, FF), f32),
            jax.ShapeDtypeStruct((1, D), f32),
        ],
        scratch_shapes=weight_scratch(),
        compiler_params=pltpu.CompilerParams(vmem_limit_bytes=VMEM_LIMIT),
        cost_estimate=cost("mlp_up"),
        name="mlp_up",
    )(place_ids, attn_o, hidden, mask, embed, mods, gain, bias, cot, *arrays)


def down_kernel(specs, place_ref, act_ref, gpre_ref, mid_ref, ap_ref, cot_ref, mods_ref, gain_ref, bias_ref, *rest):
    pieces, rest = take(specs, rest)
    out_ref, dmid_ref, gatt_ref, go_ref, stat_ref, ggain_ref = rest[:6]
    proj_ref, up_ref, down_ref, sems = rest[6:]
    step = pl.program_id(0)
    targets = (proj_ref, up_ref, down_ref)
    copies = [
        place(part, spec, place_ref, target, sems.at[i])
        for i, (part, spec, target) in enumerate(zip(pieces, specs, targets))
    ]

    @pl.when(step == 0)
    def _():
        for i in (2, 1, 0):
            for copy in copies[i]:
                copy.start()
        ggain_ref[...] = jnp.zeros_like(ggain_ref)
        for copy in copies[2]:
            copy.wait()

    mlp_out = nn(act_ref[...], down_ref[...]) + bias_ref[...]

    @pl.when(step == 0)
    def _():
        for i in (1, 0):
            for copy in copies[i]:
                copy.wait()

    g_n = nt(gpre_ref[...], up_ref[...])
    for sub in range(SUB):
        rows = slice(sub * CLEN, (sub + 1) * CLEN)
        row = pl.ds(step * SUB + sub, 1)
        middle, cot, grad = mid_ref[rows, :], cot_ref[rows, :].astype(f32), g_n[rows]
        gate_attn, gate_mlp = mods_ref[row, 2 * D : 3 * D], mods_ref[row, 5 * D : 6 * D]
        scale = 1.0 + mods_ref[row, 4 * D : 5 * D]
        out_ref[rows, :] = (middle + gate_mlp * mlp_out[rows]).astype(bf16)
        normed, inv_std = layer_norm(middle)
        along = jnp.sum(grad * normed, 0, keepdims=True)
        ggain_ref[...] += along * scale
        d_middle = cot + norm_back(grad * (scale * gain_ref[...]), normed, inv_std)
        dmid_ref[rows, :] = d_middle
        gatt_ref[rows, :] = (gate_attn * d_middle).astype(bf16)
        stat_ref[row, 0:D] = jnp.sum(d_middle * ap_ref[rows, :], 0, keepdims=True)
        stat_ref[row, D : 2 * D] = jnp.sum(grad, 0, keepdims=True)
        stat_ref[row, 2 * D : 3 * D] = along * gain_ref[...]
        stat_ref[row, 3 * D : 4 * D] = jnp.sum(cot * mlp_out[rows], 0, keepdims=True)
    go_ref[...] = nt(gatt_ref[...], proj_ref[...]).astype(bf16)


def down_call(place_ids, act, gpre, middle, attn_proj, cot, mods, gain, bias, proj, up, down):
    weights = (proj, up, down)
    n = sum(w.count for w in weights)
    specs = tuple(w.spec for w in weights)
    arrays = [a for w in weights for a in w.arrays]
    rows = PROMPT
    return pl.pallas_call(
        partial(down_kernel, specs),
        grid=(rows // TILE,),
        in_specs=[
            SCALAR,
            tile_block(FF),
            tile_block(FF),
            tile_block(D),
            tile_block(D),
            tile_block(D),
            whole(mods.shape),
            whole((1, D)),
            whole((1, D)),
        ]
        + [ANY] * n,
        out_specs=[tile_block(D)] * 4 + [whole((CONTS, 4 * D)), whole((1, D))],
        out_shape=[
            jax.ShapeDtypeStruct((rows, D), bf16),
            jax.ShapeDtypeStruct((rows, D), f32),
            jax.ShapeDtypeStruct((rows, D), bf16),
            jax.ShapeDtypeStruct((rows, D), bf16),
            jax.ShapeDtypeStruct((CONTS, 4 * D), f32),
            jax.ShapeDtypeStruct((1, D), f32),
        ],
        scratch_shapes=weight_scratch(),
        compiler_params=pltpu.CompilerParams(vmem_limit_bytes=VMEM_LIMIT),
        cost_estimate=cost("mlp_down"),
        name="mlp_down",
    )(place_ids, act, gpre, middle, attn_proj, cot, mods, gain, bias, *arrays)


def split_store(total, keep_ref, send_ref, core, lead, at):
    for pair in range(total.shape[0] // lead // 2):
        even = total[2 * pair * lead : (2 * pair + 1) * lead].astype(bf16)
        odd = total[(2 * pair + 1) * lead : (2 * pair + 2) * lead].astype(bf16)
        keep_ref[pair, at : at + lead, :] = jnp.where(core == 0, even, odd)
        send_ref[pair, at : at + lead, :] = jnp.where(core == 0, odd, even)


def wgrad_kernel(lead, place_ref, left_ref, right_ref, keep_ref, send_ref):
    split_store(tn(left_ref[...], right_ref[...]), keep_ref, send_ref, place_ref[1], lead, 0)


def wgrad_call(place_ids, left, right, n, name):
    lead = D // n
    blocks = right.shape[1] // D
    out = pl.BlockSpec((n // 2, lead, D), lambda j: (0, j, 0))
    shape = jax.ShapeDtypeStruct((n // 2, blocks * lead, D), bf16)
    return pl.pallas_call(
        partial(wgrad_kernel, lead),
        grid=(blocks,),
        in_specs=[SCALAR, whole((PROMPT, D)), pl.BlockSpec((PROMPT, D), lambda j: (0, j))],
        out_specs=[out, out],
        out_shape=[shape, shape],
        compiler_params=pltpu.CompilerParams(vmem_limit_bytes=VMEM_LIMIT),
        cost_estimate=cost(name),
        name=name,
    )(place_ids, left, right)


def down_grad_kernel(_ids, left_ref, right_ref, keep_ref, send_ref):
    half = pl.num_programs(0) // 2
    total = tn(left_ref[...], right_ref[...]).astype(bf16)

    @pl.when(pl.program_id(0) < half)
    def _():
        send_ref[0] = total

    @pl.when(pl.program_id(0) >= half)
    def _():
        keep_ref[0] = total


def down_grad_call(place_ids, act, g_mlp, n):
    rows = FF // n
    half = n // 2

    def shard(j, ids):
        core = ids[1]
        return 0, jnp.where(j < half, 2 * j + 1 - core, 2 * (j - half) + core)

    shape = jax.ShapeDtypeStruct((half, rows, D), bf16)
    return pl.pallas_call(
        down_grad_kernel,
        grid_spec=pltpu.PrefetchScalarGridSpec(
            num_scalar_prefetch=1,
            grid=(n,),
            in_specs=[pl.BlockSpec((PROMPT, rows), shard), pl.BlockSpec((PROMPT, D), lambda j, ids: (0, 0))],
            out_specs=[
                pl.BlockSpec((1, rows, D), lambda j, ids: (jnp.maximum(j - half, 0), 0, 0)),
                pl.BlockSpec((1, rows, D), lambda j, ids: (jnp.minimum(j, half - 1), 0, 0)),
            ],
        ),
        out_shape=[shape, shape],
        compiler_params=pltpu.CompilerParams(vmem_limit_bytes=VMEM_LIMIT),
        cost_estimate=cost("down_grad"),
        name="down_grad",
    )(place_ids, act, g_mlp)


def down_grad_any(place_ids, act, g_mlp, n):
    if (FF // n) % 128 == 0 and n == 4:
        return down_grad_call(place_ids, act, g_mlp, n)
    full = wide_grad_call(act, g_mlp)
    core = lax.axis_index("shard") % 2
    parts = full.reshape(n // 2, 2, -1, D)
    keep = lax.dynamic_index_in_dim(parts, core, 1, False)
    return keep, lax.dynamic_index_in_dim(parts, 1 - core, 1, False)


def wide_grad_kernel(left_ref, right_ref, out_ref):
    out_ref[...] = tn(left_ref[...], right_ref[...]).astype(bf16)


def wide_grad_call(act, g_mlp):
    return pl.pallas_call(
        wide_grad_kernel,
        grid=(FF // D,),
        in_specs=[pl.BlockSpec((PROMPT, D), lambda j: (0, j)), whole((PROMPT, D))],
        out_specs=pl.BlockSpec((D, D), lambda j: (j, 0)),
        out_shape=jax.ShapeDtypeStruct((FF, D), bf16),
        compiler_params=pltpu.CompilerParams(vmem_limit_bytes=VMEM_LIMIT),
        name="wide_grad",
    )(act, g_mlp)


def qkv_grad_kernel(lead, with_proj, with_ada, place_ref, x_ref, gq_ref, gc_ref, dp_ref, got_ref, cos_ref, sin_ref, *rest):
    keep_ref, send_ref, g_ref = rest[-3:]
    core = place_ref[1]
    g_ref[:, 0:GROUP] = gq_ref[...]
    total_k = dp_ref[0] + got_ref[0].astype(f32)
    total_v = dp_ref[1] + got_ref[1].astype(f32)
    g_ref[0:HALF, GROUP : 2 * GROUP] = rotate(total_k, cos_ref[...], -sin_ref[...]).astype(bf16)
    g_ref[0:HALF, 2 * GROUP : 3 * GROUP] = total_v.astype(bf16)
    g_ref[HALF:PROMPT, GROUP : 2 * GROUP] = gc_ref[0]
    g_ref[HALF:PROMPT, 2 * GROUP : 3 * GROUP] = gc_ref[1]
    split_store(tn(x_ref[...], g_ref[...]), keep_ref, send_ref, core, lead, 0)
    at = lead
    if with_proj:
        split_store(tn(rest[0][...], rest[1][...]), keep_ref, send_ref, core, lead, at)
        at += lead
        rest = rest[2:]
    if with_ada:
        cond = rest[0][...]
        silu = (cond / (1.0 + jnp.exp(-cond))).astype(bf16).astype(f32)
        few = cond.shape[1] * lead // D
        for col in range(4):
            total = exact(silu, rest[1][:, col * D : (col + 1) * D], ((0,), (0,)))
            split_store(total, keep_ref, send_ref, core, few, at)
            at += few


def qkv_grad_call(place_ids, x, gq, gc, dp, got, cosine, sine, n, name, proj, ada):
    lead = D // n
    rows = lead
    extra = []
    if proj is not None:
        extra += list(proj)
        rows += lead
    if ada is not None:
        extra += list(ada)
        rows += 4 * (ada[0].shape[1] // n)
    out = whole((n // 2, rows, D))
    shape = jax.ShapeDtypeStruct((n // 2, rows, D), bf16)
    return pl.pallas_call(
        partial(qkv_grad_kernel, lead, proj is not None, ada is not None),
        grid=(1,),
        in_specs=[
            SCALAR,
            whole((PROMPT, D)),
            whole((PROMPT, GROUP)),
            whole((2, HALF, GROUP)),
            whole((2, HALF, GROUP)),
            whole((2, HALF, GROUP)),
            whole((HALF, 128)),
            whole((HALF, 128)),
        ]
        + [whole(e.shape) for e in extra],
        out_specs=[out, out, whole((PROMPT, D))],
        out_shape=[shape, shape, jax.ShapeDtypeStruct((PROMPT, D), bf16)],
        compiler_params=pltpu.CompilerParams(vmem_limit_bytes=VMEM_LIMIT),
        cost_estimate=cost(name),
        name=name,
    )(place_ids, x, gq, gc, dp, got, cosine, sine, *extra)


def start_kernel(spec, place_ref, hid_ref, mask_ref, embed_ref, mods_ref, gain_ref, dmid_ref, *rest):
    n = len(spec)
    grads, pieces = rest[:N_GROUP], rest[N_GROUP : N_GROUP + n]
    gh_ref, stat_ref, ggain_ref, gmask_ref, w_ref, sem = rest[N_GROUP + n :]
    step = pl.program_id(0)

    @pl.when(step == 0)
    def _():
        copies = place(pieces, spec, place_ref, w_ref, sem)
        for copy in copies:
            copy.start()
        ggain_ref[...] = jnp.zeros_like(ggain_ref)
        gmask_ref[...] = jnp.zeros_like(gmask_ref)
        for copy in copies:
            copy.wait()

    g_n = None
    for group in range(N_GROUP):
        for third in range(3):
            at = third * D + group * GROUP
            term = nt(grads[group][:, third * GROUP : (third + 1) * GROUP], w_ref[:, at : at + GROUP])
            g_n = term if g_n is None else g_n + term
    for sub in range(SUB):
        rows = slice(sub * CLEN, (sub + 1) * CLEN)
        row = pl.ds(step * SUB + sub, 1)
        masked = mask_ref[rows, :] > 0.5
        start = jnp.where(masked, embed_ref[...], hid_ref[rows, :].astype(f32))
        normed, inv_std = layer_norm(start)
        scale = 1.0 + mods_ref[row, D : 2 * D]
        grad = g_n[rows]
        along = jnp.sum(grad * normed, 0, keepdims=True)
        ggain_ref[...] += along * scale
        stat_ref[row, 0:D] = jnp.sum(grad, 0, keepdims=True)
        stat_ref[row, D : 2 * D] = along * gain_ref[...]
        d_start = dmid_ref[rows, :] + norm_back(grad * (scale * gain_ref[...]), normed, inv_std)
        gh_ref[rows, :] = jnp.where(masked, 0.0, d_start)
        gmask_ref[...] += jnp.sum(jnp.where(masked, d_start, 0.0), 0, keepdims=True)


def start_call(place_ids, hidden, mask, embed, mods, gain, d_middle, grads, weight):
    n = weight.count
    rows = PROMPT
    return pl.pallas_call(
        partial(start_kernel, weight.spec),
        grid=(rows // TILE,),
        in_specs=[
            SCALAR,
            tile_block(D),
            tile_block(1),
            whole((1, D)),
            whole(mods.shape),
            whole((1, D)),
            tile_block(D),
        ]
        + [tile_block(D)] * N_GROUP
        + [ANY] * n,
        out_specs=[tile_block(D), whole((CONTS, 2 * D)), whole((1, D)), whole((1, D))],
        out_shape=[
            jax.ShapeDtypeStruct((rows, D), f32),
            jax.ShapeDtypeStruct((CONTS, 2 * D), f32),
            jax.ShapeDtypeStruct((1, D), f32),
            jax.ShapeDtypeStruct((1, D), f32),
        ],
        scratch_shapes=[pltpu.VMEM((D, 3 * D), bf16), pltpu.SemaphoreType.DMA],
        compiler_params=pltpu.CompilerParams(vmem_limit_bytes=VMEM_LIMIT),
        cost_estimate=cost("start_grad"),
        name="start_grad",
    )(place_ids, hidden, mask, embed, mods, gain, d_middle, *grads, *weight.arrays)


def pack_kernel(*refs):
    out_ref = refs[-1]
    out_ref[...] = jnp.zeros_like(out_ref)
    for i, ref in enumerate(refs[:-1]):
        out_ref[i : i + 1, 0 : ref.shape[0]] = ref[...].astype(f32).reshape(1, -1)


def pack_call(vectors):
    shape = (8, max(v.shape[0] for v in vectors))
    return pl.pallas_call(
        pack_kernel,
        grid=(1,),
        in_specs=[whole(v.shape) for v in vectors],
        out_specs=whole(shape),
        out_shape=jax.ShapeDtypeStruct(shape, f32),
        name="pack",
    )(*vectors)


def mods_kernel(spec, lengths, times_ref, place_ref, table_ref, hid_ref, mask_ref, *rest):
    n = len(spec)
    pieces, rest = rest[:n], rest[n:]
    count = len(lengths)
    n_row = len(rest) - count - 7
    rows, rest = rest[:n_row], rest[n_row:]
    mods_ref, cond_ref, ada_ref = rest[:3]
    out_refs = rest[3 : 3 + count - 1]
    x_ref, bias_ref, row_ref, sem, row_sem = rest[3 + count - 1 :]
    gain_ref, embed_ref = out_refs[0], out_refs[4]
    copies = place(pieces, spec, place_ref, ada_ref, sem)
    row_copies = [
        pltpu.make_async_copy(row, row_ref.at[place_ref[0] ^ offset], row_sem) for offset, row in enumerate(rows)
    ]
    for copy in row_copies + copies:
        copy.start()
    for block in range(CONTS):
        cond_ref[pl.ds(block, 1), :] = table_ref[pl.ds(times_ref[block], 1), :]
    cond = cond_ref[...]
    silu = (cond / (1.0 + jnp.exp(-cond))).astype(bf16)
    for copy in row_copies:
        copy.wait()
    for shard in range(n_row):
        for i, (length, ref) in enumerate(zip(lengths, (*out_refs, bias_ref))):
            ref[0:1, shard * length : (shard + 1) * length] = row_ref[shard, i : i + 1, 0:length]
    for copy in copies:
        copy.wait()
    mods_ref[...] = nn(silu, ada_ref[...]) + bias_ref[...]

    @pl.loop(0, CONTS)
    def _(block):
        rows = pl.ds(pl.multiple_of(block * CLEN, CLEN), CLEN)
        start = jnp.where(mask_ref[rows, :] > 0.5, embed_ref[...], hid_ref[rows, :].astype(f32))
        normed, _inv = layer_norm(start)
        row = pl.ds(block, 1)
        shift, scale = mods_ref[row, 0:D], mods_ref[row, D : 2 * D]
        x_ref[rows, :] = (normed * gain_ref[...] * (1.0 + scale) + shift).astype(bf16)


def mods_call(times, place_ids, table, hidden, mask, weight, rows, lengths):
    width = weight.arrays[0].shape[1]
    n = len(rows)
    vectors = [(1, n * length) for length in lengths]
    shapes = [(CONTS, width), (CONTS, table.shape[1])]
    return pl.pallas_call(
        partial(mods_kernel, weight.spec, tuple(lengths)),
        in_specs=[SCALAR, SCALAR, whole(table.shape), whole(hidden.shape), whole(mask.shape)] + [ANY] * (weight.count + n),
        out_specs=[whole(s) for s in shapes] + [whole((table.shape[1], width))] + [whole(v) for v in vectors[:-1]] + [whole((PROMPT, D))],
        out_shape=[jax.ShapeDtypeStruct(s, f32) for s in shapes]
        + [jax.ShapeDtypeStruct((table.shape[1], width), bf16)]
        + [jax.ShapeDtypeStruct(v, f32) for v in vectors[:-1]]
        + [jax.ShapeDtypeStruct((PROMPT, D), bf16)],
        grid=(1,),
        scratch_shapes=[
            pltpu.VMEM(vectors[-1], f32),
            pltpu.VMEM((n,) + rows[0].shape, f32),
            pltpu.SemaphoreType.DMA,
            pltpu.SemaphoreType.DMA,
        ],
        compiler_params=pltpu.CompilerParams(vmem_limit_bytes=VMEM_LIMIT),
        cost_estimate=cost("mods"),
        name="mods",
    )(times, place_ids, table, hidden, mask, *weight.arrays, *rows)


def last_kernel(
    lead, time_rows, place_ref, cond_ref, ada_ref, stat1_ref, stat2_ref, ga_ref, gm_ref, bu_ref, bd_ref, me_ref,
    keep_ref, send_ref, small_ref,
):
    core, pair = place_ref[1], place_ref[2]
    cond = cond_ref[...]
    gate = 1.0 / (1.0 + jnp.exp(-cond))
    silu = (cond * gate).astype(bf16).astype(f32)
    stat1, stat2 = stat1_ref[...], stat2_ref[...]
    ada_late = exact(silu, stat1, ((0,), (0,)))
    ada = ada_ref[...].astype(f32)
    g_silu = exact(stat1, ada[:, : 2 * D], ((1,), (1,))) + exact(stat2, ada[:, 2 * D :], ((1,), (1,)))
    g_cond = g_silu * (gate * (1.0 + cond * (1.0 - gate)))
    small_ref[...] = jnp.zeros_like(small_ref)
    at = time_rows
    small_ref[at : at + 1, :] = ga_ref[...]
    small_ref[at + 1 : at + 2, :] = gm_ref[...]
    for i in range(FF // D):
        small_ref[at + 2 + i : at + 3 + i, :] = bu_ref[:, i * D : (i + 1) * D]
    small_ref[at + 6 : at + 7, :] = bd_ref[...]
    for i in range(2):
        small_ref[at + 7 + i : at + 8 + i, :] = jnp.sum(stat1[:, i * D : (i + 1) * D], 0, keepdims=True)
    for i in range(4):
        small_ref[at + 9 + i : at + 10 + i, :] = jnp.sum(stat2[:, i * D : (i + 1) * D], 0, keepdims=True)
    small_ref[at + 13 : at + 14, :] = me_ref[...]
    half = CONTS // 2
    prompt = jnp.sum(g_cond[:half], 0, keepdims=True)
    values = [prompt] + [g_cond[half + i : half + i + 1] for i in range(half)]
    base = pair * (CONTS + 1)
    where_to = [base] + [base + 1 + core * half + i for i in range(half)]
    for lane in range(D // 128):
        row = lax.broadcasted_iota(jnp.int32, (time_rows, 128), 0) + lane * time_rows
        placed = jnp.zeros((time_rows, 128), f32)
        for index, value in zip(where_to, values):
            placed = placed + jnp.where(row == index, value, 0.0)
        small_ref[0:time_rows, lane * 128 : (lane + 1) * 128] = placed
    small = small_ref[...]
    high = small.astype(bf16)
    rows = small.shape[0]
    low = (small[time_rows:] - high[time_rows:].astype(f32)).astype(bf16)
    for j in range(keep_ref.shape[0]):
        for col in range(2):
            split_store(ada_late[:, col * D : (col + 1) * D], keep_ref, send_ref, core, lead, col * lead)
        row = 2 * lead
        for ref in (keep_ref, send_ref):
            ref[j, row : row + rows, :] = high
            ref[j, row + rows : row + rows + 16, :] = low


def last_call(place_ids, cond, ada, stat1, stat2, vectors, n, time_rows):
    lead = ada.shape[0] // n
    rows = 16 + time_rows
    args = (cond, ada, stat1, stat2) + tuple(vectors)
    out = whole((n // 2, 2 * lead + rows + 16, D))
    shape = jax.ShapeDtypeStruct((n // 2, 2 * lead + rows + 16, D), bf16)
    return pl.pallas_call(
        partial(last_kernel, lead, time_rows),
        grid=(1,),
        in_specs=[SCALAR] + [whole(a.shape) for a in args],
        out_specs=[out, out],
        out_shape=[shape, shape],
        scratch_shapes=[pltpu.VMEM((rows, D), f32)],
        compiler_params=pltpu.CompilerParams(vmem_limit_bytes=VMEM_LIMIT),
        cost_estimate=cost("last"),
        name="last",
    )(place_ids, *args)


def swap(value, axis, mask):
    pairs = [(source, source ^ mask) for source in range(lax.axis_size(axis))]
    return lax.ppermute(value, axis, pairs)


def gather_far(piece):
    pieces = {0: piece}
    mask = lax.axis_size("shard") // 2
    while mask > 1:
        for offset in list(pieces):
            pieces[offset | mask] = swap(pieces[offset], "shard", mask)
        mask //= 2
    return pieces


def gather_near(pieces):
    pieces = dict(pieces)
    for offset in list(pieces):
        pieces[offset | 1] = swap(pieces[offset], "shard", 1)
    return [pieces[offset] for offset in range(len(pieces))]


def sides():
    rep = lax.axis_index("rep")
    return rep % 2, rep % 4


def far_parts(piece, split=1):
    rows = piece.shape[0] // split
    if split == 1 or rows % 16:
        return 1, gather_far(piece)
    side = sides()[0 if split == 2 else 1]
    found = gather_far(lax.dynamic_slice_in_dim(piece, side * rows, rows, 0))
    found[0] = piece
    return split, found


def far_weight(split, found, tie=None):
    if tie is not None:
        found, _ = lax.optimization_barrier((found, tie))
    spec, arrays = [], []
    for offset, part in found.items():
        if split == 1 or not offset:
            spec.append((offset, 1, 0))
            arrays.append(part)
            continue
        spec += [(offset, split, code) for code in range(split)]
        arrays += [part] + [swap(part, "rep", code) for code in range(1, split)]
    return Weight(spec, arrays)


def near_weight(far):
    spec, arrays = list(far.spec), list(far.arrays)
    for (offset, split, code), part in zip(far.spec, far.arrays):
        spec.append((offset | 1, split, code))
        arrays.append(swap(part, "shard", 1))
    if all(part.shape[0] % 16 == 0 for part in arrays):
        return Weight(spec, arrays)
    mine = lax.axis_index("shard")
    rows = arrays[0].shape[0]
    out = jnp.zeros((rows * len(arrays),) + arrays[0].shape[1:], arrays[0].dtype)
    for (offset, _split, _code), part in zip(spec, arrays):
        out = lax.dynamic_update_slice_in_dim(out, part, (mine ^ offset) * rows, 0)
    return Weight([(None, 1, 0)], [out])


def add_plain(left, right):
    return left.astype(f32) + right.astype(f32)


def add_packed(left, right):
    rows = left.shape[-2] - 16
    total = add_plain(left[..., :rows, :], right[..., :rows, :])
    rest = add_plain(left[..., rows:, :], right[..., rows:, :])
    return jnp.concatenate([total[..., : rows - 16, :], total[..., rows - 16 :, :] + rest], -2)


def pack_plain(value):
    return value.astype(bf16)


def pack_packed(value):
    high = value.astype(bf16)
    low = value[..., -16:, :] - high[..., -16:, :].astype(f32)
    return jnp.concatenate([high, low.astype(bf16)], -2)


def reduce_chain(keep, send, steps, add=add_plain, pack=pack_plain):
    mine, rep = lax.axis_index("shard"), lax.axis_index("rep")

    def parts(values, axis, bit):
        kept, sent = [
            pack(add(*(lax.dynamic_index_in_dim(v, b, axis, False) for v in values))) for b in (bit, 1 - bit)
        ]
        return kept, sent

    got = yield send, swap(send, "shard", 1)
    terms = (keep, got)
    mask = 2
    while mask < lax.axis_size("shard"):
        halves = [t.reshape((-1, 2) + t.shape[1:]) for t in terms]
        kept, send = parts(halves, 1, (mine // mask) % 2)
        got = yield send, swap(send, "shard", mask)
        terms = (kept, got)
        mask *= 2
    terms = tuple(t[0] for t in terms)
    joined = None
    more = range(3, lax.axis_size("rep").bit_length() - 1)
    steps = [(bit, "all") for bit in more] + list(steps)
    for at, kind in steps:
        bit = (rep >> at) % 2
        if kind == "split":
            kept, send = parts([t.reshape(2, -1, t.shape[-1]) for t in terms], 0, bit)
            got = yield send, swap(send, "rep", 1 << at)
            terms = (kept, got)
            continue
        value = pack(add(*terms)) if joined is None else joined
        got = yield value, swap(value, "rep", 1 << at)
        if kind == "join":
            last = (value, got, at)
            first, second = jnp.where(bit == 0, value, got), jnp.where(bit == 0, got, value)
            joined = jnp.concatenate([first, second], 0)
        else:
            last = (value, got, None)
            terms, joined = (value, got), None
    return last


class Schedule:
    def __init__(self, ids, rows):
        self.ids = ids
        self.chains = {}
        self.sent = {}
        self.done = {}
        self.final = {}
        self.rows = rows

    def begin(self, name, keep, send, *how):
        chain = reduce_chain(keep, send, *how)
        self.chains[name] = chain
        _sent, self.sent[name] = next(chain)

    def start(self, name, keep, send, names):
        (send,) = self.sync(*(other for other in names if other != name), after=(send,))
        self.begin(name, keep, send, ROUTES[name])
        self.sync(*(other for other in names if other == name), after=(send,))

    def sync(self, *names, after=()):
        for name in names or (None,):
            if name is not None and name not in self.sent:
                continue
            got = self.sent.pop(name, None)
            self.ids, got, after = lax.optimization_barrier((self.ids, got, tuple(after)))
            if got is None:
                continue
            try:
                sent, self.sent[name] = self.chains[name].send(got)
                self.ids, _ = lax.optimization_barrier((self.ids, sent))
            except StopIteration as stop:
                self.done[name] = stop.value
                if name in self.rows:
                    self.final[name] = finish_blocks(self.ids, stop.value, *self.rows[name], f"finish_{name}")
        return after

    def finish(self, *names):
        for name in names:
            self.sync(name)
        while self.sent:
            self.sync(next(iter(self.sent)))


def add_two(a_ref, b_ref):
    return a_ref[...].astype(f32) + b_ref[...].astype(f32)


def bit_of(place_ref, at):
    return place_ref[4] // (1 << at) % 2


def whole_sum(place_ref, a_ref, b_ref, at):
    if at is None:
        return add_two(a_ref, b_ref)
    first, second = a_ref[...].astype(f32), b_ref[...].astype(f32)
    swapped = bit_of(place_ref, at) == 1
    return jnp.concatenate([jnp.where(swapped, second, first), jnp.where(swapped, first, second)], 0)


def finish_kernel(at, place_ref, a_ref, b_ref, out_ref):
    if at is None:
        out_ref[...] = add_two(a_ref, b_ref)
    else:
        late = 2 * pl.program_id(0) // pl.num_programs(0)
        out_ref[...] = jnp.where(late == bit_of(place_ref, at), a_ref[...], b_ref[...]).astype(f32)


def finish_blocks(place_ids, result, rows, wide, name):
    a, b, at = result
    count = (a.shape[0] if at is None else 2 * a.shape[0]) // rows
    had = a.shape[0] // rows
    block = pl.BlockSpec((rows, D), lambda j: (j % had, 0))
    return pl.pallas_call(
        partial(finish_kernel, at),
        grid=(count,),
        in_specs=[SCALAR, block, block],
        out_specs=pl.BlockSpec((rows, D), lambda j: (0, j) if wide else (j, 0)),
        out_shape=jax.ShapeDtypeStruct((rows, count * D) if wide else (count * rows, D), f32),
        cost_estimate=cost(name),
        name=name,
    )(place_ids, a, b)


def finish_qkv_kernel(lead, ats, place_ref, *refs):
    qkv_ref, proj_ref = refs[2 * N_GROUP :]
    for group, at in enumerate(ats):
        total = whole_sum(place_ref, refs[2 * group], refs[2 * group + 1], at)
        for third in range(3):
            col = third * D + group * GROUP
            qkv_ref[:, col : col + GROUP] = total[:lead, third * GROUP : (third + 1) * GROUP]
        if group == 1:
            proj_ref[...] = total[lead : 2 * lead]


def finish_qkv(place_ids, results, lead):
    arrays = [a for result in results for a in result[:2]]
    shapes = [(lead, 3 * D), (lead, D)]
    return pl.pallas_call(
        partial(finish_qkv_kernel, lead, tuple(result[2] for result in results)),
        grid=(1,),
        in_specs=[SCALAR] + [whole(a.shape) for a in arrays],
        out_specs=[whole(s) for s in shapes],
        out_shape=[jax.ShapeDtypeStruct(s, f32) for s in shapes],
        cost_estimate=cost("finish_qkv"),
        compiler_params=pltpu.CompilerParams(vmem_limit_bytes=VMEM_LIMIT),
        name="finish_qkv",
    )(place_ids, *arrays)


def finish_last_kernel(
    n, lead, time_rows, few, early_at, place_ref, ids_ref, a_ref, b_ref, ea_ref, eb_ref, ada_ref, time_ref, *out_refs
):
    mine = place_ref[0]
    for i in range(2):
        rows = slice(i * few, (i + 1) * few)
        ada_ref[:, i * D : (i + 1) * D] = add_two(a_ref.at[rows], b_ref.at[rows])
    early = whole_sum(place_ref, ea_ref, eb_ref, early_at)
    for i in range(4):
        ada_ref[:, (2 + i) * D : (3 + i) * D] = early[lead + i * few : lead + (i + 1) * few]
    at = 2 * few
    times = add_two(a_ref.at[at : at + time_rows], b_ref.at[at : at + time_rows])
    times = jnp.concatenate([times[:, i * 128 : (i + 1) * 128] for i in range(D // 128)], 0)
    steps = lax.broadcasted_iota(jnp.int32, (STEPS, times.shape[0]), 0)
    hot = jnp.where(steps == ids_ref[...], 1.0, 0.0).astype(f32)
    time_ref[...] = exact(hot, times, ((1,), (0,)))
    at += time_rows
    high = add_two(a_ref.at[at : at + 16], b_ref.at[at : at + 16])
    small = high + add_two(a_ref.at[at + 16 : at + 32], b_ref.at[at + 16 : at + 32])
    first = 0
    for ref, count in zip(out_refs, (1, 1, 4, 1, 6, 1)):
        flat = jnp.concatenate([small[first + i : first + i + 1] for i in range(count)], 1)
        size = count * D // n
        share = flat[:, 0:size]
        for shard in range(1, n):
            share = jnp.where(mine == shard, flat[:, shard * size : (shard + 1) * size], share)
        ref[...] = share.reshape(size)
        first += count


def finish_last(place_ids, ids, pair, early, n, time_rows, few):
    lead = D // n
    sizes = [(count * D // n,) for count in (1, 1, 4, 1, 6, 1)]
    shapes = [(few, 6 * D), (STEPS, 128)] + sizes
    arrays = [ids, *pair[:2], *early[:2]]
    return pl.pallas_call(
        partial(finish_last_kernel, n, lead, time_rows, few, early[2]),
        grid=(1,),
        in_specs=[SCALAR] + [whole(a.shape) for a in arrays],
        out_specs=[whole(s) for s in shapes],
        out_shape=[jax.ShapeDtypeStruct(s, f32) for s in shapes],
        cost_estimate=cost("finish_last"),
        compiler_params=pltpu.CompilerParams(vmem_limit_bytes=VMEM_LIMIT),
        name="finish_last",
    )(place_ids, *arrays)


ROUTES = {'down': ((0, 'split'), (1, 'all'), (2, 'all'), (0, 'join')),
 'last': ((1, 'all'), (0, 'all'), (2, 'all')),
 'qkv0': ((1, 'split'), (0, 'all'), (2, 'all'), (1, 'join')),
 'qkv1': ((0, 'split'), (1, 'split'), (2, 'all'), (1, 'join'), (0, 'join')),
 'qkv2': ((1, 'split'), (0, 'all'), (2, 'all'), (1, 'join')),
 'up': ((0, 'split'), (1, 'all'), (2, 'all'), (0, 'join'))}
SYNCS = (('up', 'down'),
 ('down',),
 ('up', 'down'),
 (),
 ('up', 'qkv0', 'down'),
 (),
 ('up', 'qkv0', 'qkv1', 'down', 'qkv2'),
 ('qkv0', 'qkv1'),
 ('qkv2',
  'up',
  'qkv0',
  'last',
  'qkv1',
  'qkv2',
  'last',
  'qkv1',
  'up',
  'qkv0',
  'qkv2',
  'last',
  'qkv1',
  'qkv0',
  'last',
  'qkv2',
  'qkv1',
  'qkv1',
  'qkv2',
  'last'),
 ('down',))


def on_device(
    hidden_in,
    mask_ids,
    time_ids,
    time_table,
    w_qkv,
    w_proj,
    w_up,
    w_down,
    w_ada,
    gain_attn,
    gain_mlp,
    bias_up,
    bias_down,
    bias_ada,
    mask_embed,
    cotangent,
):
    n = lax.axis_size("shard")
    mine = lax.axis_index("shard")
    core = mine % 2
    pair = (lax.axis_index("rep") * n + mine) // 2
    ids = jnp.stack([mine, core, pair, *sides()]).astype(jnp.int32)
    barrier = lax.optimization_barrier

    vectors = (gain_attn, gain_mlp, bias_up, bias_down, mask_embed, bias_ada)
    lengths = [v.shape[0] for v in vectors]
    row_far = gather_far(pack_call(vectors))
    local = jnp.arange(PROMPT, dtype=jnp.int32)
    positions = jnp.where(local < HALF, core * HALF + local, PROMPT + local % CLEN).astype(f32)
    freqs = 10000.0 ** (-(2.0 * jnp.arange(HDIM // 2, dtype=f32)) / HDIM)
    lanes = jnp.tile(freqs, 4)
    angles = positions[:, None] * lanes[None, :]
    sign = jnp.where(jnp.arange(128) % HDIM < HDIM // 2, -1.0, 1.0).astype(f32)
    cosine, sine = jnp.cos(angles), jnp.sin(angles) * sign[None, :]
    mask = (mask_ids == 1).astype(f32)[:, None]
    ada_far = far_weight(*far_parts(w_ada), (cosine, sine, mask))
    qkv_far = far_weight(*far_parts(w_qkv, 4))
    ada_weight = near_weight(ada_far)
    rows = gather_near(row_far)
    (proj_own, up_own, down_own), _ = barrier(((w_proj, w_up, w_down), ada_far.arrays))
    up_split, up_found = far_parts(up_own, 4)
    proj_far = far_weight(*far_parts(proj_own))
    down_split, down_found = far_parts(down_own, 2)

    block = jnp.arange(CONTS, dtype=jnp.int32)
    seg = jnp.where(block < CONTS // 2, 0, 1 + core * (CONTS // 2) + block - CONTS // 2)
    my_times = lax.dynamic_slice_in_dim(time_ids, pair, 1, 0)
    times = jnp.sum(jnp.where(seg[:, None] == jnp.arange(CONTS + 1, dtype=jnp.int32)[None], my_times, 0), 1)
    mods, cond, ada_mat, attn_gain, mlp_gain, up_bias, down_bias, embed, x = mods_call(
        times, ids, time_table, hidden_in, mask, ada_weight, rows, lengths
    )

    qkv_weight = near_weight(qkv_far.tied(mods))
    q, kvp, kvc = qkv_call(ids, x, cosine, sine, qkv_weight)
    kvp, (proj_far.arrays, up_found) = barrier((kvp, (proj_far.arrays, up_found)))
    kvr = swap(kvp, "shard", 1)
    up_far = far_weight(up_split, up_found)
    early = attn_fwd(0, 4, q, kvp, kvc, kvr)
    early, up_far.arrays, down_found = barrier((early, up_far.arrays, down_found))
    proj_weight = near_weight(proj_far.tied(early))
    up_weight = near_weight(up_far.tied(early))
    early, _ = barrier((early, proj_weight.arrays))
    down_far = far_weight(down_split, down_found)
    attn_o, lse = attn_fwd(4, 2, q, kvp, kvc, kvr, early)
    attn_o, down_far.arrays = barrier((attn_o, down_far.arrays))
    down_weight = near_weight(down_far.tied(attn_o))
    attn_proj, middle, x_mlp, act, g_pre, g_mlp, g_bias_up, g_bias_down = up_call(
        ids, attn_o, hidden_in, mask, embed, mods, mlp_gain, up_bias, cotangent, proj_weight, up_weight, down_weight
    )
    plan = Schedule(ids, {"down": (FF // n // 2, False), "up": (D // n, True)})
    down_keep, down_send = down_grad_any(plan.ids, act, g_mlp, n)
    plan.begin("down", down_keep, down_send, ROUTES["down"])
    plan.sync(after=(down_keep,))
    up_keep, up_send = wgrad_call(plan.ids, x_mlp, g_pre, n, "up_grad")
    plan.start("up", up_keep, up_send, SYNCS[9])
    block_out, d_middle, g_att, g_o, stat2, g_gain_mlp = down_call(
        plan.ids, act, g_pre, middle, attn_proj, cotangent, mods, mlp_gain, down_bias, proj_weight, up_weight, down_weight
    )
    plan.sync(*SYNCS[0], after=(g_o,))
    parts, others = [], []

    def backward(group, names):
        gq, gc, dp, dr = attn_bwd(plan.ids, group, q, kvp, kvc, kvr, g_o, lse, cosine, sine)
        parts.append((gq, gc, dp))
        (dr,) = plan.sync(*names, after=(dr,))
        others.append(swap(dr, "shard", 1))

    grads = []

    def weight(group, proj, ada, names):
        keep, send, total = qkv_grad_call(
            plan.ids, x, *parts[group], others[group], cosine, sine, n, f"qkv_grad{group}", proj, ada
        )
        grads.append(total)
        plan.start(f"qkv{group}", keep, send, names)

    backward(0, SYNCS[1])
    backward(1, SYNCS[2])
    weight(0, None, (cond, stat2), SYNCS[3])
    backward(2, SYNCS[4])
    weight(1, (attn_o, g_att), None, SYNCS[5])
    weight(2, None, None, SYNCS[6])
    grad_hidden, stat1, g_gain_attn, g_mask = start_call(
        plan.ids, hidden_in, mask, embed, mods, attn_gain, d_middle, grads, qkv_weight
    )
    plan.sync(*SYNCS[7], after=(stat1,))
    time_rows = -(-time_ids.size // 6 // 8) * 8
    vector_grads = (g_gain_attn, g_gain_mlp, g_bias_up, g_bias_down, g_mask)
    keep, send = last_call(plan.ids, cond, ada_mat, stat1, stat2, vector_grads, n, time_rows)
    plan.begin("last", keep, send, ROUTES["last"], add_packed, pack_packed)
    plan.finish(*SYNCS[8])

    done = plan.done
    few = w_ada.shape[0]
    flat_ids = time_ids.reshape(1, -1)
    flat_ids = jnp.pad(flat_ids, ((0, 0), (0, 6 * time_rows - flat_ids.shape[1])), constant_values=-1)
    grad_qkv, grad_proj = finish_qkv(plan.ids, [done[f"qkv{g}"] for g in range(N_GROUP)], D // n)
    grad_ada, grad_time, *shares = finish_last(plan.ids, flat_ids, done["last"], done["qkv0"], n, time_rows, few)
    return (block_out, grad_hidden, grad_time, grad_qkv, grad_proj, plan.final["up"], plan.final["down"], grad_ada, *shares)


def solution(mesh):
    in_specs = (
        P(("rep", "shard"), None),
        P(("rep", "shard")),
        P(),
        P(),
        P("shard", None),
        P("shard", None),
        P("shard", None),
        P("shard", None),
        P("shard", None),
        P("shard"),
        P("shard"),
        P("shard"),
        P("shard"),
        P("shard"),
        P("shard"),
        P(("rep", "shard"), None),
    )
    out_specs = (
        P(("rep", "shard"), None),
        P(("rep", "shard"), None),
        P(),
        P("shard", None),
        P("shard", None),
        P("shard", None),
        P("shard", None),
        P("shard", None),
        P("shard"),
        P("shard"),
        P("shard"),
        P("shard"),
        P("shard"),
        P("shard"),
    )
    return jax.shard_map(
        on_device, mesh=mesh, in_specs=in_specs, out_specs=out_specs, check_vma=False
    )
```

```python
from functools import partial

import jax
import jax.numpy as jnp
from jax import lax
from jax.experimental import pallas as pl
from jax.experimental.pallas import tpu as pltpu
from jax.sharding import PartitionSpec as P

D = 768
HEADS = 12
HDIM = 64
FF = 3072
STEPS = 1000
CLEN = 128
CONTS = 8
PROMPT = 1024
HALF = PROMPT // 2
PAIRS = HEADS // 2
GROUP = 256
N_GROUP = D // GROUP
TILE = 256
SUB = TILE // CLEN
CHUNK = 512
eps_norm = 1e-06
bf16 = jnp.bfloat16
f32 = jnp.float32
VMEM_LIMIT = 62 * 2**20
COSTS = {'attn_bwd0': 52.5,
 'attn_bwd1': 52.8,
 'attn_bwd2': 53.4,
 'attn_fwd0': 55.5,
 'attn_fwd2': 55.8,
 'attn_fwd4': 30.9,
 'combine': 4.8,
 'down_grad': 31.5,
 'finish_down': 8.4,
 'finish_last': 12.6,
 'finish_qkv': 9.0,
 'finish_up': 11.7,
 'last': 14.7,
 'mlp_down': 75.6,
 'mlp_up': 74.4,
 'mods': 19.5,
 'pack': 4.2,
 'qkv': 25.5,
 'qkv_grad0': 25.5,
 'qkv_grad01': 46.5,
 'qkv_grad1': 21.9,
 'qkv_grad12': 39,
 'qkv_grad2': 16.8,
 'start_grad': 35.1,
 'up_grad': 27.6,
 'wide_grad': 27}


def cost(name):
    return pl.CostEstimate(flops=int(COSTS.get(name, 1.0) * 1e9), bytes_accessed=0, transcendentals=0)


def nt(left, right):
    return lax.dot_general(left, right, (((1,), (1,)), ((), ())), preferred_element_type=f32)


def nn(left, right):
    return lax.dot_general(left, right, (((1,), (0,)), ((), ())), preferred_element_type=f32)


def tn(left, right):
    return lax.dot_general(left, right, (((0,), (0,)), ((), ())), preferred_element_type=f32)


def exact(left, right, contract):
    return lax.dot_general(
        left, right, (contract, ((), ())), preferred_element_type=f32, precision=lax.Precision.HIGHEST
    )


def layer_norm(values):
    mean_value = jnp.mean(values, -1, keepdims=True)
    centered = values - mean_value
    inv_std = lax.rsqrt(jnp.mean(centered * centered, -1, keepdims=True) + eps_norm)
    return (centered * inv_std, inv_std)


def norm_back(gradient, normed, inv_std):
    return inv_std * (
        gradient
        - jnp.mean(gradient, -1, keepdims=True)
        - normed * jnp.mean(gradient * normed, -1, keepdims=True)
    )


def rotate(values, cosine, sine):
    lane = lax.broadcasted_iota(jnp.int32, cosine.shape, 1) % HDIM
    out = []
    for col in range(0, values.shape[1], 128):
        part = values[:, col : col + 128]
        other = jnp.where(lane < HDIM // 2, pltpu.roll(part, 96, 1), pltpu.roll(part, 32, 1))
        out.append(part * cosine + other * sine)
    return out[0] if len(out) == 1 else jnp.concatenate(out, 1)


def whole(shape):
    return pl.BlockSpec(shape, lambda *_: (0,) * len(shape))


ANY = pl.BlockSpec(memory_space=pl.ANY)
SCALAR = pl.BlockSpec(memory_space=pltpu.SMEM)


def place(pieces, spec, place_ref, target, sem):
    mine = place_ref[0]
    copies = []
    for (offset, split, part), piece in zip(spec, pieces):
        rows = piece.shape[0]
        if offset is None:
            where = target
        else:
            start = (mine ^ offset) * (split * rows)
            if split > 1:
                start = start + (place_ref[3 if split == 2 else 4] ^ part) * rows
            where = target.at[pl.ds(pl.multiple_of(start, 16), rows)]
        copies.append(pltpu.make_async_copy(piece, where, sem))
    return copies


class Weight:
    def __init__(self, spec, arrays):
        self.spec = tuple(spec)
        self.arrays = list(arrays)
        self.count = len(self.arrays)

    def tied(self, *values):
        arrays, _ = lax.optimization_barrier((self.arrays, values))
        return Weight(self.spec, arrays)


def qkv_kernel(
    spec, place_ref, x_ref, cos_ref, sin_ref, *rest
):
    n = len(spec)
    pieces = rest[:n]
    q_ref, kvp_ref, kvc_ref, w_ref, sem = rest[n:]
    step = pl.program_id(0)

    @pl.when(step == 0)
    def _():
        copies = place(pieces, spec, place_ref, w_ref, sem)
        for copy in copies:
            copy.start()
        for copy in copies:
            copy.wait()

    x = x_ref[...]
    cosine, sine = cos_ref[...], sin_ref[...]

    def part(third):
        return nn(x, w_ref[:, pl.ds(pl.multiple_of(third * D + step * GROUP, 128), GROUP)])

    q_ref[...] = (rotate(part(0), cosine, sine) * HDIM**-0.5).astype(bf16)
    k = rotate(part(1), cosine, sine).astype(bf16)
    kvp_ref[0], kvc_ref[0] = k[:HALF], k[HALF:]
    v = part(2).astype(bf16)
    kvp_ref[1], kvc_ref[1] = v[:HALF], v[HALF:]


def qkv_call(place_ids, x, cosine, sine, weight):
    n = weight.count
    width = weight.arrays[0].shape[1]
    half = pl.BlockSpec((2, HALF, GROUP), lambda g: (0, 0, g))
    return pl.pallas_call(
        partial(qkv_kernel, weight.spec),
        grid=(N_GROUP,),
        in_specs=[
            SCALAR,
            whole((PROMPT, D)),
            whole((PROMPT, 128)),
            whole((PROMPT, 128)),
        ]
        + [ANY] * n,
        out_specs=[pl.BlockSpec((PROMPT, GROUP), lambda g: (0, g)), half, half],
        out_shape=[
            jax.ShapeDtypeStruct((PROMPT, D), bf16),
            jax.ShapeDtypeStruct((2, HALF, D), bf16),
            jax.ShapeDtypeStruct((2, HALF, D), bf16),
        ],
        scratch_shapes=[pltpu.VMEM((D, width), bf16), pltpu.SemaphoreType.DMA],
        compiler_params=pltpu.CompilerParams(vmem_limit_bytes=VMEM_LIMIT),
        cost_estimate=cost("qkv"),
        name="qkv",
    )(place_ids, x, cosine, sine, *weight.arrays)


def head_only(values, head):
    lane = lax.broadcasted_iota(jnp.int32, values.shape, 1)
    return jnp.where((lane < HDIM) if head == 0 else (lane >= HDIM), values, jnp.zeros_like(values))


def key_parts(prompt, other, own, rows, first):
    parts = [nt(prompt, rows), nt(other, rows)]
    if not first:
        cols = range(0, HALF, CLEN)
        parts.append(
            jnp.concatenate([nt(own[c : c + CLEN], rows[c : c + CLEN]) for c in cols], 1)
        )
    return parts


def attn_fwd_kernel(q_ref, kvp_ref, kvc_ref, kvr_ref, o_ref, lse_ref):
    kp, kc, kr = kvp_ref[0], kvc_ref[0], kvr_ref[0]
    vp_t, vc_t, vr_t = kvp_ref[1].T, kvc_ref[1].T, kvr_ref[1].T
    for start in (0, HALF):
        outs = []
        q_tile = q_ref[pl.ds(start, HALF), :]
        for head in range(2):
            lanes = slice(HDIM * head, HDIM * (head + 1))
            scores = key_parts(kp, kr, kc, head_only(q_tile, head), start == 0)
            top = jnp.max(scores[0], 0, keepdims=True)
            for part in scores[1:]:
                top = jnp.maximum(top, jnp.max(part, 0, keepdims=True))
            powers = [jnp.exp(part - top) for part in scores]
            total = jnp.sum(powers[0], 0, keepdims=True)
            for part in powers[1:]:
                total = total + jnp.sum(part, 0, keepdims=True)
            lse_ref[0, pl.ds(head, 1), pl.ds(start, HALF)] = top + jnp.log(total)
            scale = 1.0 / total
            probs = [(part * scale).astype(bf16) for part in powers]
            out = nn(vp_t[lanes], probs[0]) + nn(vr_t[lanes], probs[1])
            if start:
                cols = [slice(c, c + CLEN) for c in range(0, HALF, CLEN)]
                out = out + jnp.concatenate([nn(vc_t[lanes, c], probs[2][:, c]) for c in cols], 1)
            outs.append(out)
        o_ref[pl.ds(start, HALF), :] = jnp.concatenate(outs, 0).T.astype(bf16)


def pair_block(rows, first=0):
    return pl.BlockSpec((rows, 2 * HDIM), lambda pair: (0, first + pair))


def pair_half(first=0):
    return pl.BlockSpec((2, HALF, 2 * HDIM), lambda pair: (0, 0, first + pair))


def lse_block(first=0):
    return pl.BlockSpec((1, 2, PROMPT), lambda pair: (first + pair, 0, 0))


def attn_fwd(first, pairs, q, kvp, kvc, kvr, before=None):
    inputs = (q, kvp, kvc, kvr)
    in_specs = [pair_block(PROMPT, first)] + [pair_half(first)] * 3
    body = attn_fwd_kernel
    aliases = {}
    if before is not None:
        inputs += tuple(before)
        in_specs += [ANY, ANY]
        aliases = {4: 0, 5: 1}

        def body(q_ref, kvp_ref, kvc_ref, kvr_ref, _o, _lse, o_ref, lse_ref):
            attn_fwd_kernel(q_ref, kvp_ref, kvc_ref, kvr_ref, o_ref, lse_ref)

    return pl.pallas_call(
        body,
        grid=(pairs,),
        in_specs=in_specs,
        out_specs=[pair_block(PROMPT, first), lse_block(first)],
        out_shape=[
            jax.ShapeDtypeStruct((PROMPT, D), bf16),
            jax.ShapeDtypeStruct((PAIRS, 2, PROMPT), f32),
        ],
        input_output_aliases=aliases,
        compiler_params=pltpu.CompilerParams(vmem_limit_bytes=VMEM_LIMIT),
        cost_estimate=cost(f"attn_fwd{first}"),
        name=f"attn_fwd{first}",
    )(*inputs)


def attn_bwd_kernel(
    _ids, q_ref, kvp_ref, kvc_ref, kvr_ref, g_ref, lse_ref, cos_ref, sin_ref, gq_ref, gc_ref, dp_ref, dr_ref
):
    kp, kc, kr = kvp_ref[0], kvc_ref[0], kvr_ref[0]
    vp, vc, vr = kvp_ref[1], kvc_ref[1], kvr_ref[1]
    kp_t, kc_t, kr_t = kp.T, kc.T, kr.T
    first = lax.broadcasted_iota(jnp.int32, (HALF, 2 * HDIM), 1) < HDIM
    for start in (0, HALF):
        tile = pl.ds(start, HALF)
        q_tile, g_tile = q_ref[tile, :], g_ref[tile, :]
        cols = [slice(c, c + CLEN) for c in range(0, HALF, CLEN)]
        dqs, dks, dvs = [], [], []
        for head in range(2):
            lanes = slice(HDIM * head, HDIM * (head + 1))
            scores = key_parts(kp, kr, kc, head_only(q_tile, head), start == 0)
            dps = key_parts(vp, vr, vc, head_only(g_tile, head), start == 0)
            lse = lse_ref[0, pl.ds(head, 1), tile]
            probs = [jnp.exp(part - lse) for part in scores]
            row_dot = jnp.sum(probs[0] * dps[0], 0, keepdims=True)
            for p_part, d_part in zip(probs[1:], dps[1:]):
                row_dot = row_dot + jnp.sum(p_part * d_part, 0, keepdims=True)
            ds = [(p * (d - row_dot)).astype(bf16) for p, d in zip(probs, dps)]
            probs = [p.astype(bf16) for p in probs]
            dq = nn(kp_t[lanes], ds[0]) + nn(kr_t[lanes], ds[1])
            dk = [nn(ds[0], q_tile), nn(ds[1], q_tile)]
            dv = [nn(probs[0], g_tile), nn(probs[1], g_tile)]
            if start:
                dq = dq + jnp.concatenate([nn(kc_t[lanes, c], ds[2][:, c]) for c in cols], 1)
                dk.append(jnp.concatenate([nn(ds[2][:, c], q_tile[c]) for c in cols], 0))
                dv.append(jnp.concatenate([nn(probs[2][:, c], g_tile[c]) for c in cols], 0))
            dqs.append(dq)
            dks.append(dk)
            dvs.append(dv)
        cosine, sine = cos_ref[tile, :], sin_ref[tile, :]
        dq = jnp.concatenate(dqs, 0).T * HDIM**-0.5
        gq_ref[tile, :] = rotate(dq, cosine, -sine).astype(bf16)
        for which, parts in enumerate((dks, dvs)):
            merged = [jnp.where(first, a, b) for a, b in zip(*parts)]
            if start:
                dp_ref[which] += merged[0]
                dr_ref[which] += merged[1]
                last = merged[2] if which else rotate(merged[2], cosine, -sine)
                gc_ref[which] = last.astype(bf16)
            else:
                dp_ref[which] = merged[0]
                dr_ref[which] = merged[1]


def attn_bwd(ids, group, q, kvp, kvc, kvr, g, lse, cosine, sine):
    pairs = GROUP // (2 * HDIM)
    first = group * pairs
    return pl.pallas_call(
        attn_bwd_kernel,
        grid=(pairs,),
        in_specs=[SCALAR, pair_block(PROMPT, first)]
        + [pair_half(first)] * 3
        + [pair_block(PROMPT, first), lse_block(first), whole((PROMPT, 128)), whole((PROMPT, 128))],
        out_specs=[pair_block(PROMPT), pair_half(), pair_half(), pair_half()],
        out_shape=[
            jax.ShapeDtypeStruct((PROMPT, GROUP), bf16),
            jax.ShapeDtypeStruct((2, HALF, GROUP), bf16),
            jax.ShapeDtypeStruct((2, HALF, GROUP), f32),
            jax.ShapeDtypeStruct((2, HALF, GROUP), f32),
        ],
        compiler_params=pltpu.CompilerParams(vmem_limit_bytes=VMEM_LIMIT),
        cost_estimate=cost(f"attn_bwd{group}"),
        name=f"attn_bwd{group}",
    )(ids, q, kvp, kvc, kvr, g, lse, cosine, sine)


def up_kernel(
    specs,
    place_ref,
    o_ref,
    hid_ref,
    mask_ref,
    embed_ref,
    mods_ref,
    gain_ref,
    bias_ref,
    cot_ref,
    *rest,
):
    pieces, rest = take(specs, rest)
    ap_ref, mid_ref, x_ref, act_ref, gpre_ref, gmlp_ref, gbu_ref, gbd_ref = rest[:8]
    proj_ref, up_ref, down_ref, sems = rest[8:]
    step = pl.program_id(0)
    targets = (proj_ref, up_ref, down_ref)
    copies = [
        place(part, spec, place_ref, target, sems.at[i])
        for i, (part, spec, target) in enumerate(zip(pieces, specs, targets))
    ]

    @pl.when(step == 0)
    def _():
        for group in copies:
            for copy in group:
                copy.start()
        gbu_ref[...] = jnp.zeros_like(gbu_ref)
        gbd_ref[...] = jnp.zeros_like(gbd_ref)
        for copy in copies[0]:
            copy.wait()

    attn_proj = nn(o_ref[...], proj_ref[...])
    ap_ref[...] = attn_proj
    for sub in range(SUB):
        rows = slice(sub * CLEN, (sub + 1) * CLEN)
        row = pl.ds(step * SUB + sub, 1)
        start = jnp.where(mask_ref[rows, :] > 0.5, embed_ref[...], hid_ref[rows, :].astype(f32))
        middle = start + mods_ref[row, 2 * D : 3 * D] * attn_proj[rows]
        mid_ref[rows, :] = middle
        normed, _inv = layer_norm(middle)
        shift, scale = mods_ref[row, 3 * D : 4 * D], mods_ref[row, 4 * D : 5 * D]
        x_ref[rows, :] = (normed * gain_ref[...] * (1.0 + scale) + shift).astype(bf16)
        g_mlp = (mods_ref[row, 5 * D : 6 * D] * cot_ref[rows, :].astype(f32)).astype(bf16)
        gmlp_ref[rows, :] = g_mlp
        gbd_ref[...] += jnp.sum(g_mlp.astype(f32), 0, keepdims=True)

    @pl.when(step == 0)
    def _():
        for group in copies[1:]:
            for copy in group:
                copy.wait()

    x, g_mlp = x_ref[...], gmlp_ref[...]
    root = (2.0 / jnp.pi) ** 0.5
    for col in range(0, FF, CHUNK):
        cols = slice(col, col + CHUNK)
        pre = nn(x, up_ref[:, cols]) + bias_ref[:, cols]
        square = pre * pre
        curve = jnp.tanh(root * pre * (1.0 + 0.044715 * square))
        half_up = 0.5 * (1.0 + curve)
        act_ref[:, cols] = (pre * half_up).astype(bf16)
        slope = half_up + (0.5 * root) * pre * (1.0 - curve * curve) * (1.0 + 0.134145 * square)
        g_pre = (nt(g_mlp, down_ref[cols, :]) * slope).astype(bf16)
        gpre_ref[:, cols] = g_pre
        gbu_ref[:, cols] += jnp.sum(g_pre.astype(f32), 0, keepdims=True)


def take(specs, refs):
    pieces = []
    for spec in specs:
        pieces.append(refs[: len(spec)])
        refs = refs[len(spec) :]
    return pieces, refs


def tile_block(width):
    return pl.BlockSpec((TILE, width), lambda step: (step, 0))


def weight_scratch():
    return [
        pltpu.VMEM((D, D), bf16),
        pltpu.VMEM((D, FF), bf16),
        pltpu.VMEM((FF, D), bf16),
        pltpu.SemaphoreType.DMA((3,)),
    ]


def up_call(place_ids, attn_o, hidden, mask, embed, mods, gain, bias, cot, proj, up, down):
    weights = (proj, up, down)
    n = sum(w.count for w in weights)
    specs = tuple(w.spec for w in weights)
    arrays = [a for w in weights for a in w.arrays]
    rows = PROMPT
    return pl.pallas_call(
        partial(up_kernel, specs),
        grid=(rows // TILE,),
        in_specs=[
            SCALAR,
            tile_block(D),
            tile_block(D),
            tile_block(1),
            whole((1, D)),
            whole(mods.shape),
            whole((1, D)),
            whole((1, FF)),
            tile_block(D),
        ]
        + [ANY] * n,
        out_specs=[tile_block(D)] * 3
        + [tile_block(FF)] * 2
        + [tile_block(D), whole((1, FF)), whole((1, D))],
        out_shape=[
            jax.ShapeDtypeStruct((rows, D), f32),
            jax.ShapeDtypeStruct((rows, D), f32),
            jax.ShapeDtypeStruct((rows, D), bf16),
            jax.ShapeDtypeStruct((rows, FF), bf16),
            jax.ShapeDtypeStruct((rows, FF), bf16),
            jax.ShapeDtypeStruct((rows, D), bf16),
            jax.ShapeDtypeStruct((1, FF), f32),
            jax.ShapeDtypeStruct((1, D), f32),
        ],
        scratch_shapes=weight_scratch(),
        compiler_params=pltpu.CompilerParams(vmem_limit_bytes=VMEM_LIMIT),
        cost_estimate=cost("mlp_up"),
        name="mlp_up",
    )(place_ids, attn_o, hidden, mask, embed, mods, gain, bias, cot, *arrays)


def down_kernel(specs, place_ref, act_ref, gpre_ref, mid_ref, ap_ref, cot_ref, mods_ref, gain_ref, bias_ref, *rest):
    pieces, rest = take(specs, rest)
    out_ref, dmid_ref, gatt_ref, go_ref, stat_ref, ggain_ref = rest[:6]
    proj_ref, up_ref, down_ref, sems = rest[6:]
    step = pl.program_id(0)
    targets = (proj_ref, up_ref, down_ref)
    copies = [
        place(part, spec, place_ref, target, sems.at[i])
        for i, (part, spec, target) in enumerate(zip(pieces, specs, targets))
    ]

    @pl.when(step == 0)
    def _():
        for i in (2, 1, 0):
            for copy in copies[i]:
                copy.start()
        ggain_ref[...] = jnp.zeros_like(ggain_ref)
        for copy in copies[2]:
            copy.wait()

    mlp_out = nn(act_ref[...], down_ref[...]) + bias_ref[...]

    @pl.when(step == 0)
    def _():
        for i in (1, 0):
            for copy in copies[i]:
                copy.wait()

    g_n = nt(gpre_ref[...], up_ref[...])
    for sub in range(SUB):
        rows = slice(sub * CLEN, (sub + 1) * CLEN)
        row = pl.ds(step * SUB + sub, 1)
        middle, cot, grad = mid_ref[rows, :], cot_ref[rows, :].astype(f32), g_n[rows]
        gate_attn, gate_mlp = mods_ref[row, 2 * D : 3 * D], mods_ref[row, 5 * D : 6 * D]
        scale = 1.0 + mods_ref[row, 4 * D : 5 * D]
        out_ref[rows, :] = (middle + gate_mlp * mlp_out[rows]).astype(bf16)
        normed, inv_std = layer_norm(middle)
        along = jnp.sum(grad * normed, 0, keepdims=True)
        ggain_ref[...] += along * scale
        d_middle = cot + norm_back(grad * (scale * gain_ref[...]), normed, inv_std)
        dmid_ref[rows, :] = d_middle
        gatt_ref[rows, :] = (gate_attn * d_middle).astype(bf16)
        stat_ref[row, 0:D] = jnp.sum(d_middle * ap_ref[rows, :], 0, keepdims=True)
        stat_ref[row, D : 2 * D] = jnp.sum(grad, 0, keepdims=True)
        stat_ref[row, 2 * D : 3 * D] = along * gain_ref[...]
        stat_ref[row, 3 * D : 4 * D] = jnp.sum(cot * mlp_out[rows], 0, keepdims=True)
    go_ref[...] = nt(gatt_ref[...], proj_ref[...]).astype(bf16)


def down_call(place_ids, act, gpre, middle, attn_proj, cot, mods, gain, bias, proj, up, down):
    weights = (proj, up, down)
    n = sum(w.count for w in weights)
    specs = tuple(w.spec for w in weights)
    arrays = [a for w in weights for a in w.arrays]
    rows = PROMPT
    return pl.pallas_call(
        partial(down_kernel, specs),
        grid=(rows // TILE,),
        in_specs=[
            SCALAR,
            tile_block(FF),
            tile_block(FF),
            tile_block(D),
            tile_block(D),
            tile_block(D),
            whole(mods.shape),
            whole((1, D)),
            whole((1, D)),
        ]
        + [ANY] * n,
        out_specs=[tile_block(D)] * 4 + [whole((CONTS, 4 * D)), whole((1, D))],
        out_shape=[
            jax.ShapeDtypeStruct((rows, D), bf16),
            jax.ShapeDtypeStruct((rows, D), f32),
            jax.ShapeDtypeStruct((rows, D), bf16),
            jax.ShapeDtypeStruct((rows, D), bf16),
            jax.ShapeDtypeStruct((CONTS, 4 * D), f32),
            jax.ShapeDtypeStruct((1, D), f32),
        ],
        scratch_shapes=weight_scratch(),
        compiler_params=pltpu.CompilerParams(vmem_limit_bytes=VMEM_LIMIT),
        cost_estimate=cost("mlp_down"),
        name="mlp_down",
    )(place_ids, act, gpre, middle, attn_proj, cot, mods, gain, bias, *arrays)


def split_store(total, keep_ref, send_ref, core, lead, at):
    for pair in range(total.shape[0] // lead // 2):
        even = total[2 * pair * lead : (2 * pair + 1) * lead].astype(bf16)
        odd = total[(2 * pair + 1) * lead : (2 * pair + 2) * lead].astype(bf16)
        keep_ref[pair, at : at + lead, :] = jnp.where(core == 0, even, odd)
        send_ref[pair, at : at + lead, :] = jnp.where(core == 0, odd, even)


def wgrad_kernel(lead, place_ref, left_ref, right_ref, keep_ref, send_ref):
    split_store(tn(left_ref[...], right_ref[...]), keep_ref, send_ref, place_ref[1], lead, 0)


def wgrad_call(place_ids, left, right, n, name):
    lead = D // n
    blocks = right.shape[1] // D
    out = pl.BlockSpec((n // 2, lead, D), lambda j: (0, j, 0))
    shape = jax.ShapeDtypeStruct((n // 2, blocks * lead, D), bf16)
    return pl.pallas_call(
        partial(wgrad_kernel, lead),
        grid=(blocks,),
        in_specs=[SCALAR, whole((PROMPT, D)), pl.BlockSpec((PROMPT, D), lambda j: (0, j))],
        out_specs=[out, out],
        out_shape=[shape, shape],
        compiler_params=pltpu.CompilerParams(vmem_limit_bytes=VMEM_LIMIT),
        cost_estimate=cost(name),
        name=name,
    )(place_ids, left, right)


def down_grad_kernel(_ids, left_ref, right_ref, keep_ref, send_ref):
    half = pl.num_programs(0) // 2
    total = tn(left_ref[...], right_ref[...]).astype(bf16)

    @pl.when(pl.program_id(0) < half)
    def _():
        send_ref[0] = total

    @pl.when(pl.program_id(0) >= half)
    def _():
        keep_ref[0] = total


def down_grad_call(place_ids, act, g_mlp, n):
    rows = FF // n
    half = n // 2

    def shard(j, ids):
        core = ids[1]
        return 0, jnp.where(j < half, 2 * j + 1 - core, 2 * (j - half) + core)

    shape = jax.ShapeDtypeStruct((half, rows, D), bf16)
    return pl.pallas_call(
        down_grad_kernel,
        grid_spec=pltpu.PrefetchScalarGridSpec(
            num_scalar_prefetch=1,
            grid=(n,),
            in_specs=[pl.BlockSpec((PROMPT, rows), shard), pl.BlockSpec((PROMPT, D), lambda j, ids: (0, 0))],
            out_specs=[
                pl.BlockSpec((1, rows, D), lambda j, ids: (jnp.maximum(j - half, 0), 0, 0)),
                pl.BlockSpec((1, rows, D), lambda j, ids: (jnp.minimum(j, half - 1), 0, 0)),
            ],
        ),
        out_shape=[shape, shape],
        compiler_params=pltpu.CompilerParams(vmem_limit_bytes=VMEM_LIMIT),
        cost_estimate=cost("down_grad"),
        name="down_grad",
    )(place_ids, act, g_mlp)


def down_grad_any(place_ids, act, g_mlp, n):
    if (FF // n) % 128 == 0 and n == 4:
        return down_grad_call(place_ids, act, g_mlp, n)
    full = wide_grad_call(act, g_mlp)
    core = lax.axis_index("shard") % 2
    parts = full.reshape(n // 2, 2, -1, D)
    keep = lax.dynamic_index_in_dim(parts, core, 1, False)
    return keep, lax.dynamic_index_in_dim(parts, 1 - core, 1, False)


def wide_grad_kernel(left_ref, right_ref, out_ref):
    out_ref[...] = tn(left_ref[...], right_ref[...]).astype(bf16)


def wide_grad_call(act, g_mlp):
    return pl.pallas_call(
        wide_grad_kernel,
        grid=(FF // D,),
        in_specs=[pl.BlockSpec((PROMPT, D), lambda j: (0, j)), whole((PROMPT, D))],
        out_specs=pl.BlockSpec((D, D), lambda j: (j, 0)),
        out_shape=jax.ShapeDtypeStruct((FF, D), bf16),
        compiler_params=pltpu.CompilerParams(vmem_limit_bytes=VMEM_LIMIT),
        name="wide_grad",
    )(act, g_mlp)


def qkv_grad_kernel(lead, with_proj, with_ada, place_ref, x_ref, gq_ref, gc_ref, dp_ref, got_ref, cos_ref, sin_ref, *rest):
    keep_ref, send_ref, g_ref = rest[-3:]
    core = place_ref[1]
    g_ref[:, 0:GROUP] = gq_ref[...]
    total_k = dp_ref[0] + got_ref[0].astype(f32)
    total_v = dp_ref[1] + got_ref[1].astype(f32)
    g_ref[0:HALF, GROUP : 2 * GROUP] = rotate(total_k, cos_ref[...], -sin_ref[...]).astype(bf16)
    g_ref[0:HALF, 2 * GROUP : 3 * GROUP] = total_v.astype(bf16)
    g_ref[HALF:PROMPT, GROUP : 2 * GROUP] = gc_ref[0]
    g_ref[HALF:PROMPT, 2 * GROUP : 3 * GROUP] = gc_ref[1]
    split_store(tn(x_ref[...], g_ref[...]), keep_ref, send_ref, core, lead, 0)
    at = lead
    if with_proj:
        split_store(tn(rest[0][...], rest[1][...]), keep_ref, send_ref, core, lead, at)
        at += lead
        rest = rest[2:]
    if with_ada:
        cond = rest[0][...]
        silu = (cond / (1.0 + jnp.exp(-cond))).astype(bf16).astype(f32)
        few = cond.shape[1] * lead // D
        for col in range(4):
            total = exact(silu, rest[1][:, col * D : (col + 1) * D], ((0,), (0,)))
            split_store(total, keep_ref, send_ref, core, few, at)
            at += few


def qkv_grad_call(place_ids, x, gq, gc, dp, got, cosine, sine, n, name, proj, ada):
    lead = D // n
    rows = lead
    extra = []
    if proj is not None:
        extra += list(proj)
        rows += lead
    if ada is not None:
        extra += list(ada)
        rows += 4 * (ada[0].shape[1] // n)
    out = whole((n // 2, rows, D))
    shape = jax.ShapeDtypeStruct((n // 2, rows, D), bf16)
    return pl.pallas_call(
        partial(qkv_grad_kernel, lead, proj is not None, ada is not None),
        grid=(1,),
        in_specs=[
            SCALAR,
            whole((PROMPT, D)),
            whole((PROMPT, GROUP)),
            whole((2, HALF, GROUP)),
            whole((2, HALF, GROUP)),
            whole((2, HALF, GROUP)),
            whole((HALF, 128)),
            whole((HALF, 128)),
        ]
        + [whole(e.shape) for e in extra],
        out_specs=[out, out, whole((PROMPT, D))],
        out_shape=[shape, shape, jax.ShapeDtypeStruct((PROMPT, D), bf16)],
        compiler_params=pltpu.CompilerParams(vmem_limit_bytes=VMEM_LIMIT),
        cost_estimate=cost(name),
        name=name,
    )(place_ids, x, gq, gc, dp, got, cosine, sine, *extra)


def start_kernel(spec, place_ref, hid_ref, mask_ref, embed_ref, mods_ref, gain_ref, dmid_ref, *rest):
    n = len(spec)
    grads, pieces = rest[:N_GROUP], rest[N_GROUP : N_GROUP + n]
    gh_ref, stat_ref, ggain_ref, gmask_ref, w_ref, sem = rest[N_GROUP + n :]
    step = pl.program_id(0)

    @pl.when(step == 0)
    def _():
        copies = place(pieces, spec, place_ref, w_ref, sem)
        for copy in copies:
            copy.start()
        ggain_ref[...] = jnp.zeros_like(ggain_ref)
        gmask_ref[...] = jnp.zeros_like(gmask_ref)
        for copy in copies:
            copy.wait()

    g_n = None
    for group in range(N_GROUP):
        for third in range(3):
            at = third * D + group * GROUP
            term = nt(grads[group][:, third * GROUP : (third + 1) * GROUP], w_ref[:, at : at + GROUP])
            g_n = term if g_n is None else g_n + term
    for sub in range(SUB):
        rows = slice(sub * CLEN, (sub + 1) * CLEN)
        row = pl.ds(step * SUB + sub, 1)
        masked = mask_ref[rows, :] > 0.5
        start = jnp.where(masked, embed_ref[...], hid_ref[rows, :].astype(f32))
        normed, inv_std = layer_norm(start)
        scale = 1.0 + mods_ref[row, D : 2 * D]
        grad = g_n[rows]
        along = jnp.sum(grad * normed, 0, keepdims=True)
        ggain_ref[...] += along * scale
        stat_ref[row, 0:D] = jnp.sum(grad, 0, keepdims=True)
        stat_ref[row, D : 2 * D] = along * gain_ref[...]
        d_start = dmid_ref[rows, :] + norm_back(grad * (scale * gain_ref[...]), normed, inv_std)
        gh_ref[rows, :] = jnp.where(masked, 0.0, d_start)
        gmask_ref[...] += jnp.sum(jnp.where(masked, d_start, 0.0), 0, keepdims=True)


def start_call(place_ids, hidden, mask, embed, mods, gain, d_middle, grads, weight):
    n = weight.count
    rows = PROMPT
    return pl.pallas_call(
        partial(start_kernel, weight.spec),
        grid=(rows // TILE,),
        in_specs=[
            SCALAR,
            tile_block(D),
            tile_block(1),
            whole((1, D)),
            whole(mods.shape),
            whole((1, D)),
            tile_block(D),
        ]
        + [tile_block(D)] * N_GROUP
        + [ANY] * n,
        out_specs=[tile_block(D), whole((CONTS, 2 * D)), whole((1, D)), whole((1, D))],
        out_shape=[
            jax.ShapeDtypeStruct((rows, D), f32),
            jax.ShapeDtypeStruct((CONTS, 2 * D), f32),
            jax.ShapeDtypeStruct((1, D), f32),
            jax.ShapeDtypeStruct((1, D), f32),
        ],
        scratch_shapes=[pltpu.VMEM((D, 3 * D), bf16), pltpu.SemaphoreType.DMA],
        compiler_params=pltpu.CompilerParams(vmem_limit_bytes=VMEM_LIMIT),
        cost_estimate=cost("start_grad"),
        name="start_grad",
    )(place_ids, hidden, mask, embed, mods, gain, d_middle, *grads, *weight.arrays)


def pack_kernel(*refs):
    out_ref = refs[-1]
    out_ref[...] = jnp.zeros_like(out_ref)
    for i, ref in enumerate(refs[:-1]):
        out_ref[i : i + 1, 0 : ref.shape[0]] = ref[...].astype(f32).reshape(1, -1)


def pack_call(vectors):
    shape = (8, max(v.shape[0] for v in vectors))
    return pl.pallas_call(
        pack_kernel,
        grid=(1,),
        in_specs=[whole(v.shape) for v in vectors],
        out_specs=whole(shape),
        out_shape=jax.ShapeDtypeStruct(shape, f32),
        name="pack",
    )(*vectors)


def mods_kernel(spec, lengths, times_ref, place_ref, table_ref, hid_ref, mask_ref, *rest):
    n = len(spec)
    pieces, rest = rest[:n], rest[n:]
    count = len(lengths)
    n_row = len(rest) - count - 7
    rows, rest = rest[:n_row], rest[n_row:]
    mods_ref, cond_ref, ada_ref = rest[:3]
    out_refs = rest[3 : 3 + count - 1]
    x_ref, bias_ref, row_ref, sem, row_sem = rest[3 + count - 1 :]
    gain_ref, embed_ref = out_refs[0], out_refs[4]
    copies = place(pieces, spec, place_ref, ada_ref, sem)
    row_copies = [
        pltpu.make_async_copy(row, row_ref.at[place_ref[0] ^ offset], row_sem) for offset, row in enumerate(rows)
    ]
    for copy in row_copies + copies:
        copy.start()
    for block in range(CONTS):
        cond_ref[pl.ds(block, 1), :] = table_ref[pl.ds(times_ref[block], 1), :]
    cond = cond_ref[...]
    silu = (cond / (1.0 + jnp.exp(-cond))).astype(bf16)
    for copy in row_copies:
        copy.wait()
    for shard in range(n_row):
        for i, (length, ref) in enumerate(zip(lengths, (*out_refs, bias_ref))):
            ref[0:1, shard * length : (shard + 1) * length] = row_ref[shard, i : i + 1, 0:length]
    for copy in copies:
        copy.wait()
    mods_ref[...] = nn(silu, ada_ref[...]) + bias_ref[...]

    @pl.loop(0, CONTS)
    def _(block):
        rows = pl.ds(pl.multiple_of(block * CLEN, CLEN), CLEN)
        start = jnp.where(mask_ref[rows, :] > 0.5, embed_ref[...], hid_ref[rows, :].astype(f32))
        normed, _inv = layer_norm(start)
        row = pl.ds(block, 1)
        shift, scale = mods_ref[row, 0:D], mods_ref[row, D : 2 * D]
        x_ref[rows, :] = (normed * gain_ref[...] * (1.0 + scale) + shift).astype(bf16)


def mods_call(times, place_ids, table, hidden, mask, weight, rows, lengths):
    width = weight.arrays[0].shape[1]
    n = len(rows)
    vectors = [(1, n * length) for length in lengths]
    shapes = [(CONTS, width), (CONTS, table.shape[1])]
    return pl.pallas_call(
        partial(mods_kernel, weight.spec, tuple(lengths)),
        in_specs=[SCALAR, SCALAR, whole(table.shape), whole(hidden.shape), whole(mask.shape)] + [ANY] * (weight.count + n),
        out_specs=[whole(s) for s in shapes] + [whole((table.shape[1], width))] + [whole(v) for v in vectors[:-1]] + [whole((PROMPT, D))],
        out_shape=[jax.ShapeDtypeStruct(s, f32) for s in shapes]
        + [jax.ShapeDtypeStruct((table.shape[1], width), bf16)]
        + [jax.ShapeDtypeStruct(v, f32) for v in vectors[:-1]]
        + [jax.ShapeDtypeStruct((PROMPT, D), bf16)],
        grid=(1,),
        scratch_shapes=[
            pltpu.VMEM(vectors[-1], f32),
            pltpu.VMEM((n,) + rows[0].shape, f32),
            pltpu.SemaphoreType.DMA,
            pltpu.SemaphoreType.DMA,
        ],
        compiler_params=pltpu.CompilerParams(vmem_limit_bytes=VMEM_LIMIT),
        cost_estimate=cost("mods"),
        name="mods",
    )(times, place_ids, table, hidden, mask, *weight.arrays, *rows)


def last_kernel(
    lead, time_rows, place_ref, cond_ref, ada_ref, stat1_ref, stat2_ref, ga_ref, gm_ref, bu_ref, bd_ref, me_ref,
    keep_ref, send_ref, small_ref,
):
    core, pair = place_ref[1], place_ref[2]
    cond = cond_ref[...]
    gate = 1.0 / (1.0 + jnp.exp(-cond))
    silu = (cond * gate).astype(bf16).astype(f32)
    stat1, stat2 = stat1_ref[...], stat2_ref[...]
    ada_late = exact(silu, stat1, ((0,), (0,)))
    ada = ada_ref[...].astype(f32)
    g_silu = exact(stat1, ada[:, : 2 * D], ((1,), (1,))) + exact(stat2, ada[:, 2 * D :], ((1,), (1,)))
    g_cond = g_silu * (gate * (1.0 + cond * (1.0 - gate)))
    small_ref[...] = jnp.zeros_like(small_ref)
    at = time_rows
    small_ref[at : at + 1, :] = ga_ref[...]
    small_ref[at + 1 : at + 2, :] = gm_ref[...]
    for i in range(FF // D):
        small_ref[at + 2 + i : at + 3 + i, :] = bu_ref[:, i * D : (i + 1) * D]
    small_ref[at + 6 : at + 7, :] = bd_ref[...]
    for i in range(2):
        small_ref[at + 7 + i : at + 8 + i, :] = jnp.sum(stat1[:, i * D : (i + 1) * D], 0, keepdims=True)
    for i in range(4):
        small_ref[at + 9 + i : at + 10 + i, :] = jnp.sum(stat2[:, i * D : (i + 1) * D], 0, keepdims=True)
    small_ref[at + 13 : at + 14, :] = me_ref[...]
    half = CONTS // 2
    prompt = jnp.sum(g_cond[:half], 0, keepdims=True)
    values = [prompt] + [g_cond[half + i : half + i + 1] for i in range(half)]
    base = pair * (CONTS + 1)
    where_to = [base] + [base + 1 + core * half + i for i in range(half)]
    for lane in range(D // 128):
        row = lax.broadcasted_iota(jnp.int32, (time_rows, 128), 0) + lane * time_rows
        placed = jnp.zeros((time_rows, 128), f32)
        for index, value in zip(where_to, values):
            placed = placed + jnp.where(row == index, value, 0.0)
        small_ref[0:time_rows, lane * 128 : (lane + 1) * 128] = placed
    small = small_ref[...]
    high = small.astype(bf16)
    rows = small.shape[0]
    low = (small[time_rows:] - high[time_rows:].astype(f32)).astype(bf16)
    for j in range(keep_ref.shape[0]):
        for col in range(2):
            split_store(ada_late[:, col * D : (col + 1) * D], keep_ref, send_ref, core, lead, col * lead)
        row = 2 * lead
        for ref in (keep_ref, send_ref):
            ref[j, row : row + rows, :] = high
            ref[j, row + rows : row + rows + 16, :] = low


def last_call(place_ids, cond, ada, stat1, stat2, vectors, n, time_rows):
    lead = ada.shape[0] // n
    rows = 16 + time_rows
    args = (cond, ada, stat1, stat2) + tuple(vectors)
    out = whole((n // 2, 2 * lead + rows + 16, D))
    shape = jax.ShapeDtypeStruct((n // 2, 2 * lead + rows + 16, D), bf16)
    return pl.pallas_call(
        partial(last_kernel, lead, time_rows),
        grid=(1,),
        in_specs=[SCALAR] + [whole(a.shape) for a in args],
        out_specs=[out, out],
        out_shape=[shape, shape],
        scratch_shapes=[pltpu.VMEM((rows, D), f32)],
        compiler_params=pltpu.CompilerParams(vmem_limit_bytes=VMEM_LIMIT),
        cost_estimate=cost("last"),
        name="last",
    )(place_ids, *args)


def swap(value, axis, mask):
    pairs = [(source, source ^ mask) for source in range(lax.axis_size(axis))]
    return lax.ppermute(value, axis, pairs)


def gather_far(piece):
    pieces = {0: piece}
    mask = lax.axis_size("shard") // 2
    while mask > 1:
        for offset in list(pieces):
            pieces[offset | mask] = swap(pieces[offset], "shard", mask)
        mask //= 2
    return pieces


def gather_near(pieces):
    pieces = dict(pieces)
    for offset in list(pieces):
        pieces[offset | 1] = swap(pieces[offset], "shard", 1)
    return [pieces[offset] for offset in range(len(pieces))]


def sides():
    rep = lax.axis_index("rep")
    return rep % 2, rep % 4


def far_parts(piece, split=1):
    rows = piece.shape[0] // split
    if split == 1 or rows % 16:
        return 1, gather_far(piece)
    side = sides()[0 if split == 2 else 1]
    found = gather_far(lax.dynamic_slice_in_dim(piece, side * rows, rows, 0))
    found[0] = piece
    return split, found


def far_weight(split, found, tie=None):
    if tie is not None:
        found, _ = lax.optimization_barrier((found, tie))
    spec, arrays = [], []
    for offset, part in found.items():
        if split == 1 or not offset:
            spec.append((offset, 1, 0))
            arrays.append(part)
            continue
        spec += [(offset, split, code) for code in range(split)]
        arrays += [part] + [swap(part, "rep", code) for code in range(1, split)]
    return Weight(spec, arrays)


def near_weight(far):
    spec, arrays = list(far.spec), list(far.arrays)
    for (offset, split, code), part in zip(far.spec, far.arrays):
        spec.append((offset | 1, split, code))
        arrays.append(swap(part, "shard", 1))
    if all(part.shape[0] % 16 == 0 for part in arrays):
        return Weight(spec, arrays)
    mine = lax.axis_index("shard")
    rows = arrays[0].shape[0]
    out = jnp.zeros((rows * len(arrays),) + arrays[0].shape[1:], arrays[0].dtype)
    for (offset, _split, _code), part in zip(spec, arrays):
        out = lax.dynamic_update_slice_in_dim(out, part, (mine ^ offset) * rows, 0)
    return Weight([(None, 1, 0)], [out])


def add_plain(left, right):
    return left.astype(f32) + right.astype(f32)


def add_packed(left, right):
    rows = left.shape[-2] - 16
    total = add_plain(left[..., :rows, :], right[..., :rows, :])
    rest = add_plain(left[..., rows:, :], right[..., rows:, :])
    return jnp.concatenate([total[..., : rows - 16, :], total[..., rows - 16 :, :] + rest], -2)


def pack_plain(value):
    return value.astype(bf16)


def pack_packed(value):
    high = value.astype(bf16)
    low = value[..., -16:, :] - high[..., -16:, :].astype(f32)
    return jnp.concatenate([high, low.astype(bf16)], -2)


def reduce_chain(keep, send, steps, add=add_plain, pack=pack_plain):
    mine, rep = lax.axis_index("shard"), lax.axis_index("rep")

    def part(values, axis, bit):
        return pack(add(*(lax.dynamic_index_in_dim(v, bit, axis, False) for v in values)))

    def kept_part(values, axis, bit, got):
        values, got = lax.optimization_barrier((values, got))
        return part(values, axis, bit), got

    got = yield send, swap(send, "shard", 1)
    terms = (keep, got)
    mask = 2
    while mask < lax.axis_size("shard"):
        halves = [t.reshape((-1, 2) + t.shape[1:]) for t in terms]
        bit = (mine // mask) % 2
        send = part(halves, 1, 1 - bit)
        got = yield send, swap(send, "shard", mask)
        terms = kept_part(halves, 1, bit, got)
        mask *= 2
    terms = tuple(t[0] for t in terms)
    joined = None
    more = range(3, lax.axis_size("rep").bit_length() - 1)
    steps = [(bit, "all") for bit in more] + list(steps)
    for at, kind in steps:
        bit = (rep >> at) % 2
        if kind == "split":
            halves = [t.reshape(2, -1, t.shape[-1]) for t in terms]
            send = part(halves, 0, 1 - bit)
            got = yield send, swap(send, "rep", 1 << at)
            terms = kept_part(halves, 0, bit, got)
            continue
        value = pack(add(*terms)) if joined is None else joined
        got = yield value, swap(value, "rep", 1 << at)
        if kind == "join":
            last = (value, got, at)
            first, second = jnp.where(bit == 0, value, got), jnp.where(bit == 0, got, value)
            joined = jnp.concatenate([first, second], 0)
        else:
            last = (value, got, None)
            terms, joined = (value, got), None
    return last


class Schedule:
    def __init__(self, ids, rows):
        self.ids = ids
        self.chains = {}
        self.sent = {}
        self.done = {}
        self.final = {}
        self.rows = rows

    def begin(self, name, keep, send, *how):
        chain = reduce_chain(keep, send, *how)
        self.chains[name] = chain
        _sent, self.sent[name] = next(chain)

    def start(self, name, keep, send, names):
        (send,) = self.sync(*(other for other in names if other != name), after=(send,))
        self.begin(name, keep, send, ROUTES[name])
        self.sync(*(other for other in names if other == name), after=(send,))

    def sync(self, *names, after=()):
        for name in names or (None,):
            if name is not None and name not in self.sent:
                continue
            got = self.sent.pop(name, None)
            self.ids, got, after = lax.optimization_barrier((self.ids, got, tuple(after)))
            if got is None:
                continue
            try:
                sent, self.sent[name] = self.chains[name].send(got)
                self.ids, _ = lax.optimization_barrier((self.ids, sent))
            except StopIteration as stop:
                self.done[name] = stop.value
                if name in self.rows:
                    self.final[name] = finish_blocks(stop.value, *self.rows[name])
        return after

    def finish(self, *names):
        for name in names:
            self.sync(name)
        while self.sent:
            self.sync(next(iter(self.sent)))


def add_two(a_ref, b_ref):
    return a_ref[...].astype(f32) + b_ref[...].astype(f32)


def bit_of(place_ref, at):
    return place_ref[4] // (1 << at) % 2


def whole_sum(place_ref, a_ref, b_ref, at):
    if at is None:
        return add_two(a_ref, b_ref)
    first, second = a_ref[...].astype(f32), b_ref[...].astype(f32)
    swapped = bit_of(place_ref, at) == 1
    return jnp.concatenate([jnp.where(swapped, second, first), jnp.where(swapped, first, second)], 0)


def finish_blocks(result, rows, wide):
    value, got, at = result
    if at is None:
        total = value.astype(f32) + got.astype(f32)
    else:
        bit = (lax.axis_index("rep") >> at) % 2
        first, second = jnp.where(bit == 0, value, got), jnp.where(bit == 0, got, value)
        total = jnp.concatenate([first, second], 0).astype(f32)
    if not wide:
        return total
    return jnp.concatenate([total[i : i + rows] for i in range(0, total.shape[0], rows)], 1)


def finish_last_kernel(
    n, lead, time_rows, few, ats, place_ref, ids_ref, a_ref, b_ref, *refs
):
    mine = place_ref[0]
    groups, (qkv_ref, proj_ref, ada_ref, time_ref, *out_refs) = refs[: 2 * N_GROUP], refs[2 * N_GROUP :]
    totals = [whole_sum(place_ref, groups[2 * i], groups[2 * i + 1], at) for i, at in enumerate(ats)]
    for group, total in enumerate(totals):
        for third in range(3):
            col = third * D + group * GROUP
            qkv_ref[:, col : col + GROUP] = total[:lead, third * GROUP : (third + 1) * GROUP]
    proj_ref[...] = totals[1][lead : 2 * lead]
    early = totals[0]
    for i in range(2):
        rows = slice(i * few, (i + 1) * few)
        ada_ref[:, i * D : (i + 1) * D] = add_two(a_ref.at[rows], b_ref.at[rows])
    for i in range(4):
        ada_ref[:, (2 + i) * D : (3 + i) * D] = early[lead + i * few : lead + (i + 1) * few]
    at = 2 * few
    times = add_two(a_ref.at[at : at + time_rows], b_ref.at[at : at + time_rows])
    times = jnp.concatenate([times[:, i * 128 : (i + 1) * 128] for i in range(D // 128)], 0)
    steps = lax.broadcasted_iota(jnp.int32, (STEPS, times.shape[0]), 0)
    hot = jnp.where(steps == ids_ref[...], 1.0, 0.0).astype(f32)
    time_ref[...] = exact(hot, times, ((1,), (0,)))
    at += time_rows
    high = add_two(a_ref.at[at : at + 16], b_ref.at[at : at + 16])
    small = high + add_two(a_ref.at[at + 16 : at + 32], b_ref.at[at + 16 : at + 32])
    first = 0
    for ref, count in zip(out_refs, (1, 1, 4, 1, 6, 1)):
        flat = jnp.concatenate([small[first + i : first + i + 1] for i in range(count)], 1)
        size = count * D // n
        share = flat[:, 0:size]
        for shard in range(1, n):
            share = jnp.where(mine == shard, flat[:, shard * size : (shard + 1) * size], share)
        ref[...] = share.reshape(size)
        first += count


def finish_last(place_ids, ids, last, results, n, time_rows, few):
    lead = D // n
    sizes = [(count * D // n,) for count in (1, 1, 4, 1, 6, 1)]
    shapes = [(lead, 3 * D), (lead, D), (few, 6 * D), (STEPS, 128)] + sizes
    arrays = [ids, *last[:2]] + [a for result in results for a in result[:2]]
    ats = tuple(result[2] for result in results)
    return pl.pallas_call(
        partial(finish_last_kernel, n, lead, time_rows, few, ats),
        grid=(1,),
        in_specs=[SCALAR] + [whole(a.shape) for a in arrays],
        out_specs=[whole(s) for s in shapes],
        out_shape=[jax.ShapeDtypeStruct(s, f32) for s in shapes],
        cost_estimate=cost("finish_last"),
        compiler_params=pltpu.CompilerParams(vmem_limit_bytes=VMEM_LIMIT),
        name="finish_last",
    )(place_ids, *arrays)


ROUTES = {'down': ((0, 'split'), (1, 'all'), (2, 'all'), (0, 'join')),
 'last': ((1, 'all'), (0, 'all'), (2, 'all')),
 'qkv0': ((1, 'split'), (0, 'all'), (2, 'all'), (1, 'join')),
 'qkv1': ((0, 'split'), (1, 'split'), (2, 'all'), (1, 'join'), (0, 'join')),
 'qkv2': ((1, 'split'), (0, 'all'), (2, 'all'), (1, 'join')),
 'up': ((0, 'split'), (1, 'all'), (2, 'all'), (0, 'join'))}
SYNCS = (('up', 'down'),
 ('down',),
 ('up', 'down'),
 (),
 ('up', 'qkv0', 'down'),
 (),
 ('up', 'qkv0', 'qkv1', 'down', 'qkv2'),
 ('qkv0', 'qkv1'),
 ('qkv2',
  'up',
  'qkv0',
  'last',
  'qkv1',
  'qkv2',
  'last',
  'qkv1',
  'up',
  'qkv0',
  'qkv2',
  'last',
  'qkv1',
  'qkv0',
  'last',
  'qkv2',
  'qkv1',
  'qkv1',
  'qkv2',
  'last'),
 ('down',))


def on_device(
    hidden_in,
    mask_ids,
    time_ids,
    time_table,
    w_qkv,
    w_proj,
    w_up,
    w_down,
    w_ada,
    gain_attn,
    gain_mlp,
    bias_up,
    bias_down,
    bias_ada,
    mask_embed,
    cotangent,
):
    n = lax.axis_size("shard")
    mine = lax.axis_index("shard")
    core = mine % 2
    pair = (lax.axis_index("rep") * n + mine) // 2
    ids = jnp.stack([mine, core, pair, *sides()]).astype(jnp.int32)
    barrier = lax.optimization_barrier

    vectors = (gain_attn, gain_mlp, bias_up, bias_down, mask_embed, bias_ada)
    lengths = [v.shape[0] for v in vectors]
    row_far = gather_far(pack_call(vectors))
    local = jnp.arange(PROMPT, dtype=jnp.int32)
    positions = jnp.where(local < HALF, core * HALF + local, PROMPT + local % CLEN).astype(f32)
    freqs = 10000.0 ** (-(2.0 * jnp.arange(HDIM // 2, dtype=f32)) / HDIM)
    lanes = jnp.tile(freqs, 4)
    angles = positions[:, None] * lanes[None, :]
    sign = jnp.where(jnp.arange(128) % HDIM < HDIM // 2, -1.0, 1.0).astype(f32)
    cosine, sine = jnp.cos(angles), jnp.sin(angles) * sign[None, :]
    mask = (mask_ids == 1).astype(f32)[:, None]
    ada_far = far_weight(*far_parts(w_ada), (cosine, sine, mask))
    qkv_far = far_weight(*far_parts(w_qkv, 4))
    ada_weight = near_weight(ada_far)
    rows = gather_near(row_far)
    (proj_own, up_own, down_own), _ = barrier(((w_proj, w_up, w_down), ada_far.arrays))
    up_split, up_found = far_parts(up_own, 4)
    proj_far = far_weight(*far_parts(proj_own))
    down_split, down_found = far_parts(down_own, 2)

    block = jnp.arange(CONTS, dtype=jnp.int32)
    seg = jnp.where(block < CONTS // 2, 0, 1 + core * (CONTS // 2) + block - CONTS // 2)
    my_times = lax.dynamic_slice_in_dim(time_ids, pair, 1, 0)
    times = jnp.sum(jnp.where(seg[:, None] == jnp.arange(CONTS + 1, dtype=jnp.int32)[None], my_times, 0), 1)
    mods, cond, ada_mat, attn_gain, mlp_gain, up_bias, down_bias, embed, x = mods_call(
        times, ids, time_table, hidden_in, mask, ada_weight, rows, lengths
    )

    qkv_weight = near_weight(qkv_far.tied(mods))
    q, kvp, kvc = qkv_call(ids, x, cosine, sine, qkv_weight)
    kvp, up_found = barrier((kvp, up_found))
    kvr = swap(kvp, "shard", 1)
    up_far = far_weight(up_split, up_found)
    early = attn_fwd(0, 4, q, kvp, kvc, kvr)
    early, up_far.arrays, proj_far.arrays, down_found = barrier((early, up_far.arrays, proj_far.arrays, down_found))
    proj_weight = near_weight(proj_far.tied(early))
    up_weight = near_weight(up_far.tied(early))
    early, _ = barrier((early, proj_weight.arrays))
    down_far = far_weight(down_split, down_found)
    attn_o, lse = attn_fwd(4, PAIRS - 4, q, kvp, kvc, kvr, early)
    attn_o, down_far.arrays = barrier((attn_o, down_far.arrays))
    down_weight = near_weight(down_far.tied(attn_o))
    attn_proj, middle, x_mlp, act, g_pre, g_mlp, g_bias_up, g_bias_down = up_call(
        ids, attn_o, hidden_in, mask, embed, mods, mlp_gain, up_bias, cotangent, proj_weight, up_weight, down_weight
    )
    plan = Schedule(ids, {"down": (FF // n // 2, False), "up": (D // n, True)})
    down_keep, down_send = down_grad_any(plan.ids, act, g_mlp, n)
    plan.begin("down", down_keep, down_send, ROUTES["down"])
    plan.sync(after=(down_keep,))
    up_keep, up_send = wgrad_call(plan.ids, x_mlp, g_pre, n, "up_grad")
    plan.start("up", up_keep, up_send, SYNCS[9])
    block_out, d_middle, g_att, g_o, stat2, g_gain_mlp = down_call(
        plan.ids, act, g_pre, middle, attn_proj, cotangent, mods, mlp_gain, down_bias, proj_weight, up_weight, down_weight
    )
    plan.sync(*SYNCS[0], after=(g_o,))
    parts, others = [], []

    def backward(group, names):
        gq, gc, dp, dr = attn_bwd(plan.ids, group, q, kvp, kvc, kvr, g_o, lse, cosine, sine)
        parts.append((gq, gc, dp))
        (dr,) = plan.sync(*names, after=(dr,))
        others.append(swap(dr, "shard", 1))

    grads = []

    def weight(group, proj, ada, names):
        keep, send, total = qkv_grad_call(
            plan.ids, x, *parts[group], others[group], cosine, sine, n, f"qkv_grad{group}", proj, ada
        )
        grads.append(total)
        plan.start(f"qkv{group}", keep, send, names)

    backward(0, SYNCS[1])
    backward(1, SYNCS[2])
    weight(0, None, (cond, stat2), SYNCS[3])
    backward(2, SYNCS[4])
    weight(1, (attn_o, g_att), None, SYNCS[5])
    weight(2, None, None, SYNCS[6])
    grad_hidden, stat1, g_gain_attn, g_mask = start_call(
        plan.ids, hidden_in, mask, embed, mods, attn_gain, d_middle, grads, qkv_weight
    )
    plan.sync(*SYNCS[7], after=(stat1,))
    time_rows = -(-time_ids.size // 6 // 8) * 8
    vector_grads = (g_gain_attn, g_gain_mlp, g_bias_up, g_bias_down, g_mask)
    keep, send = last_call(plan.ids, cond, ada_mat, stat1, stat2, vector_grads, n, time_rows)
    plan.begin("last", keep, send, ROUTES["last"], add_packed, pack_packed)
    plan.finish(*SYNCS[8])

    done = plan.done
    few = w_ada.shape[0]
    flat_ids = time_ids.reshape(1, -1)
    flat_ids = jnp.pad(flat_ids, ((0, 0), (0, 6 * time_rows - flat_ids.shape[1])), constant_values=-1)
    results = [done[f"qkv{g}"] for g in range(N_GROUP)]
    grad_qkv, grad_proj, grad_ada, grad_time, *shares = finish_last(
        plan.ids, flat_ids, done["last"], results, n, time_rows, few
    )
    return (block_out, grad_hidden, grad_time, grad_qkv, grad_proj, plan.final["up"], plan.final["down"], grad_ada, *shares)


def solution(mesh):
    in_specs = (
        P(("rep", "shard"), None),
        P(("rep", "shard")),
        P(),
        P(),
        P("shard", None),
        P("shard", None),
        P("shard", None),
        P("shard", None),
        P("shard", None),
        P("shard"),
        P("shard"),
        P("shard"),
        P("shard"),
        P("shard"),
        P("shard"),
        P(("rep", "shard"), None),
    )
    out_specs = (
        P(("rep", "shard"), None),
        P(("rep", "shard"), None),
        P(),
        P("shard", None),
        P("shard", None),
        P("shard", None),
        P("shard", None),
        P("shard", None),
        P("shard"),
        P("shard"),
        P("shard"),
        P("shard"),
        P("shard"),
        P("shard"),
    )
    return jax.shard_map(
        on_device, mesh=mesh, in_specs=in_specs, out_specs=out_specs, check_vma=False
    )
```

```python
from functools import partial

import jax
import jax.numpy as jnp
from jax import lax
from jax.experimental import pallas as pl
from jax.experimental.pallas import tpu as pltpu
from jax.sharding import PartitionSpec as P

D = 768
HEADS = 12
HDIM = 64
FF = 3072
STEPS = 1000
CLEN = 128
CONTS = 8
PROMPT = 1024
HALF = PROMPT // 2
PAIRS = HEADS // 2
GROUP = 256
N_GROUP = D // GROUP
TILE = 256
SUB = TILE // CLEN
CHUNK = 512
eps_norm = 1e-06
bf16 = jnp.bfloat16
f32 = jnp.float32
VMEM_LIMIT = 62 * 2**20
COSTS = {'attn_bwd0': 52.5,
 'attn_bwd1': 52.8,
 'attn_bwd2': 53.4,
 'attn_fwd0': 55.5,
 'attn_fwd2': 55.8,
 'attn_fwd4': 30.9,
 'combine': 4.8,
 'down_grad': 31.5,
 'finish_down': 8.4,
 'finish_last': 12.6,
 'finish_qkv': 9.0,
 'finish_up': 11.7,
 'last': 14.7,
 'mlp_down': 75.6,
 'mlp_up': 74.4,
 'mods': 19.5,
 'pack': 4.2,
 'qkv': 25.5,
 'qkv_grad0': 25.5,
 'qkv_grad01': 46.5,
 'qkv_grad1': 21.9,
 'qkv_grad12': 39,
 'qkv_grad2': 16.8,
 'start_grad': 35.1,
 'up_grad': 27.6,
 'wide_grad': 27}


def cost(name):
    return pl.CostEstimate(flops=int(COSTS.get(name, 1.0) * 1e9), bytes_accessed=0, transcendentals=0)


def nt(left, right):
    return lax.dot_general(left, right, (((1,), (1,)), ((), ())), preferred_element_type=f32)


def nn(left, right):
    return lax.dot_general(left, right, (((1,), (0,)), ((), ())), preferred_element_type=f32)


def tn(left, right):
    return lax.dot_general(left, right, (((0,), (0,)), ((), ())), preferred_element_type=f32)


def exact(left, right, contract):
    return lax.dot_general(
        left, right, (contract, ((), ())), preferred_element_type=f32, precision=lax.Precision.HIGHEST
    )


def layer_norm(values):
    mean_value = jnp.mean(values, -1, keepdims=True)
    centered = values - mean_value
    inv_std = lax.rsqrt(jnp.mean(centered * centered, -1, keepdims=True) + eps_norm)
    return (centered * inv_std, inv_std)


def norm_back(gradient, normed, inv_std):
    return inv_std * (
        gradient
        - jnp.mean(gradient, -1, keepdims=True)
        - normed * jnp.mean(gradient * normed, -1, keepdims=True)
    )


def rotate(values, cosine, sine):
    lane = lax.broadcasted_iota(jnp.int32, cosine.shape, 1) % HDIM
    out = []
    for col in range(0, values.shape[1], 128):
        part = values[:, col : col + 128]
        other = jnp.where(lane < HDIM // 2, pltpu.roll(part, 96, 1), pltpu.roll(part, 32, 1))
        out.append(part * cosine + other * sine)
    return out[0] if len(out) == 1 else jnp.concatenate(out, 1)


def whole(shape):
    return pl.BlockSpec(shape, lambda *_: (0,) * len(shape))


ANY = pl.BlockSpec(memory_space=pl.ANY)
SCALAR = pl.BlockSpec(memory_space=pltpu.SMEM)


def place(pieces, spec, place_ref, target, sem):
    mine = place_ref[0]
    copies = []
    for (offset, split, part), piece in zip(spec, pieces):
        rows = piece.shape[0]
        if offset is None:
            where = target
        else:
            start = (mine ^ offset) * (split * rows)
            if split > 1:
                start = start + (place_ref[3 if split == 2 else 4] ^ part) * rows
            where = target.at[pl.ds(pl.multiple_of(start, 16), rows)]
        copies.append(pltpu.make_async_copy(piece, where, sem))
    return copies


class Weight:
    def __init__(self, spec, arrays):
        self.spec = tuple(spec)
        self.arrays = list(arrays)
        self.count = len(self.arrays)

    def tied(self, *values):
        arrays, _ = lax.optimization_barrier((self.arrays, values))
        return Weight(self.spec, arrays)


def qkv_kernel(
    spec, place_ref, x_ref, cos_ref, sin_ref, *rest
):
    n = len(spec)
    pieces = rest[:n]
    q_ref, kvp_ref, kvc_ref, w_ref, sem = rest[n:]
    step = pl.program_id(0)

    @pl.when(step == 0)
    def _():
        copies = place(pieces, spec, place_ref, w_ref, sem)
        for copy in copies:
            copy.start()
        for copy in copies:
            copy.wait()

    x = x_ref[...]
    cosine, sine = cos_ref[...], sin_ref[...]

    def part(third):
        return nn(x, w_ref[:, pl.ds(pl.multiple_of(third * D + step * GROUP, 128), GROUP)])

    q_ref[...] = (rotate(part(0), cosine, sine) * HDIM**-0.5).astype(bf16)
    k = rotate(part(1), cosine, sine).astype(bf16)
    kvp_ref[0], kvc_ref[0] = k[:HALF], k[HALF:]
    v = part(2).astype(bf16)
    kvp_ref[1], kvc_ref[1] = v[:HALF], v[HALF:]


def qkv_call(place_ids, x, cosine, sine, weight):
    n = weight.count
    width = weight.arrays[0].shape[1]
    half = pl.BlockSpec((2, HALF, GROUP), lambda g: (0, 0, g))
    return pl.pallas_call(
        partial(qkv_kernel, weight.spec),
        grid=(N_GROUP,),
        in_specs=[
            SCALAR,
            whole((PROMPT, D)),
            whole((PROMPT, 128)),
            whole((PROMPT, 128)),
        ]
        + [ANY] * n,
        out_specs=[pl.BlockSpec((PROMPT, GROUP), lambda g: (0, g)), half, half],
        out_shape=[
            jax.ShapeDtypeStruct((PROMPT, D), bf16),
            jax.ShapeDtypeStruct((2, HALF, D), bf16),
            jax.ShapeDtypeStruct((2, HALF, D), bf16),
        ],
        scratch_shapes=[pltpu.VMEM((D, width), bf16), pltpu.SemaphoreType.DMA],
        compiler_params=pltpu.CompilerParams(vmem_limit_bytes=VMEM_LIMIT),
        cost_estimate=cost("qkv"),
        name="qkv",
    )(place_ids, x, cosine, sine, *weight.arrays)


def head_only(values, head):
    lane = lax.broadcasted_iota(jnp.int32, values.shape, 1)
    return jnp.where((lane < HDIM) if head == 0 else (lane >= HDIM), values, jnp.zeros_like(values))


def key_parts(prompt, other, own, rows, first):
    parts = [nt(prompt, rows), nt(other, rows)]
    if not first:
        cols = range(0, HALF, CLEN)
        parts.append(
            jnp.concatenate([nt(own[c : c + CLEN], rows[c : c + CLEN]) for c in cols], 1)
        )
    return parts


def attn_fwd_kernel(q_ref, kvp_ref, kvc_ref, kvr_ref, o_ref, lse_ref):
    kp, kc, kr = kvp_ref[0], kvc_ref[0], kvr_ref[0]
    vp_t, vc_t, vr_t = kvp_ref[1].T, kvc_ref[1].T, kvr_ref[1].T
    for start in (0, HALF):
        outs = []
        q_tile = q_ref[pl.ds(start, HALF), :]
        for head in range(2):
            lanes = slice(HDIM * head, HDIM * (head + 1))
            scores = key_parts(kp, kr, kc, head_only(q_tile, head), start == 0)
            top = jnp.max(scores[0], 0, keepdims=True)
            for part in scores[1:]:
                top = jnp.maximum(top, jnp.max(part, 0, keepdims=True))
            powers = [jnp.exp(part - top) for part in scores]
            total = jnp.sum(powers[0], 0, keepdims=True)
            for part in powers[1:]:
                total = total + jnp.sum(part, 0, keepdims=True)
            lse_ref[0, pl.ds(head, 1), pl.ds(start, HALF)] = top + jnp.log(total)
            scale = 1.0 / total
            probs = [(part * scale).astype(bf16) for part in powers]
            out = nn(vp_t[lanes], probs[0]) + nn(vr_t[lanes], probs[1])
            if start:
                cols = [slice(c, c + CLEN) for c in range(0, HALF, CLEN)]
                out = out + jnp.concatenate([nn(vc_t[lanes, c], probs[2][:, c]) for c in cols], 1)
            outs.append(out)
        o_ref[pl.ds(start, HALF), :] = jnp.concatenate(outs, 0).T.astype(bf16)


def pair_block(rows, first=0):
    return pl.BlockSpec((rows, 2 * HDIM), lambda pair: (0, first + pair))


def pair_half(first=0):
    return pl.BlockSpec((2, HALF, 2 * HDIM), lambda pair: (0, 0, first + pair))


def lse_block(first=0):
    return pl.BlockSpec((1, 2, PROMPT), lambda pair: (first + pair, 0, 0))


def attn_fwd(first, pairs, q, kvp, kvc, kvr, before=None):
    inputs = (q, kvp, kvc, kvr)
    in_specs = [pair_block(PROMPT, first)] + [pair_half(first)] * 3
    body = attn_fwd_kernel
    aliases = {}
    if before is not None:
        inputs += tuple(before)
        in_specs += [ANY, ANY]
        aliases = {4: 0, 5: 1}

        def body(q_ref, kvp_ref, kvc_ref, kvr_ref, _o, _lse, o_ref, lse_ref):
            attn_fwd_kernel(q_ref, kvp_ref, kvc_ref, kvr_ref, o_ref, lse_ref)

    return pl.pallas_call(
        body,
        grid=(pairs,),
        in_specs=in_specs,
        out_specs=[pair_block(PROMPT, first), lse_block(first)],
        out_shape=[
            jax.ShapeDtypeStruct((PROMPT, D), bf16),
            jax.ShapeDtypeStruct((PAIRS, 2, PROMPT), f32),
        ],
        input_output_aliases=aliases,
        compiler_params=pltpu.CompilerParams(vmem_limit_bytes=VMEM_LIMIT),
        cost_estimate=cost(f"attn_fwd{first}"),
        name=f"attn_fwd{first}",
    )(*inputs)


def attn_bwd_kernel(
    _ids, q_ref, kvp_ref, kvc_ref, kvr_ref, g_ref, lse_ref, cos_ref, sin_ref, gq_ref, gc_ref, dp_ref, dr_ref
):
    kp, kc, kr = kvp_ref[0], kvc_ref[0], kvr_ref[0]
    vp, vc, vr = kvp_ref[1], kvc_ref[1], kvr_ref[1]
    kp_t, kc_t, kr_t = kp.T, kc.T, kr.T
    first = lax.broadcasted_iota(jnp.int32, (HALF, 2 * HDIM), 1) < HDIM
    for start in (0, HALF):
        tile = pl.ds(start, HALF)
        q_tile, g_tile = q_ref[tile, :], g_ref[tile, :]
        cols = [slice(c, c + CLEN) for c in range(0, HALF, CLEN)]
        dqs, dks, dvs = [], [], []
        for head in range(2):
            lanes = slice(HDIM * head, HDIM * (head + 1))
            scores = key_parts(kp, kr, kc, head_only(q_tile, head), start == 0)
            dps = key_parts(vp, vr, vc, head_only(g_tile, head), start == 0)
            lse = lse_ref[0, pl.ds(head, 1), tile]
            probs = [jnp.exp(part - lse) for part in scores]
            row_dot = jnp.sum(probs[0] * dps[0], 0, keepdims=True)
            for p_part, d_part in zip(probs[1:], dps[1:]):
                row_dot = row_dot + jnp.sum(p_part * d_part, 0, keepdims=True)
            ds = [(p * (d - row_dot)).astype(bf16) for p, d in zip(probs, dps)]
            probs = [p.astype(bf16) for p in probs]
            dq = nn(kp_t[lanes], ds[0]) + nn(kr_t[lanes], ds[1])
            dk = [nn(ds[0], q_tile), nn(ds[1], q_tile)]
            dv = [nn(probs[0], g_tile), nn(probs[1], g_tile)]
            if start:
                dq = dq + jnp.concatenate([nn(kc_t[lanes, c], ds[2][:, c]) for c in cols], 1)
                dk.append(jnp.concatenate([nn(ds[2][:, c], q_tile[c]) for c in cols], 0))
                dv.append(jnp.concatenate([nn(probs[2][:, c], g_tile[c]) for c in cols], 0))
            dqs.append(dq)
            dks.append(dk)
            dvs.append(dv)
        cosine, sine = cos_ref[tile, :], sin_ref[tile, :]
        dq = jnp.concatenate(dqs, 0).T * HDIM**-0.5
        gq_ref[tile, :] = rotate(dq, cosine, -sine).astype(bf16)
        for which, parts in enumerate((dks, dvs)):
            merged = [jnp.where(first, a, b) for a, b in zip(*parts)]
            if start:
                dp_ref[which] += merged[0]
                dr_ref[which] += merged[1]
                last = merged[2] if which else rotate(merged[2], cosine, -sine)
                gc_ref[which] = last.astype(bf16)
            else:
                dp_ref[which] = merged[0]
                dr_ref[which] = merged[1]


def attn_bwd(ids, group, q, kvp, kvc, kvr, g, lse, cosine, sine):
    pairs = GROUP // (2 * HDIM)
    first = group * pairs
    return pl.pallas_call(
        attn_bwd_kernel,
        grid=(pairs,),
        in_specs=[SCALAR, pair_block(PROMPT, first)]
        + [pair_half(first)] * 3
        + [pair_block(PROMPT, first), lse_block(first), whole((PROMPT, 128)), whole((PROMPT, 128))],
        out_specs=[pair_block(PROMPT), pair_half(), pair_half(), pair_half()],
        out_shape=[
            jax.ShapeDtypeStruct((PROMPT, GROUP), bf16),
            jax.ShapeDtypeStruct((2, HALF, GROUP), bf16),
            jax.ShapeDtypeStruct((2, HALF, GROUP), f32),
            jax.ShapeDtypeStruct((2, HALF, GROUP), f32),
        ],
        compiler_params=pltpu.CompilerParams(vmem_limit_bytes=VMEM_LIMIT),
        cost_estimate=cost(f"attn_bwd{group}"),
        name=f"attn_bwd{group}",
    )(ids, q, kvp, kvc, kvr, g, lse, cosine, sine)


def up_kernel(
    specs,
    place_ref,
    o_ref,
    hid_ref,
    mask_ref,
    embed_ref,
    mods_ref,
    gain_ref,
    bias_ref,
    cot_ref,
    *rest,
):
    pieces, rest = take(specs, rest)
    ap_ref, mid_ref, x_ref, act_ref, gpre_ref, gmlp_ref, gbu_ref, gbd_ref = rest[:8]
    proj_ref, up_ref, down_ref, sems = rest[8:]
    step = pl.program_id(0)
    targets = (proj_ref, up_ref, down_ref)
    copies = [
        place(part, spec, place_ref, target, sems.at[i])
        for i, (part, spec, target) in enumerate(zip(pieces, specs, targets))
    ]

    @pl.when(step == 0)
    def _():
        for group in copies:
            for copy in group:
                copy.start()
        gbu_ref[...] = jnp.zeros_like(gbu_ref)
        gbd_ref[...] = jnp.zeros_like(gbd_ref)
        for copy in copies[0]:
            copy.wait()

    attn_proj = nn(o_ref[...], proj_ref[...])
    ap_ref[...] = attn_proj
    for sub in range(SUB):
        rows = slice(sub * CLEN, (sub + 1) * CLEN)
        row = pl.ds(step * SUB + sub, 1)
        start = jnp.where(mask_ref[rows, :] > 0.5, embed_ref[...], hid_ref[rows, :].astype(f32))
        middle = start + mods_ref[row, 2 * D : 3 * D] * attn_proj[rows]
        mid_ref[rows, :] = middle
        normed, _inv = layer_norm(middle)
        shift, scale = mods_ref[row, 3 * D : 4 * D], mods_ref[row, 4 * D : 5 * D]
        x_ref[rows, :] = (normed * gain_ref[...] * (1.0 + scale) + shift).astype(bf16)
        g_mlp = (mods_ref[row, 5 * D : 6 * D] * cot_ref[rows, :].astype(f32)).astype(bf16)
        gmlp_ref[rows, :] = g_mlp
        gbd_ref[...] += jnp.sum(g_mlp.astype(f32), 0, keepdims=True)

    @pl.when(step == 0)
    def _():
        for group in copies[1:]:
            for copy in group:
                copy.wait()

    x, g_mlp = x_ref[...], gmlp_ref[...]
    root = (2.0 / jnp.pi) ** 0.5
    for col in range(0, FF, CHUNK):
        cols = slice(col, col + CHUNK)
        pre = nn(x, up_ref[:, cols]) + bias_ref[:, cols]
        square = pre * pre
        curve = jnp.tanh(root * pre * (1.0 + 0.044715 * square))
        half_up = 0.5 * (1.0 + curve)
        act_ref[:, cols] = (pre * half_up).astype(bf16)
        slope = half_up + (0.5 * root) * pre * (1.0 - curve * curve) * (1.0 + 0.134145 * square)
        g_pre = (nt(g_mlp, down_ref[cols, :]) * slope).astype(bf16)
        gpre_ref[:, cols] = g_pre
        gbu_ref[:, cols] += jnp.sum(g_pre.astype(f32), 0, keepdims=True)


def take(specs, refs):
    pieces = []
    for spec in specs:
        pieces.append(refs[: len(spec)])
        refs = refs[len(spec) :]
    return pieces, refs


def tile_block(width):
    return pl.BlockSpec((TILE, width), lambda step: (step, 0))


def weight_scratch():
    return [
        pltpu.VMEM((D, D), bf16),
        pltpu.VMEM((D, FF), bf16),
        pltpu.VMEM((FF, D), bf16),
        pltpu.SemaphoreType.DMA((3,)),
    ]


def up_call(place_ids, attn_o, hidden, mask, embed, mods, gain, bias, cot, proj, up, down):
    weights = (proj, up, down)
    n = sum(w.count for w in weights)
    specs = tuple(w.spec for w in weights)
    arrays = [a for w in weights for a in w.arrays]
    rows = PROMPT
    return pl.pallas_call(
        partial(up_kernel, specs),
        grid=(rows // TILE,),
        in_specs=[
            SCALAR,
            tile_block(D),
            tile_block(D),
            tile_block(1),
            whole((1, D)),
            whole(mods.shape),
            whole((1, D)),
            whole((1, FF)),
            tile_block(D),
        ]
        + [ANY] * n,
        out_specs=[tile_block(D)] * 3
        + [tile_block(FF)] * 2
        + [tile_block(D), whole((1, FF)), whole((1, D))],
        out_shape=[
            jax.ShapeDtypeStruct((rows, D), f32),
            jax.ShapeDtypeStruct((rows, D), f32),
            jax.ShapeDtypeStruct((rows, D), bf16),
            jax.ShapeDtypeStruct((rows, FF), bf16),
            jax.ShapeDtypeStruct((rows, FF), bf16),
            jax.ShapeDtypeStruct((rows, D), bf16),
            jax.ShapeDtypeStruct((1, FF), f32),
            jax.ShapeDtypeStruct((1, D), f32),
        ],
        scratch_shapes=weight_scratch(),
        compiler_params=pltpu.CompilerParams(vmem_limit_bytes=VMEM_LIMIT),
        cost_estimate=cost("mlp_up"),
        name="mlp_up",
    )(place_ids, attn_o, hidden, mask, embed, mods, gain, bias, cot, *arrays)


def down_kernel(specs, place_ref, act_ref, gpre_ref, mid_ref, ap_ref, cot_ref, mods_ref, gain_ref, bias_ref, *rest):
    pieces, rest = take(specs, rest)
    out_ref, dmid_ref, gatt_ref, go_ref, stat_ref, ggain_ref = rest[:6]
    proj_ref, up_ref, down_ref, sems = rest[6:]
    step = pl.program_id(0)
    targets = (proj_ref, up_ref, down_ref)
    copies = [
        place(part, spec, place_ref, target, sems.at[i])
        for i, (part, spec, target) in enumerate(zip(pieces, specs, targets))
    ]

    @pl.when(step == 0)
    def _():
        for i in (2, 1, 0):
            for copy in copies[i]:
                copy.start()
        ggain_ref[...] = jnp.zeros_like(ggain_ref)
        for copy in copies[2]:
            copy.wait()

    mlp_out = nn(act_ref[...], down_ref[...]) + bias_ref[...]

    @pl.when(step == 0)
    def _():
        for i in (1, 0):
            for copy in copies[i]:
                copy.wait()

    g_n = nt(gpre_ref[...], up_ref[...])
    for sub in range(SUB):
        rows = slice(sub * CLEN, (sub + 1) * CLEN)
        row = pl.ds(step * SUB + sub, 1)
        middle, cot, grad = mid_ref[rows, :], cot_ref[rows, :].astype(f32), g_n[rows]
        gate_attn, gate_mlp = mods_ref[row, 2 * D : 3 * D], mods_ref[row, 5 * D : 6 * D]
        scale = 1.0 + mods_ref[row, 4 * D : 5 * D]
        out_ref[rows, :] = (middle + gate_mlp * mlp_out[rows]).astype(bf16)
        normed, inv_std = layer_norm(middle)
        along = jnp.sum(grad * normed, 0, keepdims=True)
        ggain_ref[...] += along * scale
        d_middle = cot + norm_back(grad * (scale * gain_ref[...]), normed, inv_std)
        dmid_ref[rows, :] = d_middle
        gatt_ref[rows, :] = (gate_attn * d_middle).astype(bf16)
        stat_ref[row, 0:D] = jnp.sum(d_middle * ap_ref[rows, :], 0, keepdims=True)
        stat_ref[row, D : 2 * D] = jnp.sum(grad, 0, keepdims=True)
        stat_ref[row, 2 * D : 3 * D] = along * gain_ref[...]
        stat_ref[row, 3 * D : 4 * D] = jnp.sum(cot * mlp_out[rows], 0, keepdims=True)
    go_ref[...] = nt(gatt_ref[...], proj_ref[...]).astype(bf16)


def down_call(place_ids, act, gpre, middle, attn_proj, cot, mods, gain, bias, proj, up, down):
    weights = (proj, up, down)
    n = sum(w.count for w in weights)
    specs = tuple(w.spec for w in weights)
    arrays = [a for w in weights for a in w.arrays]
    rows = PROMPT
    return pl.pallas_call(
        partial(down_kernel, specs),
        grid=(rows // TILE,),
        in_specs=[
            SCALAR,
            tile_block(FF),
            tile_block(FF),
            tile_block(D),
            tile_block(D),
            tile_block(D),
            whole(mods.shape),
            whole((1, D)),
            whole((1, D)),
        ]
        + [ANY] * n,
        out_specs=[tile_block(D)] * 4 + [whole((CONTS, 4 * D)), whole((1, D))],
        out_shape=[
            jax.ShapeDtypeStruct((rows, D), bf16),
            jax.ShapeDtypeStruct((rows, D), f32),
            jax.ShapeDtypeStruct((rows, D), bf16),
            jax.ShapeDtypeStruct((rows, D), bf16),
            jax.ShapeDtypeStruct((CONTS, 4 * D), f32),
            jax.ShapeDtypeStruct((1, D), f32),
        ],
        scratch_shapes=weight_scratch(),
        compiler_params=pltpu.CompilerParams(vmem_limit_bytes=VMEM_LIMIT),
        cost_estimate=cost("mlp_down"),
        name="mlp_down",
    )(place_ids, act, gpre, middle, attn_proj, cot, mods, gain, bias, *arrays)


def split_store(total, keep_ref, send_ref, core, lead, at):
    for pair in range(total.shape[0] // lead // 2):
        even = total[2 * pair * lead : (2 * pair + 1) * lead].astype(bf16)
        odd = total[(2 * pair + 1) * lead : (2 * pair + 2) * lead].astype(bf16)
        keep_ref[pair, at : at + lead, :] = jnp.where(core == 0, even, odd)
        send_ref[pair, at : at + lead, :] = jnp.where(core == 0, odd, even)


def wgrad_kernel(lead, place_ref, left_ref, right_ref, keep_ref, send_ref):
    split_store(tn(left_ref[...], right_ref[...]), keep_ref, send_ref, place_ref[1], lead, 0)


def wgrad_call(place_ids, left, right, n, name):
    lead = D // n
    blocks = right.shape[1] // D
    out = pl.BlockSpec((n // 2, lead, D), lambda j: (0, j, 0))
    shape = jax.ShapeDtypeStruct((n // 2, blocks * lead, D), bf16)
    return pl.pallas_call(
        partial(wgrad_kernel, lead),
        grid=(blocks,),
        in_specs=[SCALAR, whole((PROMPT, D)), pl.BlockSpec((PROMPT, D), lambda j: (0, j))],
        out_specs=[out, out],
        out_shape=[shape, shape],
        compiler_params=pltpu.CompilerParams(vmem_limit_bytes=VMEM_LIMIT),
        cost_estimate=cost(name),
        name=name,
    )(place_ids, left, right)


def down_grad_kernel(_ids, left_ref, right_ref, keep_ref, send_ref):
    half = pl.num_programs(0) // 2
    total = tn(left_ref[...], right_ref[...]).astype(bf16)

    @pl.when(pl.program_id(0) < half)
    def _():
        send_ref[0] = total

    @pl.when(pl.program_id(0) >= half)
    def _():
        keep_ref[0] = total


def down_grad_call(place_ids, act, g_mlp, n):
    rows = FF // n
    half = n // 2

    def shard(j, ids):
        core = ids[1]
        return 0, jnp.where(j < half, 2 * j + 1 - core, 2 * (j - half) + core)

    shape = jax.ShapeDtypeStruct((half, rows, D), bf16)
    return pl.pallas_call(
        down_grad_kernel,
        grid_spec=pltpu.PrefetchScalarGridSpec(
            num_scalar_prefetch=1,
            grid=(n,),
            in_specs=[pl.BlockSpec((PROMPT, rows), shard), pl.BlockSpec((PROMPT, D), lambda j, ids: (0, 0))],
            out_specs=[
                pl.BlockSpec((1, rows, D), lambda j, ids: (jnp.maximum(j - half, 0), 0, 0)),
                pl.BlockSpec((1, rows, D), lambda j, ids: (jnp.minimum(j, half - 1), 0, 0)),
            ],
        ),
        out_shape=[shape, shape],
        compiler_params=pltpu.CompilerParams(vmem_limit_bytes=VMEM_LIMIT),
        cost_estimate=cost("down_grad"),
        name="down_grad",
    )(place_ids, act, g_mlp)


def down_grad_any(place_ids, act, g_mlp, n):
    if (FF // n) % 128 == 0 and n == 4:
        return down_grad_call(place_ids, act, g_mlp, n)
    full = wide_grad_call(act, g_mlp)
    core = lax.axis_index("shard") % 2
    parts = full.reshape(n // 2, 2, -1, D)
    keep = lax.dynamic_index_in_dim(parts, core, 1, False)
    return keep, lax.dynamic_index_in_dim(parts, 1 - core, 1, False)


def wide_grad_kernel(left_ref, right_ref, out_ref):
    out_ref[...] = tn(left_ref[...], right_ref[...]).astype(bf16)


def wide_grad_call(act, g_mlp):
    return pl.pallas_call(
        wide_grad_kernel,
        grid=(FF // D,),
        in_specs=[pl.BlockSpec((PROMPT, D), lambda j: (0, j)), whole((PROMPT, D))],
        out_specs=pl.BlockSpec((D, D), lambda j: (j, 0)),
        out_shape=jax.ShapeDtypeStruct((FF, D), bf16),
        compiler_params=pltpu.CompilerParams(vmem_limit_bytes=VMEM_LIMIT),
        name="wide_grad",
    )(act, g_mlp)


def qkv_grad_kernel(lead, with_proj, with_ada, place_ref, x_ref, gq_ref, gc_ref, dp_ref, got_ref, cos_ref, sin_ref, *rest):
    keep_ref, send_ref, g_ref = rest[-3:]
    core = place_ref[1]
    g_ref[:, 0:GROUP] = gq_ref[...]
    total_k = dp_ref[0] + got_ref[0].astype(f32)
    total_v = dp_ref[1] + got_ref[1].astype(f32)
    g_ref[0:HALF, GROUP : 2 * GROUP] = rotate(total_k, cos_ref[...], -sin_ref[...]).astype(bf16)
    g_ref[0:HALF, 2 * GROUP : 3 * GROUP] = total_v.astype(bf16)
    g_ref[HALF:PROMPT, GROUP : 2 * GROUP] = gc_ref[0]
    g_ref[HALF:PROMPT, 2 * GROUP : 3 * GROUP] = gc_ref[1]
    split_store(tn(x_ref[...], g_ref[...]), keep_ref, send_ref, core, lead, 0)
    at = lead
    if with_proj:
        split_store(tn(rest[0][...], rest[1][...]), keep_ref, send_ref, core, lead, at)
        at += lead
        rest = rest[2:]
    if with_ada:
        cond = rest[0][...]
        silu = (cond / (1.0 + jnp.exp(-cond))).astype(bf16).astype(f32)
        few = cond.shape[1] * lead // D
        for col in range(4):
            total = exact(silu, rest[1][:, col * D : (col + 1) * D], ((0,), (0,)))
            split_store(total, keep_ref, send_ref, core, few, at)
            at += few


def qkv_grad_call(place_ids, x, gq, gc, dp, got, cosine, sine, n, name, proj, ada):
    lead = D // n
    rows = lead
    extra = []
    if proj is not None:
        extra += list(proj)
        rows += lead
    if ada is not None:
        extra += list(ada)
        rows += 4 * (ada[0].shape[1] // n)
    out = whole((n // 2, rows, D))
    shape = jax.ShapeDtypeStruct((n // 2, rows, D), bf16)
    return pl.pallas_call(
        partial(qkv_grad_kernel, lead, proj is not None, ada is not None),
        grid=(1,),
        in_specs=[
            SCALAR,
            whole((PROMPT, D)),
            whole((PROMPT, GROUP)),
            whole((2, HALF, GROUP)),
            whole((2, HALF, GROUP)),
            whole((2, HALF, GROUP)),
            whole((HALF, 128)),
            whole((HALF, 128)),
        ]
        + [whole(e.shape) for e in extra],
        out_specs=[out, out, whole((PROMPT, D))],
        out_shape=[shape, shape, jax.ShapeDtypeStruct((PROMPT, D), bf16)],
        compiler_params=pltpu.CompilerParams(vmem_limit_bytes=VMEM_LIMIT),
        cost_estimate=cost(name),
        name=name,
    )(place_ids, x, gq, gc, dp, got, cosine, sine, *extra)


def start_kernel(spec, place_ref, hid_ref, mask_ref, embed_ref, mods_ref, gain_ref, dmid_ref, *rest):
    n = len(spec)
    grads, pieces = rest[:N_GROUP], rest[N_GROUP : N_GROUP + n]
    gh_ref, stat_ref, ggain_ref, gmask_ref, w_ref, sem = rest[N_GROUP + n :]
    step = pl.program_id(0)

    @pl.when(step == 0)
    def _():
        copies = place(pieces, spec, place_ref, w_ref, sem)
        for copy in copies:
            copy.start()
        ggain_ref[...] = jnp.zeros_like(ggain_ref)
        gmask_ref[...] = jnp.zeros_like(gmask_ref)
        for copy in copies:
            copy.wait()

    g_n = None
    for group in range(N_GROUP):
        for third in range(3):
            at = third * D + group * GROUP
            term = nt(grads[group][:, third * GROUP : (third + 1) * GROUP], w_ref[:, at : at + GROUP])
            g_n = term if g_n is None else g_n + term
    for sub in range(SUB):
        rows = slice(sub * CLEN, (sub + 1) * CLEN)
        row = pl.ds(step * SUB + sub, 1)
        masked = mask_ref[rows, :] > 0.5
        start = jnp.where(masked, embed_ref[...], hid_ref[rows, :].astype(f32))
        normed, inv_std = layer_norm(start)
        scale = 1.0 + mods_ref[row, D : 2 * D]
        grad = g_n[rows]
        along = jnp.sum(grad * normed, 0, keepdims=True)
        ggain_ref[...] += along * scale
        stat_ref[row, 0:D] = jnp.sum(grad, 0, keepdims=True)
        stat_ref[row, D : 2 * D] = along * gain_ref[...]
        d_start = dmid_ref[rows, :] + norm_back(grad * (scale * gain_ref[...]), normed, inv_std)
        gh_ref[rows, :] = jnp.where(masked, 0.0, d_start)
        gmask_ref[...] += jnp.sum(jnp.where(masked, d_start, 0.0), 0, keepdims=True)


def start_call(place_ids, hidden, mask, embed, mods, gain, d_middle, grads, weight):
    n = weight.count
    rows = PROMPT
    return pl.pallas_call(
        partial(start_kernel, weight.spec),
        grid=(rows // TILE,),
        in_specs=[
            SCALAR,
            tile_block(D),
            tile_block(1),
            whole((1, D)),
            whole(mods.shape),
            whole((1, D)),
            tile_block(D),
        ]
        + [tile_block(D)] * N_GROUP
        + [ANY] * n,
        out_specs=[tile_block(D), whole((CONTS, 2 * D)), whole((1, D)), whole((1, D))],
        out_shape=[
            jax.ShapeDtypeStruct((rows, D), f32),
            jax.ShapeDtypeStruct((CONTS, 2 * D), f32),
            jax.ShapeDtypeStruct((1, D), f32),
            jax.ShapeDtypeStruct((1, D), f32),
        ],
        scratch_shapes=[pltpu.VMEM((D, 3 * D), bf16), pltpu.SemaphoreType.DMA],
        compiler_params=pltpu.CompilerParams(vmem_limit_bytes=VMEM_LIMIT),
        cost_estimate=cost("start_grad"),
        name="start_grad",
    )(place_ids, hidden, mask, embed, mods, gain, d_middle, *grads, *weight.arrays)


def pack_kernel(*refs):
    out_ref = refs[-1]
    out_ref[...] = jnp.zeros_like(out_ref)
    for i, ref in enumerate(refs[:-1]):
        out_ref[i : i + 1, 0 : ref.shape[0]] = ref[...].astype(f32).reshape(1, -1)


def pack_call(vectors):
    shape = (8, max(v.shape[0] for v in vectors))
    return pl.pallas_call(
        pack_kernel,
        grid=(1,),
        in_specs=[whole(v.shape) for v in vectors],
        out_specs=whole(shape),
        out_shape=jax.ShapeDtypeStruct(shape, f32),
        name="pack",
    )(*vectors)


def mods_kernel(spec, lengths, times_ref, place_ref, table_ref, hid_ref, mask_ref, *rest):
    n = len(spec)
    pieces, rest = rest[:n], rest[n:]
    count = len(lengths)
    n_row = len(rest) - count - 7
    rows, rest = rest[:n_row], rest[n_row:]
    mods_ref, cond_ref, ada_ref = rest[:3]
    out_refs = rest[3 : 3 + count - 1]
    x_ref, bias_ref, row_ref, sem, row_sem = rest[3 + count - 1 :]
    gain_ref, embed_ref = out_refs[0], out_refs[4]
    copies = place(pieces, spec, place_ref, ada_ref, sem)
    row_copies = [
        pltpu.make_async_copy(row, row_ref.at[place_ref[0] ^ offset], row_sem) for offset, row in enumerate(rows)
    ]
    for copy in row_copies + copies:
        copy.start()
    for block in range(CONTS):
        cond_ref[pl.ds(block, 1), :] = table_ref[pl.ds(times_ref[block], 1), :]
    cond = cond_ref[...]
    silu = (cond / (1.0 + jnp.exp(-cond))).astype(bf16)
    for copy in row_copies:
        copy.wait()
    for shard in range(n_row):
        for i, (length, ref) in enumerate(zip(lengths, (*out_refs, bias_ref))):
            ref[0:1, shard * length : (shard + 1) * length] = row_ref[shard, i : i + 1, 0:length]
    for copy in copies:
        copy.wait()
    mods_ref[...] = nn(silu, ada_ref[...]) + bias_ref[...]

    @pl.loop(0, CONTS)
    def _(block):
        rows = pl.ds(pl.multiple_of(block * CLEN, CLEN), CLEN)
        start = jnp.where(mask_ref[rows, :] > 0.5, embed_ref[...], hid_ref[rows, :].astype(f32))
        normed, _inv = layer_norm(start)
        row = pl.ds(block, 1)
        shift, scale = mods_ref[row, 0:D], mods_ref[row, D : 2 * D]
        x_ref[rows, :] = (normed * gain_ref[...] * (1.0 + scale) + shift).astype(bf16)


def mods_call(times, place_ids, table, hidden, mask, weight, rows, lengths):
    width = weight.arrays[0].shape[1]
    n = len(rows)
    vectors = [(1, n * length) for length in lengths]
    shapes = [(CONTS, width), (CONTS, table.shape[1])]
    return pl.pallas_call(
        partial(mods_kernel, weight.spec, tuple(lengths)),
        in_specs=[SCALAR, SCALAR, whole(table.shape), whole(hidden.shape), whole(mask.shape)] + [ANY] * (weight.count + n),
        out_specs=[whole(s) for s in shapes] + [whole((table.shape[1], width))] + [whole(v) for v in vectors[:-1]] + [whole((PROMPT, D))],
        out_shape=[jax.ShapeDtypeStruct(s, f32) for s in shapes]
        + [jax.ShapeDtypeStruct((table.shape[1], width), bf16)]
        + [jax.ShapeDtypeStruct(v, f32) for v in vectors[:-1]]
        + [jax.ShapeDtypeStruct((PROMPT, D), bf16)],
        grid=(1,),
        scratch_shapes=[
            pltpu.VMEM(vectors[-1], f32),
            pltpu.VMEM((n,) + rows[0].shape, f32),
            pltpu.SemaphoreType.DMA,
            pltpu.SemaphoreType.DMA,
        ],
        compiler_params=pltpu.CompilerParams(vmem_limit_bytes=VMEM_LIMIT),
        cost_estimate=cost("mods"),
        name="mods",
    )(times, place_ids, table, hidden, mask, *weight.arrays, *rows)


def last_kernel(
    lead, time_rows, place_ref, cond_ref, ada_ref, stat1_ref, stat2_ref, ga_ref, gm_ref, bu_ref, bd_ref, me_ref,
    keep_ref, send_ref, small_ref,
):
    core, pair = place_ref[1], place_ref[2]
    cond = cond_ref[...]
    gate = 1.0 / (1.0 + jnp.exp(-cond))
    silu = (cond * gate).astype(bf16).astype(f32)
    stat1, stat2 = stat1_ref[...], stat2_ref[...]
    ada_late = exact(silu, stat1, ((0,), (0,)))
    ada = ada_ref[...].astype(f32)
    g_silu = exact(stat1, ada[:, : 2 * D], ((1,), (1,))) + exact(stat2, ada[:, 2 * D :], ((1,), (1,)))
    g_cond = g_silu * (gate * (1.0 + cond * (1.0 - gate)))
    small_ref[...] = jnp.zeros_like(small_ref)
    at = time_rows
    small_ref[at : at + 1, :] = ga_ref[...]
    small_ref[at + 1 : at + 2, :] = gm_ref[...]
    for i in range(FF // D):
        small_ref[at + 2 + i : at + 3 + i, :] = bu_ref[:, i * D : (i + 1) * D]
    small_ref[at + 6 : at + 7, :] = bd_ref[...]
    for i in range(2):
        small_ref[at + 7 + i : at + 8 + i, :] = jnp.sum(stat1[:, i * D : (i + 1) * D], 0, keepdims=True)
    for i in range(4):
        small_ref[at + 9 + i : at + 10 + i, :] = jnp.sum(stat2[:, i * D : (i + 1) * D], 0, keepdims=True)
    small_ref[at + 13 : at + 14, :] = me_ref[...]
    half = CONTS // 2
    prompt = jnp.sum(g_cond[:half], 0, keepdims=True)
    values = [prompt] + [g_cond[half + i : half + i + 1] for i in range(half)]
    base = pair * (CONTS + 1)
    where_to = [base] + [base + 1 + core * half + i for i in range(half)]
    for lane in range(D // 128):
        row = lax.broadcasted_iota(jnp.int32, (time_rows, 128), 0) + lane * time_rows
        placed = jnp.zeros((time_rows, 128), f32)
        for index, value in zip(where_to, values):
            placed = placed + jnp.where(row == index, value, 0.0)
        small_ref[0:time_rows, lane * 128 : (lane + 1) * 128] = placed
    small = small_ref[...]
    high = small.astype(bf16)
    rows = small.shape[0]
    low = (small[time_rows:] - high[time_rows:].astype(f32)).astype(bf16)
    for j in range(keep_ref.shape[0]):
        for col in range(2):
            split_store(ada_late[:, col * D : (col + 1) * D], keep_ref, send_ref, core, lead, col * lead)
        row = 2 * lead
        for ref in (keep_ref, send_ref):
            ref[j, row : row + rows, :] = high
            ref[j, row + rows : row + rows + 16, :] = low


def last_call(place_ids, cond, ada, stat1, stat2, vectors, n, time_rows):
    lead = ada.shape[0] // n
    rows = 16 + time_rows
    args = (cond, ada, stat1, stat2) + tuple(vectors)
    out = whole((n // 2, 2 * lead + rows + 16, D))
    shape = jax.ShapeDtypeStruct((n // 2, 2 * lead + rows + 16, D), bf16)
    return pl.pallas_call(
        partial(last_kernel, lead, time_rows),
        grid=(1,),
        in_specs=[SCALAR] + [whole(a.shape) for a in args],
        out_specs=[out, out],
        out_shape=[shape, shape],
        scratch_shapes=[pltpu.VMEM((rows, D), f32)],
        compiler_params=pltpu.CompilerParams(vmem_limit_bytes=VMEM_LIMIT),
        cost_estimate=cost("last"),
        name="last",
    )(place_ids, *args)


def swap(value, axis, mask):
    pairs = [(source, source ^ mask) for source in range(lax.axis_size(axis))]
    return lax.ppermute(value, axis, pairs)


def gather_far(piece):
    pieces = {0: piece}
    mask = lax.axis_size("shard") // 2
    while mask > 1:
        for offset in list(pieces):
            pieces[offset | mask] = swap(pieces[offset], "shard", mask)
        mask //= 2
    return pieces


def gather_near(pieces):
    pieces = dict(pieces)
    for offset in list(pieces):
        pieces[offset | 1] = swap(pieces[offset], "shard", 1)
    return [pieces[offset] for offset in range(len(pieces))]


def sides():
    rep = lax.axis_index("rep")
    return rep % 2, rep % 4


def far_parts(piece, split=1):
    rows = piece.shape[0] // split
    if split == 1 or rows % 16:
        return 1, gather_far(piece)
    side = sides()[0 if split == 2 else 1]
    found = gather_far(lax.dynamic_slice_in_dim(piece, side * rows, rows, 0))
    found[0] = piece
    return split, found


def far_weight(split, found, tie=None):
    if tie is not None:
        found, _ = lax.optimization_barrier((found, tie))
    spec, arrays = [], []
    for offset, part in found.items():
        if split == 1 or not offset:
            spec.append((offset, 1, 0))
            arrays.append(part)
            continue
        spec += [(offset, split, code) for code in range(split)]
        arrays += [part] + [swap(part, "rep", code) for code in range(1, split)]
    return Weight(spec, arrays)


def near_weight(far):
    spec, arrays = list(far.spec), list(far.arrays)
    for (offset, split, code), part in zip(far.spec, far.arrays):
        spec.append((offset | 1, split, code))
        arrays.append(swap(part, "shard", 1))
    if all(part.shape[0] % 16 == 0 for part in arrays):
        return Weight(spec, arrays)
    mine = lax.axis_index("shard")
    rows = arrays[0].shape[0]
    out = jnp.zeros((rows * len(arrays),) + arrays[0].shape[1:], arrays[0].dtype)
    for (offset, _split, _code), part in zip(spec, arrays):
        out = lax.dynamic_update_slice_in_dim(out, part, (mine ^ offset) * rows, 0)
    return Weight([(None, 1, 0)], [out])


def add_plain(left, right):
    return left.astype(f32) + right.astype(f32)


def add_packed(left, right):
    rows = left.shape[-2] - 16
    total = add_plain(left[..., :rows, :], right[..., :rows, :])
    rest = add_plain(left[..., rows:, :], right[..., rows:, :])
    return jnp.concatenate([total[..., : rows - 16, :], total[..., rows - 16 :, :] + rest], -2)


def pack_plain(value):
    return value.astype(bf16)


def pack_packed(value):
    high = value.astype(bf16)
    low = value[..., -16:, :] - high[..., -16:, :].astype(f32)
    return jnp.concatenate([high, low.astype(bf16)], -2)


def reduce_chain(keep, send, steps, add=add_plain, pack=pack_plain):
    mine, rep = lax.axis_index("shard"), lax.axis_index("rep")

    def parts(values, axis, bit):
        kept, sent = [
            pack(add(*(lax.dynamic_index_in_dim(v, b, axis, False) for v in values))) for b in (bit, 1 - bit)
        ]
        return kept, sent

    got = yield send, swap(send, "shard", 1)
    terms = (keep, got)
    mask = 2
    while mask < lax.axis_size("shard"):
        halves = [t.reshape((-1, 2) + t.shape[1:]) for t in terms]
        kept, send = parts(halves, 1, (mine // mask) % 2)
        got = yield send, swap(send, "shard", mask)
        terms = (kept, got)
        mask *= 2
    terms = tuple(t[0] for t in terms)
    joined = None
    more = range(3, lax.axis_size("rep").bit_length() - 1)
    steps = [(bit, "all") for bit in more] + list(steps)
    for at, kind in steps:
        bit = (rep >> at) % 2
        if kind == "split":
            kept, send = parts([t.reshape(2, -1, t.shape[-1]) for t in terms], 0, bit)
            got = yield send, swap(send, "rep", 1 << at)
            terms = (kept, got)
            continue
        value = pack(add(*terms)) if joined is None else joined
        got = yield value, swap(value, "rep", 1 << at)
        if kind == "join":
            last = (value, got, at)
            first, second = jnp.where(bit == 0, value, got), jnp.where(bit == 0, got, value)
            joined = jnp.concatenate([first, second], 0)
        else:
            last = (value, got, None)
            terms, joined = (value, got), None
    return last


class Schedule:
    def __init__(self, ids, rows):
        self.ids = ids
        self.chains = {}
        self.sent = {}
        self.done = {}
        self.final = {}
        self.rows = rows

    def begin(self, name, keep, send, *how):
        chain = reduce_chain(keep, send, *how)
        self.chains[name] = chain
        _sent, self.sent[name] = next(chain)

    def start(self, name, keep, send, names):
        (send,) = self.sync(*(other for other in names if other != name), after=(send,))
        self.begin(name, keep, send, ROUTES[name])
        self.sync(*(other for other in names if other == name), after=(send,))

    def sync(self, *names, after=()):
        for name in names or (None,):
            if name is not None and name not in self.sent:
                continue
            got = self.sent.pop(name, None)
            self.ids, got, after = lax.optimization_barrier((self.ids, got, tuple(after)))
            if got is None:
                continue
            try:
                sent, self.sent[name] = self.chains[name].send(got)
                self.ids, _ = lax.optimization_barrier((self.ids, sent))
            except StopIteration as stop:
                self.done[name] = stop.value
                if name in self.rows:
                    self.final[name] = finish_blocks(stop.value, *self.rows[name])
        return after

    def finish(self, *names):
        for name in names:
            self.sync(name)
        while self.sent:
            self.sync(next(iter(self.sent)))


def add_two(a_ref, b_ref):
    return a_ref[...].astype(f32) + b_ref[...].astype(f32)


def bit_of(place_ref, at):
    return place_ref[4] // (1 << at) % 2


def whole_sum(place_ref, a_ref, b_ref, at):
    if at is None:
        return add_two(a_ref, b_ref)
    first, second = a_ref[...].astype(f32), b_ref[...].astype(f32)
    swapped = bit_of(place_ref, at) == 1
    return jnp.concatenate([jnp.where(swapped, second, first), jnp.where(swapped, first, second)], 0)


def finish_blocks(result, rows, wide):
    value, got, at = result
    if at is None:
        total = value.astype(f32) + got.astype(f32)
    else:
        bit = (lax.axis_index("rep") >> at) % 2
        first, second = jnp.where(bit == 0, value, got), jnp.where(bit == 0, got, value)
        total = jnp.concatenate([first, second], 0).astype(f32)
    if not wide:
        return total
    return jnp.concatenate([total[i : i + rows] for i in range(0, total.shape[0], rows)], 1)


def finish_last_kernel(
    n, lead, time_rows, few, ats, place_ref, ids_ref, a_ref, b_ref, *refs
):
    mine = place_ref[0]
    groups, (qkv_ref, proj_ref, ada_ref, time_ref, *out_refs) = refs[: 2 * N_GROUP], refs[2 * N_GROUP :]
    totals = [whole_sum(place_ref, groups[2 * i], groups[2 * i + 1], at) for i, at in enumerate(ats)]
    for group, total in enumerate(totals):
        for third in range(3):
            col = third * D + group * GROUP
            qkv_ref[:, col : col + GROUP] = total[:lead, third * GROUP : (third + 1) * GROUP]
    proj_ref[...] = totals[1][lead : 2 * lead]
    early = totals[0]
    for i in range(2):
        rows = slice(i * few, (i + 1) * few)
        ada_ref[:, i * D : (i + 1) * D] = add_two(a_ref.at[rows], b_ref.at[rows])
    for i in range(4):
        ada_ref[:, (2 + i) * D : (3 + i) * D] = early[lead + i * few : lead + (i + 1) * few]
    at = 2 * few
    times = add_two(a_ref.at[at : at + time_rows], b_ref.at[at : at + time_rows])
    times = jnp.concatenate([times[:, i * 128 : (i + 1) * 128] for i in range(D // 128)], 0)
    steps = lax.broadcasted_iota(jnp.int32, (STEPS, times.shape[0]), 0)
    hot = jnp.where(steps == ids_ref[...], 1.0, 0.0).astype(f32)
    time_ref[...] = exact(hot, times, ((1,), (0,)))
    at += time_rows
    high = add_two(a_ref.at[at : at + 16], b_ref.at[at : at + 16])
    small = high + add_two(a_ref.at[at + 16 : at + 32], b_ref.at[at + 16 : at + 32])
    first = 0
    for ref, count in zip(out_refs, (1, 1, 4, 1, 6, 1)):
        flat = jnp.concatenate([small[first + i : first + i + 1] for i in range(count)], 1)
        size = count * D // n
        share = flat[:, 0:size]
        for shard in range(1, n):
            share = jnp.where(mine == shard, flat[:, shard * size : (shard + 1) * size], share)
        ref[...] = share.reshape(size)
        first += count


def finish_last(place_ids, ids, last, results, n, time_rows, few):
    lead = D // n
    sizes = [(count * D // n,) for count in (1, 1, 4, 1, 6, 1)]
    shapes = [(lead, 3 * D), (lead, D), (few, 6 * D), (STEPS, 128)] + sizes
    arrays = [ids, *last[:2]] + [a for result in results for a in result[:2]]
    ats = tuple(result[2] for result in results)
    return pl.pallas_call(
        partial(finish_last_kernel, n, lead, time_rows, few, ats),
        grid=(1,),
        in_specs=[SCALAR] + [whole(a.shape) for a in arrays],
        out_specs=[whole(s) for s in shapes],
        out_shape=[jax.ShapeDtypeStruct(s, f32) for s in shapes],
        cost_estimate=cost("finish_last"),
        compiler_params=pltpu.CompilerParams(vmem_limit_bytes=VMEM_LIMIT),
        name="finish_last",
    )(place_ids, *arrays)


ROUTES = {'down': ((0, 'split'), (1, 'all'), (2, 'all'), (0, 'join')),
 'last': ((1, 'all'), (0, 'all'), (2, 'all')),
 'qkv0': ((1, 'split'), (0, 'all'), (2, 'all'), (1, 'join')),
 'qkv1': ((0, 'split'), (1, 'split'), (2, 'all'), (1, 'join'), (0, 'join')),
 'qkv2': ((1, 'split'), (0, 'all'), (2, 'all'), (1, 'join')),
 'up': ((0, 'split'), (1, 'all'), (2, 'all'), (0, 'join'))}
SYNCS = (('up', 'down'),
 ('down',),
 ('up', 'down'),
 (),
 ('up', 'qkv0', 'down'),
 (),
 ('up', 'qkv0', 'qkv1', 'down', 'qkv2'),
 ('qkv0', 'qkv1'),
 ('qkv2',
  'up',
  'qkv0',
  'last',
  'qkv1',
  'qkv2',
  'last',
  'qkv1',
  'up',
  'qkv0',
  'qkv2',
  'last',
  'qkv1',
  'qkv0',
  'last',
  'qkv2',
  'qkv1',
  'qkv1',
  'qkv2',
  'last'),
 ('down',))


def on_device(
    hidden_in,
    mask_ids,
    time_ids,
    time_table,
    w_qkv,
    w_proj,
    w_up,
    w_down,
    w_ada,
    gain_attn,
    gain_mlp,
    bias_up,
    bias_down,
    bias_ada,
    mask_embed,
    cotangent,
):
    n = lax.axis_size("shard")
    mine = lax.axis_index("shard")
    core = mine % 2
    pair = (lax.axis_index("rep") * n + mine) // 2
    ids = jnp.stack([mine, core, pair, *sides()]).astype(jnp.int32)
    barrier = lax.optimization_barrier

    vectors = (gain_attn, gain_mlp, bias_up, bias_down, mask_embed, bias_ada)
    lengths = [v.shape[0] for v in vectors]
    row_far = gather_far(pack_call(vectors))
    local = jnp.arange(PROMPT, dtype=jnp.int32)
    positions = jnp.where(local < HALF, core * HALF + local, PROMPT + local % CLEN).astype(f32)
    freqs = 10000.0 ** (-(2.0 * jnp.arange(HDIM // 2, dtype=f32)) / HDIM)
    lanes = jnp.tile(freqs, 4)
    angles = positions[:, None] * lanes[None, :]
    sign = jnp.where(jnp.arange(128) % HDIM < HDIM // 2, -1.0, 1.0).astype(f32)
    cosine, sine = jnp.cos(angles), jnp.sin(angles) * sign[None, :]
    mask = (mask_ids == 1).astype(f32)[:, None]
    ada_far = far_weight(*far_parts(w_ada), (cosine, sine, mask))
    qkv_far = far_weight(*far_parts(w_qkv, 4))
    ada_weight = near_weight(ada_far)
    rows = gather_near(row_far)
    (proj_own, up_own, down_own), _ = barrier(((w_proj, w_up, w_down), ada_far.arrays))
    up_split, up_found = far_parts(up_own, 4)
    proj_far = far_weight(*far_parts(proj_own))
    down_split, down_found = far_parts(down_own, 2)

    block = jnp.arange(CONTS, dtype=jnp.int32)
    seg = jnp.where(block < CONTS // 2, 0, 1 + core * (CONTS // 2) + block - CONTS // 2)
    my_times = lax.dynamic_slice_in_dim(time_ids, pair, 1, 0)
    times = jnp.sum(jnp.where(seg[:, None] == jnp.arange(CONTS + 1, dtype=jnp.int32)[None], my_times, 0), 1)
    mods, cond, ada_mat, attn_gain, mlp_gain, up_bias, down_bias, embed, x = mods_call(
        times, ids, time_table, hidden_in, mask, ada_weight, rows, lengths
    )

    qkv_weight = near_weight(qkv_far.tied(mods))
    q, kvp, kvc = qkv_call(ids, x, cosine, sine, qkv_weight)
    kvp, up_found = barrier((kvp, up_found))
    kvr = swap(kvp, "shard", 1)
    up_far = far_weight(up_split, up_found)
    early = attn_fwd(0, 4, q, kvp, kvc, kvr)
    early, up_far.arrays, proj_far.arrays, down_found = barrier((early, up_far.arrays, proj_far.arrays, down_found))
    proj_weight = near_weight(proj_far.tied(early))
    up_weight = near_weight(up_far.tied(early))
    early, _ = barrier((early, proj_weight.arrays))
    down_far = far_weight(down_split, down_found)
    attn_o, lse = attn_fwd(4, PAIRS - 4, q, kvp, kvc, kvr, early)
    attn_o, down_far.arrays = barrier((attn_o, down_far.arrays))
    down_weight = near_weight(down_far.tied(attn_o))
    attn_proj, middle, x_mlp, act, g_pre, g_mlp, g_bias_up, g_bias_down = up_call(
        ids, attn_o, hidden_in, mask, embed, mods, mlp_gain, up_bias, cotangent, proj_weight, up_weight, down_weight
    )
    plan = Schedule(ids, {"down": (FF // n // 2, False), "up": (D // n, True)})
    down_keep, down_send = down_grad_any(plan.ids, act, g_mlp, n)
    plan.begin("down", down_keep, down_send, ROUTES["down"])
    plan.sync(after=(down_keep,))
    up_keep, up_send = wgrad_call(plan.ids, x_mlp, g_pre, n, "up_grad")
    plan.start("up", up_keep, up_send, SYNCS[9])
    block_out, d_middle, g_att, g_o, stat2, g_gain_mlp = down_call(
        plan.ids, act, g_pre, middle, attn_proj, cotangent, mods, mlp_gain, down_bias, proj_weight, up_weight, down_weight
    )
    plan.sync(*SYNCS[0], after=(g_o,))
    parts, others = [], []

    def backward(group, names):
        gq, gc, dp, dr = attn_bwd(plan.ids, group, q, kvp, kvc, kvr, g_o, lse, cosine, sine)
        parts.append((gq, gc, dp))
        (dr,) = plan.sync(*names, after=(dr,))
        others.append(swap(dr, "shard", 1))

    grads = []

    def weight(group, proj, ada, names):
        keep, send, total = qkv_grad_call(
            plan.ids, x, *parts[group], others[group], cosine, sine, n, f"qkv_grad{group}", proj, ada
        )
        grads.append(total)
        plan.start(f"qkv{group}", keep, send, names)

    backward(0, SYNCS[1])
    backward(1, SYNCS[2])
    weight(0, None, (cond, stat2), SYNCS[3])
    backward(2, SYNCS[4])
    weight(1, (attn_o, g_att), None, SYNCS[5])
    weight(2, None, None, SYNCS[6])
    grad_hidden, stat1, g_gain_attn, g_mask = start_call(
        plan.ids, hidden_in, mask, embed, mods, attn_gain, d_middle, grads, qkv_weight
    )
    plan.sync(*SYNCS[7], after=(stat1,))
    time_rows = -(-time_ids.size // 6 // 8) * 8
    vector_grads = (g_gain_attn, g_gain_mlp, g_bias_up, g_bias_down, g_mask)
    keep, send = last_call(plan.ids, cond, ada_mat, stat1, stat2, vector_grads, n, time_rows)
    plan.begin("last", keep, send, ROUTES["last"], add_packed, pack_packed)
    plan.finish(*SYNCS[8])

    done = plan.done
    few = w_ada.shape[0]
    flat_ids = time_ids.reshape(1, -1)
    flat_ids = jnp.pad(flat_ids, ((0, 0), (0, 6 * time_rows - flat_ids.shape[1])), constant_values=-1)
    results = [done[f"qkv{g}"] for g in range(N_GROUP)]
    grad_qkv, grad_proj, grad_ada, grad_time, *shares = finish_last(
        plan.ids, flat_ids, done["last"], results, n, time_rows, few
    )
    return (block_out, grad_hidden, grad_time, grad_qkv, grad_proj, plan.final["up"], plan.final["down"], grad_ada, *shares)


def solution(mesh):
    in_specs = (
        P(("rep", "shard"), None),
        P(("rep", "shard")),
        P(),
        P(),
        P("shard", None),
        P("shard", None),
        P("shard", None),
        P("shard", None),
        P("shard", None),
        P("shard"),
        P("shard"),
        P("shard"),
        P("shard"),
        P("shard"),
        P("shard"),
        P(("rep", "shard"), None),
    )
    out_specs = (
        P(("rep", "shard"), None),
        P(("rep", "shard"), None),
        P(),
        P("shard", None),
        P("shard", None),
        P("shard", None),
        P("shard", None),
        P("shard", None),
        P("shard"),
        P("shard"),
        P("shard"),
        P("shard"),
        P("shard"),
        P("shard"),
    )
    return jax.shard_map(
        on_device, mesh=mesh, in_specs=in_specs, out_specs=out_specs, check_vma=False
    )
```

```python
from functools import partial

import jax
import jax.numpy as jnp
from jax import lax
from jax.experimental import pallas as pl
from jax.experimental.pallas import tpu as pltpu
from jax.sharding import PartitionSpec as P

D = 768
HEADS = 12
HDIM = 64
FF = 3072
STEPS = 1000
CLEN = 128
CONTS = 8
PROMPT = 1024
HALF = PROMPT // 2
PAIRS = HEADS // 2
GROUP = 256
N_GROUP = D // GROUP
TILE = 256
SUB = TILE // CLEN
CHUNK = 512
eps_norm = 1e-06
bf16 = jnp.bfloat16
f32 = jnp.float32
VMEM_LIMIT = 62 * 2**20
COSTS = {'attn_bwd0': 52.5,
 'attn_bwd1': 52.8,
 'attn_bwd2': 53.4,
 'attn_fwd0': 55.5,
 'attn_fwd2': 55.8,
 'attn_fwd4': 30.9,
 'combine': 4.8,
 'down_grad': 31.5,
 'finish_down': 8.4,
 'finish_last': 12.6,
 'finish_qkv': 9.0,
 'finish_up': 11.7,
 'last': 14.7,
 'mlp_down': 75.6,
 'mlp_up': 74.4,
 'mods': 19.5,
 'pack': 4.2,
 'qkv': 25.5,
 'qkv_grad0': 25.5,
 'qkv_grad01': 46.5,
 'qkv_grad1': 21.9,
 'qkv_grad12': 39,
 'qkv_grad2': 16.8,
 'start_grad': 35.1,
 'up_grad': 27.6,
 'wide_grad': 27}


def cost(name):
    return pl.CostEstimate(flops=int(COSTS.get(name, 1.0) * 1e9), bytes_accessed=0, transcendentals=0)


def nt(left, right):
    return lax.dot_general(left, right, (((1,), (1,)), ((), ())), preferred_element_type=f32)


def nn(left, right):
    return lax.dot_general(left, right, (((1,), (0,)), ((), ())), preferred_element_type=f32)


def tn(left, right):
    return lax.dot_general(left, right, (((0,), (0,)), ((), ())), preferred_element_type=f32)


def exact(left, right, contract):
    return lax.dot_general(
        left, right, (contract, ((), ())), preferred_element_type=f32, precision=lax.Precision.HIGHEST
    )


def layer_norm(values):
    mean_value = jnp.mean(values, -1, keepdims=True)
    centered = values - mean_value
    inv_std = lax.rsqrt(jnp.mean(centered * centered, -1, keepdims=True) + eps_norm)
    return (centered * inv_std, inv_std)


def norm_back(gradient, normed, inv_std):
    return inv_std * (
        gradient
        - jnp.mean(gradient, -1, keepdims=True)
        - normed * jnp.mean(gradient * normed, -1, keepdims=True)
    )


def rotate(values, cosine, sine):
    lane = lax.broadcasted_iota(jnp.int32, cosine.shape, 1) % HDIM
    out = []
    for col in range(0, values.shape[1], 128):
        part = values[:, col : col + 128]
        other = jnp.where(lane < HDIM // 2, pltpu.roll(part, 96, 1), pltpu.roll(part, 32, 1))
        out.append(part * cosine + other * sine)
    return out[0] if len(out) == 1 else jnp.concatenate(out, 1)


def whole(shape):
    return pl.BlockSpec(shape, lambda *_: (0,) * len(shape))


ANY = pl.BlockSpec(memory_space=pl.ANY)
SCALAR = pl.BlockSpec(memory_space=pltpu.SMEM)


def place(pieces, spec, place_ref, target, sem):
    mine = place_ref[0]
    copies = []
    for (offset, split, part), piece in zip(spec, pieces):
        rows = piece.shape[0]
        if offset is None:
            where = target
        else:
            start = (mine ^ offset) * (split * rows)
            if split > 1:
                start = start + (place_ref[3 if split == 2 else 4] ^ part) * rows
            where = target.at[pl.ds(pl.multiple_of(start, 16), rows)]
        copies.append(pltpu.make_async_copy(piece, where, sem))
    return copies


class Weight:
    def __init__(self, spec, arrays):
        self.spec = tuple(spec)
        self.arrays = list(arrays)
        self.count = len(self.arrays)

    def tied(self, *values):
        arrays, _ = lax.optimization_barrier((self.arrays, values))
        return Weight(self.spec, arrays)


def qkv_kernel(
    spec, place_ref, x_ref, cos_ref, sin_ref, *rest
):
    n = len(spec)
    pieces = rest[:n]
    q_ref, kvp_ref, kvc_ref, w_ref, sem = rest[n:]
    step = pl.program_id(0)

    @pl.when(step == 0)
    def _():
        copies = place(pieces, spec, place_ref, w_ref, sem)
        for copy in copies:
            copy.start()
        for copy in copies:
            copy.wait()

    x = x_ref[...]
    cosine, sine = cos_ref[...], sin_ref[...]

    def part(third):
        return nn(x, w_ref[:, pl.ds(pl.multiple_of(third * D + step * GROUP, 128), GROUP)])

    q_ref[...] = (rotate(part(0), cosine, sine) * HDIM**-0.5).astype(bf16)
    k = rotate(part(1), cosine, sine).astype(bf16)
    kvp_ref[0], kvc_ref[0] = k[:HALF], k[HALF:]
    v = part(2).astype(bf16)
    kvp_ref[1], kvc_ref[1] = v[:HALF], v[HALF:]


def qkv_call(place_ids, x, cosine, sine, weight):
    n = weight.count
    width = weight.arrays[0].shape[1]
    half = pl.BlockSpec((2, HALF, GROUP), lambda g: (0, 0, g))
    return pl.pallas_call(
        partial(qkv_kernel, weight.spec),
        grid=(N_GROUP,),
        in_specs=[
            SCALAR,
            whole((PROMPT, D)),
            whole((PROMPT, 128)),
            whole((PROMPT, 128)),
        ]
        + [ANY] * n,
        out_specs=[pl.BlockSpec((PROMPT, GROUP), lambda g: (0, g)), half, half],
        out_shape=[
            jax.ShapeDtypeStruct((PROMPT, D), bf16),
            jax.ShapeDtypeStruct((2, HALF, D), bf16),
            jax.ShapeDtypeStruct((2, HALF, D), bf16),
        ],
        scratch_shapes=[pltpu.VMEM((D, width), bf16), pltpu.SemaphoreType.DMA],
        compiler_params=pltpu.CompilerParams(vmem_limit_bytes=VMEM_LIMIT),
        cost_estimate=cost("qkv"),
        name="qkv",
    )(place_ids, x, cosine, sine, *weight.arrays)


def head_only(values, head):
    lane = lax.broadcasted_iota(jnp.int32, values.shape, 1)
    return jnp.where((lane < HDIM) if head == 0 else (lane >= HDIM), values, jnp.zeros_like(values))


def key_parts(prompt, other, own, rows, first):
    parts = [nt(prompt, rows), nt(other, rows)]
    if not first:
        cols = range(0, HALF, CLEN)
        parts.append(
            jnp.concatenate([nt(own[c : c + CLEN], rows[c : c + CLEN]) for c in cols], 1)
        )
    return parts


def attn_fwd_kernel(q_ref, kvp_ref, kvc_ref, kvr_ref, o_ref, lse_ref):
    kp, kc, kr = kvp_ref[0], kvc_ref[0], kvr_ref[0]
    vp_t, vc_t, vr_t = kvp_ref[1].T, kvc_ref[1].T, kvr_ref[1].T
    for start in (0, HALF):
        outs = []
        q_tile = q_ref[pl.ds(start, HALF), :]
        for head in range(2):
            lanes = slice(HDIM * head, HDIM * (head + 1))
            scores = key_parts(kp, kr, kc, head_only(q_tile, head), start == 0)
            top = jnp.max(scores[0], 0, keepdims=True)
            for part in scores[1:]:
                top = jnp.maximum(top, jnp.max(part, 0, keepdims=True))
            powers = [jnp.exp(part - top) for part in scores]
            total = jnp.sum(powers[0], 0, keepdims=True)
            for part in powers[1:]:
                total = total + jnp.sum(part, 0, keepdims=True)
            lse_ref[0, pl.ds(head, 1), pl.ds(start, HALF)] = top + jnp.log(total)
            scale = 1.0 / total
            probs = [(part * scale).astype(bf16) for part in powers]
            out = nn(vp_t[lanes], probs[0]) + nn(vr_t[lanes], probs[1])
            if start:
                cols = [slice(c, c + CLEN) for c in range(0, HALF, CLEN)]
                out = out + jnp.concatenate([nn(vc_t[lanes, c], probs[2][:, c]) for c in cols], 1)
            outs.append(out)
        o_ref[pl.ds(start, HALF), :] = jnp.concatenate(outs, 0).T.astype(bf16)


def pair_block(rows, first=0):
    return pl.BlockSpec((rows, 2 * HDIM), lambda pair: (0, first + pair))


def pair_half(first=0):
    return pl.BlockSpec((2, HALF, 2 * HDIM), lambda pair: (0, 0, first + pair))


def lse_block(first=0):
    return pl.BlockSpec((1, 2, PROMPT), lambda pair: (first + pair, 0, 0))


def attn_fwd(first, pairs, q, kvp, kvc, kvr, before=None):
    inputs = (q, kvp, kvc, kvr)
    in_specs = [pair_block(PROMPT, first)] + [pair_half(first)] * 3
    body = attn_fwd_kernel
    aliases = {}
    if before is not None:
        inputs += tuple(before)
        in_specs += [ANY, ANY]
        aliases = {4: 0, 5: 1}

        def body(q_ref, kvp_ref, kvc_ref, kvr_ref, _o, _lse, o_ref, lse_ref):
            attn_fwd_kernel(q_ref, kvp_ref, kvc_ref, kvr_ref, o_ref, lse_ref)

    return pl.pallas_call(
        body,
        grid=(pairs,),
        in_specs=in_specs,
        out_specs=[pair_block(PROMPT, first), lse_block(first)],
        out_shape=[
            jax.ShapeDtypeStruct((PROMPT, D), bf16),
            jax.ShapeDtypeStruct((PAIRS, 2, PROMPT), f32),
        ],
        input_output_aliases=aliases,
        compiler_params=pltpu.CompilerParams(vmem_limit_bytes=VMEM_LIMIT),
        cost_estimate=cost(f"attn_fwd{first}"),
        name=f"attn_fwd{first}",
    )(*inputs)


def attn_bwd_kernel(
    _ids, q_ref, kvp_ref, kvc_ref, kvr_ref, g_ref, lse_ref, cos_ref, sin_ref, gq_ref, gc_ref, dp_ref, dr_ref
):
    kp, kc, kr = kvp_ref[0], kvc_ref[0], kvr_ref[0]
    vp, vc, vr = kvp_ref[1], kvc_ref[1], kvr_ref[1]
    kp_t, kc_t, kr_t = kp.T, kc.T, kr.T
    first = lax.broadcasted_iota(jnp.int32, (HALF, 2 * HDIM), 1) < HDIM
    for start in (0, HALF):
        tile = pl.ds(start, HALF)
        q_tile, g_tile = q_ref[tile, :], g_ref[tile, :]
        cols = [slice(c, c + CLEN) for c in range(0, HALF, CLEN)]
        dqs, dks, dvs = [], [], []
        for head in range(2):
            lanes = slice(HDIM * head, HDIM * (head + 1))
            scores = key_parts(kp, kr, kc, head_only(q_tile, head), start == 0)
            dps = key_parts(vp, vr, vc, head_only(g_tile, head), start == 0)
            lse = lse_ref[0, pl.ds(head, 1), tile]
            probs = [jnp.exp(part - lse) for part in scores]
            row_dot = jnp.sum(probs[0] * dps[0], 0, keepdims=True)
            for p_part, d_part in zip(probs[1:], dps[1:]):
                row_dot = row_dot + jnp.sum(p_part * d_part, 0, keepdims=True)
            ds = [(p * (d - row_dot)).astype(bf16) for p, d in zip(probs, dps)]
            probs = [p.astype(bf16) for p in probs]
            dq = nn(kp_t[lanes], ds[0]) + nn(kr_t[lanes], ds[1])
            dk = [nn(ds[0], q_tile), nn(ds[1], q_tile)]
            dv = [nn(probs[0], g_tile), nn(probs[1], g_tile)]
            if start:
                dq = dq + jnp.concatenate([nn(kc_t[lanes, c], ds[2][:, c]) for c in cols], 1)
                dk.append(jnp.concatenate([nn(ds[2][:, c], q_tile[c]) for c in cols], 0))
                dv.append(jnp.concatenate([nn(probs[2][:, c], g_tile[c]) for c in cols], 0))
            dqs.append(dq)
            dks.append(dk)
            dvs.append(dv)
        cosine, sine = cos_ref[tile, :], sin_ref[tile, :]
        dq = jnp.concatenate(dqs, 0).T * HDIM**-0.5
        gq_ref[tile, :] = rotate(dq, cosine, -sine).astype(bf16)
        for which, parts in enumerate((dks, dvs)):
            merged = [jnp.where(first, a, b) for a, b in zip(*parts)]
            if start:
                dp_ref[which] += merged[0]
                dr_ref[which] += merged[1]
                last = merged[2] if which else rotate(merged[2], cosine, -sine)
                gc_ref[which] = last.astype(bf16)
            else:
                dp_ref[which] = merged[0]
                dr_ref[which] = merged[1]


def attn_bwd(ids, group, q, kvp, kvc, kvr, g, lse, cosine, sine):
    pairs = GROUP // (2 * HDIM)
    first = group * pairs
    return pl.pallas_call(
        attn_bwd_kernel,
        grid=(pairs,),
        in_specs=[SCALAR, pair_block(PROMPT, first)]
        + [pair_half(first)] * 3
        + [pair_block(PROMPT, first), lse_block(first), whole((PROMPT, 128)), whole((PROMPT, 128))],
        out_specs=[pair_block(PROMPT), pair_half(), pair_half(), pair_half()],
        out_shape=[
            jax.ShapeDtypeStruct((PROMPT, GROUP), bf16),
            jax.ShapeDtypeStruct((2, HALF, GROUP), bf16),
            jax.ShapeDtypeStruct((2, HALF, GROUP), f32),
            jax.ShapeDtypeStruct((2, HALF, GROUP), f32),
        ],
        compiler_params=pltpu.CompilerParams(vmem_limit_bytes=VMEM_LIMIT),
        cost_estimate=cost(f"attn_bwd{group}"),
        name=f"attn_bwd{group}",
    )(ids, q, kvp, kvc, kvr, g, lse, cosine, sine)


def up_kernel(
    specs,
    place_ref,
    o_ref,
    hid_ref,
    mask_ref,
    embed_ref,
    mods_ref,
    gain_ref,
    bias_ref,
    cot_ref,
    *rest,
):
    pieces, rest = take(specs, rest)
    ap_ref, mid_ref, x_ref, act_ref, gpre_ref, gmlp_ref, gbu_ref, gbd_ref = rest[:8]
    proj_ref, up_ref, down_ref, sems = rest[8:]
    step = pl.program_id(0)
    targets = (proj_ref, up_ref, down_ref)
    copies = [
        place(part, spec, place_ref, target, sems.at[i])
        for i, (part, spec, target) in enumerate(zip(pieces, specs, targets))
    ]

    @pl.when(step == 0)
    def _():
        for group in copies:
            for copy in group:
                copy.start()
        gbu_ref[...] = jnp.zeros_like(gbu_ref)
        gbd_ref[...] = jnp.zeros_like(gbd_ref)
        for copy in copies[0]:
            copy.wait()

    attn_proj = nn(o_ref[...], proj_ref[...])
    ap_ref[...] = attn_proj
    for sub in range(SUB):
        rows = slice(sub * CLEN, (sub + 1) * CLEN)
        row = pl.ds(step * SUB + sub, 1)
        start = jnp.where(mask_ref[rows, :] > 0.5, embed_ref[...], hid_ref[rows, :].astype(f32))
        middle = start + mods_ref[row, 2 * D : 3 * D] * attn_proj[rows]
        mid_ref[rows, :] = middle
        normed, _inv = layer_norm(middle)
        shift, scale = mods_ref[row, 3 * D : 4 * D], mods_ref[row, 4 * D : 5 * D]
        x_ref[rows, :] = (normed * gain_ref[...] * (1.0 + scale) + shift).astype(bf16)
        g_mlp = (mods_ref[row, 5 * D : 6 * D] * cot_ref[rows, :].astype(f32)).astype(bf16)
        gmlp_ref[rows, :] = g_mlp
        gbd_ref[...] += jnp.sum(g_mlp.astype(f32), 0, keepdims=True)

    @pl.when(step == 0)
    def _():
        for group in copies[1:]:
            for copy in group:
                copy.wait()

    x, g_mlp = x_ref[...], gmlp_ref[...]
    root = (2.0 / jnp.pi) ** 0.5
    for col in range(0, FF, CHUNK):
        cols = slice(col, col + CHUNK)
        pre = nn(x, up_ref[:, cols]) + bias_ref[:, cols]
        square = pre * pre
        curve = jnp.tanh(root * pre * (1.0 + 0.044715 * square))
        half_up = 0.5 * (1.0 + curve)
        act_ref[:, cols] = (pre * half_up).astype(bf16)
        slope = half_up + (0.5 * root) * pre * (1.0 - curve * curve) * (1.0 + 0.134145 * square)
        g_pre = (nt(g_mlp, down_ref[cols, :]) * slope).astype(bf16)
        gpre_ref[:, cols] = g_pre
        gbu_ref[:, cols] += jnp.sum(g_pre.astype(f32), 0, keepdims=True)


def take(specs, refs):
    pieces = []
    for spec in specs:
        pieces.append(refs[: len(spec)])
        refs = refs[len(spec) :]
    return pieces, refs


def tile_block(width):
    return pl.BlockSpec((TILE, width), lambda step: (step, 0))


def weight_scratch():
    return [
        pltpu.VMEM((D, D), bf16),
        pltpu.VMEM((D, FF), bf16),
        pltpu.VMEM((FF, D), bf16),
        pltpu.SemaphoreType.DMA((3,)),
    ]


def up_call(place_ids, attn_o, hidden, mask, embed, mods, gain, bias, cot, proj, up, down):
    weights = (proj, up, down)
    n = sum(w.count for w in weights)
    specs = tuple(w.spec for w in weights)
    arrays = [a for w in weights for a in w.arrays]
    rows = PROMPT
    return pl.pallas_call(
        partial(up_kernel, specs),
        grid=(rows // TILE,),
        in_specs=[
            SCALAR,
            tile_block(D),
            tile_block(D),
            tile_block(1),
            whole((1, D)),
            whole(mods.shape),
            whole((1, D)),
            whole((1, FF)),
            tile_block(D),
        ]
        + [ANY] * n,
        out_specs=[tile_block(D)] * 3
        + [tile_block(FF)] * 2
        + [tile_block(D), whole((1, FF)), whole((1, D))],
        out_shape=[
            jax.ShapeDtypeStruct((rows, D), f32),
            jax.ShapeDtypeStruct((rows, D), f32),
            jax.ShapeDtypeStruct((rows, D), bf16),
            jax.ShapeDtypeStruct((rows, FF), bf16),
            jax.ShapeDtypeStruct((rows, FF), bf16),
            jax.ShapeDtypeStruct((rows, D), bf16),
            jax.ShapeDtypeStruct((1, FF), f32),
            jax.ShapeDtypeStruct((1, D), f32),
        ],
        scratch_shapes=weight_scratch(),
        compiler_params=pltpu.CompilerParams(vmem_limit_bytes=VMEM_LIMIT),
        cost_estimate=cost("mlp_up"),
        name="mlp_up",
    )(place_ids, attn_o, hidden, mask, embed, mods, gain, bias, cot, *arrays)


def down_kernel(specs, place_ref, act_ref, gpre_ref, mid_ref, ap_ref, cot_ref, mods_ref, gain_ref, bias_ref, *rest):
    pieces, rest = take(specs, rest)
    out_ref, dmid_ref, gatt_ref, go_ref, stat_ref, ggain_ref = rest[:6]
    proj_ref, up_ref, down_ref, sems = rest[6:]
    step = pl.program_id(0)
    targets = (proj_ref, up_ref, down_ref)
    copies = [
        place(part, spec, place_ref, target, sems.at[i])
        for i, (part, spec, target) in enumerate(zip(pieces, specs, targets))
    ]

    @pl.when(step == 0)
    def _():
        for i in (2, 1, 0):
            for copy in copies[i]:
                copy.start()
        ggain_ref[...] = jnp.zeros_like(ggain_ref)
        for copy in copies[2]:
            copy.wait()

    mlp_out = nn(act_ref[...], down_ref[...]) + bias_ref[...]

    @pl.when(step == 0)
    def _():
        for i in (1, 0):
            for copy in copies[i]:
                copy.wait()

    g_n = nt(gpre_ref[...], up_ref[...])
    for sub in range(SUB):
        rows = slice(sub * CLEN, (sub + 1) * CLEN)
        row = pl.ds(step * SUB + sub, 1)
        middle, cot, grad = mid_ref[rows, :], cot_ref[rows, :].astype(f32), g_n[rows]
        gate_attn, gate_mlp = mods_ref[row, 2 * D : 3 * D], mods_ref[row, 5 * D : 6 * D]
        scale = 1.0 + mods_ref[row, 4 * D : 5 * D]
        out_ref[rows, :] = (middle + gate_mlp * mlp_out[rows]).astype(bf16)
        normed, inv_std = layer_norm(middle)
        along = jnp.sum(grad * normed, 0, keepdims=True)
        ggain_ref[...] += along * scale
        d_middle = cot + norm_back(grad * (scale * gain_ref[...]), normed, inv_std)
        dmid_ref[rows, :] = d_middle
        gatt_ref[rows, :] = (gate_attn * d_middle).astype(bf16)
        stat_ref[row, 0:D] = jnp.sum(d_middle * ap_ref[rows, :], 0, keepdims=True)
        stat_ref[row, D : 2 * D] = jnp.sum(grad, 0, keepdims=True)
        stat_ref[row, 2 * D : 3 * D] = along * gain_ref[...]
        stat_ref[row, 3 * D : 4 * D] = jnp.sum(cot * mlp_out[rows], 0, keepdims=True)
    go_ref[...] = nt(gatt_ref[...], proj_ref[...]).astype(bf16)


def down_call(place_ids, act, gpre, middle, attn_proj, cot, mods, gain, bias, proj, up, down):
    weights = (proj, up, down)
    n = sum(w.count for w in weights)
    specs = tuple(w.spec for w in weights)
    arrays = [a for w in weights for a in w.arrays]
    rows = PROMPT
    return pl.pallas_call(
        partial(down_kernel, specs),
        grid=(rows // TILE,),
        in_specs=[
            SCALAR,
            tile_block(FF),
            tile_block(FF),
            tile_block(D),
            tile_block(D),
            tile_block(D),
            whole(mods.shape),
            whole((1, D)),
            whole((1, D)),
        ]
        + [ANY] * n,
        out_specs=[tile_block(D)] * 4 + [whole((CONTS, 4 * D)), whole((1, D))],
        out_shape=[
            jax.ShapeDtypeStruct((rows, D), bf16),
            jax.ShapeDtypeStruct((rows, D), f32),
            jax.ShapeDtypeStruct((rows, D), bf16),
            jax.ShapeDtypeStruct((rows, D), bf16),
            jax.ShapeDtypeStruct((CONTS, 4 * D), f32),
            jax.ShapeDtypeStruct((1, D), f32),
        ],
        scratch_shapes=weight_scratch(),
        compiler_params=pltpu.CompilerParams(vmem_limit_bytes=VMEM_LIMIT),
        cost_estimate=cost("mlp_down"),
        name="mlp_down",
    )(place_ids, act, gpre, middle, attn_proj, cot, mods, gain, bias, *arrays)


def split_store(total, keep_ref, send_ref, core, lead, at):
    for pair in range(total.shape[0] // lead // 2):
        even = total[2 * pair * lead : (2 * pair + 1) * lead].astype(bf16)
        odd = total[(2 * pair + 1) * lead : (2 * pair + 2) * lead].astype(bf16)
        keep_ref[pair, at : at + lead, :] = jnp.where(core == 0, even, odd)
        send_ref[pair, at : at + lead, :] = jnp.where(core == 0, odd, even)


def wgrad_kernel(lead, place_ref, left_ref, right_ref, keep_ref, send_ref):
    split_store(tn(left_ref[...], right_ref[...]), keep_ref, send_ref, place_ref[1], lead, 0)


def wgrad_call(place_ids, left, right, n, name):
    lead = D // n
    blocks = right.shape[1] // D
    out = pl.BlockSpec((n // 2, lead, D), lambda j: (0, j, 0))
    shape = jax.ShapeDtypeStruct((n // 2, blocks * lead, D), bf16)
    return pl.pallas_call(
        partial(wgrad_kernel, lead),
        grid=(blocks,),
        in_specs=[SCALAR, whole((PROMPT, D)), pl.BlockSpec((PROMPT, D), lambda j: (0, j))],
        out_specs=[out, out],
        out_shape=[shape, shape],
        compiler_params=pltpu.CompilerParams(vmem_limit_bytes=VMEM_LIMIT),
        cost_estimate=cost(name),
        name=name,
    )(place_ids, left, right)


def down_grad_kernel(_ids, left_ref, right_ref, keep_ref, send_ref):
    half = pl.num_programs(0) // 2
    total = tn(left_ref[...], right_ref[...]).astype(bf16)

    @pl.when(pl.program_id(0) < half)
    def _():
        send_ref[0] = total

    @pl.when(pl.program_id(0) >= half)
    def _():
        keep_ref[0] = total


def down_grad_call(place_ids, act, g_mlp, n):
    rows = FF // n
    half = n // 2

    def shard(j, ids):
        core = ids[1]
        return 0, jnp.where(j < half, 2 * j + 1 - core, 2 * (j - half) + core)

    shape = jax.ShapeDtypeStruct((half, rows, D), bf16)
    return pl.pallas_call(
        down_grad_kernel,
        grid_spec=pltpu.PrefetchScalarGridSpec(
            num_scalar_prefetch=1,
            grid=(n,),
            in_specs=[pl.BlockSpec((PROMPT, rows), shard), pl.BlockSpec((PROMPT, D), lambda j, ids: (0, 0))],
            out_specs=[
                pl.BlockSpec((1, rows, D), lambda j, ids: (jnp.maximum(j - half, 0), 0, 0)),
                pl.BlockSpec((1, rows, D), lambda j, ids: (jnp.minimum(j, half - 1), 0, 0)),
            ],
        ),
        out_shape=[shape, shape],
        compiler_params=pltpu.CompilerParams(vmem_limit_bytes=VMEM_LIMIT),
        cost_estimate=cost("down_grad"),
        name="down_grad",
    )(place_ids, act, g_mlp)


def down_grad_any(place_ids, act, g_mlp, n):
    if (FF // n) % 128 == 0 and n == 4:
        return down_grad_call(place_ids, act, g_mlp, n)
    full = wide_grad_call(act, g_mlp)
    core = lax.axis_index("shard") % 2
    parts = full.reshape(n // 2, 2, -1, D)
    keep = lax.dynamic_index_in_dim(parts, core, 1, False)
    return keep, lax.dynamic_index_in_dim(parts, 1 - core, 1, False)


def wide_grad_kernel(left_ref, right_ref, out_ref):
    out_ref[...] = tn(left_ref[...], right_ref[...]).astype(bf16)


def wide_grad_call(act, g_mlp):
    return pl.pallas_call(
        wide_grad_kernel,
        grid=(FF // D,),
        in_specs=[pl.BlockSpec((PROMPT, D), lambda j: (0, j)), whole((PROMPT, D))],
        out_specs=pl.BlockSpec((D, D), lambda j: (j, 0)),
        out_shape=jax.ShapeDtypeStruct((FF, D), bf16),
        compiler_params=pltpu.CompilerParams(vmem_limit_bytes=VMEM_LIMIT),
        name="wide_grad",
    )(act, g_mlp)


def qkv_grad_kernel(lead, with_proj, with_ada, place_ref, x_ref, gq_ref, gc_ref, dp_ref, got_ref, cos_ref, sin_ref, *rest):
    keep_ref, send_ref, g_ref = rest[-3:]
    core = place_ref[1]
    g_ref[:, 0:GROUP] = gq_ref[...]
    total_k = dp_ref[0] + got_ref[0].astype(f32)
    total_v = dp_ref[1] + got_ref[1].astype(f32)
    g_ref[0:HALF, GROUP : 2 * GROUP] = rotate(total_k, cos_ref[...], -sin_ref[...]).astype(bf16)
    g_ref[0:HALF, 2 * GROUP : 3 * GROUP] = total_v.astype(bf16)
    g_ref[HALF:PROMPT, GROUP : 2 * GROUP] = gc_ref[0]
    g_ref[HALF:PROMPT, 2 * GROUP : 3 * GROUP] = gc_ref[1]
    split_store(tn(x_ref[...], g_ref[...]), keep_ref, send_ref, core, lead, 0)
    at = lead
    if with_proj:
        split_store(tn(rest[0][...], rest[1][...]), keep_ref, send_ref, core, lead, at)
        at += lead
        rest = rest[2:]
    if with_ada:
        cond = rest[0][...]
        silu = (cond / (1.0 + jnp.exp(-cond))).astype(bf16).astype(f32)
        few = cond.shape[1] * lead // D
        for col in range(4):
            total = exact(silu, rest[1][:, col * D : (col + 1) * D], ((0,), (0,)))
            split_store(total, keep_ref, send_ref, core, few, at)
            at += few


def qkv_grad_call(place_ids, x, gq, gc, dp, got, cosine, sine, n, name, proj, ada):
    lead = D // n
    rows = lead
    extra = []
    if proj is not None:
        extra += list(proj)
        rows += lead
    if ada is not None:
        extra += list(ada)
        rows += 4 * (ada[0].shape[1] // n)
    out = whole((n // 2, rows, D))
    shape = jax.ShapeDtypeStruct((n // 2, rows, D), bf16)
    return pl.pallas_call(
        partial(qkv_grad_kernel, lead, proj is not None, ada is not None),
        grid=(1,),
        in_specs=[
            SCALAR,
            whole((PROMPT, D)),
            whole((PROMPT, GROUP)),
            whole((2, HALF, GROUP)),
            whole((2, HALF, GROUP)),
            whole((2, HALF, GROUP)),
            whole((HALF, 128)),
            whole((HALF, 128)),
        ]
        + [whole(e.shape) for e in extra],
        out_specs=[out, out, whole((PROMPT, D))],
        out_shape=[shape, shape, jax.ShapeDtypeStruct((PROMPT, D), bf16)],
        compiler_params=pltpu.CompilerParams(vmem_limit_bytes=VMEM_LIMIT),
        cost_estimate=cost(name),
        name=name,
    )(place_ids, x, gq, gc, dp, got, cosine, sine, *extra)


def start_kernel(spec, place_ref, hid_ref, mask_ref, embed_ref, mods_ref, gain_ref, dmid_ref, *rest):
    n = len(spec)
    grads, pieces = rest[:N_GROUP], rest[N_GROUP : N_GROUP + n]
    gh_ref, stat_ref, ggain_ref, gmask_ref, w_ref, sem = rest[N_GROUP + n :]
    step = pl.program_id(0)

    @pl.when(step == 0)
    def _():
        copies = place(pieces, spec, place_ref, w_ref, sem)
        for copy in copies:
            copy.start()
        ggain_ref[...] = jnp.zeros_like(ggain_ref)
        gmask_ref[...] = jnp.zeros_like(gmask_ref)
        for copy in copies:
            copy.wait()

    g_n = None
    for group in range(N_GROUP):
        for third in range(3):
            at = third * D + group * GROUP
            term = nt(grads[group][:, third * GROUP : (third + 1) * GROUP], w_ref[:, at : at + GROUP])
            g_n = term if g_n is None else g_n + term
    for sub in range(SUB):
        rows = slice(sub * CLEN, (sub + 1) * CLEN)
        row = pl.ds(step * SUB + sub, 1)
        masked = mask_ref[rows, :] > 0.5
        start = jnp.where(masked, embed_ref[...], hid_ref[rows, :].astype(f32))
        normed, inv_std = layer_norm(start)
        scale = 1.0 + mods_ref[row, D : 2 * D]
        grad = g_n[rows]
        along = jnp.sum(grad * normed, 0, keepdims=True)
        ggain_ref[...] += along * scale
        stat_ref[row, 0:D] = jnp.sum(grad, 0, keepdims=True)
        stat_ref[row, D : 2 * D] = along * gain_ref[...]
        d_start = dmid_ref[rows, :] + norm_back(grad * (scale * gain_ref[...]), normed, inv_std)
        gh_ref[rows, :] = jnp.where(masked, 0.0, d_start)
        gmask_ref[...] += jnp.sum(jnp.where(masked, d_start, 0.0), 0, keepdims=True)


def start_call(place_ids, hidden, mask, embed, mods, gain, d_middle, grads, weight):
    n = weight.count
    rows = PROMPT
    return pl.pallas_call(
        partial(start_kernel, weight.spec),
        grid=(rows // TILE,),
        in_specs=[
            SCALAR,
            tile_block(D),
            tile_block(1),
            whole((1, D)),
            whole(mods.shape),
            whole((1, D)),
            tile_block(D),
        ]
        + [tile_block(D)] * N_GROUP
        + [ANY] * n,
        out_specs=[tile_block(D), whole((CONTS, 2 * D)), whole((1, D)), whole((1, D))],
        out_shape=[
            jax.ShapeDtypeStruct((rows, D), f32),
            jax.ShapeDtypeStruct((CONTS, 2 * D), f32),
            jax.ShapeDtypeStruct((1, D), f32),
            jax.ShapeDtypeStruct((1, D), f32),
        ],
        scratch_shapes=[pltpu.VMEM((D, 3 * D), bf16), pltpu.SemaphoreType.DMA],
        compiler_params=pltpu.CompilerParams(vmem_limit_bytes=VMEM_LIMIT),
        cost_estimate=cost("start_grad"),
        name="start_grad",
    )(place_ids, hidden, mask, embed, mods, gain, d_middle, *grads, *weight.arrays)


def pack_kernel(*refs):
    out_ref = refs[-1]
    out_ref[...] = jnp.zeros_like(out_ref)
    for i, ref in enumerate(refs[:-1]):
        out_ref[i : i + 1, 0 : ref.shape[0]] = ref[...].astype(f32).reshape(1, -1)


def pack_call(vectors):
    shape = (8, max(v.shape[0] for v in vectors))
    return pl.pallas_call(
        pack_kernel,
        grid=(1,),
        in_specs=[whole(v.shape) for v in vectors],
        out_specs=whole(shape),
        out_shape=jax.ShapeDtypeStruct(shape, f32),
        name="pack",
    )(*vectors)


def mods_kernel(spec, lengths, times_ref, place_ref, table_ref, hid_ref, mask_ref, *rest):
    n = len(spec)
    pieces, rest = rest[:n], rest[n:]
    count = len(lengths)
    n_row = len(rest) - count - 7
    rows, rest = rest[:n_row], rest[n_row:]
    mods_ref, cond_ref, ada_ref = rest[:3]
    out_refs = rest[3 : 3 + count - 1]
    x_ref, bias_ref, row_ref, sem, row_sem = rest[3 + count - 1 :]
    gain_ref, embed_ref = out_refs[0], out_refs[4]
    copies = place(pieces, spec, place_ref, ada_ref, sem)
    row_copies = [
        pltpu.make_async_copy(row, row_ref.at[place_ref[0] ^ offset], row_sem) for offset, row in enumerate(rows)
    ]
    for copy in row_copies + copies:
        copy.start()
    for block in range(CONTS):
        cond_ref[pl.ds(block, 1), :] = table_ref[pl.ds(times_ref[block], 1), :]
    cond = cond_ref[...]
    silu = (cond / (1.0 + jnp.exp(-cond))).astype(bf16)
    for copy in row_copies:
        copy.wait()
    for shard in range(n_row):
        for i, (length, ref) in enumerate(zip(lengths, (*out_refs, bias_ref))):
            ref[0:1, shard * length : (shard + 1) * length] = row_ref[shard, i : i + 1, 0:length]
    for copy in copies:
        copy.wait()
    mods_ref[...] = nn(silu, ada_ref[...]) + bias_ref[...]

    @pl.loop(0, CONTS)
    def _(block):
        rows = pl.ds(pl.multiple_of(block * CLEN, CLEN), CLEN)
        start = jnp.where(mask_ref[rows, :] > 0.5, embed_ref[...], hid_ref[rows, :].astype(f32))
        normed, _inv = layer_norm(start)
        row = pl.ds(block, 1)
        shift, scale = mods_ref[row, 0:D], mods_ref[row, D : 2 * D]
        x_ref[rows, :] = (normed * gain_ref[...] * (1.0 + scale) + shift).astype(bf16)


def mods_call(times, place_ids, table, hidden, mask, weight, rows, lengths):
    width = weight.arrays[0].shape[1]
    n = len(rows)
    vectors = [(1, n * length) for length in lengths]
    shapes = [(CONTS, width), (CONTS, table.shape[1])]
    return pl.pallas_call(
        partial(mods_kernel, weight.spec, tuple(lengths)),
        in_specs=[SCALAR, SCALAR, whole(table.shape), whole(hidden.shape), whole(mask.shape)] + [ANY] * (weight.count + n),
        out_specs=[whole(s) for s in shapes] + [whole((table.shape[1], width))] + [whole(v) for v in vectors[:-1]] + [whole((PROMPT, D))],
        out_shape=[jax.ShapeDtypeStruct(s, f32) for s in shapes]
        + [jax.ShapeDtypeStruct((table.shape[1], width), bf16)]
        + [jax.ShapeDtypeStruct(v, f32) for v in vectors[:-1]]
        + [jax.ShapeDtypeStruct((PROMPT, D), bf16)],
        grid=(1,),
        scratch_shapes=[
            pltpu.VMEM(vectors[-1], f32),
            pltpu.VMEM((n,) + rows[0].shape, f32),
            pltpu.SemaphoreType.DMA,
            pltpu.SemaphoreType.DMA,
        ],
        compiler_params=pltpu.CompilerParams(vmem_limit_bytes=VMEM_LIMIT),
        cost_estimate=cost("mods"),
        name="mods",
    )(times, place_ids, table, hidden, mask, *weight.arrays, *rows)


def last_kernel(
    lead, time_rows, place_ref, cond_ref, ada_ref, stat1_ref, stat2_ref, ga_ref, gm_ref, bu_ref, bd_ref, me_ref,
    keep_ref, send_ref, small_ref,
):
    core, pair = place_ref[1], place_ref[2]
    cond = cond_ref[...]
    gate = 1.0 / (1.0 + jnp.exp(-cond))
    silu = (cond * gate).astype(bf16).astype(f32)
    stat1, stat2 = stat1_ref[...], stat2_ref[...]
    ada_late = exact(silu, stat1, ((0,), (0,)))
    ada = ada_ref[...].astype(f32)
    g_silu = exact(stat1, ada[:, : 2 * D], ((1,), (1,))) + exact(stat2, ada[:, 2 * D :], ((1,), (1,)))
    g_cond = g_silu * (gate * (1.0 + cond * (1.0 - gate)))
    small_ref[...] = jnp.zeros_like(small_ref)
    at = time_rows
    small_ref[at : at + 1, :] = ga_ref[...]
    small_ref[at + 1 : at + 2, :] = gm_ref[...]
    for i in range(FF // D):
        small_ref[at + 2 + i : at + 3 + i, :] = bu_ref[:, i * D : (i + 1) * D]
    small_ref[at + 6 : at + 7, :] = bd_ref[...]
    for i in range(2):
        small_ref[at + 7 + i : at + 8 + i, :] = jnp.sum(stat1[:, i * D : (i + 1) * D], 0, keepdims=True)
    for i in range(4):
        small_ref[at + 9 + i : at + 10 + i, :] = jnp.sum(stat2[:, i * D : (i + 1) * D], 0, keepdims=True)
    small_ref[at + 13 : at + 14, :] = me_ref[...]
    half = CONTS // 2
    prompt = jnp.sum(g_cond[:half], 0, keepdims=True)
    values = [prompt] + [g_cond[half + i : half + i + 1] for i in range(half)]
    base = pair * (CONTS + 1)
    where_to = [base] + [base + 1 + core * half + i for i in range(half)]
    for lane in range(D // 128):
        row = lax.broadcasted_iota(jnp.int32, (time_rows, 128), 0) + lane * time_rows
        placed = jnp.zeros((time_rows, 128), f32)
        for index, value in zip(where_to, values):
            placed = placed + jnp.where(row == index, value, 0.0)
        small_ref[0:time_rows, lane * 128 : (lane + 1) * 128] = placed
    small = small_ref[...]
    high = small.astype(bf16)
    rows = small.shape[0]
    low = (small[time_rows:] - high[time_rows:].astype(f32)).astype(bf16)
    for j in range(keep_ref.shape[0]):
        for col in range(2):
            split_store(ada_late[:, col * D : (col + 1) * D], keep_ref, send_ref, core, lead, col * lead)
        row = 2 * lead
        for ref in (keep_ref, send_ref):
            ref[j, row : row + rows, :] = high
            ref[j, row + rows : row + rows + 16, :] = low


def last_call(place_ids, cond, ada, stat1, stat2, vectors, n, time_rows):
    lead = ada.shape[0] // n
    rows = 16 + time_rows
    args = (cond, ada, stat1, stat2) + tuple(vectors)
    out = whole((n // 2, 2 * lead + rows + 16, D))
    shape = jax.ShapeDtypeStruct((n // 2, 2 * lead + rows + 16, D), bf16)
    return pl.pallas_call(
        partial(last_kernel, lead, time_rows),
        grid=(1,),
        in_specs=[SCALAR] + [whole(a.shape) for a in args],
        out_specs=[out, out],
        out_shape=[shape, shape],
        scratch_shapes=[pltpu.VMEM((rows, D), f32)],
        compiler_params=pltpu.CompilerParams(vmem_limit_bytes=VMEM_LIMIT),
        cost_estimate=cost("last"),
        name="last",
    )(place_ids, *args)


def swap(value, axis, mask):
    pairs = [(source, source ^ mask) for source in range(lax.axis_size(axis))]
    return lax.ppermute(value, axis, pairs)


def gather_far(piece):
    pieces = {0: piece}
    mask = lax.axis_size("shard") // 2
    while mask > 1:
        for offset in list(pieces):
            pieces[offset | mask] = swap(pieces[offset], "shard", mask)
        mask //= 2
    return pieces


def gather_near(pieces):
    pieces = dict(pieces)
    for offset in list(pieces):
        pieces[offset | 1] = swap(pieces[offset], "shard", 1)
    return [pieces[offset] for offset in range(len(pieces))]


def sides():
    rep = lax.axis_index("rep")
    return rep % 2, rep % 4


def far_parts(piece, split=1):
    rows = piece.shape[0] // split
    if split == 1 or rows % 16:
        return 1, gather_far(piece)
    side = sides()[0 if split == 2 else 1]
    found = gather_far(lax.dynamic_slice_in_dim(piece, side * rows, rows, 0))
    found[0] = piece
    return split, found


def far_weight(split, found, tie=None):
    if tie is not None:
        found, _ = lax.optimization_barrier((found, tie))
    spec, arrays = [], []
    for offset, part in found.items():
        if split == 1 or not offset:
            spec.append((offset, 1, 0))
            arrays.append(part)
            continue
        spec += [(offset, split, code) for code in range(split)]
        arrays += [part] + [swap(part, "rep", code) for code in range(1, split)]
    return Weight(spec, arrays)


def near_weight(far):
    spec, arrays = list(far.spec), list(far.arrays)
    for (offset, split, code), part in zip(far.spec, far.arrays):
        spec.append((offset | 1, split, code))
        arrays.append(swap(part, "shard", 1))
    if all(part.shape[0] % 16 == 0 for part in arrays):
        return Weight(spec, arrays)
    mine = lax.axis_index("shard")
    rows = arrays[0].shape[0]
    out = jnp.zeros((rows * len(arrays),) + arrays[0].shape[1:], arrays[0].dtype)
    for (offset, _split, _code), part in zip(spec, arrays):
        out = lax.dynamic_update_slice_in_dim(out, part, (mine ^ offset) * rows, 0)
    return Weight([(None, 1, 0)], [out])


def add_plain(left, right):
    return left.astype(f32) + right.astype(f32)


def add_packed(left, right):
    rows = left.shape[-2] - 16
    total = add_plain(left[..., :rows, :], right[..., :rows, :])
    rest = add_plain(left[..., rows:, :], right[..., rows:, :])
    return jnp.concatenate([total[..., : rows - 16, :], total[..., rows - 16 :, :] + rest], -2)


def pack_plain(value):
    return value.astype(bf16)


def pack_packed(value):
    high = value.astype(bf16)
    low = value[..., -16:, :] - high[..., -16:, :].astype(f32)
    return jnp.concatenate([high, low.astype(bf16)], -2)


def reduce_chain(keep, send, steps, add=add_plain, pack=pack_plain):
    mine, rep = lax.axis_index("shard"), lax.axis_index("rep")

    def parts(values, axis, bit):
        kept, sent = [
            pack(add(*(lax.dynamic_index_in_dim(v, b, axis, False) for v in values))) for b in (bit, 1 - bit)
        ]
        return kept, sent

    got = yield send, swap(send, "shard", 1)
    terms = (keep, got)
    mask = 2
    while mask < lax.axis_size("shard"):
        halves = [t.reshape((-1, 2) + t.shape[1:]) for t in terms]
        kept, send = parts(halves, 1, (mine // mask) % 2)
        got = yield send, swap(send, "shard", mask)
        terms = (kept, got)
        mask *= 2
    terms = tuple(t[0] for t in terms)
    joined = None
    more = range(3, lax.axis_size("rep").bit_length() - 1)
    steps = [(bit, "all") for bit in more] + list(steps)
    for at, kind in steps:
        bit = (rep >> at) % 2
        if kind == "split":
            kept, send = parts([t.reshape(2, -1, t.shape[-1]) for t in terms], 0, bit)
            got = yield send, swap(send, "rep", 1 << at)
            terms = (kept, got)
            continue
        value = pack(add(*terms)) if joined is None else joined
        got = yield value, swap(value, "rep", 1 << at)
        if kind == "join":
            last = (value, got, at)
            first, second = jnp.where(bit == 0, value, got), jnp.where(bit == 0, got, value)
            joined = jnp.concatenate([first, second], 0)
        else:
            last = (value, got, None)
            terms, joined = (value, got), None
    return last


class Schedule:
    def __init__(self, ids, rows):
        self.ids = ids
        self.chains = {}
        self.sent = {}
        self.done = {}
        self.final = {}
        self.rows = rows

    def begin(self, name, keep, send, *how):
        chain = reduce_chain(keep, send, *how)
        self.chains[name] = chain
        _sent, self.sent[name] = next(chain)

    def start(self, name, keep, send, names):
        (send,) = self.sync(*(other for other in names if other != name), after=(send,))
        self.begin(name, keep, send, ROUTES[name])
        self.sync(*(other for other in names if other == name), after=(send,))

    def sync(self, *names, after=()):
        for name in names or (None,):
            if name is not None and name not in self.sent:
                continue
            got = self.sent.pop(name, None)
            self.ids, got, after = lax.optimization_barrier((self.ids, got, tuple(after)))
            if got is None:
                continue
            try:
                sent, self.sent[name] = self.chains[name].send(got)
                self.ids, _ = lax.optimization_barrier((self.ids, sent))
            except StopIteration as stop:
                self.done[name] = stop.value
                if name in self.rows:
                    self.final[name] = finish_blocks(stop.value, *self.rows[name])
        return after

    def finish(self, *names):
        for name in names:
            self.sync(name)
        while self.sent:
            self.sync(next(iter(self.sent)))


def add_two(a_ref, b_ref):
    return a_ref[...].astype(f32) + b_ref[...].astype(f32)


def bit_of(place_ref, at):
    return place_ref[4] // (1 << at) % 2


def whole_sum(place_ref, a_ref, b_ref, at):
    if at is None:
        return add_two(a_ref, b_ref)
    first, second = a_ref[...].astype(f32), b_ref[...].astype(f32)
    swapped = bit_of(place_ref, at) == 1
    return jnp.concatenate([jnp.where(swapped, second, first), jnp.where(swapped, first, second)], 0)


def finish_blocks(result, rows, wide):
    value, got, at = result
    if at is None:
        total = value.astype(f32) + got.astype(f32)
    else:
        bit = (lax.axis_index("rep") >> at) % 2
        first, second = jnp.where(bit == 0, value, got), jnp.where(bit == 0, got, value)
        total = jnp.concatenate([first, second], 0).astype(f32)
    if not wide:
        return total
    return jnp.concatenate([total[i : i + rows] for i in range(0, total.shape[0], rows)], 1)


def finish_last_kernel(
    n, lead, time_rows, few, ats, place_ref, ids_ref, a_ref, b_ref, *refs
):
    mine = place_ref[0]
    groups, (qkv_ref, proj_ref, ada_ref, time_ref, *out_refs) = refs[: 2 * N_GROUP], refs[2 * N_GROUP :]
    totals = [whole_sum(place_ref, groups[2 * i], groups[2 * i + 1], at) for i, at in enumerate(ats)]
    for group, total in enumerate(totals):
        for third in range(3):
            col = third * D + group * GROUP
            qkv_ref[:, col : col + GROUP] = total[:lead, third * GROUP : (third + 1) * GROUP]
    proj_ref[...] = totals[1][lead : 2 * lead]
    early = totals[0]
    for i in range(2):
        rows = slice(i * few, (i + 1) * few)
        ada_ref[:, i * D : (i + 1) * D] = add_two(a_ref.at[rows], b_ref.at[rows])
    for i in range(4):
        ada_ref[:, (2 + i) * D : (3 + i) * D] = early[lead + i * few : lead + (i + 1) * few]
    at = 2 * few
    times = add_two(a_ref.at[at : at + time_rows], b_ref.at[at : at + time_rows])
    times = jnp.concatenate([times[:, i * 128 : (i + 1) * 128] for i in range(D // 128)], 0)
    steps = lax.broadcasted_iota(jnp.int32, (STEPS, times.shape[0]), 0)
    hot = jnp.where(steps == ids_ref[...], 1.0, 0.0).astype(f32)
    time_ref[...] = exact(hot, times, ((1,), (0,)))
    at += time_rows
    high = add_two(a_ref.at[at : at + 16], b_ref.at[at : at + 16])
    small = high + add_two(a_ref.at[at + 16 : at + 32], b_ref.at[at + 16 : at + 32])
    first = 0
    for ref, count in zip(out_refs, (1, 1, 4, 1, 6, 1)):
        flat = jnp.concatenate([small[first + i : first + i + 1] for i in range(count)], 1)
        size = count * D // n
        share = flat[:, 0:size]
        for shard in range(1, n):
            share = jnp.where(mine == shard, flat[:, shard * size : (shard + 1) * size], share)
        ref[...] = share.reshape(size)
        first += count


def finish_last(place_ids, ids, last, results, n, time_rows, few):
    lead = D // n
    sizes = [(count * D // n,) for count in (1, 1, 4, 1, 6, 1)]
    shapes = [(lead, 3 * D), (lead, D), (few, 6 * D), (STEPS, 128)] + sizes
    arrays = [ids, *last[:2]] + [a for result in results for a in result[:2]]
    ats = tuple(result[2] for result in results)
    return pl.pallas_call(
        partial(finish_last_kernel, n, lead, time_rows, few, ats),
        grid=(1,),
        in_specs=[SCALAR] + [whole(a.shape) for a in arrays],
        out_specs=[whole(s) for s in shapes],
        out_shape=[jax.ShapeDtypeStruct(s, f32) for s in shapes],
        cost_estimate=cost("finish_last"),
        compiler_params=pltpu.CompilerParams(vmem_limit_bytes=VMEM_LIMIT),
        name="finish_last",
    )(place_ids, *arrays)


ROUTES = {'down': ((0, 'split'), (1, 'all'), (2, 'all'), (0, 'join')),
 'last': ((1, 'all'), (0, 'all'), (2, 'all')),
 'qkv0': ((1, 'split'), (0, 'all'), (2, 'all'), (1, 'join')),
 'qkv1': ((0, 'split'), (1, 'split'), (2, 'all'), (1, 'join'), (0, 'join')),
 'qkv2': ((1, 'split'), (0, 'all'), (2, 'all'), (1, 'join')),
 'up': ((0, 'split'), (1, 'all'), (2, 'all'), (0, 'join'))}
SYNCS = (('up', 'down'),
 ('down',),
 ('up', 'down'),
 (),
 ('up', 'qkv0', 'down'),
 (),
 ('up', 'qkv0', 'qkv1', 'down', 'qkv2'),
 ('qkv0', 'qkv1'),
 ('qkv2',
  'up',
  'qkv0',
  'last',
  'qkv1',
  'qkv2',
  'last',
  'qkv1',
  'up',
  'qkv0',
  'qkv2',
  'last',
  'qkv1',
  'qkv0',
  'last',
  'qkv2',
  'qkv1',
  'qkv1',
  'qkv2',
  'last'),
 ('down',))


def on_device(
    hidden_in,
    mask_ids,
    time_ids,
    time_table,
    w_qkv,
    w_proj,
    w_up,
    w_down,
    w_ada,
    gain_attn,
    gain_mlp,
    bias_up,
    bias_down,
    bias_ada,
    mask_embed,
    cotangent,
):
    n = lax.axis_size("shard")
    mine = lax.axis_index("shard")
    core = mine % 2
    pair = (lax.axis_index("rep") * n + mine) // 2
    ids = jnp.stack([mine, core, pair, *sides()]).astype(jnp.int32)
    barrier = lax.optimization_barrier

    vectors = (gain_attn, gain_mlp, bias_up, bias_down, mask_embed, bias_ada)
    lengths = [v.shape[0] for v in vectors]
    row_far = gather_far(pack_call(vectors))
    local = jnp.arange(PROMPT, dtype=jnp.int32)
    positions = jnp.where(local < HALF, core * HALF + local, PROMPT + local % CLEN).astype(f32)
    freqs = 10000.0 ** (-(2.0 * jnp.arange(HDIM // 2, dtype=f32)) / HDIM)
    lanes = jnp.tile(freqs, 4)
    angles = positions[:, None] * lanes[None, :]
    sign = jnp.where(jnp.arange(128) % HDIM < HDIM // 2, -1.0, 1.0).astype(f32)
    cosine, sine = jnp.cos(angles), jnp.sin(angles) * sign[None, :]
    mask = (mask_ids == 1).astype(f32)[:, None]
    ada_far = far_weight(*far_parts(w_ada), (cosine, sine, mask))
    qkv_far = far_weight(*far_parts(w_qkv, 4))
    ada_weight = near_weight(ada_far)
    rows = gather_near(row_far)
    (proj_own, up_own, down_own), _ = barrier(((w_proj, w_up, w_down), ada_far.arrays))
    up_split, up_found = far_parts(up_own, 4)
    proj_far = far_weight(*far_parts(proj_own))
    down_split, down_found = far_parts(down_own, 2)

    block = jnp.arange(CONTS, dtype=jnp.int32)
    seg = jnp.where(block < CONTS // 2, 0, 1 + core * (CONTS // 2) + block - CONTS // 2)
    my_times = lax.dynamic_slice_in_dim(time_ids, pair, 1, 0)
    times = jnp.sum(jnp.where(seg[:, None] == jnp.arange(CONTS + 1, dtype=jnp.int32)[None], my_times, 0), 1)
    mods, cond, ada_mat, attn_gain, mlp_gain, up_bias, down_bias, embed, x = mods_call(
        times, ids, time_table, hidden_in, mask, ada_weight, rows, lengths
    )

    qkv_weight = near_weight(qkv_far.tied(mods))
    q, kvp, kvc = qkv_call(ids, x, cosine, sine, qkv_weight)
    kvp, up_found = barrier((kvp, up_found))
    kvr = swap(kvp, "shard", 1)
    up_far = far_weight(up_split, up_found)
    early = attn_fwd(0, 4, q, kvp, kvc, kvr)
    early, up_far.arrays, proj_far.arrays, down_found = barrier((early, up_far.arrays, proj_far.arrays, down_found))
    proj_weight = near_weight(proj_far.tied(early))
    up_weight = near_weight(up_far.tied(early))
    early, _ = barrier((early, (proj_weight.arrays, up_weight.arrays)))
    down_far = far_weight(down_split, down_found)
    soon = near_weight(Weight(down_far.spec[:2], down_far.arrays[:2]))
    late = Weight(down_far.spec[2:], down_far.arrays[2:])
    attn_o, lse = attn_fwd(4, PAIRS - 4, q, kvp, kvc, kvr, early)
    attn_o, late.arrays = barrier((attn_o, late.arrays))
    down_weight = near_weight(late.tied(attn_o))
    down_weight = Weight(soon.spec + down_weight.spec, soon.arrays + down_weight.arrays)
    attn_proj, middle, x_mlp, act, g_pre, g_mlp, g_bias_up, g_bias_down = up_call(
        ids, attn_o, hidden_in, mask, embed, mods, mlp_gain, up_bias, cotangent, proj_weight, up_weight, down_weight
    )
    plan = Schedule(ids, {"down": (FF // n // 2, False), "up": (D // n, True)})
    down_keep, down_send = down_grad_any(plan.ids, act, g_mlp, n)
    plan.begin("down", down_keep, down_send, ROUTES["down"])
    plan.sync(after=(down_keep,))
    up_keep, up_send = wgrad_call(plan.ids, x_mlp, g_pre, n, "up_grad")
    plan.start("up", up_keep, up_send, SYNCS[9])
    block_out, d_middle, g_att, g_o, stat2, g_gain_mlp = down_call(
        plan.ids, act, g_pre, middle, attn_proj, cotangent, mods, mlp_gain, down_bias, proj_weight, up_weight, down_weight
    )
    plan.sync(*SYNCS[0], after=(g_o,))
    parts, others = [], []

    def backward(group, names):
        gq, gc, dp, dr = attn_bwd(plan.ids, group, q, kvp, kvc, kvr, g_o, lse, cosine, sine)
        parts.append((gq, gc, dp))
        (dr,) = plan.sync(*names, after=(dr,))
        others.append(swap(dr, "shard", 1))

    grads = []

    def weight(group, proj, ada, names):
        keep, send, total = qkv_grad_call(
            plan.ids, x, *parts[group], others[group], cosine, sine, n, f"qkv_grad{group}", proj, ada
        )
        grads.append(total)
        plan.start(f"qkv{group}", keep, send, names)

    backward(0, SYNCS[1])
    backward(1, SYNCS[2])
    weight(0, None, (cond, stat2), SYNCS[3])
    backward(2, SYNCS[4])
    weight(1, (attn_o, g_att), None, SYNCS[5])
    weight(2, None, None, SYNCS[6])
    grad_hidden, stat1, g_gain_attn, g_mask = start_call(
        plan.ids, hidden_in, mask, embed, mods, attn_gain, d_middle, grads, qkv_weight
    )
    plan.sync(*SYNCS[7], after=(stat1,))
    time_rows = -(-time_ids.size // 6 // 8) * 8
    vector_grads = (g_gain_attn, g_gain_mlp, g_bias_up, g_bias_down, g_mask)
    keep, send = last_call(plan.ids, cond, ada_mat, stat1, stat2, vector_grads, n, time_rows)
    plan.begin("last", keep, send, ROUTES["last"], add_packed, pack_packed)
    plan.finish(*SYNCS[8])

    done = plan.done
    few = w_ada.shape[0]
    flat_ids = time_ids.reshape(1, -1)
    flat_ids = jnp.pad(flat_ids, ((0, 0), (0, 6 * time_rows - flat_ids.shape[1])), constant_values=-1)
    results = [done[f"qkv{g}"] for g in range(N_GROUP)]
    grad_qkv, grad_proj, grad_ada, grad_time, *shares = finish_last(
        plan.ids, flat_ids, done["last"], results, n, time_rows, few
    )
    return (block_out, grad_hidden, grad_time, grad_qkv, grad_proj, plan.final["up"], plan.final["down"], grad_ada, *shares)


def solution(mesh):
    in_specs = (
        P(("rep", "shard"), None),
        P(("rep", "shard")),
        P(),
        P(),
        P("shard", None),
        P("shard", None),
        P("shard", None),
        P("shard", None),
        P("shard", None),
        P("shard"),
        P("shard"),
        P("shard"),
        P("shard"),
        P("shard"),
        P("shard"),
        P(("rep", "shard"), None),
    )
    out_specs = (
        P(("rep", "shard"), None),
        P(("rep", "shard"), None),
        P(),
        P("shard", None),
        P("shard", None),
        P("shard", None),
        P("shard", None),
        P("shard", None),
        P("shard"),
        P("shard"),
        P("shard"),
        P("shard"),
        P("shard"),
        P("shard"),
    )
    return jax.shard_map(
        on_device, mesh=mesh, in_specs=in_specs, out_specs=out_specs, check_vma=False
    )
```

```python
from functools import partial

import jax
import jax.numpy as jnp
from jax import lax
from jax.experimental import pallas as pl
from jax.experimental.pallas import tpu as pltpu
from jax.sharding import PartitionSpec as P

D = 768
HEADS = 12
HDIM = 64
FF = 3072
STEPS = 1000
CLEN = 128
CONTS = 8
PROMPT = 1024
HALF = PROMPT // 2
PAIRS = HEADS // 2
GROUP = 256
N_GROUP = D // GROUP
TILE = 256
SUB = TILE // CLEN
CHUNK = 512
eps_norm = 1e-06
bf16 = jnp.bfloat16
f32 = jnp.float32
VMEM_LIMIT = 62 * 2**20
COSTS = {'attn_bwd0': 52.5,
 'attn_bwd1': 52.8,
 'attn_bwd2': 53.4,
 'attn_fwd0': 55.5,
 'attn_fwd2': 55.8,
 'attn_fwd4': 30.9,
 'combine': 4.8,
 'down_grad': 31.5,
 'finish_down': 8.4,
 'finish_last': 12.6,
 'finish_qkv': 9.0,
 'finish_up': 11.7,
 'last': 14.7,
 'mlp_down': 75.6,
 'mlp_up': 74.4,
 'mods': 19.5,
 'pack': 4.2,
 'qkv': 25.5,
 'qkv_grad0': 25.5,
 'qkv_grad01': 46.5,
 'qkv_grad1': 21.9,
 'qkv_grad12': 39,
 'qkv_grad2': 16.8,
 'start_grad': 35.1,
 'up_grad': 27.6,
 'wide_grad': 27}


def cost(name):
    return pl.CostEstimate(flops=int(COSTS.get(name, 1.0) * 1e9), bytes_accessed=0, transcendentals=0)


def nt(left, right):
    return lax.dot_general(left, right, (((1,), (1,)), ((), ())), preferred_element_type=f32)


def nn(left, right):
    return lax.dot_general(left, right, (((1,), (0,)), ((), ())), preferred_element_type=f32)


def tn(left, right):
    return lax.dot_general(left, right, (((0,), (0,)), ((), ())), preferred_element_type=f32)


def exact(left, right, contract):
    return lax.dot_general(
        left, right, (contract, ((), ())), preferred_element_type=f32, precision=lax.Precision.HIGHEST
    )


def layer_norm(values):
    mean_value = jnp.mean(values, -1, keepdims=True)
    centered = values - mean_value
    inv_std = lax.rsqrt(jnp.mean(centered * centered, -1, keepdims=True) + eps_norm)
    return (centered * inv_std, inv_std)


def norm_back(gradient, normed, inv_std):
    return inv_std * (
        gradient
        - jnp.mean(gradient, -1, keepdims=True)
        - normed * jnp.mean(gradient * normed, -1, keepdims=True)
    )


def rotate(values, cosine, sine):
    lane = lax.broadcasted_iota(jnp.int32, cosine.shape, 1) % HDIM
    out = []
    for col in range(0, values.shape[1], 128):
        part = values[:, col : col + 128]
        other = jnp.where(lane < HDIM // 2, pltpu.roll(part, 96, 1), pltpu.roll(part, 32, 1))
        out.append(part * cosine + other * sine)
    return out[0] if len(out) == 1 else jnp.concatenate(out, 1)


def whole(shape):
    return pl.BlockSpec(shape, lambda *_: (0,) * len(shape))


ANY = pl.BlockSpec(memory_space=pl.ANY)
SCALAR = pl.BlockSpec(memory_space=pltpu.SMEM)


def place(pieces, spec, place_ref, target, sem):
    mine = place_ref[0]
    copies = []
    for (offset, split, part), piece in zip(spec, pieces):
        rows = piece.shape[0]
        if offset is None:
            where = target
        else:
            start = (mine ^ offset) * (split * rows)
            if split > 1:
                start = start + (place_ref[3 if split == 2 else 4] ^ part) * rows
            where = target.at[pl.ds(pl.multiple_of(start, 16), rows)]
        copies.append(pltpu.make_async_copy(piece, where, sem))
    return copies


class Weight:
    def __init__(self, spec, arrays):
        self.spec = tuple(spec)
        self.arrays = list(arrays)
        self.count = len(self.arrays)

    def tied(self, *values):
        arrays, _ = lax.optimization_barrier((self.arrays, values))
        return Weight(self.spec, arrays)


def qkv_kernel(
    spec, place_ref, x_ref, cos_ref, sin_ref, *rest
):
    n = len(spec)
    pieces = rest[:n]
    q_ref, kvp_ref, kvc_ref, w_ref, sem = rest[n:]
    step = pl.program_id(0)

    @pl.when(step == 0)
    def _():
        copies = place(pieces, spec, place_ref, w_ref, sem)
        for copy in copies:
            copy.start()
        for copy in copies:
            copy.wait()

    x = x_ref[...]
    cosine, sine = cos_ref[...], sin_ref[...]

    def part(third):
        return nn(x, w_ref[:, pl.ds(pl.multiple_of(third * D + step * GROUP, 128), GROUP)])

    q_ref[...] = (rotate(part(0), cosine, sine) * HDIM**-0.5).astype(bf16)
    k = rotate(part(1), cosine, sine).astype(bf16)
    kvp_ref[0], kvc_ref[0] = k[:HALF], k[HALF:]
    v = part(2).astype(bf16)
    kvp_ref[1], kvc_ref[1] = v[:HALF], v[HALF:]


def qkv_call(place_ids, x, cosine, sine, weight):
    n = weight.count
    width = weight.arrays[0].shape[1]
    half = pl.BlockSpec((2, HALF, GROUP), lambda g: (0, 0, g))
    return pl.pallas_call(
        partial(qkv_kernel, weight.spec),
        grid=(N_GROUP,),
        in_specs=[
            SCALAR,
            whole((PROMPT, D)),
            whole((PROMPT, 128)),
            whole((PROMPT, 128)),
        ]
        + [ANY] * n,
        out_specs=[pl.BlockSpec((PROMPT, GROUP), lambda g: (0, g)), half, half],
        out_shape=[
            jax.ShapeDtypeStruct((PROMPT, D), bf16),
            jax.ShapeDtypeStruct((2, HALF, D), bf16),
            jax.ShapeDtypeStruct((2, HALF, D), bf16),
        ],
        scratch_shapes=[pltpu.VMEM((D, width), bf16), pltpu.SemaphoreType.DMA],
        compiler_params=pltpu.CompilerParams(vmem_limit_bytes=VMEM_LIMIT),
        cost_estimate=cost("qkv"),
        name="qkv",
    )(place_ids, x, cosine, sine, *weight.arrays)


def head_only(values, head):
    lane = lax.broadcasted_iota(jnp.int32, values.shape, 1)
    return jnp.where((lane < HDIM) if head == 0 else (lane >= HDIM), values, jnp.zeros_like(values))


def key_parts(prompt, other, own, rows, first):
    parts = [nt(prompt, rows), nt(other, rows)]
    if not first:
        cols = range(0, HALF, CLEN)
        parts.append(
            jnp.concatenate([nt(own[c : c + CLEN], rows[c : c + CLEN]) for c in cols], 1)
        )
    return parts


def attn_fwd_kernel(q_ref, kvp_ref, kvc_ref, kvr_ref, o_ref, lse_ref):
    kp, kc, kr = kvp_ref[0], kvc_ref[0], kvr_ref[0]
    vp_t, vc_t, vr_t = kvp_ref[1].T, kvc_ref[1].T, kvr_ref[1].T
    for start in (0, HALF):
        outs = []
        q_tile = q_ref[pl.ds(start, HALF), :]
        for head in range(2):
            lanes = slice(HDIM * head, HDIM * (head + 1))
            scores = key_parts(kp, kr, kc, head_only(q_tile, head), start == 0)
            top = jnp.max(scores[0], 0, keepdims=True)
            for part in scores[1:]:
                top = jnp.maximum(top, jnp.max(part, 0, keepdims=True))
            powers = [jnp.exp(part - top) for part in scores]
            total = jnp.sum(powers[0], 0, keepdims=True)
            for part in powers[1:]:
                total = total + jnp.sum(part, 0, keepdims=True)
            lse_ref[0, pl.ds(head, 1), pl.ds(start, HALF)] = top + jnp.log(total)
            scale = 1.0 / total
            probs = [(part * scale).astype(bf16) for part in powers]
            out = nn(vp_t[lanes], probs[0]) + nn(vr_t[lanes], probs[1])
            if start:
                cols = [slice(c, c + CLEN) for c in range(0, HALF, CLEN)]
                out = out + jnp.concatenate([nn(vc_t[lanes, c], probs[2][:, c]) for c in cols], 1)
            outs.append(out)
        o_ref[pl.ds(start, HALF), :] = jnp.concatenate(outs, 0).T.astype(bf16)


def pair_block(rows, first=0):
    return pl.BlockSpec((rows, 2 * HDIM), lambda pair: (0, first + pair))


def pair_half(first=0):
    return pl.BlockSpec((2, HALF, 2 * HDIM), lambda pair: (0, 0, first + pair))


def lse_block(first=0):
    return pl.BlockSpec((1, 2, PROMPT), lambda pair: (first + pair, 0, 0))


def attn_fwd(first, pairs, q, kvp, kvc, kvr, before=None):
    inputs = (q, kvp, kvc, kvr)
    in_specs = [pair_block(PROMPT, first)] + [pair_half(first)] * 3
    body = attn_fwd_kernel
    aliases = {}
    if before is not None:
        inputs += tuple(before)
        in_specs += [ANY, ANY]
        aliases = {4: 0, 5: 1}

        def body(q_ref, kvp_ref, kvc_ref, kvr_ref, _o, _lse, o_ref, lse_ref):
            attn_fwd_kernel(q_ref, kvp_ref, kvc_ref, kvr_ref, o_ref, lse_ref)

    return pl.pallas_call(
        body,
        grid=(pairs,),
        in_specs=in_specs,
        out_specs=[pair_block(PROMPT, first), lse_block(first)],
        out_shape=[
            jax.ShapeDtypeStruct((PROMPT, D), bf16),
            jax.ShapeDtypeStruct((PAIRS, 2, PROMPT), f32),
        ],
        input_output_aliases=aliases,
        compiler_params=pltpu.CompilerParams(vmem_limit_bytes=VMEM_LIMIT),
        cost_estimate=cost(f"attn_fwd{first}"),
        name=f"attn_fwd{first}",
    )(*inputs)


def attn_bwd_kernel(
    _ids, q_ref, kvp_ref, kvc_ref, kvr_ref, g_ref, lse_ref, cos_ref, sin_ref, gq_ref, gc_ref, dp_ref, dr_ref
):
    kp, kc, kr = kvp_ref[0], kvc_ref[0], kvr_ref[0]
    vp, vc, vr = kvp_ref[1], kvc_ref[1], kvr_ref[1]
    kp_t, kc_t, kr_t = kp.T, kc.T, kr.T
    first = lax.broadcasted_iota(jnp.int32, (HALF, 2 * HDIM), 1) < HDIM
    for start in (0, HALF):
        tile = pl.ds(start, HALF)
        q_tile, g_tile = q_ref[tile, :], g_ref[tile, :]
        cols = [slice(c, c + CLEN) for c in range(0, HALF, CLEN)]
        dqs, dks, dvs = [], [], []
        for head in range(2):
            lanes = slice(HDIM * head, HDIM * (head + 1))
            scores = key_parts(kp, kr, kc, head_only(q_tile, head), start == 0)
            dps = key_parts(vp, vr, vc, head_only(g_tile, head), start == 0)
            lse = lse_ref[0, pl.ds(head, 1), tile]
            probs = [jnp.exp(part - lse) for part in scores]
            row_dot = jnp.sum(probs[0] * dps[0], 0, keepdims=True)
            for p_part, d_part in zip(probs[1:], dps[1:]):
                row_dot = row_dot + jnp.sum(p_part * d_part, 0, keepdims=True)
            ds = [(p * (d - row_dot)).astype(bf16) for p, d in zip(probs, dps)]
            probs = [p.astype(bf16) for p in probs]
            dq = nn(kp_t[lanes], ds[0]) + nn(kr_t[lanes], ds[1])
            dk = [nn(ds[0], q_tile), nn(ds[1], q_tile)]
            dv = [nn(probs[0], g_tile), nn(probs[1], g_tile)]
            if start:
                dq = dq + jnp.concatenate([nn(kc_t[lanes, c], ds[2][:, c]) for c in cols], 1)
                dk.append(jnp.concatenate([nn(ds[2][:, c], q_tile[c]) for c in cols], 0))
                dv.append(jnp.concatenate([nn(probs[2][:, c], g_tile[c]) for c in cols], 0))
            dqs.append(dq)
            dks.append(dk)
            dvs.append(dv)
        cosine, sine = cos_ref[tile, :], sin_ref[tile, :]
        dq = jnp.concatenate(dqs, 0).T * HDIM**-0.5
        gq_ref[tile, :] = rotate(dq, cosine, -sine).astype(bf16)
        for which, parts in enumerate((dks, dvs)):
            merged = [jnp.where(first, a, b) for a, b in zip(*parts)]
            if start:
                dp_ref[which] += merged[0]
                dr_ref[which] += merged[1]
                last = merged[2] if which else rotate(merged[2], cosine, -sine)
                gc_ref[which] = last.astype(bf16)
            else:
                dp_ref[which] = merged[0]
                dr_ref[which] = merged[1]


def attn_bwd(ids, group, q, kvp, kvc, kvr, g, lse, cosine, sine):
    pairs = GROUP // (2 * HDIM)
    first = group * pairs
    return pl.pallas_call(
        attn_bwd_kernel,
        grid=(pairs,),
        in_specs=[SCALAR, pair_block(PROMPT, first)]
        + [pair_half(first)] * 3
        + [pair_block(PROMPT, first), lse_block(first), whole((PROMPT, 128)), whole((PROMPT, 128))],
        out_specs=[pair_block(PROMPT), pair_half(), pair_half(), pair_half()],
        out_shape=[
            jax.ShapeDtypeStruct((PROMPT, GROUP), bf16),
            jax.ShapeDtypeStruct((2, HALF, GROUP), bf16),
            jax.ShapeDtypeStruct((2, HALF, GROUP), f32),
            jax.ShapeDtypeStruct((2, HALF, GROUP), f32),
        ],
        compiler_params=pltpu.CompilerParams(vmem_limit_bytes=VMEM_LIMIT),
        cost_estimate=cost(f"attn_bwd{group}"),
        name=f"attn_bwd{group}",
    )(ids, q, kvp, kvc, kvr, g, lse, cosine, sine)


def up_kernel(
    specs,
    place_ref,
    o_ref,
    hid_ref,
    mask_ref,
    embed_ref,
    mods_ref,
    gain_ref,
    bias_ref,
    cot_ref,
    *rest,
):
    pieces, rest = take(specs, rest)
    ap_ref, mid_ref, x_ref, act_ref, gpre_ref, gmlp_ref, gbu_ref, gbd_ref = rest[:8]
    proj_ref, up_ref, down_ref, sems = rest[8:]
    step = pl.program_id(0)
    targets = (proj_ref, up_ref, down_ref)
    copies = [
        place(part, spec, place_ref, target, sems.at[i])
        for i, (part, spec, target) in enumerate(zip(pieces, specs, targets))
    ]

    @pl.when(step == 0)
    def _():
        for group in copies:
            for copy in group:
                copy.start()
        gbu_ref[...] = jnp.zeros_like(gbu_ref)
        gbd_ref[...] = jnp.zeros_like(gbd_ref)
        for copy in copies[0]:
            copy.wait()

    attn_proj = nn(o_ref[...], proj_ref[...])
    ap_ref[...] = attn_proj
    for sub in range(SUB):
        rows = slice(sub * CLEN, (sub + 1) * CLEN)
        row = pl.ds(step * SUB + sub, 1)
        start = jnp.where(mask_ref[rows, :] > 0.5, embed_ref[...], hid_ref[rows, :].astype(f32))
        middle = start + mods_ref[row, 2 * D : 3 * D] * attn_proj[rows]
        mid_ref[rows, :] = middle
        normed, _inv = layer_norm(middle)
        shift, scale = mods_ref[row, 3 * D : 4 * D], mods_ref[row, 4 * D : 5 * D]
        x_ref[rows, :] = (normed * gain_ref[...] * (1.0 + scale) + shift).astype(bf16)
        g_mlp = (mods_ref[row, 5 * D : 6 * D] * cot_ref[rows, :].astype(f32)).astype(bf16)
        gmlp_ref[rows, :] = g_mlp
        gbd_ref[...] += jnp.sum(g_mlp.astype(f32), 0, keepdims=True)

    @pl.when(step == 0)
    def _():
        for group in copies[1:]:
            for copy in group:
                copy.wait()

    x, g_mlp = x_ref[...], gmlp_ref[...]
    root = (2.0 / jnp.pi) ** 0.5
    for col in range(0, FF, CHUNK):
        cols = slice(col, col + CHUNK)
        pre = nn(x, up_ref[:, cols]) + bias_ref[:, cols]
        square = pre * pre
        curve = jnp.tanh(root * pre * (1.0 + 0.044715 * square))
        half_up = 0.5 * (1.0 + curve)
        act_ref[:, cols] = (pre * half_up).astype(bf16)
        slope = half_up + (0.5 * root) * pre * (1.0 - curve * curve) * (1.0 + 0.134145 * square)
        g_pre = (nt(g_mlp, down_ref[cols, :]) * slope).astype(bf16)
        gpre_ref[:, cols] = g_pre
        gbu_ref[:, cols] += jnp.sum(g_pre.astype(f32), 0, keepdims=True)


def take(specs, refs):
    pieces = []
    for spec in specs:
        pieces.append(refs[: len(spec)])
        refs = refs[len(spec) :]
    return pieces, refs


def tile_block(width):
    return pl.BlockSpec((TILE, width), lambda step: (step, 0))


def weight_scratch():
    return [
        pltpu.VMEM((D, D), bf16),
        pltpu.VMEM((D, FF), bf16),
        pltpu.VMEM((FF, D), bf16),
        pltpu.SemaphoreType.DMA((3,)),
    ]


def up_call(place_ids, attn_o, hidden, mask, embed, mods, gain, bias, cot, proj, up, down):
    weights = (proj, up, down)
    n = sum(w.count for w in weights)
    specs = tuple(w.spec for w in weights)
    arrays = [a for w in weights for a in w.arrays]
    rows = PROMPT
    return pl.pallas_call(
        partial(up_kernel, specs),
        grid=(rows // TILE,),
        in_specs=[
            SCALAR,
            tile_block(D),
            tile_block(D),
            tile_block(1),
            whole((1, D)),
            whole(mods.shape),
            whole((1, D)),
            whole((1, FF)),
            tile_block(D),
        ]
        + [ANY] * n,
        out_specs=[tile_block(D)] * 3
        + [tile_block(FF)] * 2
        + [tile_block(D), whole((1, FF)), whole((1, D))],
        out_shape=[
            jax.ShapeDtypeStruct((rows, D), f32),
            jax.ShapeDtypeStruct((rows, D), f32),
            jax.ShapeDtypeStruct((rows, D), bf16),
            jax.ShapeDtypeStruct((rows, FF), bf16),
            jax.ShapeDtypeStruct((rows, FF), bf16),
            jax.ShapeDtypeStruct((rows, D), bf16),
            jax.ShapeDtypeStruct((1, FF), f32),
            jax.ShapeDtypeStruct((1, D), f32),
        ],
        scratch_shapes=weight_scratch(),
        compiler_params=pltpu.CompilerParams(vmem_limit_bytes=VMEM_LIMIT),
        cost_estimate=cost("mlp_up"),
        name="mlp_up",
    )(place_ids, attn_o, hidden, mask, embed, mods, gain, bias, cot, *arrays)


def down_kernel(specs, place_ref, act_ref, gpre_ref, mid_ref, ap_ref, cot_ref, mods_ref, gain_ref, bias_ref, *rest):
    pieces, rest = take(specs, rest)
    out_ref, dmid_ref, gatt_ref, go_ref, stat_ref, ggain_ref = rest[:6]
    proj_ref, up_ref, down_ref, sems = rest[6:]
    step = pl.program_id(0)
    targets = (proj_ref, up_ref, down_ref)
    copies = [
        place(part, spec, place_ref, target, sems.at[i])
        for i, (part, spec, target) in enumerate(zip(pieces, specs, targets))
    ]

    @pl.when(step == 0)
    def _():
        for i in (2, 1, 0):
            for copy in copies[i]:
                copy.start()
        ggain_ref[...] = jnp.zeros_like(ggain_ref)
        for copy in copies[2]:
            copy.wait()

    mlp_out = nn(act_ref[...], down_ref[...]) + bias_ref[...]

    @pl.when(step == 0)
    def _():
        for i in (1, 0):
            for copy in copies[i]:
                copy.wait()

    g_n = nt(gpre_ref[...], up_ref[...])
    for sub in range(SUB):
        rows = slice(sub * CLEN, (sub + 1) * CLEN)
        row = pl.ds(step * SUB + sub, 1)
        middle, cot, grad = mid_ref[rows, :], cot_ref[rows, :].astype(f32), g_n[rows]
        gate_attn, gate_mlp = mods_ref[row, 2 * D : 3 * D], mods_ref[row, 5 * D : 6 * D]
        scale = 1.0 + mods_ref[row, 4 * D : 5 * D]
        out_ref[rows, :] = (middle + gate_mlp * mlp_out[rows]).astype(bf16)
        normed, inv_std = layer_norm(middle)
        along = jnp.sum(grad * normed, 0, keepdims=True)
        ggain_ref[...] += along * scale
        d_middle = cot + norm_back(grad * (scale * gain_ref[...]), normed, inv_std)
        dmid_ref[rows, :] = d_middle
        gatt_ref[rows, :] = (gate_attn * d_middle).astype(bf16)
        stat_ref[row, 0:D] = jnp.sum(d_middle * ap_ref[rows, :], 0, keepdims=True)
        stat_ref[row, D : 2 * D] = jnp.sum(grad, 0, keepdims=True)
        stat_ref[row, 2 * D : 3 * D] = along * gain_ref[...]
        stat_ref[row, 3 * D : 4 * D] = jnp.sum(cot * mlp_out[rows], 0, keepdims=True)
    go_ref[...] = nt(gatt_ref[...], proj_ref[...]).astype(bf16)


def down_call(place_ids, act, gpre, middle, attn_proj, cot, mods, gain, bias, proj, up, down):
    weights = (proj, up, down)
    n = sum(w.count for w in weights)
    specs = tuple(w.spec for w in weights)
    arrays = [a for w in weights for a in w.arrays]
    rows = PROMPT
    return pl.pallas_call(
        partial(down_kernel, specs),
        grid=(rows // TILE,),
        in_specs=[
            SCALAR,
            tile_block(FF),
            tile_block(FF),
            tile_block(D),
            tile_block(D),
            tile_block(D),
            whole(mods.shape),
            whole((1, D)),
            whole((1, D)),
        ]
        + [ANY] * n,
        out_specs=[tile_block(D)] * 4 + [whole((CONTS, 4 * D)), whole((1, D))],
        out_shape=[
            jax.ShapeDtypeStruct((rows, D), bf16),
            jax.ShapeDtypeStruct((rows, D), f32),
            jax.ShapeDtypeStruct((rows, D), bf16),
            jax.ShapeDtypeStruct((rows, D), bf16),
            jax.ShapeDtypeStruct((CONTS, 4 * D), f32),
            jax.ShapeDtypeStruct((1, D), f32),
        ],
        scratch_shapes=weight_scratch(),
        compiler_params=pltpu.CompilerParams(vmem_limit_bytes=VMEM_LIMIT),
        cost_estimate=cost("mlp_down"),
        name="mlp_down",
    )(place_ids, act, gpre, middle, attn_proj, cot, mods, gain, bias, *arrays)


def split_store(total, keep_ref, send_ref, core, lead, at):
    for pair in range(total.shape[0] // lead // 2):
        even = total[2 * pair * lead : (2 * pair + 1) * lead].astype(bf16)
        odd = total[(2 * pair + 1) * lead : (2 * pair + 2) * lead].astype(bf16)
        keep_ref[pair, at : at + lead, :] = jnp.where(core == 0, even, odd)
        send_ref[pair, at : at + lead, :] = jnp.where(core == 0, odd, even)


def wgrad_kernel(lead, place_ref, left_ref, right_ref, keep_ref, send_ref):
    split_store(tn(left_ref[...], right_ref[...]), keep_ref, send_ref, place_ref[1], lead, 0)


def wgrad_call(place_ids, left, right, n, name):
    lead = D // n
    blocks = right.shape[1] // D
    out = pl.BlockSpec((n // 2, lead, D), lambda j: (0, j, 0))
    shape = jax.ShapeDtypeStruct((n // 2, blocks * lead, D), bf16)
    return pl.pallas_call(
        partial(wgrad_kernel, lead),
        grid=(blocks,),
        in_specs=[SCALAR, whole((PROMPT, D)), pl.BlockSpec((PROMPT, D), lambda j: (0, j))],
        out_specs=[out, out],
        out_shape=[shape, shape],
        compiler_params=pltpu.CompilerParams(vmem_limit_bytes=VMEM_LIMIT),
        cost_estimate=cost(name),
        name=name,
    )(place_ids, left, right)


def down_grad_kernel(_ids, left_ref, right_ref, keep_ref, send_ref):
    half = pl.num_programs(0) // 2
    total = tn(left_ref[...], right_ref[...]).astype(bf16)

    @pl.when(pl.program_id(0) < half)
    def _():
        send_ref[0] = total

    @pl.when(pl.program_id(0) >= half)
    def _():
        keep_ref[0] = total


def down_grad_call(place_ids, act, g_mlp, n):
    rows = FF // n
    half = n // 2

    def shard(j, ids):
        core = ids[1]
        return 0, jnp.where(j < half, 2 * j + 1 - core, 2 * (j - half) + core)

    shape = jax.ShapeDtypeStruct((half, rows, D), bf16)
    return pl.pallas_call(
        down_grad_kernel,
        grid_spec=pltpu.PrefetchScalarGridSpec(
            num_scalar_prefetch=1,
            grid=(n,),
            in_specs=[pl.BlockSpec((PROMPT, rows), shard), pl.BlockSpec((PROMPT, D), lambda j, ids: (0, 0))],
            out_specs=[
                pl.BlockSpec((1, rows, D), lambda j, ids: (jnp.maximum(j - half, 0), 0, 0)),
                pl.BlockSpec((1, rows, D), lambda j, ids: (jnp.minimum(j, half - 1), 0, 0)),
            ],
        ),
        out_shape=[shape, shape],
        compiler_params=pltpu.CompilerParams(vmem_limit_bytes=VMEM_LIMIT),
        cost_estimate=cost("down_grad"),
        name="down_grad",
    )(place_ids, act, g_mlp)


def down_grad_any(place_ids, act, g_mlp, n):
    if (FF // n) % 128 == 0 and n == 4:
        return down_grad_call(place_ids, act, g_mlp, n)
    full = wide_grad_call(act, g_mlp)
    core = lax.axis_index("shard") % 2
    parts = full.reshape(n // 2, 2, -1, D)
    keep = lax.dynamic_index_in_dim(parts, core, 1, False)
    return keep, lax.dynamic_index_in_dim(parts, 1 - core, 1, False)


def wide_grad_kernel(left_ref, right_ref, out_ref):
    out_ref[...] = tn(left_ref[...], right_ref[...]).astype(bf16)


def wide_grad_call(act, g_mlp):
    return pl.pallas_call(
        wide_grad_kernel,
        grid=(FF // D,),
        in_specs=[pl.BlockSpec((PROMPT, D), lambda j: (0, j)), whole((PROMPT, D))],
        out_specs=pl.BlockSpec((D, D), lambda j: (j, 0)),
        out_shape=jax.ShapeDtypeStruct((FF, D), bf16),
        compiler_params=pltpu.CompilerParams(vmem_limit_bytes=VMEM_LIMIT),
        name="wide_grad",
    )(act, g_mlp)


def qkv_grad_kernel(lead, with_proj, with_ada, place_ref, x_ref, gq_ref, gc_ref, dp_ref, got_ref, cos_ref, sin_ref, *rest):
    keep_ref, send_ref, g_ref = rest[-3:]
    core = place_ref[1]
    g_ref[:, 0:GROUP] = gq_ref[...]
    total_k = dp_ref[0] + got_ref[0].astype(f32)
    total_v = dp_ref[1] + got_ref[1].astype(f32)
    g_ref[0:HALF, GROUP : 2 * GROUP] = rotate(total_k, cos_ref[...], -sin_ref[...]).astype(bf16)
    g_ref[0:HALF, 2 * GROUP : 3 * GROUP] = total_v.astype(bf16)
    g_ref[HALF:PROMPT, GROUP : 2 * GROUP] = gc_ref[0]
    g_ref[HALF:PROMPT, 2 * GROUP : 3 * GROUP] = gc_ref[1]
    split_store(tn(x_ref[...], g_ref[...]), keep_ref, send_ref, core, lead, 0)
    at = lead
    if with_proj:
        split_store(tn(rest[0][...], rest[1][...]), keep_ref, send_ref, core, lead, at)
        at += lead
        rest = rest[2:]
    if with_ada:
        cond = rest[0][...]
        silu = (cond / (1.0 + jnp.exp(-cond))).astype(bf16).astype(f32)
        few = cond.shape[1] * lead // D
        for col in range(4):
            total = exact(silu, rest[1][:, col * D : (col + 1) * D], ((0,), (0,)))
            split_store(total, keep_ref, send_ref, core, few, at)
            at += few


def qkv_grad_call(place_ids, x, gq, gc, dp, got, cosine, sine, n, name, proj, ada):
    lead = D // n
    rows = lead
    extra = []
    if proj is not None:
        extra += list(proj)
        rows += lead
    if ada is not None:
        extra += list(ada)
        rows += 4 * (ada[0].shape[1] // n)
    out = whole((n // 2, rows, D))
    shape = jax.ShapeDtypeStruct((n // 2, rows, D), bf16)
    return pl.pallas_call(
        partial(qkv_grad_kernel, lead, proj is not None, ada is not None),
        grid=(1,),
        in_specs=[
            SCALAR,
            whole((PROMPT, D)),
            whole((PROMPT, GROUP)),
            whole((2, HALF, GROUP)),
            whole((2, HALF, GROUP)),
            whole((2, HALF, GROUP)),
            whole((HALF, 128)),
            whole((HALF, 128)),
        ]
        + [whole(e.shape) for e in extra],
        out_specs=[out, out, whole((PROMPT, D))],
        out_shape=[shape, shape, jax.ShapeDtypeStruct((PROMPT, D), bf16)],
        compiler_params=pltpu.CompilerParams(vmem_limit_bytes=VMEM_LIMIT),
        cost_estimate=cost(name),
        name=name,
    )(place_ids, x, gq, gc, dp, got, cosine, sine, *extra)


def start_kernel(spec, place_ref, hid_ref, mask_ref, embed_ref, mods_ref, gain_ref, dmid_ref, *rest):
    n = len(spec)
    grads, pieces = rest[:N_GROUP], rest[N_GROUP : N_GROUP + n]
    gh_ref, stat_ref, ggain_ref, gmask_ref, w_ref, sem = rest[N_GROUP + n :]
    step = pl.program_id(0)

    @pl.when(step == 0)
    def _():
        copies = place(pieces, spec, place_ref, w_ref, sem)
        for copy in copies:
            copy.start()
        ggain_ref[...] = jnp.zeros_like(ggain_ref)
        gmask_ref[...] = jnp.zeros_like(gmask_ref)
        for copy in copies:
            copy.wait()

    g_n = None
    for group in range(N_GROUP):
        for third in range(3):
            at = third * D + group * GROUP
            term = nt(grads[group][:, third * GROUP : (third + 1) * GROUP], w_ref[:, at : at + GROUP])
            g_n = term if g_n is None else g_n + term
    for sub in range(SUB):
        rows = slice(sub * CLEN, (sub + 1) * CLEN)
        row = pl.ds(step * SUB + sub, 1)
        masked = mask_ref[rows, :] > 0.5
        start = jnp.where(masked, embed_ref[...], hid_ref[rows, :].astype(f32))
        normed, inv_std = layer_norm(start)
        scale = 1.0 + mods_ref[row, D : 2 * D]
        grad = g_n[rows]
        along = jnp.sum(grad * normed, 0, keepdims=True)
        ggain_ref[...] += along * scale
        stat_ref[row, 0:D] = jnp.sum(grad, 0, keepdims=True)
        stat_ref[row, D : 2 * D] = along * gain_ref[...]
        d_start = dmid_ref[rows, :] + norm_back(grad * (scale * gain_ref[...]), normed, inv_std)
        gh_ref[rows, :] = jnp.where(masked, 0.0, d_start)
        gmask_ref[...] += jnp.sum(jnp.where(masked, d_start, 0.0), 0, keepdims=True)


def start_call(place_ids, hidden, mask, embed, mods, gain, d_middle, grads, weight):
    n = weight.count
    rows = PROMPT
    return pl.pallas_call(
        partial(start_kernel, weight.spec),
        grid=(rows // TILE,),
        in_specs=[
            SCALAR,
            tile_block(D),
            tile_block(1),
            whole((1, D)),
            whole(mods.shape),
            whole((1, D)),
            tile_block(D),
        ]
        + [tile_block(D)] * N_GROUP
        + [ANY] * n,
        out_specs=[tile_block(D), whole((CONTS, 2 * D)), whole((1, D)), whole((1, D))],
        out_shape=[
            jax.ShapeDtypeStruct((rows, D), f32),
            jax.ShapeDtypeStruct((CONTS, 2 * D), f32),
            jax.ShapeDtypeStruct((1, D), f32),
            jax.ShapeDtypeStruct((1, D), f32),
        ],
        scratch_shapes=[pltpu.VMEM((D, 3 * D), bf16), pltpu.SemaphoreType.DMA],
        compiler_params=pltpu.CompilerParams(vmem_limit_bytes=VMEM_LIMIT),
        cost_estimate=cost("start_grad"),
        name="start_grad",
    )(place_ids, hidden, mask, embed, mods, gain, d_middle, *grads, *weight.arrays)


def pack_kernel(*refs):
    out_ref = refs[-1]
    out_ref[...] = jnp.zeros_like(out_ref)
    for i, ref in enumerate(refs[:-1]):
        out_ref[i : i + 1, 0 : ref.shape[0]] = ref[...].astype(f32).reshape(1, -1)


def pack_call(vectors):
    shape = (8, max(v.shape[0] for v in vectors))
    return pl.pallas_call(
        pack_kernel,
        grid=(1,),
        in_specs=[whole(v.shape) for v in vectors],
        out_specs=whole(shape),
        out_shape=jax.ShapeDtypeStruct(shape, f32),
        name="pack",
    )(*vectors)


def mods_kernel(spec, lengths, times_ref, place_ref, table_ref, hid_ref, mask_ref, *rest):
    n = len(spec)
    pieces, rest = rest[:n], rest[n:]
    count = len(lengths)
    n_row = len(rest) - count - 7
    rows, rest = rest[:n_row], rest[n_row:]
    mods_ref, cond_ref, ada_ref = rest[:3]
    out_refs = rest[3 : 3 + count - 1]
    x_ref, bias_ref, row_ref, sem, row_sem = rest[3 + count - 1 :]
    gain_ref, embed_ref = out_refs[0], out_refs[4]
    copies = place(pieces, spec, place_ref, ada_ref, sem)
    row_copies = [
        pltpu.make_async_copy(row, row_ref.at[place_ref[0] ^ offset], row_sem) for offset, row in enumerate(rows)
    ]
    for copy in row_copies + copies:
        copy.start()
    for block in range(CONTS):
        cond_ref[pl.ds(block, 1), :] = table_ref[pl.ds(times_ref[block], 1), :]
    cond = cond_ref[...]
    silu = (cond / (1.0 + jnp.exp(-cond))).astype(bf16)
    for copy in row_copies:
        copy.wait()
    for shard in range(n_row):
        for i, (length, ref) in enumerate(zip(lengths, (*out_refs, bias_ref))):
            ref[0:1, shard * length : (shard + 1) * length] = row_ref[shard, i : i + 1, 0:length]
    for copy in copies:
        copy.wait()
    mods_ref[...] = nn(silu, ada_ref[...]) + bias_ref[...]

    @pl.loop(0, CONTS)
    def _(block):
        rows = pl.ds(pl.multiple_of(block * CLEN, CLEN), CLEN)
        start = jnp.where(mask_ref[rows, :] > 0.5, embed_ref[...], hid_ref[rows, :].astype(f32))
        normed, _inv = layer_norm(start)
        row = pl.ds(block, 1)
        shift, scale = mods_ref[row, 0:D], mods_ref[row, D : 2 * D]
        x_ref[rows, :] = (normed * gain_ref[...] * (1.0 + scale) + shift).astype(bf16)


def mods_call(times, place_ids, table, hidden, mask, weight, rows, lengths):
    width = weight.arrays[0].shape[1]
    n = len(rows)
    vectors = [(1, n * length) for length in lengths]
    shapes = [(CONTS, width), (CONTS, table.shape[1])]
    return pl.pallas_call(
        partial(mods_kernel, weight.spec, tuple(lengths)),
        in_specs=[SCALAR, SCALAR, whole(table.shape), whole(hidden.shape), whole(mask.shape)] + [ANY] * (weight.count + n),
        out_specs=[whole(s) for s in shapes] + [whole((table.shape[1], width))] + [whole(v) for v in vectors[:-1]] + [whole((PROMPT, D))],
        out_shape=[jax.ShapeDtypeStruct(s, f32) for s in shapes]
        + [jax.ShapeDtypeStruct((table.shape[1], width), bf16)]
        + [jax.ShapeDtypeStruct(v, f32) for v in vectors[:-1]]
        + [jax.ShapeDtypeStruct((PROMPT, D), bf16)],
        grid=(1,),
        scratch_shapes=[
            pltpu.VMEM(vectors[-1], f32),
            pltpu.VMEM((n,) + rows[0].shape, f32),
            pltpu.SemaphoreType.DMA,
            pltpu.SemaphoreType.DMA,
        ],
        compiler_params=pltpu.CompilerParams(vmem_limit_bytes=VMEM_LIMIT),
        cost_estimate=cost("mods"),
        name="mods",
    )(times, place_ids, table, hidden, mask, *weight.arrays, *rows)


def last_kernel(
    lead, time_rows, place_ref, cond_ref, ada_ref, stat1_ref, stat2_ref, ga_ref, gm_ref, bu_ref, bd_ref, me_ref,
    keep_ref, send_ref, small_ref,
):
    core, pair = place_ref[1], place_ref[2]
    cond = cond_ref[...]
    gate = 1.0 / (1.0 + jnp.exp(-cond))
    silu = (cond * gate).astype(bf16).astype(f32)
    stat1, stat2 = stat1_ref[...], stat2_ref[...]
    ada_late = exact(silu, stat1, ((0,), (0,)))
    ada = ada_ref[...].astype(f32)
    g_silu = exact(stat1, ada[:, : 2 * D], ((1,), (1,))) + exact(stat2, ada[:, 2 * D :], ((1,), (1,)))
    g_cond = g_silu * (gate * (1.0 + cond * (1.0 - gate)))
    small_ref[...] = jnp.zeros_like(small_ref)
    at = time_rows
    small_ref[at : at + 1, :] = ga_ref[...]
    small_ref[at + 1 : at + 2, :] = gm_ref[...]
    for i in range(FF // D):
        small_ref[at + 2 + i : at + 3 + i, :] = bu_ref[:, i * D : (i + 1) * D]
    small_ref[at + 6 : at + 7, :] = bd_ref[...]
    for i in range(2):
        small_ref[at + 7 + i : at + 8 + i, :] = jnp.sum(stat1[:, i * D : (i + 1) * D], 0, keepdims=True)
    for i in range(4):
        small_ref[at + 9 + i : at + 10 + i, :] = jnp.sum(stat2[:, i * D : (i + 1) * D], 0, keepdims=True)
    small_ref[at + 13 : at + 14, :] = me_ref[...]
    half = CONTS // 2
    prompt = jnp.sum(g_cond[:half], 0, keepdims=True)
    values = [prompt] + [g_cond[half + i : half + i + 1] for i in range(half)]
    base = pair * (CONTS + 1)
    where_to = [base] + [base + 1 + core * half + i for i in range(half)]
    for lane in range(D // 128):
        row = lax.broadcasted_iota(jnp.int32, (time_rows, 128), 0) + lane * time_rows
        placed = jnp.zeros((time_rows, 128), f32)
        for index, value in zip(where_to, values):
            placed = placed + jnp.where(row == index, value, 0.0)
        small_ref[0:time_rows, lane * 128 : (lane + 1) * 128] = placed
    small = small_ref[...]
    high = small.astype(bf16)
    rows = small.shape[0]
    low = (small[time_rows:] - high[time_rows:].astype(f32)).astype(bf16)
    for j in range(keep_ref.shape[0]):
        for col in range(2):
            split_store(ada_late[:, col * D : (col + 1) * D], keep_ref, send_ref, core, lead, col * lead)
        row = 2 * lead
        for ref in (keep_ref, send_ref):
            ref[j, row : row + rows, :] = high
            ref[j, row + rows : row + rows + 16, :] = low


def last_call(place_ids, cond, ada, stat1, stat2, vectors, n, time_rows):
    lead = ada.shape[0] // n
    rows = 16 + time_rows
    args = (cond, ada, stat1, stat2) + tuple(vectors)
    out = whole((n // 2, 2 * lead + rows + 16, D))
    shape = jax.ShapeDtypeStruct((n // 2, 2 * lead + rows + 16, D), bf16)
    return pl.pallas_call(
        partial(last_kernel, lead, time_rows),
        grid=(1,),
        in_specs=[SCALAR] + [whole(a.shape) for a in args],
        out_specs=[out, out],
        out_shape=[shape, shape],
        scratch_shapes=[pltpu.VMEM((rows, D), f32)],
        compiler_params=pltpu.CompilerParams(vmem_limit_bytes=VMEM_LIMIT),
        cost_estimate=cost("last"),
        name="last",
    )(place_ids, *args)


def swap(value, axis, mask):
    pairs = [(source, source ^ mask) for source in range(lax.axis_size(axis))]
    return lax.ppermute(value, axis, pairs)


def gather_far(piece):
    pieces = {0: piece}
    mask = lax.axis_size("shard") // 2
    while mask > 1:
        for offset in list(pieces):
            pieces[offset | mask] = swap(pieces[offset], "shard", mask)
        mask //= 2
    return pieces


def gather_near(pieces):
    pieces = dict(pieces)
    for offset in list(pieces):
        pieces[offset | 1] = swap(pieces[offset], "shard", 1)
    return [pieces[offset] for offset in range(len(pieces))]


def sides():
    rep = lax.axis_index("rep")
    return rep % 2, rep % 4


def far_parts(piece, split=1):
    rows = piece.shape[0] // split
    if split == 1 or rows % 16:
        return 1, gather_far(piece)
    side = sides()[0 if split == 2 else 1]
    found = gather_far(lax.dynamic_slice_in_dim(piece, side * rows, rows, 0))
    found[0] = piece
    return split, found


def far_weight(split, found, tie=None):
    if tie is not None:
        found, _ = lax.optimization_barrier((found, tie))
    spec, arrays = [], []
    for offset, part in found.items():
        if split == 1 or not offset:
            spec.append((offset, 1, 0))
            arrays.append(part)
            continue
        spec += [(offset, split, code) for code in range(split)]
        arrays += [part] + [swap(part, "rep", code) for code in range(1, split)]
    return Weight(spec, arrays)


def near_weight(far):
    spec, arrays = list(far.spec), list(far.arrays)
    for (offset, split, code), part in zip(far.spec, far.arrays):
        spec.append((offset | 1, split, code))
        arrays.append(swap(part, "shard", 1))
    if all(part.shape[0] % 16 == 0 for part in arrays):
        return Weight(spec, arrays)
    mine = lax.axis_index("shard")
    rows = arrays[0].shape[0]
    out = jnp.zeros((rows * len(arrays),) + arrays[0].shape[1:], arrays[0].dtype)
    for (offset, _split, _code), part in zip(spec, arrays):
        out = lax.dynamic_update_slice_in_dim(out, part, (mine ^ offset) * rows, 0)
    return Weight([(None, 1, 0)], [out])


def add_plain(left, right):
    return left.astype(f32) + right.astype(f32)


def add_packed(left, right):
    rows = left.shape[-2] - 16
    total = add_plain(left[..., :rows, :], right[..., :rows, :])
    rest = add_plain(left[..., rows:, :], right[..., rows:, :])
    return jnp.concatenate([total[..., : rows - 16, :], total[..., rows - 16 :, :] + rest], -2)


def pack_plain(value):
    return value.astype(bf16)


def pack_packed(value):
    high = value.astype(bf16)
    low = value[..., -16:, :] - high[..., -16:, :].astype(f32)
    return jnp.concatenate([high, low.astype(bf16)], -2)


def reduce_chain(keep, send, steps, add=add_plain, pack=pack_plain):
    mine, rep = lax.axis_index("shard"), lax.axis_index("rep")

    def parts(values, axis, bit):
        kept, sent = [
            pack(add(*(lax.dynamic_index_in_dim(v, b, axis, False) for v in values))) for b in (bit, 1 - bit)
        ]
        return kept, sent

    got = yield send, swap(send, "shard", 1)
    terms = (keep, got)
    mask = 2
    while mask < lax.axis_size("shard"):
        halves = [t.reshape((-1, 2) + t.shape[1:]) for t in terms]
        kept, send = parts(halves, 1, (mine // mask) % 2)
        got = yield send, swap(send, "shard", mask)
        terms = (kept, got)
        mask *= 2
    terms = tuple(t[0] for t in terms)
    joined = None
    more = range(3, lax.axis_size("rep").bit_length() - 1)
    steps = [(bit, "all") for bit in more] + list(steps)
    for at, kind in steps:
        bit = (rep >> at) % 2
        if kind == "split":
            kept, send = parts([t.reshape(2, -1, t.shape[-1]) for t in terms], 0, bit)
            got = yield send, swap(send, "rep", 1 << at)
            terms = (kept, got)
            continue
        value = pack(add(*terms)) if joined is None else joined
        got = yield value, swap(value, "rep", 1 << at)
        if kind == "join":
            last = (value, got, at)
            first, second = jnp.where(bit == 0, value, got), jnp.where(bit == 0, got, value)
            joined = jnp.concatenate([first, second], 0)
        else:
            last = (value, got, None)
            terms, joined = (value, got), None
    return last


class Schedule:
    def __init__(self, ids, rows):
        self.ids = ids
        self.chains = {}
        self.sent = {}
        self.done = {}
        self.final = {}
        self.rows = rows

    def begin(self, name, keep, send, *how):
        chain = reduce_chain(keep, send, *how)
        self.chains[name] = chain
        _sent, self.sent[name] = next(chain)

    def start(self, name, keep, send, names):
        (send,) = self.sync(*(other for other in names if other != name), after=(send,))
        self.begin(name, keep, send, ROUTES[name])
        self.sync(*(other for other in names if other == name), after=(send,))

    def sync(self, *names, after=()):
        for name in names or (None,):
            if name is not None and name not in self.sent:
                continue
            got = self.sent.pop(name, None)
            self.ids, got, after = lax.optimization_barrier((self.ids, got, tuple(after)))
            if got is None:
                continue
            try:
                sent, self.sent[name] = self.chains[name].send(got)
                self.ids, _ = lax.optimization_barrier((self.ids, sent))
            except StopIteration as stop:
                self.done[name] = stop.value
                if name in self.rows:
                    self.final[name] = finish_blocks(stop.value, *self.rows[name])
        return after

    def finish(self, *names):
        for name in names:
            self.sync(name)
        while self.sent:
            self.sync(next(iter(self.sent)))


def add_two(a_ref, b_ref):
    return a_ref[...].astype(f32) + b_ref[...].astype(f32)


def bit_of(place_ref, at):
    return place_ref[4] // (1 << at) % 2


def whole_sum(place_ref, a_ref, b_ref, at):
    if at is None:
        return add_two(a_ref, b_ref)
    first, second = a_ref[...].astype(f32), b_ref[...].astype(f32)
    swapped = bit_of(place_ref, at) == 1
    return jnp.concatenate([jnp.where(swapped, second, first), jnp.where(swapped, first, second)], 0)


def finish_blocks(result, rows, wide):
    value, got, at = result
    if at is None:
        total = value.astype(f32) + got.astype(f32)
    else:
        bit = (lax.axis_index("rep") >> at) % 2
        first, second = jnp.where(bit == 0, value, got), jnp.where(bit == 0, got, value)
        total = jnp.concatenate([first, second], 0).astype(f32)
    if not wide:
        return total
    return jnp.concatenate([total[i : i + rows] for i in range(0, total.shape[0], rows)], 1)


def finish_last_kernel(
    n, lead, time_rows, few, ats, place_ref, ids_ref, a_ref, b_ref, *refs
):
    mine = place_ref[0]
    groups, (qkv_ref, proj_ref, ada_ref, time_ref, *out_refs) = refs[: 2 * N_GROUP], refs[2 * N_GROUP :]
    totals = [whole_sum(place_ref, groups[2 * i], groups[2 * i + 1], at) for i, at in enumerate(ats)]
    for group, total in enumerate(totals):
        for third in range(3):
            col = third * D + group * GROUP
            qkv_ref[:, col : col + GROUP] = total[:lead, third * GROUP : (third + 1) * GROUP]
    proj_ref[...] = totals[1][lead : 2 * lead]
    early = totals[0]
    for i in range(2):
        rows = slice(i * few, (i + 1) * few)
        ada_ref[:, i * D : (i + 1) * D] = add_two(a_ref.at[rows], b_ref.at[rows])
    for i in range(4):
        ada_ref[:, (2 + i) * D : (3 + i) * D] = early[lead + i * few : lead + (i + 1) * few]
    at = 2 * few
    times = add_two(a_ref.at[at : at + time_rows], b_ref.at[at : at + time_rows])
    times = jnp.concatenate([times[:, i * 128 : (i + 1) * 128] for i in range(D // 128)], 0)
    steps = lax.broadcasted_iota(jnp.int32, (STEPS, times.shape[0]), 0)
    hot = jnp.where(steps == ids_ref[...], 1.0, 0.0).astype(f32)
    time_ref[...] = exact(hot, times, ((1,), (0,)))
    at += time_rows
    high = add_two(a_ref.at[at : at + 16], b_ref.at[at : at + 16])
    small = high + add_two(a_ref.at[at + 16 : at + 32], b_ref.at[at + 16 : at + 32])
    first = 0
    for ref, count in zip(out_refs, (1, 1, 4, 1, 6, 1)):
        flat = jnp.concatenate([small[first + i : first + i + 1] for i in range(count)], 1)
        size = count * D // n
        share = flat[:, 0:size]
        for shard in range(1, n):
            share = jnp.where(mine == shard, flat[:, shard * size : (shard + 1) * size], share)
        ref[...] = share.reshape(size)
        first += count


def finish_last(place_ids, ids, last, results, n, time_rows, few):
    lead = D // n
    sizes = [(count * D // n,) for count in (1, 1, 4, 1, 6, 1)]
    shapes = [(lead, 3 * D), (lead, D), (few, 6 * D), (STEPS, 128)] + sizes
    arrays = [ids, *last[:2]] + [a for result in results for a in result[:2]]
    ats = tuple(result[2] for result in results)
    return pl.pallas_call(
        partial(finish_last_kernel, n, lead, time_rows, few, ats),
        grid=(1,),
        in_specs=[SCALAR] + [whole(a.shape) for a in arrays],
        out_specs=[whole(s) for s in shapes],
        out_shape=[jax.ShapeDtypeStruct(s, f32) for s in shapes],
        cost_estimate=cost("finish_last"),
        compiler_params=pltpu.CompilerParams(vmem_limit_bytes=VMEM_LIMIT),
        name="finish_last",
    )(place_ids, *arrays)


ROUTES = {'down': ((0, 'split'), (1, 'all'), (2, 'all'), (0, 'join')),
 'last': ((1, 'all'), (0, 'all'), (2, 'all')),
 'qkv0': ((1, 'split'), (0, 'all'), (2, 'all'), (1, 'join')),
 'qkv1': ((0, 'split'), (1, 'split'), (2, 'all'), (1, 'join'), (0, 'join')),
 'qkv2': ((1, 'split'), (0, 'all'), (2, 'all'), (1, 'join')),
 'up': ((0, 'split'), (1, 'all'), (2, 'all'), (0, 'join'))}
SYNCS = (('up', 'down'),
 ('down',),
 ('up', 'down'),
 (),
 ('up', 'qkv0', 'down'),
 (),
 ('up', 'qkv0', 'qkv1', 'down', 'qkv2'),
 ('qkv0', 'qkv1'),
 ('qkv2',
  'up',
  'qkv0',
  'last',
  'qkv1',
  'qkv2',
  'last',
  'qkv1',
  'up',
  'qkv0',
  'qkv2',
  'last',
  'qkv1',
  'qkv0',
  'last',
  'qkv2',
  'qkv1',
  'qkv1',
  'qkv2',
  'last'),
 ('down',))


def on_device(
    hidden_in,
    mask_ids,
    time_ids,
    time_table,
    w_qkv,
    w_proj,
    w_up,
    w_down,
    w_ada,
    gain_attn,
    gain_mlp,
    bias_up,
    bias_down,
    bias_ada,
    mask_embed,
    cotangent,
):
    n = lax.axis_size("shard")
    mine = lax.axis_index("shard")
    core = mine % 2
    pair = (lax.axis_index("rep") * n + mine) // 2
    ids = jnp.stack([mine, core, pair, *sides()]).astype(jnp.int32)
    barrier = lax.optimization_barrier

    vectors = (gain_attn, gain_mlp, bias_up, bias_down, mask_embed, bias_ada)
    lengths = [v.shape[0] for v in vectors]
    row_far = gather_far(pack_call(vectors))
    local = jnp.arange(PROMPT, dtype=jnp.int32)
    positions = jnp.where(local < HALF, core * HALF + local, PROMPT + local % CLEN).astype(f32)
    freqs = 10000.0 ** (-(2.0 * jnp.arange(HDIM // 2, dtype=f32)) / HDIM)
    lanes = jnp.tile(freqs, 4)
    angles = positions[:, None] * lanes[None, :]
    sign = jnp.where(jnp.arange(128) % HDIM < HDIM // 2, -1.0, 1.0).astype(f32)
    cosine, sine = jnp.cos(angles), jnp.sin(angles) * sign[None, :]
    mask = (mask_ids == 1).astype(f32)[:, None]
    ada_far = far_weight(*far_parts(w_ada), (cosine, sine, mask))
    qkv_far = far_weight(*far_parts(w_qkv, 4))
    ada_weight = near_weight(ada_far)
    rows = gather_near(row_far)
    (proj_own, up_own, down_own), _ = barrier(((w_proj, w_up, w_down), ada_far.arrays))
    up_split, up_found = far_parts(up_own, 4)
    proj_far = far_weight(*far_parts(proj_own))
    down_split, down_found = far_parts(down_own, 2)

    block = jnp.arange(CONTS, dtype=jnp.int32)
    seg = jnp.where(block < CONTS // 2, 0, 1 + core * (CONTS // 2) + block - CONTS // 2)
    my_times = lax.dynamic_slice_in_dim(time_ids, pair, 1, 0)
    times = jnp.sum(jnp.where(seg[:, None] == jnp.arange(CONTS + 1, dtype=jnp.int32)[None], my_times, 0), 1)
    mods, cond, ada_mat, attn_gain, mlp_gain, up_bias, down_bias, embed, x = mods_call(
        times, ids, time_table, hidden_in, mask, ada_weight, rows, lengths
    )

    qkv_weight = near_weight(qkv_far.tied(mods))
    q, kvp, kvc = qkv_call(ids, x, cosine, sine, qkv_weight)
    kvp, up_found = barrier((kvp, up_found))
    kvr = swap(kvp, "shard", 1)
    up_far = far_weight(up_split, up_found)
    early = attn_fwd(0, 4, q, kvp, kvc, kvr)
    early, up_far.arrays, proj_far.arrays, down_found = barrier((early, up_far.arrays, proj_far.arrays, down_found))
    proj_weight = near_weight(proj_far.tied(early))
    up_weight = near_weight(up_far.tied(early))
    early, _ = barrier((early, proj_weight.arrays))
    down_far = far_weight(down_split, down_found)
    soon = near_weight(Weight(down_far.spec[:2], down_far.arrays[:2]))
    late = Weight(down_far.spec[2:], down_far.arrays[2:])
    attn_o, lse = attn_fwd(4, PAIRS - 4, q, kvp, kvc, kvr, early)
    attn_o, late.arrays = barrier((attn_o, late.arrays))
    down_weight = near_weight(late.tied(attn_o))
    down_weight = Weight(soon.spec + down_weight.spec, soon.arrays + down_weight.arrays)
    attn_proj, middle, x_mlp, act, g_pre, g_mlp, g_bias_up, g_bias_down = up_call(
        ids, attn_o, hidden_in, mask, embed, mods, mlp_gain, up_bias, cotangent, proj_weight, up_weight, down_weight
    )
    plan = Schedule(ids, {"down": (FF // n // 2, False), "up": (D // n, True)})
    down_keep, down_send = down_grad_any(plan.ids, act, g_mlp, n)
    plan.begin("down", down_keep, down_send, ROUTES["down"])
    plan.sync(after=(down_keep,))
    up_keep, up_send = wgrad_call(plan.ids, x_mlp, g_pre, n, "up_grad")
    plan.start("up", up_keep, up_send, SYNCS[9])
    block_out, d_middle, g_att, g_o, stat2, g_gain_mlp = down_call(
        plan.ids, act, g_pre, middle, attn_proj, cotangent, mods, mlp_gain, down_bias, proj_weight, up_weight, down_weight
    )
    plan.sync(*SYNCS[0], after=(g_o,))
    parts, others = [], []

    def backward(group, names):
        gq, gc, dp, dr = attn_bwd(plan.ids, group, q, kvp, kvc, kvr, g_o, lse, cosine, sine)
        parts.append((gq, gc, dp))
        (dr,) = plan.sync(*names, after=(dr,))
        others.append(swap(dr, "shard", 1))

    grads = []

    def weight(group, proj, ada, names):
        keep, send, total = qkv_grad_call(
            plan.ids, x, *parts[group], others[group], cosine, sine, n, f"qkv_grad{group}", proj, ada
        )
        grads.append(total)
        plan.start(f"qkv{group}", keep, send, names)

    backward(0, SYNCS[1])
    backward(1, SYNCS[2])
    weight(0, None, (cond, stat2), SYNCS[3])
    backward(2, SYNCS[4])
    weight(1, (attn_o, g_att), None, SYNCS[5])
    weight(2, None, None, SYNCS[6])
    grad_hidden, stat1, g_gain_attn, g_mask = start_call(
        plan.ids, hidden_in, mask, embed, mods, attn_gain, d_middle, grads, qkv_weight
    )
    plan.sync(*SYNCS[7], after=(stat1,))
    time_rows = -(-time_ids.size // 6 // 8) * 8
    vector_grads = (g_gain_attn, g_gain_mlp, g_bias_up, g_bias_down, g_mask)
    keep, send = last_call(plan.ids, cond, ada_mat, stat1, stat2, vector_grads, n, time_rows)
    plan.begin("last", keep, send, ROUTES["last"], add_packed, pack_packed)
    plan.finish(*SYNCS[8])

    done = plan.done
    few = w_ada.shape[0]
    flat_ids = time_ids.reshape(1, -1)
    flat_ids = jnp.pad(flat_ids, ((0, 0), (0, 6 * time_rows - flat_ids.shape[1])), constant_values=-1)
    results = [done[f"qkv{g}"] for g in range(N_GROUP)]
    grad_qkv, grad_proj, grad_ada, grad_time, *shares = finish_last(
        plan.ids, flat_ids, done["last"], results, n, time_rows, few
    )
    return (block_out, grad_hidden, grad_time, grad_qkv, grad_proj, plan.final["up"], plan.final["down"], grad_ada, *shares)


def solution(mesh):
    in_specs = (
        P(("rep", "shard"), None),
        P(("rep", "shard")),
        P(),
        P(),
        P("shard", None),
        P("shard", None),
        P("shard", None),
        P("shard", None),
        P("shard", None),
        P("shard"),
        P("shard"),
        P("shard"),
        P("shard"),
        P("shard"),
        P("shard"),
        P(("rep", "shard"), None),
    )
    out_specs = (
        P(("rep", "shard"), None),
        P(("rep", "shard"), None),
        P(),
        P("shard", None),
        P("shard", None),
        P("shard", None),
        P("shard", None),
        P("shard", None),
        P("shard"),
        P("shard"),
        P("shard"),
        P("shard"),
        P("shard"),
        P("shard"),
    )
    return jax.shard_map(
        on_device, mesh=mesh, in_specs=in_specs, out_specs=out_specs, check_vma=False
    )
```

```python
from functools import partial

import jax
import jax.numpy as jnp
from jax import lax
from jax.experimental import pallas as pl
from jax.experimental.pallas import tpu as pltpu
from jax.sharding import PartitionSpec as P

D = 768
HEADS = 12
HDIM = 64
FF = 3072
STEPS = 1000
CLEN = 128
CONTS = 8
PROMPT = 1024
HALF = PROMPT // 2
PAIRS = HEADS // 2
GROUP = 256
N_GROUP = D // GROUP
TILE = 256
SUB = TILE // CLEN
CHUNK = 512
eps_norm = 1e-06
bf16 = jnp.bfloat16
f32 = jnp.float32
VMEM_LIMIT = 62 * 2**20
COSTS = {'attn_bwd0': 52.5,
 'attn_bwd1': 52.8,
 'attn_bwd2': 53.4,
 'attn_fwd0': 55.5,
 'attn_fwd2': 55.8,
 'attn_fwd4': 30.9,
 'combine': 4.8,
 'down_grad': 31.5,
 'finish_down': 8.4,
 'finish_last': 12.6,
 'finish_qkv': 9.0,
 'finish_up': 11.7,
 'last': 14.7,
 'mlp_down': 75.6,
 'mlp_up': 74.4,
 'mods': 19.5,
 'pack': 4.2,
 'qkv': 25.5,
 'qkv_grad0': 25.5,
 'qkv_grad01': 46.5,
 'qkv_grad1': 21.9,
 'qkv_grad12': 39,
 'qkv_grad2': 16.8,
 'start_grad': 35.1,
 'up_grad': 27.6,
 'wide_grad': 27}


def cost(name):
    return pl.CostEstimate(flops=int(COSTS.get(name, 1.0) * 1e9), bytes_accessed=0, transcendentals=0)


def nt(left, right):
    return lax.dot_general(left, right, (((1,), (1,)), ((), ())), preferred_element_type=f32)


def nn(left, right):
    return lax.dot_general(left, right, (((1,), (0,)), ((), ())), preferred_element_type=f32)


def tn(left, right):
    return lax.dot_general(left, right, (((0,), (0,)), ((), ())), preferred_element_type=f32)


def exact(left, right, contract):
    return lax.dot_general(
        left, right, (contract, ((), ())), preferred_element_type=f32, precision=lax.Precision.HIGHEST
    )


def three_parts(values):
    high = values.astype(bf16).astype(f32)
    rest = values - high
    middle = rest.astype(bf16).astype(f32)
    return jnp.concatenate([high, middle, rest - middle], 0).astype(bf16)


def wide_nt(left, right):
    rows = left.shape[0]
    total = nt(three_parts(left), right)
    return total[:rows] + total[rows : 2 * rows] + total[2 * rows :]


def wide_tn(left, right):
    return tn(jnp.concatenate([left, left, left], 0).astype(bf16), three_parts(right))


def layer_norm(values):
    mean_value = jnp.mean(values, -1, keepdims=True)
    centered = values - mean_value
    inv_std = lax.rsqrt(jnp.mean(centered * centered, -1, keepdims=True) + eps_norm)
    return (centered * inv_std, inv_std)


def norm_back(gradient, normed, inv_std):
    return inv_std * (
        gradient
        - jnp.mean(gradient, -1, keepdims=True)
        - normed * jnp.mean(gradient * normed, -1, keepdims=True)
    )


def rotate(values, cosine, sine):
    lane = lax.broadcasted_iota(jnp.int32, cosine.shape, 1) % HDIM
    out = []
    for col in range(0, values.shape[1], 128):
        part = values[:, col : col + 128]
        other = jnp.where(lane < HDIM // 2, pltpu.roll(part, 96, 1), pltpu.roll(part, 32, 1))
        out.append(part * cosine + other * sine)
    return out[0] if len(out) == 1 else jnp.concatenate(out, 1)


def whole(shape):
    return pl.BlockSpec(shape, lambda *_: (0,) * len(shape))


ANY = pl.BlockSpec(memory_space=pl.ANY)
SCALAR = pl.BlockSpec(memory_space=pltpu.SMEM)


def place(pieces, spec, place_ref, target, sem):
    mine = place_ref[0]
    copies = []
    for (offset, split, part), piece in zip(spec, pieces):
        rows = piece.shape[0]
        if offset is None:
            where = target
        else:
            start = (mine ^ offset) * (split * rows)
            if split > 1:
                start = start + (place_ref[3 if split == 2 else 4] ^ part) * rows
            where = target.at[pl.ds(pl.multiple_of(start, 16), rows)]
        copies.append(pltpu.make_async_copy(piece, where, sem))
    return copies


class Weight:
    def __init__(self, spec, arrays):
        self.spec = tuple(spec)
        self.arrays = list(arrays)
        self.count = len(self.arrays)

    def tied(self, *values):
        arrays, _ = lax.optimization_barrier((self.arrays, values))
        return Weight(self.spec, arrays)


def qkv_kernel(
    spec, place_ref, x_ref, cos_ref, sin_ref, *rest
):
    n = len(spec)
    pieces = rest[:n]
    q_ref, kvp_ref, kvc_ref, w_ref, sem = rest[n:]
    step = pl.program_id(0)

    @pl.when(step == 0)
    def _():
        copies = place(pieces, spec, place_ref, w_ref, sem)
        for copy in copies:
            copy.start()
        for copy in copies:
            copy.wait()

    x = x_ref[...]
    cosine, sine = cos_ref[...], sin_ref[...]

    def part(third):
        return nn(x, w_ref[:, pl.ds(pl.multiple_of(third * D + step * GROUP, 128), GROUP)])

    q_ref[...] = (rotate(part(0), cosine, sine) * HDIM**-0.5).astype(bf16)
    k = rotate(part(1), cosine, sine).astype(bf16)
    kvp_ref[0], kvc_ref[0] = k[:HALF], k[HALF:]
    v = part(2).astype(bf16)
    kvp_ref[1], kvc_ref[1] = v[:HALF], v[HALF:]


def qkv_call(place_ids, x, cosine, sine, weight):
    n = weight.count
    width = weight.arrays[0].shape[1]
    half = pl.BlockSpec((2, HALF, GROUP), lambda g: (0, 0, g))
    return pl.pallas_call(
        partial(qkv_kernel, weight.spec),
        grid=(N_GROUP,),
        in_specs=[
            SCALAR,
            whole((PROMPT, D)),
            whole((PROMPT, 128)),
            whole((PROMPT, 128)),
        ]
        + [ANY] * n,
        out_specs=[pl.BlockSpec((PROMPT, GROUP), lambda g: (0, g)), half, half],
        out_shape=[
            jax.ShapeDtypeStruct((PROMPT, D), bf16),
            jax.ShapeDtypeStruct((2, HALF, D), bf16),
            jax.ShapeDtypeStruct((2, HALF, D), bf16),
        ],
        scratch_shapes=[pltpu.VMEM((D, width), bf16), pltpu.SemaphoreType.DMA],
        compiler_params=pltpu.CompilerParams(vmem_limit_bytes=VMEM_LIMIT),
        cost_estimate=cost("qkv"),
        name="qkv",
    )(place_ids, x, cosine, sine, *weight.arrays)


def head_only(values, head):
    lane = lax.broadcasted_iota(jnp.int32, values.shape, 1)
    return jnp.where((lane < HDIM) if head == 0 else (lane >= HDIM), values, jnp.zeros_like(values))


def key_parts(prompt, other, own, rows, first):
    parts = [nt(prompt, rows), nt(other, rows)]
    if not first:
        cols = range(0, HALF, CLEN)
        parts.append(
            jnp.concatenate([nt(own[c : c + CLEN], rows[c : c + CLEN]) for c in cols], 1)
        )
    return parts


def attn_fwd_kernel(q_ref, kvp_ref, kvc_ref, kvr_ref, o_ref, lse_ref):
    kp, kc, kr = kvp_ref[0], kvc_ref[0], kvr_ref[0]
    vp_t, vc_t, vr_t = kvp_ref[1].T, kvc_ref[1].T, kvr_ref[1].T
    for start in (0, HALF):
        outs = []
        q_tile = q_ref[pl.ds(start, HALF), :]
        for head in range(2):
            lanes = slice(HDIM * head, HDIM * (head + 1))
            scores = key_parts(kp, kr, kc, head_only(q_tile, head), start == 0)
            top = jnp.max(scores[0], 0, keepdims=True)
            for part in scores[1:]:
                top = jnp.maximum(top, jnp.max(part, 0, keepdims=True))
            powers = [jnp.exp(part - top) for part in scores]
            total = jnp.sum(powers[0], 0, keepdims=True)
            for part in powers[1:]:
                total = total + jnp.sum(part, 0, keepdims=True)
            lse_ref[0, pl.ds(head, 1), pl.ds(start, HALF)] = top + jnp.log(total)
            scale = 1.0 / total
            probs = [(part * scale).astype(bf16) for part in powers]
            out = nn(vp_t[lanes], probs[0]) + nn(vr_t[lanes], probs[1])
            if start:
                cols = [slice(c, c + CLEN) for c in range(0, HALF, CLEN)]
                out = out + jnp.concatenate([nn(vc_t[lanes, c], probs[2][:, c]) for c in cols], 1)
            outs.append(out)
        o_ref[pl.ds(start, HALF), :] = jnp.concatenate(outs, 0).T.astype(bf16)


def pair_block(rows, first=0):
    return pl.BlockSpec((rows, 2 * HDIM), lambda pair: (0, first + pair))


def pair_half(first=0):
    return pl.BlockSpec((2, HALF, 2 * HDIM), lambda pair: (0, 0, first + pair))


def lse_block(first=0):
    return pl.BlockSpec((1, 2, PROMPT), lambda pair: (first + pair, 0, 0))


def attn_fwd(first, pairs, q, kvp, kvc, kvr, before=None):
    inputs = (q, kvp, kvc, kvr)
    in_specs = [pair_block(PROMPT, first)] + [pair_half(first)] * 3
    body = attn_fwd_kernel
    aliases = {}
    if before is not None:
        inputs += tuple(before)
        in_specs += [ANY, ANY]
        aliases = {4: 0, 5: 1}

        def body(q_ref, kvp_ref, kvc_ref, kvr_ref, _o, _lse, o_ref, lse_ref):
            attn_fwd_kernel(q_ref, kvp_ref, kvc_ref, kvr_ref, o_ref, lse_ref)

    return pl.pallas_call(
        body,
        grid=(pairs,),
        in_specs=in_specs,
        out_specs=[pair_block(PROMPT, first), lse_block(first)],
        out_shape=[
            jax.ShapeDtypeStruct((PROMPT, D), bf16),
            jax.ShapeDtypeStruct((PAIRS, 2, PROMPT), f32),
        ],
        input_output_aliases=aliases,
        compiler_params=pltpu.CompilerParams(vmem_limit_bytes=VMEM_LIMIT),
        cost_estimate=cost(f"attn_fwd{first}"),
        name=f"attn_fwd{first}",
    )(*inputs)


def attn_bwd_kernel(
    _ids, q_ref, kvp_ref, kvc_ref, kvr_ref, g_ref, lse_ref, cos_ref, sin_ref, gq_ref, gc_ref, dp_ref, dr_ref
):
    kp, kc, kr = kvp_ref[0], kvc_ref[0], kvr_ref[0]
    vp, vc, vr = kvp_ref[1], kvc_ref[1], kvr_ref[1]
    kp_t, kc_t, kr_t = kp.T, kc.T, kr.T
    first = lax.broadcasted_iota(jnp.int32, (HALF, 2 * HDIM), 1) < HDIM
    for start in (0, HALF):
        tile = pl.ds(start, HALF)
        q_tile, g_tile = q_ref[tile, :], g_ref[tile, :]
        cols = [slice(c, c + CLEN) for c in range(0, HALF, CLEN)]
        dqs, dks, dvs = [], [], []
        for head in range(2):
            lanes = slice(HDIM * head, HDIM * (head + 1))
            scores = key_parts(kp, kr, kc, head_only(q_tile, head), start == 0)
            dps = key_parts(vp, vr, vc, head_only(g_tile, head), start == 0)
            lse = lse_ref[0, pl.ds(head, 1), tile]
            probs = [jnp.exp(part - lse) for part in scores]
            row_dot = jnp.sum(probs[0] * dps[0], 0, keepdims=True)
            for p_part, d_part in zip(probs[1:], dps[1:]):
                row_dot = row_dot + jnp.sum(p_part * d_part, 0, keepdims=True)
            ds = [(p * (d - row_dot)).astype(bf16) for p, d in zip(probs, dps)]
            probs = [p.astype(bf16) for p in probs]
            dq = nn(kp_t[lanes], ds[0]) + nn(kr_t[lanes], ds[1])
            dk = [nn(ds[0], q_tile), nn(ds[1], q_tile)]
            dv = [nn(probs[0], g_tile), nn(probs[1], g_tile)]
            if start:
                dq = dq + jnp.concatenate([nn(kc_t[lanes, c], ds[2][:, c]) for c in cols], 1)
                dk.append(jnp.concatenate([nn(ds[2][:, c], q_tile[c]) for c in cols], 0))
                dv.append(jnp.concatenate([nn(probs[2][:, c], g_tile[c]) for c in cols], 0))
            dqs.append(dq)
            dks.append(dk)
            dvs.append(dv)
        cosine, sine = cos_ref[tile, :], sin_ref[tile, :]
        dq = jnp.concatenate(dqs, 0).T * HDIM**-0.5
        gq_ref[tile, :] = rotate(dq, cosine, -sine).astype(bf16)
        for which, parts in enumerate((dks, dvs)):
            merged = [jnp.where(first, a, b) for a, b in zip(*parts)]
            if start:
                dp_ref[which] += merged[0]
                dr_ref[which] += merged[1]
                last = merged[2] if which else rotate(merged[2], cosine, -sine)
                gc_ref[which] = last.astype(bf16)
            else:
                dp_ref[which] = merged[0]
                dr_ref[which] = merged[1]


def attn_bwd(ids, group, q, kvp, kvc, kvr, g, lse, cosine, sine):
    pairs = GROUP // (2 * HDIM)
    first = group * pairs
    return pl.pallas_call(
        attn_bwd_kernel,
        grid=(pairs,),
        in_specs=[SCALAR, pair_block(PROMPT, first)]
        + [pair_half(first)] * 3
        + [pair_block(PROMPT, first), lse_block(first), whole((PROMPT, 128)), whole((PROMPT, 128))],
        out_specs=[pair_block(PROMPT), pair_half(), pair_half(), pair_half()],
        out_shape=[
            jax.ShapeDtypeStruct((PROMPT, GROUP), bf16),
            jax.ShapeDtypeStruct((2, HALF, GROUP), bf16),
            jax.ShapeDtypeStruct((2, HALF, GROUP), f32),
            jax.ShapeDtypeStruct((2, HALF, GROUP), f32),
        ],
        compiler_params=pltpu.CompilerParams(vmem_limit_bytes=VMEM_LIMIT),
        cost_estimate=cost(f"attn_bwd{group}"),
        name=f"attn_bwd{group}",
    )(ids, q, kvp, kvc, kvr, g, lse, cosine, sine)


def up_kernel(
    specs,
    place_ref,
    o_ref,
    hid_ref,
    mask_ref,
    embed_ref,
    mods_ref,
    gain_ref,
    bias_ref,
    cot_ref,
    *rest,
):
    pieces, rest = take(specs, rest)
    ap_ref, mid_ref, x_ref, act_ref, gpre_ref, gmlp_ref, gbu_ref, gbd_ref = rest[:8]
    proj_ref, up_ref, down_ref, sems = rest[8:]
    step = pl.program_id(0)
    targets = (proj_ref, up_ref, down_ref)
    copies = [
        place(part, spec, place_ref, target, sems.at[i])
        for i, (part, spec, target) in enumerate(zip(pieces, specs, targets))
    ]

    @pl.when(step == 0)
    def _():
        for group in copies:
            for copy in group:
                copy.start()
        gbu_ref[...] = jnp.zeros_like(gbu_ref)
        gbd_ref[...] = jnp.zeros_like(gbd_ref)
        for copy in copies[0]:
            copy.wait()

    attn_proj = nn(o_ref[...], proj_ref[...])
    ap_ref[...] = attn_proj
    for sub in range(SUB):
        rows = slice(sub * CLEN, (sub + 1) * CLEN)
        row = pl.ds(step * SUB + sub, 1)
        start = jnp.where(mask_ref[rows, :] > 0.5, embed_ref[...], hid_ref[rows, :].astype(f32))
        middle = start + mods_ref[row, 2 * D : 3 * D] * attn_proj[rows]
        mid_ref[rows, :] = middle
        normed, _inv = layer_norm(middle)
        shift, scale = mods_ref[row, 3 * D : 4 * D], mods_ref[row, 4 * D : 5 * D]
        x_ref[rows, :] = (normed * gain_ref[...] * (1.0 + scale) + shift).astype(bf16)
        g_mlp = (mods_ref[row, 5 * D : 6 * D] * cot_ref[rows, :].astype(f32)).astype(bf16)
        gmlp_ref[rows, :] = g_mlp
        gbd_ref[...] += jnp.sum(g_mlp.astype(f32), 0, keepdims=True)

    @pl.when(step == 0)
    def _():
        for group in copies[1:]:
            for copy in group:
                copy.wait()

    x, g_mlp = x_ref[...], gmlp_ref[...]
    root = (2.0 / jnp.pi) ** 0.5
    for col in range(0, FF, CHUNK):
        cols = slice(col, col + CHUNK)
        pre = nn(x, up_ref[:, cols]) + bias_ref[:, cols]
        square = pre * pre
        curve = jnp.tanh(root * pre * (1.0 + 0.044715 * square))
        half_up = 0.5 * (1.0 + curve)
        act_ref[:, cols] = (pre * half_up).astype(bf16)
        slope = half_up + (0.5 * root) * pre * (1.0 - curve * curve) * (1.0 + 0.134145 * square)
        g_pre = (nt(g_mlp, down_ref[cols, :]) * slope).astype(bf16)
        gpre_ref[:, cols] = g_pre
        gbu_ref[:, cols] += jnp.sum(g_pre.astype(f32), 0, keepdims=True)


def take(specs, refs):
    pieces = []
    for spec in specs:
        pieces.append(refs[: len(spec)])
        refs = refs[len(spec) :]
    return pieces, refs


def tile_block(width):
    return pl.BlockSpec((TILE, width), lambda step: (step, 0))


def weight_scratch():
    return [
        pltpu.VMEM((D, D), bf16),
        pltpu.VMEM((D, FF), bf16),
        pltpu.VMEM((FF, D), bf16),
        pltpu.SemaphoreType.DMA((3,)),
    ]


def up_call(place_ids, attn_o, hidden, mask, embed, mods, gain, bias, cot, proj, up, down):
    weights = (proj, up, down)
    n = sum(w.count for w in weights)
    specs = tuple(w.spec for w in weights)
    arrays = [a for w in weights for a in w.arrays]
    rows = PROMPT
    return pl.pallas_call(
        partial(up_kernel, specs),
        grid=(rows // TILE,),
        in_specs=[
            SCALAR,
            tile_block(D),
            tile_block(D),
            tile_block(1),
            whole((1, D)),
            whole(mods.shape),
            whole((1, D)),
            whole((1, FF)),
            tile_block(D),
        ]
        + [ANY] * n,
        out_specs=[tile_block(D)] * 3
        + [tile_block(FF)] * 2
        + [tile_block(D), whole((1, FF)), whole((1, D))],
        out_shape=[
            jax.ShapeDtypeStruct((rows, D), f32),
            jax.ShapeDtypeStruct((rows, D), f32),
            jax.ShapeDtypeStruct((rows, D), bf16),
            jax.ShapeDtypeStruct((rows, FF), bf16),
            jax.ShapeDtypeStruct((rows, FF), bf16),
            jax.ShapeDtypeStruct((rows, D), bf16),
            jax.ShapeDtypeStruct((1, FF), f32),
            jax.ShapeDtypeStruct((1, D), f32),
        ],
        scratch_shapes=weight_scratch(),
        compiler_params=pltpu.CompilerParams(vmem_limit_bytes=VMEM_LIMIT),
        cost_estimate=cost("mlp_up"),
        name="mlp_up",
    )(place_ids, attn_o, hidden, mask, embed, mods, gain, bias, cot, *arrays)


def down_kernel(specs, place_ref, act_ref, gpre_ref, mid_ref, ap_ref, cot_ref, mods_ref, gain_ref, bias_ref, *rest):
    pieces, rest = take(specs, rest)
    out_ref, dmid_ref, gatt_ref, go_ref, stat_ref, ggain_ref = rest[:6]
    proj_ref, up_ref, down_ref, sems = rest[6:]
    step = pl.program_id(0)
    targets = (proj_ref, up_ref, down_ref)
    copies = [
        place(part, spec, place_ref, target, sems.at[i])
        for i, (part, spec, target) in enumerate(zip(pieces, specs, targets))
    ]

    @pl.when(step == 0)
    def _():
        for i in (2, 1, 0):
            for copy in copies[i]:
                copy.start()
        ggain_ref[...] = jnp.zeros_like(ggain_ref)
        for copy in copies[2]:
            copy.wait()

    mlp_out = nn(act_ref[...], down_ref[...]) + bias_ref[...]

    @pl.when(step == 0)
    def _():
        for i in (1, 0):
            for copy in copies[i]:
                copy.wait()

    g_n = nt(gpre_ref[...], up_ref[...])
    for sub in range(SUB):
        rows = slice(sub * CLEN, (sub + 1) * CLEN)
        row = pl.ds(step * SUB + sub, 1)
        middle, cot, grad = mid_ref[rows, :], cot_ref[rows, :].astype(f32), g_n[rows]
        gate_attn, gate_mlp = mods_ref[row, 2 * D : 3 * D], mods_ref[row, 5 * D : 6 * D]
        scale = 1.0 + mods_ref[row, 4 * D : 5 * D]
        out_ref[rows, :] = (middle + gate_mlp * mlp_out[rows]).astype(bf16)
        normed, inv_std = layer_norm(middle)
        along = jnp.sum(grad * normed, 0, keepdims=True)
        ggain_ref[...] += along * scale
        d_middle = cot + norm_back(grad * (scale * gain_ref[...]), normed, inv_std)
        dmid_ref[rows, :] = d_middle
        gatt_ref[rows, :] = (gate_attn * d_middle).astype(bf16)
        stat_ref[row, 0:D] = jnp.sum(d_middle * ap_ref[rows, :], 0, keepdims=True)
        stat_ref[row, D : 2 * D] = jnp.sum(grad, 0, keepdims=True)
        stat_ref[row, 2 * D : 3 * D] = along * gain_ref[...]
        stat_ref[row, 3 * D : 4 * D] = jnp.sum(cot * mlp_out[rows], 0, keepdims=True)
    go_ref[...] = nt(gatt_ref[...], proj_ref[...]).astype(bf16)


def down_call(place_ids, act, gpre, middle, attn_proj, cot, mods, gain, bias, proj, up, down):
    weights = (proj, up, down)
    n = sum(w.count for w in weights)
    specs = tuple(w.spec for w in weights)
    arrays = [a for w in weights for a in w.arrays]
    rows = PROMPT
    return pl.pallas_call(
        partial(down_kernel, specs),
        grid=(rows // TILE,),
        in_specs=[
            SCALAR,
            tile_block(FF),
            tile_block(FF),
            tile_block(D),
            tile_block(D),
            tile_block(D),
            whole(mods.shape),
            whole((1, D)),
            whole((1, D)),
        ]
        + [ANY] * n,
        out_specs=[tile_block(D)] * 4 + [whole((CONTS, 4 * D)), whole((1, D))],
        out_shape=[
            jax.ShapeDtypeStruct((rows, D), bf16),
            jax.ShapeDtypeStruct((rows, D), f32),
            jax.ShapeDtypeStruct((rows, D), bf16),
            jax.ShapeDtypeStruct((rows, D), bf16),
            jax.ShapeDtypeStruct((CONTS, 4 * D), f32),
            jax.ShapeDtypeStruct((1, D), f32),
        ],
        scratch_shapes=weight_scratch(),
        compiler_params=pltpu.CompilerParams(vmem_limit_bytes=VMEM_LIMIT),
        cost_estimate=cost("mlp_down"),
        name="mlp_down",
    )(place_ids, act, gpre, middle, attn_proj, cot, mods, gain, bias, *arrays)


def split_store(total, keep_ref, send_ref, core, lead, at):
    for pair in range(total.shape[0] // lead // 2):
        even = total[2 * pair * lead : (2 * pair + 1) * lead].astype(bf16)
        odd = total[(2 * pair + 1) * lead : (2 * pair + 2) * lead].astype(bf16)
        keep_ref[pair, at : at + lead, :] = jnp.where(core == 0, even, odd)
        send_ref[pair, at : at + lead, :] = jnp.where(core == 0, odd, even)


def wgrad_kernel(lead, place_ref, left_ref, right_ref, keep_ref, send_ref):
    split_store(tn(left_ref[...], right_ref[...]), keep_ref, send_ref, place_ref[1], lead, 0)


def wgrad_call(place_ids, left, right, n, name):
    lead = D // n
    blocks = right.shape[1] // D
    out = pl.BlockSpec((n // 2, lead, D), lambda j: (0, j, 0))
    shape = jax.ShapeDtypeStruct((n // 2, blocks * lead, D), bf16)
    return pl.pallas_call(
        partial(wgrad_kernel, lead),
        grid=(blocks,),
        in_specs=[SCALAR, whole((PROMPT, D)), pl.BlockSpec((PROMPT, D), lambda j: (0, j))],
        out_specs=[out, out],
        out_shape=[shape, shape],
        compiler_params=pltpu.CompilerParams(vmem_limit_bytes=VMEM_LIMIT),
        cost_estimate=cost(name),
        name=name,
    )(place_ids, left, right)


def down_grad_kernel(_ids, left_ref, right_ref, keep_ref, send_ref):
    half = pl.num_programs(0) // 2
    total = tn(left_ref[...], right_ref[...]).astype(bf16)

    @pl.when(pl.program_id(0) < half)
    def _():
        send_ref[0] = total

    @pl.when(pl.program_id(0) >= half)
    def _():
        keep_ref[0] = total


def down_grad_call(place_ids, act, g_mlp, n):
    rows = FF // n
    half = n // 2

    def shard(j, ids):
        core = ids[1]
        return 0, jnp.where(j < half, 2 * j + 1 - core, 2 * (j - half) + core)

    shape = jax.ShapeDtypeStruct((half, rows, D), bf16)
    return pl.pallas_call(
        down_grad_kernel,
        grid_spec=pltpu.PrefetchScalarGridSpec(
            num_scalar_prefetch=1,
            grid=(n,),
            in_specs=[pl.BlockSpec((PROMPT, rows), shard), pl.BlockSpec((PROMPT, D), lambda j, ids: (0, 0))],
            out_specs=[
                pl.BlockSpec((1, rows, D), lambda j, ids: (jnp.maximum(j - half, 0), 0, 0)),
                pl.BlockSpec((1, rows, D), lambda j, ids: (jnp.minimum(j, half - 1), 0, 0)),
            ],
        ),
        out_shape=[shape, shape],
        compiler_params=pltpu.CompilerParams(vmem_limit_bytes=VMEM_LIMIT),
        cost_estimate=cost("down_grad"),
        name="down_grad",
    )(place_ids, act, g_mlp)


def down_grad_any(place_ids, act, g_mlp, n):
    if (FF // n) % 128 == 0 and n == 4:
        return down_grad_call(place_ids, act, g_mlp, n)
    full = wide_grad_call(act, g_mlp)
    core = lax.axis_index("shard") % 2
    parts = full.reshape(n // 2, 2, -1, D)
    keep = lax.dynamic_index_in_dim(parts, core, 1, False)
    return keep, lax.dynamic_index_in_dim(parts, 1 - core, 1, False)


def wide_grad_kernel(left_ref, right_ref, out_ref):
    out_ref[...] = tn(left_ref[...], right_ref[...]).astype(bf16)


def wide_grad_call(act, g_mlp):
    return pl.pallas_call(
        wide_grad_kernel,
        grid=(FF // D,),
        in_specs=[pl.BlockSpec((PROMPT, D), lambda j: (0, j)), whole((PROMPT, D))],
        out_specs=pl.BlockSpec((D, D), lambda j: (j, 0)),
        out_shape=jax.ShapeDtypeStruct((FF, D), bf16),
        compiler_params=pltpu.CompilerParams(vmem_limit_bytes=VMEM_LIMIT),
        name="wide_grad",
    )(act, g_mlp)


def qkv_grad_kernel(lead, with_proj, with_ada, place_ref, x_ref, gq_ref, gc_ref, dp_ref, got_ref, cos_ref, sin_ref, *rest):
    keep_ref, send_ref, g_ref = rest[-3:]
    core = place_ref[1]
    g_ref[:, 0:GROUP] = gq_ref[...]
    total_k = dp_ref[0] + got_ref[0].astype(f32)
    total_v = dp_ref[1] + got_ref[1].astype(f32)
    g_ref[0:HALF, GROUP : 2 * GROUP] = rotate(total_k, cos_ref[...], -sin_ref[...]).astype(bf16)
    g_ref[0:HALF, 2 * GROUP : 3 * GROUP] = total_v.astype(bf16)
    g_ref[HALF:PROMPT, GROUP : 2 * GROUP] = gc_ref[0]
    g_ref[HALF:PROMPT, 2 * GROUP : 3 * GROUP] = gc_ref[1]
    split_store(tn(x_ref[...], g_ref[...]), keep_ref, send_ref, core, lead, 0)
    at = lead
    if with_proj:
        split_store(tn(rest[0][...], rest[1][...]), keep_ref, send_ref, core, lead, at)
        at += lead
        rest = rest[2:]
    if with_ada:
        cond = rest[0][...]
        silu = (cond / (1.0 + jnp.exp(-cond))).astype(bf16).astype(f32)
        few = cond.shape[1] * lead // D
        for col in range(4):
            total = wide_tn(silu, rest[1][:, col * D : (col + 1) * D])
            split_store(total, keep_ref, send_ref, core, few, at)
            at += few


def qkv_grad_call(place_ids, x, gq, gc, dp, got, cosine, sine, n, name, proj, ada):
    lead = D // n
    rows = lead
    extra = []
    if proj is not None:
        extra += list(proj)
        rows += lead
    if ada is not None:
        extra += list(ada)
        rows += 4 * (ada[0].shape[1] // n)
    out = whole((n // 2, rows, D))
    shape = jax.ShapeDtypeStruct((n // 2, rows, D), bf16)
    return pl.pallas_call(
        partial(qkv_grad_kernel, lead, proj is not None, ada is not None),
        grid=(1,),
        in_specs=[
            SCALAR,
            whole((PROMPT, D)),
            whole((PROMPT, GROUP)),
            whole((2, HALF, GROUP)),
            whole((2, HALF, GROUP)),
            whole((2, HALF, GROUP)),
            whole((HALF, 128)),
            whole((HALF, 128)),
        ]
        + [whole(e.shape) for e in extra],
        out_specs=[out, out, whole((PROMPT, D))],
        out_shape=[shape, shape, jax.ShapeDtypeStruct((PROMPT, D), bf16)],
        compiler_params=pltpu.CompilerParams(vmem_limit_bytes=VMEM_LIMIT),
        cost_estimate=cost(name),
        name=name,
    )(place_ids, x, gq, gc, dp, got, cosine, sine, *extra)


def start_kernel(spec, place_ref, hid_ref, mask_ref, embed_ref, mods_ref, gain_ref, dmid_ref, *rest):
    n = len(spec)
    grads, pieces = rest[:N_GROUP], rest[N_GROUP : N_GROUP + n]
    gh_ref, stat_ref, ggain_ref, gmask_ref, w_ref, sem = rest[N_GROUP + n :]
    step = pl.program_id(0)

    @pl.when(step == 0)
    def _():
        copies = place(pieces, spec, place_ref, w_ref, sem)
        for copy in copies:
            copy.start()
        ggain_ref[...] = jnp.zeros_like(ggain_ref)
        gmask_ref[...] = jnp.zeros_like(gmask_ref)
        for copy in copies:
            copy.wait()

    g_n = None
    for group in range(N_GROUP):
        for third in range(3):
            at = third * D + group * GROUP
            term = nt(grads[group][:, third * GROUP : (third + 1) * GROUP], w_ref[:, at : at + GROUP])
            g_n = term if g_n is None else g_n + term
    for sub in range(SUB):
        rows = slice(sub * CLEN, (sub + 1) * CLEN)
        row = pl.ds(step * SUB + sub, 1)
        masked = mask_ref[rows, :] > 0.5
        start = jnp.where(masked, embed_ref[...], hid_ref[rows, :].astype(f32))
        normed, inv_std = layer_norm(start)
        scale = 1.0 + mods_ref[row, D : 2 * D]
        grad = g_n[rows]
        along = jnp.sum(grad * normed, 0, keepdims=True)
        ggain_ref[...] += along * scale
        stat_ref[row, 0:D] = jnp.sum(grad, 0, keepdims=True)
        stat_ref[row, D : 2 * D] = along * gain_ref[...]
        d_start = dmid_ref[rows, :] + norm_back(grad * (scale * gain_ref[...]), normed, inv_std)
        gh_ref[rows, :] = jnp.where(masked, 0.0, d_start)
        gmask_ref[...] += jnp.sum(jnp.where(masked, d_start, 0.0), 0, keepdims=True)


def start_call(place_ids, hidden, mask, embed, mods, gain, d_middle, grads, weight):
    n = weight.count
    rows = PROMPT
    return pl.pallas_call(
        partial(start_kernel, weight.spec),
        grid=(rows // TILE,),
        in_specs=[
            SCALAR,
            tile_block(D),
            tile_block(1),
            whole((1, D)),
            whole(mods.shape),
            whole((1, D)),
            tile_block(D),
        ]
        + [tile_block(D)] * N_GROUP
        + [ANY] * n,
        out_specs=[tile_block(D), whole((CONTS, 2 * D)), whole((1, D)), whole((1, D))],
        out_shape=[
            jax.ShapeDtypeStruct((rows, D), f32),
            jax.ShapeDtypeStruct((CONTS, 2 * D), f32),
            jax.ShapeDtypeStruct((1, D), f32),
            jax.ShapeDtypeStruct((1, D), f32),
        ],
        scratch_shapes=[pltpu.VMEM((D, 3 * D), bf16), pltpu.SemaphoreType.DMA],
        compiler_params=pltpu.CompilerParams(vmem_limit_bytes=VMEM_LIMIT),
        cost_estimate=cost("start_grad"),
        name="start_grad",
    )(place_ids, hidden, mask, embed, mods, gain, d_middle, *grads, *weight.arrays)


def pack_kernel(*refs):
    out_ref = refs[-1]
    out_ref[...] = jnp.zeros_like(out_ref)
    for i, ref in enumerate(refs[:-1]):
        out_ref[i : i + 1, 0 : ref.shape[0]] = ref[...].astype(f32).reshape(1, -1)


def pack_call(vectors):
    shape = (8, max(v.shape[0] for v in vectors))
    return pl.pallas_call(
        pack_kernel,
        grid=(1,),
        in_specs=[whole(v.shape) for v in vectors],
        out_specs=whole(shape),
        out_shape=jax.ShapeDtypeStruct(shape, f32),
        name="pack",
    )(*vectors)


def mods_kernel(spec, lengths, times_ref, place_ref, table_ref, hid_ref, mask_ref, *rest):
    n = len(spec)
    pieces, rest = rest[:n], rest[n:]
    count = len(lengths)
    n_row = len(rest) - count - 7
    rows, rest = rest[:n_row], rest[n_row:]
    mods_ref, cond_ref, ada_ref = rest[:3]
    out_refs = rest[3 : 3 + count - 1]
    x_ref, bias_ref, row_ref, sem, row_sem = rest[3 + count - 1 :]
    gain_ref, embed_ref = out_refs[0], out_refs[4]
    copies = place(pieces, spec, place_ref, ada_ref, sem)
    row_copies = [
        pltpu.make_async_copy(row, row_ref.at[place_ref[0] ^ offset], row_sem) for offset, row in enumerate(rows)
    ]
    for copy in row_copies + copies:
        copy.start()
    for block in range(CONTS):
        cond_ref[pl.ds(block, 1), :] = table_ref[pl.ds(times_ref[block], 1), :]
    cond = cond_ref[...]
    silu = (cond / (1.0 + jnp.exp(-cond))).astype(bf16)
    for copy in row_copies:
        copy.wait()
    for shard in range(n_row):
        for i, (length, ref) in enumerate(zip(lengths, (*out_refs, bias_ref))):
            ref[0:1, shard * length : (shard + 1) * length] = row_ref[shard, i : i + 1, 0:length]
    for copy in copies:
        copy.wait()
    mods_ref[...] = nn(silu, ada_ref[...]) + bias_ref[...]

    @pl.loop(0, CONTS)
    def _(block):
        rows = pl.ds(pl.multiple_of(block * CLEN, CLEN), CLEN)
        start = jnp.where(mask_ref[rows, :] > 0.5, embed_ref[...], hid_ref[rows, :].astype(f32))
        normed, _inv = layer_norm(start)
        row = pl.ds(block, 1)
        shift, scale = mods_ref[row, 0:D], mods_ref[row, D : 2 * D]
        x_ref[rows, :] = (normed * gain_ref[...] * (1.0 + scale) + shift).astype(bf16)


def mods_call(times, place_ids, table, hidden, mask, weight, rows, lengths):
    width = weight.arrays[0].shape[1]
    n = len(rows)
    vectors = [(1, n * length) for length in lengths]
    shapes = [(CONTS, width), (CONTS, table.shape[1])]
    return pl.pallas_call(
        partial(mods_kernel, weight.spec, tuple(lengths)),
        in_specs=[SCALAR, SCALAR, whole(table.shape), whole(hidden.shape), whole(mask.shape)] + [ANY] * (weight.count + n),
        out_specs=[whole(s) for s in shapes] + [whole((table.shape[1], width))] + [whole(v) for v in vectors[:-1]] + [whole((PROMPT, D))],
        out_shape=[jax.ShapeDtypeStruct(s, f32) for s in shapes]
        + [jax.ShapeDtypeStruct((table.shape[1], width), bf16)]
        + [jax.ShapeDtypeStruct(v, f32) for v in vectors[:-1]]
        + [jax.ShapeDtypeStruct((PROMPT, D), bf16)],
        grid=(1,),
        scratch_shapes=[
            pltpu.VMEM(vectors[-1], f32),
            pltpu.VMEM((n,) + rows[0].shape, f32),
            pltpu.SemaphoreType.DMA,
            pltpu.SemaphoreType.DMA,
        ],
        compiler_params=pltpu.CompilerParams(vmem_limit_bytes=VMEM_LIMIT),
        cost_estimate=cost("mods"),
        name="mods",
    )(times, place_ids, table, hidden, mask, *weight.arrays, *rows)


def last_kernel(
    lead, time_rows, place_ref, cond_ref, ada_ref, stat1_ref, stat2_ref, ga_ref, gm_ref, bu_ref, bd_ref, me_ref,
    keep_ref, send_ref, small_ref,
):
    core, pair = place_ref[1], place_ref[2]
    cond = cond_ref[...]
    gate = 1.0 / (1.0 + jnp.exp(-cond))
    silu = (cond * gate).astype(bf16).astype(f32)
    stat1, stat2 = stat1_ref[...], stat2_ref[...]
    ada_late = wide_tn(silu, stat1)
    g_silu = wide_nt(stat1, ada_ref[:, : 2 * D]) + wide_nt(stat2, ada_ref[:, 2 * D :])
    g_cond = g_silu * (gate * (1.0 + cond * (1.0 - gate)))
    small_ref[...] = jnp.zeros_like(small_ref)
    at = time_rows
    small_ref[at : at + 1, :] = ga_ref[...]
    small_ref[at + 1 : at + 2, :] = gm_ref[...]
    for i in range(FF // D):
        small_ref[at + 2 + i : at + 3 + i, :] = bu_ref[:, i * D : (i + 1) * D]
    small_ref[at + 6 : at + 7, :] = bd_ref[...]
    for i in range(2):
        small_ref[at + 7 + i : at + 8 + i, :] = jnp.sum(stat1[:, i * D : (i + 1) * D], 0, keepdims=True)
    for i in range(4):
        small_ref[at + 9 + i : at + 10 + i, :] = jnp.sum(stat2[:, i * D : (i + 1) * D], 0, keepdims=True)
    small_ref[at + 13 : at + 14, :] = me_ref[...]
    half = CONTS // 2
    prompt = jnp.sum(g_cond[:half], 0, keepdims=True)
    values = [prompt] + [g_cond[half + i : half + i + 1] for i in range(half)]
    base = pair * (CONTS + 1)
    where_to = [base] + [base + 1 + core * half + i for i in range(half)]
    for lane in range(D // 128):
        row = lax.broadcasted_iota(jnp.int32, (time_rows, 128), 0) + lane * time_rows
        placed = jnp.zeros((time_rows, 128), f32)
        for index, value in zip(where_to, values):
            placed = placed + jnp.where(row == index, value, 0.0)
        small_ref[0:time_rows, lane * 128 : (lane + 1) * 128] = placed
    small = small_ref[...]
    high = small.astype(bf16)
    rows = small.shape[0]
    low = (small[time_rows:] - high[time_rows:].astype(f32)).astype(bf16)
    for j in range(keep_ref.shape[0]):
        for col in range(2):
            split_store(ada_late[:, col * D : (col + 1) * D], keep_ref, send_ref, core, lead, col * lead)
        row = 2 * lead
        for ref in (keep_ref, send_ref):
            ref[j, row : row + rows, :] = high
            ref[j, row + rows : row + rows + 16, :] = low


def last_call(place_ids, cond, ada, stat1, stat2, vectors, n, time_rows):
    lead = ada.shape[0] // n
    rows = 16 + time_rows
    args = (cond, ada, stat1, stat2) + tuple(vectors)
    out = whole((n // 2, 2 * lead + rows + 16, D))
    shape = jax.ShapeDtypeStruct((n // 2, 2 * lead + rows + 16, D), bf16)
    return pl.pallas_call(
        partial(last_kernel, lead, time_rows),
        grid=(1,),
        in_specs=[SCALAR] + [whole(a.shape) for a in args],
        out_specs=[out, out],
        out_shape=[shape, shape],
        scratch_shapes=[pltpu.VMEM((rows, D), f32)],
        compiler_params=pltpu.CompilerParams(vmem_limit_bytes=VMEM_LIMIT),
        cost_estimate=cost("last"),
        name="last",
    )(place_ids, *args)


def swap(value, axis, mask):
    pairs = [(source, source ^ mask) for source in range(lax.axis_size(axis))]
    return lax.ppermute(value, axis, pairs)


def gather_far(piece):
    pieces = {0: piece}
    mask = lax.axis_size("shard") // 2
    while mask > 1:
        for offset in list(pieces):
            pieces[offset | mask] = swap(pieces[offset], "shard", mask)
        mask //= 2
    return pieces


def gather_near(pieces):
    pieces = dict(pieces)
    for offset in list(pieces):
        pieces[offset | 1] = swap(pieces[offset], "shard", 1)
    return [pieces[offset] for offset in range(len(pieces))]


def sides():
    rep = lax.axis_index("rep")
    return rep % 2, rep % 4


def far_parts(piece, split=1):
    rows = piece.shape[0] // split
    if split == 1 or rows % 16:
        return 1, gather_far(piece)
    side = sides()[0 if split == 2 else 1]
    found = gather_far(lax.dynamic_slice_in_dim(piece, side * rows, rows, 0))
    found[0] = piece
    return split, found


def far_weight(split, found, tie=None):
    if tie is not None:
        found, _ = lax.optimization_barrier((found, tie))
    spec, arrays = [], []
    for offset, part in found.items():
        if split == 1 or not offset:
            spec.append((offset, 1, 0))
            arrays.append(part)
            continue
        spec += [(offset, split, code) for code in range(split)]
        arrays += [part] + [swap(part, "rep", code) for code in range(1, split)]
    return Weight(spec, arrays)


def near_weight(far):
    spec, arrays = list(far.spec), list(far.arrays)
    for (offset, split, code), part in zip(far.spec, far.arrays):
        spec.append((offset | 1, split, code))
        arrays.append(swap(part, "shard", 1))
    if all(part.shape[0] % 16 == 0 for part in arrays):
        return Weight(spec, arrays)
    mine = lax.axis_index("shard")
    rows = arrays[0].shape[0]
    out = jnp.zeros((rows * len(arrays),) + arrays[0].shape[1:], arrays[0].dtype)
    for (offset, _split, _code), part in zip(spec, arrays):
        out = lax.dynamic_update_slice_in_dim(out, part, (mine ^ offset) * rows, 0)
    return Weight([(None, 1, 0)], [out])


def add_plain(left, right):
    return left.astype(f32) + right.astype(f32)


def add_packed(left, right):
    rows = left.shape[-2] - 16
    total = add_plain(left[..., :rows, :], right[..., :rows, :])
    rest = add_plain(left[..., rows:, :], right[..., rows:, :])
    return jnp.concatenate([total[..., : rows - 16, :], total[..., rows - 16 :, :] + rest], -2)


def pack_plain(value):
    return value.astype(bf16)


def pack_packed(value):
    high = value.astype(bf16)
    low = value[..., -16:, :] - high[..., -16:, :].astype(f32)
    return jnp.concatenate([high, low.astype(bf16)], -2)


def reduce_chain(keep, send, steps, add=add_plain, pack=pack_plain):
    mine, rep = lax.axis_index("shard"), lax.axis_index("rep")

    def parts(values, axis, bit):
        kept, sent = [
            pack(add(*(lax.dynamic_index_in_dim(v, b, axis, False) for v in values))) for b in (bit, 1 - bit)
        ]
        return kept, sent

    got = yield send, swap(send, "shard", 1)
    terms = (keep, got)
    mask = 2
    while mask < lax.axis_size("shard"):
        halves = [t.reshape((-1, 2) + t.shape[1:]) for t in terms]
        kept, send = parts(halves, 1, (mine // mask) % 2)
        got = yield send, swap(send, "shard", mask)
        terms = (kept, got)
        mask *= 2
    terms = tuple(t[0] for t in terms)
    joined = None
    more = range(3, lax.axis_size("rep").bit_length() - 1)
    steps = [(bit, "all") for bit in more] + list(steps)
    for at, kind in steps:
        bit = (rep >> at) % 2
        if kind == "split":
            kept, send = parts([t.reshape(2, -1, t.shape[-1]) for t in terms], 0, bit)
            got = yield send, swap(send, "rep", 1 << at)
            terms = (kept, got)
            continue
        value = pack(add(*terms)) if joined is None else joined
        got = yield value, swap(value, "rep", 1 << at)
        if kind == "join":
            last = (value, got, at)
            first, second = jnp.where(bit == 0, value, got), jnp.where(bit == 0, got, value)
            joined = jnp.concatenate([first, second], 0)
        else:
            last = (value, got, None)
            terms, joined = (value, got), None
    return last


class Schedule:
    def __init__(self, ids, rows):
        self.ids = ids
        self.chains = {}
        self.sent = {}
        self.done = {}
        self.final = {}
        self.rows = rows

    def begin(self, name, keep, send, *how):
        chain = reduce_chain(keep, send, *how)
        self.chains[name] = chain
        _sent, self.sent[name] = next(chain)

    def start(self, name, keep, send, names):
        (send,) = self.sync(*(other for other in names if other != name), after=(send,))
        self.begin(name, keep, send, ROUTES[name])
        self.sync(*(other for other in names if other == name), after=(send,))

    def sync(self, *names, after=()):
        for name in names or (None,):
            if name is not None and name not in self.sent:
                continue
            got = self.sent.pop(name, None)
            self.ids, got, after = lax.optimization_barrier((self.ids, got, tuple(after)))
            if got is None:
                continue
            try:
                sent, self.sent[name] = self.chains[name].send(got)
                self.ids, _ = lax.optimization_barrier((self.ids, sent))
            except StopIteration as stop:
                self.done[name] = stop.value
                if name in self.rows:
                    self.final[name] = finish_blocks(stop.value, *self.rows[name])
        return after

    def finish(self, *names):
        for name in names:
            self.sync(name)
        while self.sent:
            self.sync(next(iter(self.sent)))


def add_two(a_ref, b_ref):
    return a_ref[...].astype(f32) + b_ref[...].astype(f32)


def bit_of(place_ref, at):
    return place_ref[4] // (1 << at) % 2


def whole_sum(place_ref, a_ref, b_ref, at):
    if at is None:
        return add_two(a_ref, b_ref)
    first, second = a_ref[...].astype(f32), b_ref[...].astype(f32)
    swapped = bit_of(place_ref, at) == 1
    return jnp.concatenate([jnp.where(swapped, second, first), jnp.where(swapped, first, second)], 0)


def finish_blocks(result, rows, wide):
    value, got, at = result
    if at is None:
        total = value.astype(f32) + got.astype(f32)
    else:
        bit = (lax.axis_index("rep") >> at) % 2
        first, second = jnp.where(bit == 0, value, got), jnp.where(bit == 0, got, value)
        total = jnp.concatenate([first, second], 0).astype(f32)
    if not wide:
        return total
    return jnp.concatenate([total[i : i + rows] for i in range(0, total.shape[0], rows)], 1)


def finish_last_kernel(
    n, lead, time_rows, few, ats, place_ref, ids_ref, a_ref, b_ref, *refs
):
    mine = place_ref[0]
    groups, (qkv_ref, proj_ref, ada_ref, time_ref, *out_refs) = refs[: 2 * N_GROUP], refs[2 * N_GROUP :]
    totals = [whole_sum(place_ref, groups[2 * i], groups[2 * i + 1], at) for i, at in enumerate(ats)]
    for group, total in enumerate(totals):
        for third in range(3):
            col = third * D + group * GROUP
            qkv_ref[:, col : col + GROUP] = total[:lead, third * GROUP : (third + 1) * GROUP]
    proj_ref[...] = totals[1][lead : 2 * lead]
    early = totals[0]
    for i in range(2):
        rows = slice(i * few, (i + 1) * few)
        ada_ref[:, i * D : (i + 1) * D] = add_two(a_ref.at[rows], b_ref.at[rows])
    for i in range(4):
        ada_ref[:, (2 + i) * D : (3 + i) * D] = early[lead + i * few : lead + (i + 1) * few]
    at = 2 * few
    times = add_two(a_ref.at[at : at + time_rows], b_ref.at[at : at + time_rows])
    times = jnp.concatenate([times[:, i * 128 : (i + 1) * 128] for i in range(D // 128)], 0)
    steps = lax.broadcasted_iota(jnp.int32, (STEPS, times.shape[0]), 0)
    hot = jnp.where(steps == ids_ref[...], 1.0, 0.0).astype(f32)
    time_ref[...] = exact(hot, times, ((1,), (0,)))
    at += time_rows
    high = add_two(a_ref.at[at : at + 16], b_ref.at[at : at + 16])
    small = high + add_two(a_ref.at[at + 16 : at + 32], b_ref.at[at + 16 : at + 32])
    first = 0
    for ref, count in zip(out_refs, (1, 1, 4, 1, 6, 1)):
        flat = jnp.concatenate([small[first + i : first + i + 1] for i in range(count)], 1)
        size = count * D // n
        share = flat[:, 0:size]
        for shard in range(1, n):
            share = jnp.where(mine == shard, flat[:, shard * size : (shard + 1) * size], share)
        ref[...] = share.reshape(size)
        first += count


def finish_last(place_ids, ids, last, results, n, time_rows, few):
    lead = D // n
    sizes = [(count * D // n,) for count in (1, 1, 4, 1, 6, 1)]
    shapes = [(lead, 3 * D), (lead, D), (few, 6 * D), (STEPS, 128)] + sizes
    arrays = [ids, *last[:2]] + [a for result in results for a in result[:2]]
    ats = tuple(result[2] for result in results)
    return pl.pallas_call(
        partial(finish_last_kernel, n, lead, time_rows, few, ats),
        grid=(1,),
        in_specs=[SCALAR] + [whole(a.shape) for a in arrays],
        out_specs=[whole(s) for s in shapes],
        out_shape=[jax.ShapeDtypeStruct(s, f32) for s in shapes],
        cost_estimate=cost("finish_last"),
        compiler_params=pltpu.CompilerParams(vmem_limit_bytes=VMEM_LIMIT),
        name="finish_last",
    )(place_ids, *arrays)


ROUTES = {'down': ((0, 'split'), (1, 'all'), (2, 'all'), (0, 'join')),
 'last': ((1, 'all'), (0, 'all'), (2, 'all')),
 'qkv0': ((1, 'split'), (0, 'all'), (2, 'all'), (1, 'join')),
 'qkv1': ((0, 'split'), (1, 'split'), (2, 'all'), (1, 'join'), (0, 'join')),
 'qkv2': ((1, 'split'), (0, 'all'), (2, 'all'), (1, 'join')),
 'up': ((0, 'split'), (1, 'all'), (2, 'all'), (0, 'join'))}
SYNCS = (('up', 'down'),
 ('down',),
 ('up', 'down'),
 (),
 ('up', 'qkv0', 'down'),
 (),
 ('up', 'qkv0', 'qkv1', 'down', 'qkv2'),
 ('qkv0', 'qkv1'),
 ('qkv2',
  'up',
  'qkv0',
  'last',
  'qkv1',
  'qkv2',
  'last',
  'qkv1',
  'up',
  'qkv0',
  'qkv2',
  'last',
  'qkv1',
  'qkv0',
  'last',
  'qkv2',
  'qkv1',
  'qkv1',
  'qkv2',
  'last'),
 ('down',))


def on_device(
    hidden_in,
    mask_ids,
    time_ids,
    time_table,
    w_qkv,
    w_proj,
    w_up,
    w_down,
    w_ada,
    gain_attn,
    gain_mlp,
    bias_up,
    bias_down,
    bias_ada,
    mask_embed,
    cotangent,
):
    n = lax.axis_size("shard")
    mine = lax.axis_index("shard")
    core = mine % 2
    pair = (lax.axis_index("rep") * n + mine) // 2
    ids = jnp.stack([mine, core, pair, *sides()]).astype(jnp.int32)
    barrier = lax.optimization_barrier

    vectors = (gain_attn, gain_mlp, bias_up, bias_down, mask_embed, bias_ada)
    lengths = [v.shape[0] for v in vectors]
    row_far = gather_far(pack_call(vectors))
    local = jnp.arange(PROMPT, dtype=jnp.int32)
    positions = jnp.where(local < HALF, core * HALF + local, PROMPT + local % CLEN).astype(f32)
    freqs = 10000.0 ** (-(2.0 * jnp.arange(HDIM // 2, dtype=f32)) / HDIM)
    lanes = jnp.tile(freqs, 4)
    angles = positions[:, None] * lanes[None, :]
    sign = jnp.where(jnp.arange(128) % HDIM < HDIM // 2, -1.0, 1.0).astype(f32)
    cosine, sine = jnp.cos(angles), jnp.sin(angles) * sign[None, :]
    mask = (mask_ids == 1).astype(f32)[:, None]
    ada_far = far_weight(*far_parts(w_ada), (cosine, sine, mask))
    qkv_far = far_weight(*far_parts(w_qkv, 4))
    ada_weight = near_weight(ada_far)
    rows = gather_near(row_far)
    (proj_own, up_own, down_own), _ = barrier(((w_proj, w_up, w_down), ada_far.arrays))
    up_split, up_found = far_parts(up_own, 4)
    proj_far = far_weight(*far_parts(proj_own))
    down_split, down_found = far_parts(down_own, 2)

    block = jnp.arange(CONTS, dtype=jnp.int32)
    seg = jnp.where(block < CONTS // 2, 0, 1 + core * (CONTS // 2) + block - CONTS // 2)
    my_times = lax.dynamic_slice_in_dim(time_ids, pair, 1, 0)
    times = jnp.sum(jnp.where(seg[:, None] == jnp.arange(CONTS + 1, dtype=jnp.int32)[None], my_times, 0), 1)
    mods, cond, ada_mat, attn_gain, mlp_gain, up_bias, down_bias, embed, x = mods_call(
        times, ids, time_table, hidden_in, mask, ada_weight, rows, lengths
    )

    qkv_weight = near_weight(qkv_far.tied(mods))
    q, kvp, kvc = qkv_call(ids, x, cosine, sine, qkv_weight)
    kvp, up_found = barrier((kvp, up_found))
    kvr = swap(kvp, "shard", 1)
    up_far = far_weight(up_split, up_found)
    early = attn_fwd(0, 4, q, kvp, kvc, kvr)
    early, up_far.arrays, proj_far.arrays, down_found = barrier((early, up_far.arrays, proj_far.arrays, down_found))
    proj_weight = near_weight(proj_far.tied(early))
    up_weight = near_weight(up_far.tied(early))
    early, _ = barrier((early, proj_weight.arrays))
    down_far = far_weight(down_split, down_found)
    soon = near_weight(Weight(down_far.spec[:2], down_far.arrays[:2]))
    late = Weight(down_far.spec[2:], down_far.arrays[2:])
    attn_o, lse = attn_fwd(4, PAIRS - 4, q, kvp, kvc, kvr, early)
    attn_o, late.arrays = barrier((attn_o, late.arrays))
    down_weight = near_weight(late.tied(attn_o))
    down_weight = Weight(soon.spec + down_weight.spec, soon.arrays + down_weight.arrays)
    attn_proj, middle, x_mlp, act, g_pre, g_mlp, g_bias_up, g_bias_down = up_call(
        ids, attn_o, hidden_in, mask, embed, mods, mlp_gain, up_bias, cotangent, proj_weight, up_weight, down_weight
    )
    plan = Schedule(ids, {"down": (FF // n // 2, False), "up": (D // n, True)})
    down_keep, down_send = down_grad_any(plan.ids, act, g_mlp, n)
    plan.begin("down", down_keep, down_send, ROUTES["down"])
    plan.sync(after=(down_keep,))
    up_keep, up_send = wgrad_call(plan.ids, x_mlp, g_pre, n, "up_grad")
    plan.start("up", up_keep, up_send, SYNCS[9])
    block_out, d_middle, g_att, g_o, stat2, g_gain_mlp = down_call(
        plan.ids, act, g_pre, middle, attn_proj, cotangent, mods, mlp_gain, down_bias, proj_weight, up_weight, down_weight
    )
    plan.sync(*SYNCS[0], after=(g_o,))
    parts, others = [], []

    def backward(group, names):
        gq, gc, dp, dr = attn_bwd(plan.ids, group, q, kvp, kvc, kvr, g_o, lse, cosine, sine)
        parts.append((gq, gc, dp))
        (dr,) = plan.sync(*names, after=(dr,))
        others.append(swap(dr, "shard", 1))

    grads = []

    def weight(group, proj, ada, names):
        keep, send, total = qkv_grad_call(
            plan.ids, x, *parts[group], others[group], cosine, sine, n, f"qkv_grad{group}", proj, ada
        )
        grads.append(total)
        plan.start(f"qkv{group}", keep, send, names)

    backward(0, SYNCS[1])
    backward(1, SYNCS[2])
    weight(0, None, (cond, stat2), SYNCS[3])
    backward(2, SYNCS[4])
    weight(1, (attn_o, g_att), None, SYNCS[5])
    weight(2, None, None, SYNCS[6])
    grad_hidden, stat1, g_gain_attn, g_mask = start_call(
        plan.ids, hidden_in, mask, embed, mods, attn_gain, d_middle, grads, qkv_weight
    )
    plan.sync(*SYNCS[7], after=(stat1,))
    time_rows = -(-time_ids.size // 6 // 8) * 8
    vector_grads = (g_gain_attn, g_gain_mlp, g_bias_up, g_bias_down, g_mask)
    keep, send = last_call(plan.ids, cond, ada_mat, stat1, stat2, vector_grads, n, time_rows)
    plan.begin("last", keep, send, ROUTES["last"], add_packed, pack_packed)
    plan.finish(*SYNCS[8])

    done = plan.done
    few = w_ada.shape[0]
    flat_ids = time_ids.reshape(1, -1)
    flat_ids = jnp.pad(flat_ids, ((0, 0), (0, 6 * time_rows - flat_ids.shape[1])), constant_values=-1)
    results = [done[f"qkv{g}"] for g in range(N_GROUP)]
    grad_qkv, grad_proj, grad_ada, grad_time, *shares = finish_last(
        plan.ids, flat_ids, done["last"], results, n, time_rows, few
    )
    return (block_out, grad_hidden, grad_time, grad_qkv, grad_proj, plan.final["up"], plan.final["down"], grad_ada, *shares)


def solution(mesh):
    in_specs = (
        P(("rep", "shard"), None),
        P(("rep", "shard")),
        P(),
        P(),
        P("shard", None),
        P("shard", None),
        P("shard", None),
        P("shard", None),
        P("shard", None),
        P("shard"),
        P("shard"),
        P("shard"),
        P("shard"),
        P("shard"),
        P("shard"),
        P(("rep", "shard"), None),
    )
    out_specs = (
        P(("rep", "shard"), None),
        P(("rep", "shard"), None),
        P(),
        P("shard", None),
        P("shard", None),
        P("shard", None),
        P("shard", None),
        P("shard", None),
        P("shard"),
        P("shard"),
        P("shard"),
        P("shard"),
        P("shard"),
        P("shard"),
    )
    return jax.shard_map(
        on_device, mesh=mesh, in_specs=in_specs, out_specs=out_specs, check_vma=False
    )
```
